256 devices in a mesh: det: 4 (over x_hi, core), tm: 64 (over y, z, x_lo).
Axes of the slice: x: 4 (x_hi: 2, x_lo: 2; x = x_hi * 2 + x_lo), y: 4, z: 8, core: 2. Of those that a mesh axis runs over, the one named last changes fastest.
Arguments:
- sky_map: bfloat16 [128, 3, 128, 128], P('tm', None, 'det'), may hold values from -6 to 6
- tile_home: int32 [128], replicated, may hold values from 0 to 127, as said below
- piece_tiles: int32 [4, 64, 32], P('det', 'tm'), may hold values from 0 to 127, as said below
- run_slot: int32 [32, 1024], P('det', 'tm'), may hold values from 0 to 31
- hit_row: int32 [32, 131072], P('det', 'tm'), may hold values from 0 to 126
- hit_col: int32 [32, 131072], P('det', 'tm'), may hold values from 0 to 126
- frac_row: bfloat16 [32, 131072], P('det', 'tm'), may hold values from 0 to 1
- frac_col: bfloat16 [32, 131072], P('det', 'tm'), may hold values from 0 to 1
- angle: float32 [32, 131072], P('det', 'tm'), may hold values from -3.140625 to 3.140625
- noise_coef: float32 [32, 1025], P('det'), may hold values from -0.3 to 0.3
Outputs:
- normal_map: float32 [128, 3, 128, 128], P('tm', None, 'det')
The draws below stay inside these ranges and needn't reach their ends.
Inputs may be any that keep to these rules, and one draw needn't show every extreme that they name: A permutation: tile g lies in row tile_home[g] of sky_map. `piece_tiles`: the 32 tiles listed by one piece are distinct, and at most 1 of them lie in rows of one index of tm (rows o * 2 to o * 2 + 1 of sky_map); every piece has exactly 1 tile in each index of tm that it reads from.
All inputs are finite; a program needn't handle non-finite values.
Results may differ from the reference program's by a relative error of at most 0.0048.
Values may be sent and summed in bfloat16 or wider, within the bound.
A program may use at most 128 MiB of HBM per device.

```python
import jax
import jax.numpy as jnp
from jax import lax

PIX = 128
HALF_BAND = 1024
LISTED = 32
DET_DEV = 8
TIME_DEV = 2048
RUN = 128
TILE_DEV = 2
DETECTORS = 32
SAMPLES = 131072
TILES = 128
CAP = 1
N_DET = 4
N_TM = 64


def layout(key):
    base_key = jax.random.fold_in(key, 11)
    home_key, hot_key, owner_key, slot_key = jax.random.split(base_key, 4)
    tile_home = jax.random.permutation(home_key, TILES).astype(jnp.int32)
    tile_at = jnp.argsort(tile_home).astype(jnp.int32)
    hot_total = max(1, N_TM // 8)
    hot_owner = (jax.random.permutation(hot_key, N_TM) < hot_total).astype(jnp.int32)
    piece_total = N_DET * N_TM
    owners_used = LISTED // CAP
    owner_noise = jax.random.randint(owner_key, (piece_total, N_TM), 0, 1000)
    owner_score = (owner_noise + 600 * hot_owner[None, :]) * N_TM + jnp.arange(N_TM, dtype=jnp.int32)[None, :]
    owner_pick = lax.top_k(owner_score.astype(jnp.int32), owners_used)[1]
    slot_noise = jax.random.randint(slot_key, (piece_total, owners_used, TILE_DEV), 0, 1000)
    slot_score = slot_noise * TILE_DEV + jnp.arange(TILE_DEV, dtype=jnp.int32)
    slot_pick = lax.top_k(slot_score.astype(jnp.int32), CAP)[1]
    rows_read = owner_pick[:, :, None] * TILE_DEV + slot_pick
    piece_tiles = tile_at[rows_read.reshape(piece_total, LISTED)]
    return (tile_home, piece_tiles.reshape(N_DET, N_TM, LISTED).astype(jnp.int32))


def draw_tile_home(key, part):
    return layout(key)[0]


def draw_piece_tiles(key, part):
    return layout(key)[1]


def touch_ends(values, key, smallest, top_value):
    longest = values.shape.index(max(values.shape))
    spots = []
    for shift in (0, 1):
        where = [jax.random.randint(jax.random.fold_in(key, axis), (), 0, length) for axis, length in enumerate(values.shape)]
        where[longest] = (where[longest] + shift) % values.shape[longest]
        spots.append(tuple(where))
    return values.at[spots[0]].set(smallest).at[spots[1]].set(top_value)


def block_scale(own_key, shape, pieces, smallest, top_value):
    gain, own = 1.0, jax.random.fold_in(own_key, 6)
    for dim, shards_of in pieces:
        steps = jnp.exp(jax.random.uniform(jax.random.fold_in(own, dim), (shards_of,), jnp.float32, smallest / len(pieces), top_value / len(pieces)))
        gain = gain * jnp.repeat(steps, shape[dim] // shards_of).reshape([-1 if axis == dim else 1 for axis in range(len(shape))])
    return gain


def gaussian(own_key, shape, scale, limit, cuts=(), kind=jnp.bfloat16):
    result = scale * jax.random.normal(own_key, shape, jnp.float32)
    if cuts:
        result = result * block_scale(own_key, shape, cuts, -0.22, 0.18)
    return jnp.clip(result, -limit, limit).astype(kind)


def setup_inputs(seed: int = 0) -> dict:
    key_of = jax.random.split(jax.random.key(seed), 11)
    return {
        "sky_map": gaussian(key_of[0], (TILES, 3, PIX, PIX), 1.0, 6.0, ((0, 64), (2, 4))),
        "tile_home": draw_tile_home(jax.random.fold_in(key_of[10], 71), 0),
        "piece_tiles": draw_piece_tiles(jax.random.fold_in(key_of[10], 71), 0),
        "run_slot": touch_ends(jax.random.randint(key_of[3], (DETECTORS, SAMPLES // RUN), 0, LISTED), jax.random.fold_in(key_of[3], 1), 0, LISTED - 1).astype(jnp.int32),
        "hit_row": touch_ends(jax.random.randint(key_of[4], (DETECTORS, SAMPLES), 0, PIX - 1), jax.random.fold_in(key_of[4], 1), 0, (PIX - 1) - 1).astype(jnp.int32),
        "hit_col": touch_ends(jax.random.randint(key_of[5], (DETECTORS, SAMPLES), 0, PIX - 1), jax.random.fold_in(key_of[5], 1), 0, (PIX - 1) - 1).astype(jnp.int32),
        "frac_row": jnp.clip(1.0 * jax.random.uniform(key_of[6], (DETECTORS, SAMPLES), jnp.float32) ** block_scale(key_of[6], (DETECTORS, SAMPLES), ((0, 4), (1, 64)), -0.2, 0.2), 0.0, 1.0).astype(jnp.bfloat16),
        "frac_col": jnp.clip(1.0 * jax.random.uniform(key_of[7], (DETECTORS, SAMPLES), jnp.float32) ** block_scale(key_of[7], (DETECTORS, SAMPLES), ((0, 4), (1, 64)), -0.2, 0.2), 0.0, 1.0).astype(jnp.bfloat16),
        "angle": jnp.clip(jax.random.uniform(key_of[8], (DETECTORS, SAMPLES), jnp.float32, -3.140625, 3.140625), -3.140625, 3.140625),
        "noise_coef": gaussian(key_of[9], (DETECTORS, HALF_BAND + 1), 0.05, 0.3, ((0, 4),), jnp.float32),
    }


def rounded(values):
    return lax.optimization_barrier(values.astype(jnp.bfloat16)).astype(jnp.float32)


def reference(sky_map, tile_home, piece_tiles, run_slot, hit_row, hit_col, frac_row, frac_col, angle, noise_coef):
    position = tile_home[piece_tiles]
    det_group = (jnp.arange(DETECTORS) // DET_DEV).astype(jnp.int32)
    run_total = SAMPLES // RUN
    time_piece = (jnp.arange(run_total) * RUN // TIME_DEV).astype(jnp.int32)
    run_position = position[det_group[:, None], time_piece[None, :], run_slot]
    run_tile = jnp.repeat(run_position, RUN, axis=1).astype(jnp.int32)
    row_low = rounded(1.0 - frac_row.astype(jnp.float32))
    col_low = rounded(1.0 - frac_col.astype(jnp.float32))
    row_high = frac_row.astype(jnp.float32)
    col_high = frac_col.astype(jnp.float32)
    twice = 2.0 * angle.astype(jnp.float32)
    response = [jnp.ones_like(twice), jnp.cos(twice), jnp.sin(twice)]
    offset = (run_tile * (PIX * PIX) + hit_row * PIX + hit_col).astype(jnp.int32)
    sky_flat = sky_map.astype(jnp.float32).reshape(TILES, 3, PIX * PIX)
    signal = jnp.zeros((DETECTORS, SAMPLES), jnp.float32)
    for stokes in range(3):
        plane = sky_flat[:, stokes].reshape(-1)
        inner = row_low * (col_low * plane[offset] + col_high * plane[offset + 1])
        inner = inner + row_high * (col_low * plane[offset + PIX] + col_high * plane[offset + PIX + 1])
        signal = signal + response[stokes] * inner
    weights = jnp.concatenate([noise_coef[:, :1] + 1.0, noise_coef[:, 1:]], axis=1)
    kernel = jnp.concatenate([weights[:, ::-1], weights[:, 1:]], axis=1)
    length = SAMPLES + 2 * HALF_BAND
    spectrum = jnp.fft.rfft(signal, n=length, axis=1) * jnp.fft.rfft(kernel, n=length, axis=1)
    full_line = jnp.fft.irfft(spectrum, n=length, axis=1)
    filtered = full_line[:, HALF_BAND:HALF_BAND + SAMPLES]
    planes = []
    for stokes in range(3):
        scaled = response[stokes] * filtered
        low_part = rounded(scaled * row_low)
        high_part = rounded(scaled * row_high)
        summed = jnp.zeros((TILES * PIX * PIX,), jnp.float32)
        summed = summed.at[offset].add(low_part * col_low)
        summed = summed.at[offset + 1].add(low_part * col_high)
        summed = summed.at[offset + PIX].add(high_part * col_low)
        summed = summed.at[offset + PIX + 1].add(high_part * col_high)
        planes.append(summed.reshape(TILES, PIX, PIX))
    return jnp.stack(planes, axis=1)
```

```python
import functools

import jax
import jax.numpy as jnp
from jax import lax
from jax.experimental import pallas as pl
from jax.experimental.pallas import tpu as pltpu
from jax.sharding import PartitionSpec as P

MESH = pl.DeviceIdType.MESH
NY, NZ, NX = 4, 8, 2
NB = NY * NX
DET, RUNS, LANE = 8, 16, 128
PIX = 128
STRIP = 32
LISTED = 32
REACH = 8
UNROLL = 4
PIECE_RUNS = DET * RUNS
ALL_RUNS = NZ * PIECE_RUNS
ANY = pl.BlockSpec(memory_space=pl.ANY)
VM = pl.BlockSpec(memory_space=pltpu.VMEM)
SM = pl.BlockSpec(memory_space=pltpu.SMEM)
DMA = pltpu.SemaphoreType.DMA
PEERS = [(dy, dx) for dy in range(NY) for dx in range(NX) if (dy, dx) != (0, 0)]


def place():
    det, tm = lax.axis_index("det"), lax.axis_index("tm")
    y, z, x = tm // (NZ * NX), (tm // NX) % NZ, tm % NX
    return det, tm, y, z, x


def tm_of(y, z, x):
    return (y * NZ + z) * NX + x


def core_of(det):
    return det + 1 - 2 * (det % 2)


def hi_of(det):
    return (det + 2) % 4


def greet(peers):
    barrier = pltpu.get_barrier_semaphore()
    for peer in peers:
        pl.semaphore_signal(barrier, inc=1, device_id=peer, device_id_type=MESH)
    pl.semaphore_wait(barrier, len(peers))


def remote(src, dst, send, recv, peer):
    return pltpu.make_async_remote_copy(
        src_ref=src, dst_ref=dst, send_sem=send, recv_sem=recv, device_id=peer, device_id_type=MESH
    )


def gather_kernel(
    q_ref, f_ref, w_ref, p_ref, tiles_ref, fo_ref, wo_ref, po_ref,
    q_own, f_own, w_own, p_own, load_sem, store_sem,
    ring_send, ring_recv, tile_send, tile_recv, core_send, core_recv, hi_send, hi_recv,
):
    det, tm, y, z, x = place()
    mine = y * NX + x
    partner, across = core_of(det), hi_of(det)
    right, left = tm_of(y, (z + 1) % NZ, x), tm_of(y, (z + NZ - 1) % NZ, x)

    def strip(slot, d):
        return tiles_ref.at[slot, :, :, pl.ds(d * STRIP, STRIP), :]

    def peer_slot(dy, dx, sign):
        return ((y + sign * dy + NY) % NY), ((x + dx) % NX)

    ins = (f_ref, w_ref, p_ref)
    outs = (fo_ref, wo_ref, po_ref)
    owns = (f_own, w_own, p_own)
    loads = [pltpu.make_async_copy(a, b, load_sem.at[i]) for i, (a, b) in enumerate(zip(ins + (q_ref,), owns + (q_own,)))]
    for copy in loads:
        copy.start()

    far = [tm_of(*(lambda s: (s[0], z, s[1]))(peer_slot(dy, dx, 1))) for dy, dx in PEERS]
    greet(
        [(det, right), (det, left), (partner, tm), (across, tm)]
        + [(det, t) for t in far]
    )

    reach = (NZ // 2, NZ // 2 - 1)

    def ring(direction, step, part):
        slot = (z + NZ - step) % NZ if direction == 0 else (z + step) % NZ
        src = ins[part] if step == 0 else outs[part].at[slot]
        return remote(
            src, outs[part].at[slot], ring_send.at[direction, step, part], ring_recv.at[direction, step, part],
            (det, right if direction == 0 else left),
        )

    def ring_in(direction, step, part):
        slot = (z + NZ - step - 1) % NZ if direction == 0 else (z + step + 1) % NZ
        return remote(
            ins[part], outs[part].at[slot], ring_send.at[direction, step, part], ring_recv.at[direction, step, part],
            (det, right if direction == 0 else left),
        )

    started = []

    def start(copy):
        copy.start()
        started.append(copy)

    start(remote(q_ref, strip(mine, det), hi_send, hi_recv, (across, tm)))
    for direction in (0, 1):
        for part in range(3):
            start(ring(direction, 0, part))
    for k, (dy, dx) in enumerate(PEERS):
        start(remote(q_ref, strip(mine, det), tile_send.at[0, k], tile_recv.at[0, k], (det, far[k])))
    start(remote(q_ref, strip(mine, det), core_send.at[0, NB - 1], core_recv.at[0, NB - 1], (partner, tm)))
    stores = []
    for i, copy in enumerate(loads):
        copy.wait()
        dst = outs[i].at[z] if i < 3 else strip(mine, det)
        store = pltpu.make_async_copy((owns + (q_own,))[i], dst, store_sem.at[i])
        store.start()
        stores.append(store)

    remote(q_ref, strip(mine, across), hi_send, hi_recv, (across, tm)).wait_recv()
    for k, (dy, dx) in enumerate(PEERS):
        start(remote(strip(mine, across), strip(mine, across), tile_send.at[1, k], tile_recv.at[1, k], (det, far[k])))
    start(
        remote(strip(mine, across), strip(mine, across), core_send.at[1, NB - 1], core_recv.at[1, NB - 1], (partner, tm))
    )

    def ring_step(step):
        for part in range(3):
            for direction in (0, 1):
                if step < reach[direction]:
                    ring_in(direction, step, part).wait_recv()
                    if step + 1 < reach[direction]:
                        start(ring(direction, step + 1, part))

    def tile_step(half):
        d = det if half == 0 else across
        for k, (dy, dx) in enumerate(PEERS):
            yy, xx = peer_slot(dy, dx, -1)
            slot = yy * NX + xx
            remote(q_ref, strip(slot, d), tile_send.at[half, k], tile_recv.at[half, k], (det, far[k])).wait_recv()
            start(remote(strip(slot, d), strip(slot, d), core_send.at[half, k], core_recv.at[half, k], (partner, tm)))

    ring_step(0)
    tile_step(0)
    ring_step(1)
    tile_step(1)
    ring_step(2)
    ring_step(3)
    for half in (0, 1):
        d = partner if half == 0 else hi_of(partner)
        for k in range(NB):
            if k < NB - 1:
                yy, xx = peer_slot(*PEERS[k], -1)
                slot = yy * NX + xx
            else:
                slot = mine
            remote(q_ref, strip(slot, d), core_send.at[half, k], core_recv.at[half, k], (partner, tm)).wait_recv()
    for store in stores:
        store.wait()
    for copy in started:
        copy.wait_send()


def gather_all(quarter, floats, fracs, positions):
    bf, f32, i32 = jnp.bfloat16, jnp.float32, jnp.int32
    half = (2, 3, STRIP, PIX)
    return pl.pallas_call(
        gather_kernel,
        out_shape=(
            jax.ShapeDtypeStruct((NB, 2, 3, PIX, PIX), bf),
            jax.ShapeDtypeStruct((NZ, *floats.shape), f32),
            jax.ShapeDtypeStruct((NZ, *fracs.shape), bf),
            jax.ShapeDtypeStruct((NZ, *positions.shape), i32),
        ),
        in_specs=[ANY] * 4,
        out_specs=(ANY,) * 4,
        scratch_shapes=[
            pltpu.VMEM(half, bf),
            pltpu.VMEM(floats.shape, f32),
            pltpu.VMEM(fracs.shape, bf),
            pltpu.VMEM(positions.shape, i32),
            DMA((4,)),
            DMA((4,)),
            DMA((2, 4, 3)),
            DMA((2, 4, 3)),
            DMA((2, NB)),
            DMA((2, NB)),
            DMA((2, NB)),
            DMA((2, NB)),
            DMA,
            DMA,
        ],
        compiler_params=pltpu.CompilerParams(collective_id=0, has_side_effects=True),
        name="gather_all",
    )(quarter, floats, fracs, positions)


def sin_cos(v):
    quarter = jnp.round(v * 0.6366197723675814)
    u = v - quarter * 1.5703125
    u = u - quarter * 4.837512969970703e-4
    u = u - quarter * 7.549789948768648e-8
    u2 = u * u
    s = u + u * u2 * (-1.6666654611e-1 + u2 * (8.3321608736e-3 + u2 * -1.9515295891e-4))
    c = 1.0 - 0.5 * u2 + u2 * u2 * (4.166664568298827e-2 + u2 * (-1.388731625493765e-3 + u2 * 2.443315711809948e-5))
    q = quarter.astype(jnp.int32) & 3
    odd = (q & 1) == 1
    sin = jnp.where(odd, c, s)
    cos = jnp.where(odd, s, c)
    sin = jnp.where(q >= 2, -sin, sin)
    cos = jnp.where((q == 1) | (q == 2), -cos, cos)
    return sin, cos


def low_of(high):
    return (1.0 - high).astype(jnp.bfloat16).astype(jnp.float32)


def run_of(entry):
    run = entry % ALL_RUNS
    return entry // ALL_RUNS, run // PIECE_RUNS, (run // RUNS) % DET, run % RUNS


def line(ref, at):
    z, d, r = at
    return ref[z, d, pl.ds(r, 1), :]


def spread(index, low, high, rows):
    return jnp.where(rows == index, low, jnp.where(rows == index + 1, high, 0.0))


def forward_kernel(cnt_ref, list_ref, tiles_ref, f_ref, w_ref, sig_ref, cs_ref, hit_ref, frac_ref):
    def prepare(z, _):
        code = f_ref[z, 0].astype(jnp.int32)
        hit_ref[z, 0] = code // PIX
        hit_ref[z, 1] = code % PIX
        sin, cos = sin_cos(2.0 * f_ref[z, 1])
        cs_ref[z, 0] = cos
        cs_ref[z, 1] = sin
        frac_ref[z, 0] = w_ref[z, 0].astype(jnp.float32)
        frac_ref[z, 1] = w_ref[z, 1].astype(jnp.float32)
        sig_ref[z] = jnp.zeros_like(sig_ref[z])
        return 0

    lax.fori_loop(0, NZ, prepare, 0)
    count = cnt_ref[0]
    rows = lax.broadcasted_iota(jnp.int32, (PIX, LANE), 0)

    def body(step, _):
        for u in range(UNROLL):
            k = step * UNROLL + u
            tile, z, d, r = run_of(list_ref[k])
            at = (d, pl.ds(r, 1), slice(None))
            col_high = frac_ref[z, 1, *at]
            row_high = frac_ref[z, 0, *at]
            col_weight = spread(hit_ref[z, 1, *at], low_of(col_high), col_high, rows).astype(jnp.bfloat16)
            row_weight = spread(hit_ref[z, 0, *at], low_of(row_high), row_high, rows)
            partial = jnp.dot(tiles_ref[tile], col_weight, preferred_element_type=jnp.float32)
            value = [
                jnp.sum(partial[p * PIX : (p + 1) * PIX] * row_weight, axis=0, keepdims=True) for p in range(3)
            ]
            total = value[0] + cs_ref[z, 0, *at] * value[1] + cs_ref[z, 1, *at] * value[2]
            sig_ref[z, *at] = jnp.where(k < count, total, 0.0)
        return 0

    lax.fori_loop(0, (count + UNROLL - 1) // UNROLL, body, 0)


def forward(count, order, tiles, floats, fracs):
    f32 = jnp.float32
    block = (NZ, DET, RUNS, LANE)
    pair = (NZ, 2, DET, RUNS, LANE)
    return pl.pallas_call(
        forward_kernel,
        out_shape=(jax.ShapeDtypeStruct(block, f32), jax.ShapeDtypeStruct(pair, f32)),
        in_specs=[SM, SM, VM, VM, VM],
        out_specs=(VM, VM),
        scratch_shapes=[pltpu.VMEM(pair, jnp.int32), pltpu.VMEM(pair, f32)],
        name="forward",
    )(count, order, tiles, floats, fracs)


def backward_kernel(cnt_ref, list_ref, f_ref, w_ref, cs_ref, filt_ref, acc_ref, hit_ref, frac_ref):
    def prepare(z, _):
        code = f_ref[z, 0].astype(jnp.int32)
        hit_ref[z, 0] = code // PIX
        hit_ref[z, 1] = code % PIX
        frac_ref[z, 0] = w_ref[z, 0].astype(jnp.float32)
        frac_ref[z, 1] = w_ref[z, 1].astype(jnp.float32)
        return 0

    lax.fori_loop(0, NZ, prepare, 0)

    def clear(t, _):
        acc_ref[t] = jnp.zeros_like(acc_ref[t])
        return 0

    lax.fori_loop(0, 2 * NB, clear, 0)
    count = cnt_ref[0]
    rows = lax.broadcasted_iota(jnp.int32, (PIX, LANE), 0)

    def body(step, _):
        for u in range(UNROLL):
            k = step * UNROLL + u
            tile, z, d, r = run_of(list_ref[k])
            at = (d, pl.ds(r, 1), slice(None))
            col_high = frac_ref[z, 1, *at]
            row_high = frac_ref[z, 0, *at]
            row_low = low_of(row_high)
            col_weight = spread(hit_ref[z, 1, *at], low_of(col_high), col_high, rows).astype(jnp.bfloat16)
            filt = jnp.where(k < count, filt_ref[z, *at], 0.0)
            hit = hit_ref[z, 0, *at]
            parts = []
            for p in range(3):
                scaled = filt if p == 0 else cs_ref[z, p - 1, *at] * filt
                parts.append(spread(hit, scaled * row_low, scaled * row_high, rows).astype(jnp.bfloat16))
            weighted = jnp.concatenate(parts, axis=0)
            acc_ref[tile] += lax.dot_general(
                weighted, col_weight, (((1,), (1,)), ((), ())), preferred_element_type=jnp.float32
            )
        return 0

    lax.fori_loop(0, (count + UNROLL - 1) // UNROLL, body, 0)


def backward(count, order, floats, fracs, turns, filtered):
    f32 = jnp.float32
    pair = (NZ, 2, DET, RUNS, LANE)
    return pl.pallas_call(
        backward_kernel,
        out_shape=jax.ShapeDtypeStruct((2 * NB, 3 * PIX, PIX), f32),
        in_specs=[SM, SM, VM, VM, VM, VM],
        out_specs=VM,
        scratch_shapes=[pltpu.VMEM(pair, jnp.int32), pltpu.VMEM(pair, f32)],
        name="backward",
    )(count, order, floats, fracs, turns, filtered)


def toeplitz_kernel(w_ref, hi_ref, lo_ref):
    lanes = lax.broadcasted_iota(jnp.int32, (LANE, LANE), 1)
    rows = lax.broadcasted_iota(jnp.int32, (LANE, LANE), 0)
    upper = lanes >= rows

    def rolled(block):
        return pltpu.roll(
            jnp.broadcast_to(w_ref[0, pl.ds(block, 1), :], (LANE, LANE)), 0, 1, stride=1, stride_axis=0
        )

    before = rolled(0)
    for block in range(1, 2 * REACH + 2):
        after = rolled(block)
        m = 2 * REACH + 1 - block
        matrix = jnp.where(upper, after, before)
        high = matrix.astype(jnp.bfloat16)
        hi_ref[0, m] = high
        lo_ref[0, m] = (matrix - high.astype(jnp.float32)).astype(jnp.bfloat16)
        before = after


def toeplitz(noise_coef):
    count = noise_coef.shape[1] - 1
    weights = jnp.concatenate([noise_coef[:, :1] + 1.0, noise_coef[:, 1:]], axis=1)
    edge = jnp.zeros((DET, LANE), jnp.float32)
    line_all = jnp.concatenate([edge, weights[:, :0:-1], weights, edge[:, 1:]], axis=1)
    blocks = line_all.reshape(DET, 2 * REACH + 2, LANE)
    shape = jax.ShapeDtypeStruct((DET, 2 * REACH + 1, LANE, LANE), jnp.bfloat16)
    out = pl.BlockSpec((1, 2 * REACH + 1, LANE, LANE), lambda d: (d, 0, 0, 0))
    return pl.pallas_call(
        toeplitz_kernel,
        grid=(DET,),
        out_shape=(shape, shape),
        in_specs=[pl.BlockSpec((1, 2 * REACH + 2, LANE), lambda d: (d, 0, 0))],
        out_specs=(out, out),
        name="toeplitz",
    )(blocks)


def filter_kernel(
    part_ref, hi_ref, lo_ref, out_ref, land, ext, filt, own_sem, send, recv, halo_send, halo_recv, back_send, back_recv
):
    det, tm, y, z, x = place()
    total_tm = NY * NZ * NX
    peers = [tm_of(y, (z + k) % NZ, x) for k in range(1, NZ)]
    prior, later = (tm + total_tm - 1) % total_tm, (tm + 1) % total_tm
    greet([(det, t) for t in peers + [prior, later]])
    own = pltpu.make_async_copy(part_ref.at[z], land.at[0], own_sem)
    own.start()
    sends = []
    for k in range(1, NZ):
        copy = remote(part_ref.at[(z + k) % NZ], land.at[k], send.at[k], recv.at[k], (det, peers[k - 1]))
        copy.start()
        sends.append(copy)
    own.wait()
    total = land[0]
    for k in range(1, NZ):
        sends[k - 1].wait_recv()
        total = total + land[k]
    ext[:, REACH : REACH + RUNS, :] = total
    to_prior = remote(
        ext.at[:, pl.ds(REACH, REACH), :], ext.at[:, pl.ds(REACH + RUNS, REACH), :],
        halo_send.at[0], halo_recv.at[0], (det, prior),
    )
    to_later = remote(
        ext.at[:, pl.ds(RUNS, REACH), :], ext.at[:, pl.ds(0, REACH), :], halo_send.at[1], halo_recv.at[1], (det, later)
    )
    to_prior.start()
    to_later.start()
    to_prior.wait_recv()
    to_later.wait_recv()
    first, last = tm == 0, tm == total_tm - 1
    for d in range(DET):
        line_all = jnp.concatenate(
            [
                jnp.where(first, 0.0, ext[d, :REACH]),
                ext[d, REACH : REACH + RUNS],
                jnp.where(last, 0.0, ext[d, REACH + RUNS :]),
            ],
            axis=0,
        )
        result = jnp.zeros((RUNS, LANE), jnp.float32)
        for m in range(2 * REACH + 1):
            window = line_all[m : m + RUNS]
            high = window.astype(jnp.bfloat16)
            low = (window - high.astype(jnp.float32)).astype(jnp.bfloat16)
            both = jnp.dot(
                jnp.concatenate([high, low], axis=0), hi_ref[d, m], preferred_element_type=jnp.float32
            )
            result += both[:RUNS] + both[RUNS:]
            result += jnp.dot(high, lo_ref[d, m], preferred_element_type=jnp.float32)
        filt[d] = result
    back = []
    for k in range(1, NZ):
        copy = remote(filt, out_ref.at[z], back_send.at[k], back_recv.at[k], (det, peers[k - 1]))
        copy.start()
        back.append(copy)
    own = pltpu.make_async_copy(filt, out_ref.at[z], own_sem)
    own.start()
    own.wait()
    for k in range(1, NZ):
        remote(filt, out_ref.at[(z + NZ - k) % NZ], back_send.at[k], back_recv.at[k], (det, peers[k - 1])).wait_recv()
    for copy in sends + back + [to_prior, to_later]:
        copy.wait_send()


def filtered_of(partial, hi, lo):
    f32 = jnp.float32
    block = (DET, RUNS, LANE)
    return pl.pallas_call(
        filter_kernel,
        out_shape=jax.ShapeDtypeStruct((NZ, *block), f32),
        in_specs=[ANY, VM, VM],
        out_specs=ANY,
        scratch_shapes=[
            pltpu.VMEM((NZ, *block), f32),
            pltpu.VMEM((DET, RUNS + 2 * REACH, LANE), f32),
            pltpu.VMEM(block, f32),
            DMA,
            DMA((NZ,)),
            DMA((NZ,)),
            DMA((2,)),
            DMA((2,)),
            DMA((NZ,)),
            DMA((NZ,)),
        ],
        compiler_params=pltpu.CompilerParams(collective_id=1, has_side_effects=True),
        name="filter",
    )(partial, hi, lo)


def collect_kernel(
    acc_ref, out_ref, own, land_core, land_far, land_hi, total,
    own_sem, core_send, core_recv, far_send, far_recv, hi_send, hi_recv,
):
    det, tm, y, z, x = place()
    mine = y * NX + x
    core, hi = det % 2, det // 2
    partner, across = core_of(det), hi_of(det)
    order = PEERS + [(0, 0)]

    def slot_of(dy, dx, sign):
        return ((y + sign * dy + NY) % NY) * NX + (x + dx) % NX

    far = [tm_of((y + dy) % NY, z, (x + dx) % NX) for dy, dx in PEERS]
    loads = []
    for k, (dy, dx) in enumerate(order):
        copy = pltpu.make_async_copy(acc_ref.at[slot_of(dy, dx, 1), :, :, :, core], own.at[k], own_sem.at[k])
        copy.start()
        loads.append(copy)
    greet([(partner, tm), (across, tm)] + [(det, t) for t in far])
    swaps = []
    for k, (dy, dx) in enumerate(order):
        copy = remote(
            acc_ref.at[slot_of(dy, dx, 1), :, :, :, 1 - core], land_core.at[k], core_send.at[k], core_recv.at[k],
            (partner, tm),
        )
        copy.start()
        swaps.append(copy)
    sends = []
    for k in range(NB):
        loads[k].wait()
        swaps[k].wait_recv()
        own[k] = own[k] + land_core[k]
        if k < NB - 1:
            copy = remote(own.at[k], land_far.at[k], far_send.at[k], far_recv.at[k], (det, far[k]))
            copy.start()
            sends.append(copy)
    total[...] = own[NB - 1]
    for k in range(NB - 1):
        sends[k].wait_recv()
        total[...] = total[...] + land_far[k]
    copy = remote(total.at[:, :, 1 - hi], land_hi, hi_send, hi_recv, (across, tm))
    copy.start()
    copy.wait_recv()
    out_ref[...] = total[:, :, pl.ds(hi, 1)].reshape(out_ref.shape) + land_hi[...]
    for other in swaps + sends + [copy]:
        other.wait_send()


def collect(acc):
    f32 = jnp.float32
    half = (2, 3, 2, STRIP, PIX)
    quarter = (2, 3, STRIP, PIX)
    return pl.pallas_call(
        collect_kernel,
        out_shape=jax.ShapeDtypeStruct(quarter, f32),
        in_specs=[ANY],
        out_specs=VM,
        scratch_shapes=[
            pltpu.VMEM((NB, *half), f32),
            pltpu.VMEM((NB, *half), f32),
            pltpu.VMEM((NB - 1, *half), f32),
            pltpu.VMEM(quarter, f32),
            pltpu.VMEM(half, f32),
            DMA((NB,)),
            DMA((NB,)),
            DMA((NB,)),
            DMA((NB,)),
            DMA((NB,)),
            DMA,
            DMA,
        ],
        compiler_params=pltpu.CompilerParams(collective_id=2, has_side_effects=True),
        name="collect",
    )(acc.reshape(NB, 2, 3, 2, 2, STRIP, PIX))


def run_positions(piece_list, tile_home, run_slot):
    table = jnp.arange(tile_home.shape[0], dtype=jnp.int32)
    position = jnp.sum(jnp.where(piece_list[:, None] == table[None, :], tile_home[None, :], 0), axis=1)
    slots = jnp.arange(LISTED, dtype=jnp.int32)
    runs = run_slot.reshape(-1)
    return jnp.sum(jnp.where(runs[None, :] == slots[:, None], position[:, None], 0), axis=0)


def ordered(positions):
    _, _, _, z, _ = place()
    flat = positions.reshape(-1)
    mine = (flat // (2 * NX)) % NZ == z
    tile = (flat // (2 * NX * NZ)) * (2 * NX) + flat % (2 * NX)
    index = jnp.arange(ALL_RUNS, dtype=jnp.int32)
    key = jnp.where(mine, tile, 2 * NB) * ALL_RUNS + index
    rank = jnp.sum((key[None, :] < key[:, None]).astype(jnp.int32), axis=1)
    entry = tile * ALL_RUNS + index
    order = jnp.sum(jnp.where(rank[:, None] == index[None, :], entry[:, None], 0), axis=0)
    return jnp.sum(mine.astype(jnp.int32)).reshape(1), order


def body(
    sky_map, tile_home, piece_tiles, run_slot, hit_row, hit_col, frac_row, frac_col, angle, noise_coef
):
    shape = (DET, RUNS, LANE)
    code = (hit_row * PIX + hit_col).astype(jnp.float32)
    floats = jnp.stack([code.reshape(shape), angle.reshape(shape)])
    fracs = jnp.stack([frac_row.reshape(shape), frac_col.reshape(shape)])
    positions = run_positions(piece_tiles[0, 0], tile_home, run_slot).reshape(1, PIECE_RUNS)
    hi, lo = toeplitz(noise_coef)
    tiles, all_floats, all_fracs, all_positions = gather_all(sky_map, floats, fracs, positions)
    count, order = ordered(all_positions)
    partial, turns = forward(count, order, tiles.reshape(2 * NB, 3 * PIX, PIX), all_floats, all_fracs)
    filtered = filtered_of(partial, hi, lo)
    acc = backward(count, order, all_floats, all_fracs, turns, filtered)
    return collect(acc)


def solution(mesh):
    placed = (
        P("tm", None, "det", None),
        P(),
        P("det", "tm", None),
        P("det", "tm"),
        P("det", "tm"),
        P("det", "tm"),
        P("det", "tm"),
        P("det", "tm"),
        P("det", "tm"),
        P("det", None),
    )
    return jax.shard_map(
        body, mesh=mesh, in_specs=placed, out_specs=P("tm", None, "det", None), check_vma=False
    )
```

```python
import functools

import jax
import jax.numpy as jnp
from jax import lax
from jax.experimental import pallas as pl
from jax.experimental.pallas import tpu as pltpu
from jax.sharding import PartitionSpec as P

MESH = pl.DeviceIdType.MESH
NY, NZ, NX = 4, 8, 2
NB = NY * NX
DET, RUNS, LANE = 8, 16, 128
PIX = 128
STRIP = 32
LISTED = 32
TILE_DEV = 2
REACH = 8
UNROLL = 4
PIECE_RUNS = DET * RUNS
ALL_RUNS = NB * PIECE_RUNS
ANY = pl.BlockSpec(memory_space=pl.ANY)
VM = pl.BlockSpec(memory_space=pltpu.VMEM)
SM = pl.BlockSpec(memory_space=pltpu.SMEM)
DMA = pltpu.SemaphoreType.DMA
PEERS = [(dy, dx) for dy in range(NY) for dx in range(NX) if (dy, dx) != (0, 0)]


def place():
    det, tm = lax.axis_index("det"), lax.axis_index("tm")
    y, z, x = tm // (NZ * NX), (tm // NX) % NZ, tm % NX
    return det, tm, y, z, x


def tm_of(y, z, x):
    return (y * NZ + z) * NX + x


def core_of(det):
    return det + 1 - 2 * (det % 2)


def hi_of(det):
    return (det + 2) % 4


def greet(peers):
    barrier = pltpu.get_barrier_semaphore()
    for peer in peers:
        pl.semaphore_signal(barrier, inc=1, device_id=peer, device_id_type=MESH)
    pl.semaphore_wait(barrier, len(peers))


def remote(src, dst, send, recv, peer):
    return pltpu.make_async_remote_copy(
        src_ref=src, dst_ref=dst, send_sem=send, recv_sem=recv, device_id=peer, device_id_type=MESH
    )


def pack_kernel(home_ref, piece_ref, slot_ref, row_ref, col_ref, low_ref, high_ref, angle_ref, float_ref, frac_ref, pos_ref):
    for r in range(RUNS):
        at = slice(r * LANE, (r + 1) * LANE)
        float_ref[0, r] = (row_ref[:, at] * PIX + col_ref[:, at]).astype(jnp.float32)
        float_ref[1, r] = angle_ref[:, at]
        frac_ref[0, r] = low_ref[:, at]
        frac_ref[1, r] = high_ref[:, at]
    slots = slot_ref[...]
    position = jnp.zeros_like(slots)
    for s in range(LISTED):
        position = jnp.where(slots == s, home_ref[piece_ref[0, s]], position)
    pos_ref[...] = position


def packed(tile_home, piece_list, run_slot, hit_row, hit_col, frac_row, frac_col, angle):
    shape = (2, RUNS, DET, LANE)
    return pl.pallas_call(
        pack_kernel,
        out_shape=(
            jax.ShapeDtypeStruct(shape, jnp.float32),
            jax.ShapeDtypeStruct(shape, jnp.bfloat16),
            jax.ShapeDtypeStruct((DET, RUNS), jnp.int32),
        ),
        in_specs=[SM, SM] + [VM] * 6,
        out_specs=(VM, VM, VM),
        name="pack",
    )(tile_home, piece_list, run_slot, hit_row, hit_col, frac_row, frac_col, angle)


def run_order(pos_ref, order_ref, y, x):
    f32, i32 = jnp.float32, jnp.int32
    lanes = lax.broadcasted_iota(i32, (RUNS, LANE), 1)
    offset = lax.broadcasted_iota(i32, (RUNS, LANE), 0)
    spot = jnp.zeros((DET, LANE), f32)
    for slot in range(NB):
        placed = (lanes == offset + slot * RUNS).astype(f32).astype(jnp.bfloat16)
        spot += jnp.dot(pos_ref[slot].astype(f32).astype(jnp.bfloat16), placed, preferred_element_type=f32)
    pos = spot.astype(i32)
    here = (pos // (TILE_DEV * NX * NZ) == y) & ((pos // TILE_DEV) % NX == x)
    tile = ((pos // (TILE_DEV * NX)) % NZ) * TILE_DEV + pos % TILE_DEV
    run = lax.broadcasted_iota(i32, (DET, LANE), 0) * LANE + lax.broadcasted_iota(i32, (DET, LANE), 1)
    key = (jnp.where(here, tile, TILE_DEV * NZ) * ALL_RUNS + run).astype(f32)
    entry_t = (tile * ALL_RUNS + run).astype(f32).T
    key_t = key.T
    square = (LANE, LANE)
    ranks = []
    for d in range(DET):
        mine = jnp.broadcast_to(key[d : d + 1], square)
        less = jnp.zeros(square, f32)
        for e in range(DET):
            less += jnp.where(jnp.broadcast_to(key_t[:, e : e + 1], square) < mine, 1.0, 0.0)
        ranks.append(jnp.sum(less, axis=0, keepdims=True))
    rank_t = jnp.concatenate(ranks, axis=0).T
    place = lax.broadcasted_iota(i32, square, 1).astype(f32)
    for d in range(DET):
        found = jnp.zeros(square, f32)
        for e in range(DET):
            at = jnp.broadcast_to(rank_t[:, e : e + 1], square) - (d * LANE)
            found += jnp.where(at == place, jnp.broadcast_to(entry_t[:, e : e + 1], square), 0.0)
        order_ref[d : d + 1, :] = jnp.sum(found, axis=0, keepdims=True).astype(i32)
    count = jnp.sum(jnp.sum(here.astype(f32), axis=1, keepdims=True), axis=0, keepdims=True)
    order_ref[DET:, :] = jnp.broadcast_to(count, (DET, LANE)).astype(i32)


def gather_kernel(
    q_ref, f_ref, w_ref, p_ref, tiles_ref, fo_ref, wo_ref, order_ref,
    q_own, f_own, w_own, pos_all, load_sem, store_sem,
    pos_send, pos_recv, block_send, block_recv, ring_send, ring_recv, core_send, core_recv, hi_send, hi_recv,
):
    det, tm, y, z, x = place()
    partner, across = core_of(det), hi_of(det)
    right, left = tm_of(y, (z + 1) % NZ, x), tm_of(y, (z + NZ - 1) % NZ, x)
    ahead, behind = (y + 1) % NY, (y + NY - 1) % NY
    facing = (y + NY // 2) % NY
    other = 1 - x
    up, down, side = (det, tm_of(ahead, z, x)), (det, tm_of(behind, z, x)), (det, tm_of(y, z, other))
    far = [(det, tm_of((y + dy) % NY, z, (x + dx) % NX)) for dy, dx in PEERS]

    def strip(slot, d):
        return tiles_ref.at[slot, :, :, pl.ds(d * STRIP, STRIP), :]

    def block(slot, part):
        return fo_ref.at[slot, part] if part < 2 else wo_ref.at[slot]

    def own_block(part):
        return f_ref.at[part] if part < 2 else w_ref

    mine = y * NX + x
    loads = [
        pltpu.make_async_copy(q_ref, q_own, load_sem.at[0]),
        pltpu.make_async_copy(f_ref, f_own, load_sem.at[1]),
        pltpu.make_async_copy(w_ref, w_own, load_sem.at[2]),
        pltpu.make_async_copy(p_ref, pos_all.at[mine], load_sem.at[3]),
    ]
    for copy in loads:
        copy.start()
    greet([(det, right), (det, left), (partner, tm), (across, tm)] + far)

    started = []

    def start(copy):
        copy.start()
        started.append(copy)

    for k, peer in enumerate(far):
        start(remote(p_ref, pos_all.at[mine], pos_send.at[k], pos_recv.at[k], peer))
    start(remote(q_ref, strip(z, det), hi_send, hi_recv, (across, tm)))

    def send_block(link, slot, part, peer, own=False):
        start(
            remote(
                own_block(part) if own else block(slot, part), block(slot, part),
                block_send.at[link, part], block_recv.at[link, part], peer,
            )
        )

    def wait_block(link, slot, part):
        remote(own_block(part), block(slot, part), block_send.at[link, part], block_recv.at[link, part], side).wait_recv()

    for part in range(3):
        send_block(1, mine, part, up, True)
        send_block(2, mine, part, down, True)
        send_block(0, mine, part, side, True)

    def reach(half, direction):
        return NZ // 2 if half == direction else NZ // 2 - 1

    owner = (det, across)

    def send_strip(half, direction, step):
        slot = (z + NZ - step) % NZ if direction == 0 else (z + step) % NZ
        src = q_ref if half == 0 and step == 0 else strip(slot, owner[half])
        start(
            remote(
                src, strip(slot, owner[half]), ring_send.at[half, direction, step], ring_recv.at[half, direction, step],
                (det, right if direction == 0 else left),
            )
        )

    def take_strip(half, step):
        for direction in (0, 1):
            if step < reach(half, direction):
                slot = (z + NZ - step - 1) % NZ if direction == 0 else (z + step + 1) % NZ
                here = strip(slot, owner[half])
                remote(q_ref, here, ring_send.at[half, direction, step], ring_recv.at[half, direction, step], side).wait_recv()
                if step + 1 < reach(half, direction):
                    send_strip(half, direction, step + 1)
                index = 1 + direction * NZ // 2 + step
                start(remote(here, here, core_send.at[half, index], core_recv.at[half, index], (partner, tm)))

    for direction in (0, 1):
        send_strip(0, direction, 0)
    start(remote(q_ref, strip(z, det), core_send.at[0, 0], core_recv.at[0, 0], (partner, tm)))
    stores = []
    for i, (src, dst) in enumerate(((q_own, strip(z, det)), (f_own, fo_ref.at[mine]), (w_own, wo_ref.at[mine]))):
        loads[i].wait()
        copy = pltpu.make_async_copy(src, dst, store_sem.at[i])
        copy.start()
        stores.append(copy)

    remote(q_ref, strip(z, across), hi_send, hi_recv, (across, tm)).wait_recv()
    for direction in (0, 1):
        send_strip(1, direction, 0)
    start(remote(strip(z, across), strip(z, across), core_send.at[1, 0], core_recv.at[1, 0], (partner, tm)))

    slot_of = {1: behind * NX + x, 2: ahead * NX + x, 0: y * NX + other, 5: facing * NX + x, 6: facing * NX + other,
               3: behind * NX + other, 4: ahead * NX + other}

    def near(part):
        for link in (1, 2, 0):
            wait_block(link, slot_of[link], part)
            if link == 1 and part != 1:
                send_block(5, slot_of[1], part, up)
            if link == 2 and part == 1:
                send_block(5, slot_of[2], part, down)
            if link == 0:
                send_block(3, slot_of[0], part, up)
                send_block(4, slot_of[0], part, down)

    def opposite(part):
        wait_block(5, slot_of[5], part)
        send_block(6, slot_of[5], part, side)

    take_strip(0, 0)
    near(0)
    take_strip(1, 0)
    near(1)
    take_strip(0, 1)
    near(2)
    take_strip(1, 1)
    opposite(0)
    opposite(1)
    take_strip(0, 2)
    opposite(2)
    take_strip(1, 2)
    take_strip(0, 3)
    take_strip(1, 3)

    loads[3].wait()
    for k, peer in enumerate(far):
        remote(p_ref, pos_all.at[mine], pos_send.at[k], pos_recv.at[k], peer).wait_recv()
    run_order(pos_all, order_ref, y, x)

    for part in range(3):
        for link in (3, 4, 6):
            wait_block(link, slot_of[link], part)
    theirs = (partner, hi_of(partner))
    for half in (0, 1):
        for direction in (0, 1):
            for step in range(-1 if direction == 0 else 0, reach(half, direction)):
                slot = (z + NZ - step - 1) % NZ if direction == 0 else (z + step + 1) % NZ
                index = 0 if step < 0 else 1 + direction * NZ // 2 + step
                remote(
                    q_ref, strip(slot, theirs[half]), core_send.at[half, index], core_recv.at[half, index], (partner, tm)
                ).wait_recv()
    for copy in stores:
        copy.wait()
    for copy in started:
        copy.wait_send()


def gather_all(quarter, floats, fracs, positions):
    bf, f32, i32 = jnp.bfloat16, jnp.float32, jnp.int32
    return pl.pallas_call(
        gather_kernel,
        out_shape=(
            jax.ShapeDtypeStruct((NZ, TILE_DEV, 3, PIX, PIX), bf),
            jax.ShapeDtypeStruct((NB, *floats.shape), f32),
            jax.ShapeDtypeStruct((NB, *fracs.shape), bf),
            jax.ShapeDtypeStruct((2 * DET, LANE), i32),
        ),
        in_specs=[ANY] * 4,
        out_specs=(ANY, ANY, ANY, VM),
        scratch_shapes=[
            pltpu.VMEM(quarter.shape, bf),
            pltpu.VMEM(floats.shape, f32),
            pltpu.VMEM(fracs.shape, bf),
            pltpu.VMEM((NB, *positions.shape), i32),
            DMA((4,)),
            DMA((3,)),
            DMA((NB,)),
            DMA((NB,)),
            DMA((7, 3)),
            DMA((7, 3)),
            DMA((2, 2, NZ // 2)),
            DMA((2, 2, NZ // 2)),
            DMA((2, NZ + 1)),
            DMA((2, NZ + 1)),
            DMA,
            DMA,
        ],
        compiler_params=pltpu.CompilerParams(collective_id=0, has_side_effects=True),
        name="gather_all",
    )(quarter, floats, fracs, positions)


def sin_cos(v):
    quarter = jnp.round(v * 0.6366197723675814)
    u = v - quarter * 1.5703125
    u = u - quarter * 4.837512969970703e-4
    u = u - quarter * 7.549789948768648e-8
    u2 = u * u
    s = u + u * u2 * (-1.6666654611e-1 + u2 * (8.3321608736e-3 + u2 * -1.9515295891e-4))
    c = 1.0 - 0.5 * u2 + u2 * u2 * (4.166664568298827e-2 + u2 * (-1.388731625493765e-3 + u2 * 2.443315711809948e-5))
    q = quarter.astype(jnp.int32) & 3
    odd = (q & 1) == 1
    sin = jnp.where(odd, c, s)
    cos = jnp.where(odd, s, c)
    sin = jnp.where(q >= 2, -sin, sin)
    cos = jnp.where((q == 1) | (q == 2), -cos, cos)
    return sin, cos


def low_of(high):
    return (1.0 - high).astype(jnp.bfloat16).astype(jnp.float32)


def run_of(entry):
    run = entry & (ALL_RUNS - 1)
    return entry >> 10, (run >> 4) & (NB - 1), run >> 7, run & (RUNS - 1)


def spread(index, low, high, rows):
    return jnp.where(rows == index, low, jnp.where(rows == index + 1, high, 0.0))


def forward_kernel(list_ref, tiles_ref, f_ref, w_ref, sig_ref, cs_ref, hit_ref, frac_ref):
    def prepare(z, _):
        code = f_ref[z, 0].astype(jnp.int32)
        hit_ref[z, 0] = code // PIX
        hit_ref[z, 1] = code % PIX
        sin, cos = sin_cos(2.0 * f_ref[z, 1])
        cs_ref[z, 0] = cos
        cs_ref[z, 1] = sin
        frac_ref[z, 0] = w_ref[z, 0].astype(jnp.float32)
        frac_ref[z, 1] = w_ref[z, 1].astype(jnp.float32)
        sig_ref[z] = jnp.zeros_like(sig_ref[z])
        return 0

    lax.fori_loop(0, NB, prepare, 0)
    count = list_ref[DET, 0]
    rows = lax.broadcasted_iota(jnp.int32, (PIX, LANE), 0)

    def body(step, _):
        for u in range(UNROLL):
            k = step * UNROLL + u
            tile, z, d, r = run_of(list_ref[k >> 7, k & (LANE - 1)])
            at = (r, pl.ds(d, 1), slice(None))
            col_high = frac_ref[z, 1, *at]
            row_high = frac_ref[z, 0, *at]
            col_weight = spread(hit_ref[z, 1, *at], low_of(col_high), col_high, rows).astype(jnp.bfloat16)
            row_weight = spread(hit_ref[z, 0, *at], low_of(row_high), row_high, rows)
            partial = jnp.dot(tiles_ref[tile], col_weight, preferred_element_type=jnp.float32)
            value = [
                jnp.sum(partial[p * PIX : (p + 1) * PIX] * row_weight, axis=0, keepdims=True) for p in range(3)
            ]
            total = value[0] + cs_ref[z, 0, *at] * value[1] + cs_ref[z, 1, *at] * value[2]
            sig_ref[z, d, pl.ds(r, 1), :] = jnp.where(k < count, total, 0.0)
        return 0

    lax.fori_loop(0, (count + UNROLL - 1) // UNROLL, body, 0)


def forward(order, tiles, floats, fracs):
    f32 = jnp.float32
    block = (NB, DET, RUNS, LANE)
    pair = (NB, 2, RUNS, DET, LANE)
    return pl.pallas_call(
        forward_kernel,
        out_shape=(jax.ShapeDtypeStruct(block, f32), jax.ShapeDtypeStruct(pair, f32)),
        in_specs=[SM, VM, VM, VM],
        out_specs=(VM, VM),
        scratch_shapes=[pltpu.VMEM(pair, jnp.int32), pltpu.VMEM(pair, f32)],
        name="forward",
    )(order, tiles, floats, fracs)


def backward_kernel(list_ref, f_ref, w_ref, cs_ref, filt_ref, acc_ref, hit_ref, frac_ref):
    def prepare(z, _):
        code = f_ref[z, 0].astype(jnp.int32)
        hit_ref[z, 0] = code // PIX
        hit_ref[z, 1] = code % PIX
        frac_ref[z, 0] = w_ref[z, 0].astype(jnp.float32)
        frac_ref[z, 1] = w_ref[z, 1].astype(jnp.float32)
        return 0

    lax.fori_loop(0, NB, prepare, 0)

    def clear(t, _):
        acc_ref[t] = jnp.zeros_like(acc_ref[t])
        return 0

    lax.fori_loop(0, TILE_DEV * NZ, clear, 0)
    count = list_ref[DET, 0]
    rows = lax.broadcasted_iota(jnp.int32, (PIX, LANE), 0)

    def body(step, _):
        for u in range(UNROLL):
            k = step * UNROLL + u
            tile, z, d, r = run_of(list_ref[k >> 7, k & (LANE - 1)])
            at = (r, pl.ds(d, 1), slice(None))
            col_high = frac_ref[z, 1, *at]
            row_high = frac_ref[z, 0, *at]
            row_low = low_of(row_high)
            col_weight = spread(hit_ref[z, 1, *at], low_of(col_high), col_high, rows).astype(jnp.bfloat16)
            filt = jnp.where(k < count, filt_ref[z, d, pl.ds(r, 1), :], 0.0)
            hit = hit_ref[z, 0, *at]
            parts = []
            for p in range(3):
                scaled = filt if p == 0 else cs_ref[z, p - 1, *at] * filt
                parts.append(spread(hit, scaled * row_low, scaled * row_high, rows).astype(jnp.bfloat16))
            weighted = jnp.concatenate(parts, axis=0)
            acc_ref[tile] += lax.dot_general(
                weighted, col_weight, (((1,), (1,)), ((), ())), preferred_element_type=jnp.float32
            )
        return 0

    lax.fori_loop(0, (count + UNROLL - 1) // UNROLL, body, 0)


def backward(order, floats, fracs, turns, filtered):
    f32 = jnp.float32
    pair = (NB, 2, RUNS, DET, LANE)
    return pl.pallas_call(
        backward_kernel,
        out_shape=jax.ShapeDtypeStruct((TILE_DEV * NZ, 3 * PIX, PIX), f32),
        in_specs=[SM, VM, VM, VM, VM],
        out_specs=VM,
        scratch_shapes=[pltpu.VMEM(pair, jnp.int32), pltpu.VMEM(pair, f32)],
        name="backward",
    )(order, floats, fracs, turns, filtered)


def toeplitz(noise_ref, line_ref, hi_ref, lo_ref):
    square = (LANE, LANE)
    lanes = lax.broadcasted_iota(jnp.int32, square, 1)
    rows = lax.broadcasted_iota(jnp.int32, square, 0)
    first = lax.broadcasted_iota(jnp.int32, (DET, LANE), 1) == 0
    for q in range(REACH):
        lags = noise_ref[:, q * LANE : (q + 1) * LANE]
        line_ref[q] = jnp.where(first, lags + 1.0, lags) if q == 0 else lags
    line_ref[REACH] = jnp.where(first, jnp.broadcast_to(noise_ref[:, REACH * LANE :], (DET, LANE)), 0.0)

    def one(d, _):
        def put(q, matrix):
            high = matrix.astype(jnp.bfloat16)
            hi_ref[d, q] = high
            lo_ref[d, q] = (matrix - high.astype(jnp.float32)).astype(jnp.bfloat16)

        before = None
        for q in range(REACH + 1):
            lags = line_ref[q, pl.ds(d, 1), :]
            after = pltpu.roll(jnp.broadcast_to(lags, square), 0, 1, stride=1, stride_axis=0)
            if q == 0:
                put(0, jnp.where(lanes >= rows, after, 0.0))
                put(REACH + 1, jnp.where(lanes > rows, after, 0.0))
            else:
                put(q, jnp.where(lanes >= rows, after, before))
            before = after
        return 0

    lax.fori_loop(0, DET, one, 0)


STRAIGHT = (((1,), (0,)), ((), ()))
CROSSED = (((1,), (1,)), ((), ()))


def filter_kernel(
    part_ref, noise_ref, out_ref, land, ext, filt, lags, t_hi, t_lo,
    own_sem, send, recv, halo_send, halo_recv, back_send, back_recv,
):
    det, tm, y, z, x = place()
    total_tm = NY * NZ * NX
    mine = y * NX + x
    prior, later = (tm + total_tm - 1) % total_tm, (tm + 1) % total_tm

    def slot(k, sign):
        dy, dx = PEERS[k]
        return ((y + sign * dy + NY) % NY) * NX + (x + dx) % NX

    peers = [(det, tm_of((y + dy) % NY, z, (x + dx) % NX)) for dy, dx in PEERS]
    greet(peers + [(det, later), (det, prior)])
    own = pltpu.make_async_copy(part_ref.at[mine], land.at[NB - 1], own_sem)
    own.start()
    sends = []
    for k, peer in enumerate(peers):
        copy = remote(part_ref.at[slot(k, 1)], land.at[k], send.at[k], recv.at[k], peer)
        copy.start()
        sends.append(copy)
    toeplitz(noise_ref, lags, t_hi, t_lo)
    own.wait()
    total = land[NB - 1]
    for k in range(NB - 1):
        sends[k].wait_recv()
        total = total + land[k]
    ext[:, REACH : REACH + RUNS, :] = total
    to_prior = remote(
        ext.at[:, pl.ds(REACH, REACH), :], ext.at[:, pl.ds(REACH + RUNS, REACH), :],
        halo_send.at[0], halo_recv.at[0], (det, prior),
    )
    to_later = remote(
        ext.at[:, pl.ds(RUNS, REACH), :], ext.at[:, pl.ds(0, REACH), :], halo_send.at[1], halo_recv.at[1], (det, later)
    )
    to_prior.start()
    to_later.start()
    to_prior.wait_recv()
    to_later.wait_recv()
    first, last = tm == 0, tm == total_tm - 1

    def product(left, right, crossed):
        return lax.dot_general(left, right, CROSSED if crossed else STRAIGHT, preferred_element_type=jnp.float32)

    for d in range(DET):
        line_all = jnp.concatenate(
            [
                jnp.where(first, 0.0, ext[d, :REACH]),
                ext[d, REACH : REACH + RUNS],
                jnp.where(last, 0.0, ext[d, REACH + RUNS :]),
            ],
            axis=0,
        )
        result = jnp.zeros((RUNS, LANE), jnp.float32)
        for m in range(2 * REACH + 1):
            window = line_all[m : m + RUNS]
            high = window.astype(jnp.bfloat16)
            low = (window - high.astype(jnp.float32)).astype(jnp.bfloat16)
            stack = jnp.concatenate([high, low], axis=0)
            q = REACH - m
            for index, crossed in [(q, False)] if q > 0 else [(-q, True)] if q < 0 else [(0, False), (REACH + 1, True)]:
                both = product(stack, t_hi[d, index], crossed)
                result += both[:RUNS] + both[RUNS:] + product(high, t_lo[d, index], crossed)
        filt[d] = result
    back = []
    for k, peer in enumerate(peers):
        copy = remote(filt, out_ref.at[mine], back_send.at[k], back_recv.at[k], peer)
        copy.start()
        back.append(copy)
    own = pltpu.make_async_copy(filt, out_ref.at[mine], own_sem)
    own.start()
    own.wait()
    for k, peer in enumerate(peers):
        remote(filt, out_ref.at[slot(k, -1)], back_send.at[k], back_recv.at[k], peer).wait_recv()
    for copy in sends + back + [to_prior, to_later]:
        copy.wait_send()


def filtered_of(partial, noise_coef):
    f32, bf = jnp.float32, jnp.bfloat16
    block = (DET, RUNS, LANE)
    matrices = (DET, REACH + 2, LANE, LANE)
    return pl.pallas_call(
        filter_kernel,
        out_shape=jax.ShapeDtypeStruct((NB, *block), f32),
        in_specs=[ANY, VM],
        out_specs=ANY,
        scratch_shapes=[
            pltpu.VMEM((NB, *block), f32),
            pltpu.VMEM((DET, RUNS + 2 * REACH, LANE), f32),
            pltpu.VMEM(block, f32),
            pltpu.VMEM((REACH + 1, DET, LANE), f32),
            pltpu.VMEM(matrices, bf),
            pltpu.VMEM(matrices, bf),
            DMA,
            DMA((NB,)),
            DMA((NB,)),
            DMA((2,)),
            DMA((2,)),
            DMA((NB,)),
            DMA((NB,)),
        ],
        compiler_params=pltpu.CompilerParams(collective_id=1, has_side_effects=True),
        name="filter",
    )(partial, noise_coef)


CHUNKS = [(t, p) for t in range(TILE_DEV) for p in range(3)]
HALF_Z = NZ // 2
OFFSETS = [4, 3, -3, 2, -2, 1, -1, 0]


def collect_kernel(
    acc_ref, out_ref, own, land_core, land, land_hi, total,
    own_sem, core_send, core_recv, ring_send, ring_recv, hi_send, hi_recv,
):
    det, tm, y, z, x = place()
    core, hi = det % 2, det // 2
    partner, across = core_of(det), hi_of(det)
    neighbours = ((det, tm_of(y, (z + 1) % NZ, x)), (det, tm_of(y, (z + NZ - 1) % NZ, x)))
    loads = []
    for k, offset in enumerate(OFFSETS):
        copy = pltpu.make_async_copy(acc_ref.at[(z + offset + NZ) % NZ, :, :, :, core], own.at[k], own_sem.at[k])
        copy.start()
        loads.append(copy)
    greet([(partner, tm), (across, tm), *neighbours])
    started = []

    def start(copy):
        copy.start()
        started.append(copy)

    for k, offset in enumerate(OFFSETS):
        start(
            remote(
                acc_ref.at[(z + offset + NZ) % NZ, :, :, :, 1 - core], land_core.at[k], core_send.at[k], core_recv.at[k],
                (partner, tm),
            )
        )

    def ring(direction, step, c):
        t, p = CHUNKS[c]
        sign = 1 if direction == 0 else -1
        k = OFFSETS.index(sign * (HALF_Z - step)) if step else 0
        return remote(
            own.at[k, t, p], land.at[direction, step, t, p],
            ring_send.at[direction, step, c], ring_recv.at[direction, step, c], neighbours[direction],
        )

    def swapped(k):
        loads[k].wait()
        remote(acc_ref.at[0, :, :, :, 0], land_core.at[k], core_send.at[k], core_recv.at[k], (partner, tm)).wait_recv()

    swapped(0)
    for direction in (0, 1):
        for c, (t, p) in enumerate(CHUNKS):
            if t == direction:
                own[0, t, p] = own[0, t, p] + land_core[0, t, p]
    for p in range(3):
        for direction in (0, 1):
            start(ring(direction, 0, direction * 3 + p))
    for step in range(1, HALF_Z):
        keys = [OFFSETS.index(HALF_Z - step), OFFSETS.index(step - HALF_Z)]
        for k in keys:
            swapped(k)
        for i in range(len(CHUNKS)):
            for direction in (0, 1):
                c = (i + 3 * (1 - direction)) % len(CHUNKS) if step == 1 else i
                t, p = CHUNKS[c]
                k = keys[direction]
                value = own[k, t, p] + land_core[k, t, p]
                if step > 1 or t == direction:
                    ring(direction, step - 1, c).wait_recv()
                    value = value + land[direction, step - 1, t, p]
                own[k, t, p] = value
                start(ring(direction, step, c))
    last = len(OFFSETS) - 1
    swapped(last)

    def across_copy(c):
        t, p = CHUNKS[c]
        return remote(total.at[t, p, 1 - hi], land_hi.at[t, p], hi_send.at[c], hi_recv.at[c], (across, tm))

    for c, (t, p) in enumerate(CHUNKS):
        value = own[last, t, p] + land_core[last, t, p]
        for direction in (0, 1):
            ring(direction, HALF_Z - 1, c).wait_recv()
            value = value + land[direction, HALF_Z - 1, t, p]
        total[t, p] = value
        start(across_copy(c))
    for c, (t, p) in enumerate(CHUNKS):
        across_copy(c).wait_recv()
        out_ref[t, p] = total[t, p, hi] + land_hi[t, p]
    for copy in started:
        copy.wait_send()


def collect(acc):
    f32 = jnp.float32
    half = (TILE_DEV, 3, 2, STRIP, PIX)
    quarter = (TILE_DEV, 3, STRIP, PIX)
    return pl.pallas_call(
        collect_kernel,
        out_shape=jax.ShapeDtypeStruct(quarter, f32),
        in_specs=[ANY],
        out_specs=VM,
        scratch_shapes=[
            pltpu.VMEM((NZ, *half), f32),
            pltpu.VMEM((NZ, *half), f32),
            pltpu.VMEM((2, HALF_Z, *half), f32),
            pltpu.VMEM(quarter, f32),
            pltpu.VMEM(half, f32),
            DMA((NZ,)),
            DMA((NZ,)),
            DMA((NZ,)),
            DMA((2, HALF_Z, 6)),
            DMA((2, HALF_Z, 6)),
            DMA((6,)),
            DMA((6,)),
        ],
        compiler_params=pltpu.CompilerParams(collective_id=2, has_side_effects=True),
        name="collect",
    )(acc.reshape(NZ, TILE_DEV, 3, 2, 2, STRIP, PIX))


def body(
    sky_map, tile_home, piece_tiles, run_slot, hit_row, hit_col, frac_row, frac_col, angle, noise_coef
):
    floats, fracs, positions = packed(
        tile_home, piece_tiles.reshape(1, LISTED), run_slot, hit_row, hit_col, frac_row, frac_col, angle
    )
    tiles, all_floats, all_fracs, order = gather_all(sky_map, floats, fracs, positions)
    partial, turns = forward(order, tiles.reshape(TILE_DEV * NZ, 3 * PIX, PIX), all_floats, all_fracs)
    filtered = filtered_of(partial, noise_coef)
    acc = backward(order, all_floats, all_fracs, turns, filtered)
    return collect(acc)


def solution(mesh):
    placed = (
        P("tm", None, "det", None),
        P(),
        P("det", "tm", None),
        P("det", "tm"),
        P("det", "tm"),
        P("det", "tm"),
        P("det", "tm"),
        P("det", "tm"),
        P("det", "tm"),
        P("det", None),
    )
    return jax.shard_map(
        body, mesh=mesh, in_specs=placed, out_specs=P("tm", None, "det", None), check_vma=False
    )
```

```python
import functools

import jax
import jax.numpy as jnp
from jax import lax
from jax.experimental import pallas as pl
from jax.experimental.pallas import tpu as pltpu
from jax.sharding import PartitionSpec as P

MESH = pl.DeviceIdType.MESH
NY, NZ, NX = 4, 8, 2
NB = NY * NX
DET, RUNS, LANE = 8, 16, 128
PIX = 128
STRIP = 32
LISTED = 32
TILE_DEV = 2
REACH = 8
UNROLL = 16
HALF = 16
PIECE_RUNS = DET * RUNS
ALL_RUNS = NB * PIECE_RUNS
ANY = pl.BlockSpec(memory_space=pl.ANY)
VM = pl.BlockSpec(memory_space=pltpu.VMEM)
SM = pl.BlockSpec(memory_space=pltpu.SMEM)
DMA = pltpu.SemaphoreType.DMA
PEERS = [(dy, dx) for dy in range(NY) for dx in range(NX) if (dy, dx) != (0, 0)]


def place():
    det, tm = lax.axis_index("det"), lax.axis_index("tm")
    y, z, x = tm // (NZ * NX), (tm // NX) % NZ, tm % NX
    return det, tm, y, z, x


def tm_of(y, z, x):
    return (y * NZ + z) * NX + x


def core_of(det):
    return det + 1 - 2 * (det % 2)


def hi_of(det):
    return (det + 2) % 4


def greet(peers):
    barrier = pltpu.get_barrier_semaphore()
    for peer in peers:
        pl.semaphore_signal(barrier, inc=1, device_id=peer, device_id_type=MESH)
    pl.semaphore_wait(barrier, len(peers))


def remote(src, dst, send, recv, peer):
    return pltpu.make_async_remote_copy(
        src_ref=src, dst_ref=dst, send_sem=send, recv_sem=recv, device_id=peer, device_id_type=MESH
    )


def pack_kernel(home_ref, piece_ref, slot_ref, row_ref, col_ref, low_ref, high_ref, angle_ref, float_ref, frac_ref, pos_ref):
    for r in range(RUNS):
        at = slice(r * LANE, (r + 1) * LANE)
        float_ref[0, r] = (row_ref[:, at] * PIX + col_ref[:, at]).astype(jnp.float32)
        float_ref[1, r] = angle_ref[:, at]
        frac_ref[0, r] = low_ref[:, at]
        frac_ref[1, r] = high_ref[:, at]
    slots = slot_ref[...]
    position = jnp.zeros_like(slots)
    for s in range(LISTED):
        position = jnp.where(slots == s, home_ref[piece_ref[0, s]], position)
    pos_ref[...] = position


def packed(tile_home, piece_list, run_slot, hit_row, hit_col, frac_row, frac_col, angle):
    shape = (2, RUNS, DET, LANE)
    return pl.pallas_call(
        pack_kernel,
        out_shape=(
            jax.ShapeDtypeStruct(shape, jnp.float32),
            jax.ShapeDtypeStruct(shape, jnp.bfloat16),
            jax.ShapeDtypeStruct((DET, RUNS), jnp.int32),
        ),
        in_specs=[SM, SM] + [VM] * 6,
        out_specs=(VM, VM, VM),
        name="pack",
    )(tile_home, piece_list, run_slot, hit_row, hit_col, frac_row, frac_col, angle)


def run_order(pos_ref, order_ref, y, x):
    f32, i32 = jnp.float32, jnp.int32
    lanes = lax.broadcasted_iota(i32, (RUNS, LANE), 1)
    offset = lax.broadcasted_iota(i32, (RUNS, LANE), 0)
    spot = jnp.zeros((DET, LANE), f32)
    for slot in range(NB):
        placed = (lanes == offset + slot * RUNS).astype(f32).astype(jnp.bfloat16)
        spot += jnp.dot(pos_ref[slot].astype(f32).astype(jnp.bfloat16), placed, preferred_element_type=f32)
    pos = spot.astype(i32)
    here = (pos // (TILE_DEV * NX * NZ) == y) & ((pos // TILE_DEV) % NX == x)
    tile = ((pos // (TILE_DEV * NX)) % NZ) * TILE_DEV + pos % TILE_DEV
    run = lax.broadcasted_iota(i32, (DET, LANE), 0) * LANE + lax.broadcasted_iota(i32, (DET, LANE), 1)
    key = (jnp.where(here, tile, TILE_DEV * NZ) * ALL_RUNS + run).astype(f32)
    entry_t = (tile * ALL_RUNS + run).astype(f32).T
    key_t = key.T
    square = (LANE, LANE)
    ranks = []
    for d in range(DET):
        mine = jnp.broadcast_to(key[d : d + 1], square)
        less = jnp.zeros(square, f32)
        for e in range(DET):
            less += jnp.where(jnp.broadcast_to(key_t[:, e : e + 1], square) < mine, 1.0, 0.0)
        ranks.append(jnp.sum(less, axis=0, keepdims=True))
    rank_t = jnp.concatenate(ranks, axis=0).T
    place = lax.broadcasted_iota(i32, square, 1).astype(f32)
    for d in range(DET):
        found = jnp.zeros(square, f32)
        for e in range(DET):
            at = jnp.broadcast_to(rank_t[:, e : e + 1], square) - (d * LANE)
            found += jnp.where(at == place, jnp.broadcast_to(entry_t[:, e : e + 1], square), 0.0)
        order_ref[d : d + 1, :] = jnp.sum(found, axis=0, keepdims=True).astype(i32)
    count = jnp.sum(jnp.sum(here.astype(f32), axis=1, keepdims=True), axis=0, keepdims=True)
    order_ref[DET:, :] = jnp.broadcast_to(count, (DET, LANE)).astype(i32)


def gather_kernel(
    q_ref, f_ref, w_ref, p_ref, tiles_ref, fo_ref, wo_ref, order_ref,
    q_own, f_own, w_own, pos_all, load_sem, store_sem,
    pos_send, pos_recv, block_send, block_recv, ring_send, ring_recv, core_send, core_recv, hi_send, hi_recv,
):
    det, tm, y, z, x = place()
    partner, across = core_of(det), hi_of(det)
    right, left = tm_of(y, (z + 1) % NZ, x), tm_of(y, (z + NZ - 1) % NZ, x)
    ahead, behind = (y + 1) % NY, (y + NY - 1) % NY
    facing = (y + NY // 2) % NY
    other = 1 - x
    up, down, side = (det, tm_of(ahead, z, x)), (det, tm_of(behind, z, x)), (det, tm_of(y, z, other))
    far = [(det, tm_of((y + dy) % NY, z, (x + dx) % NX)) for dy, dx in PEERS]

    def strip(slot, d):
        return tiles_ref.at[slot, :, :, pl.ds(d * STRIP, STRIP), :]

    def block(slot, part):
        return fo_ref.at[slot, part] if part < 2 else wo_ref.at[slot]

    def own_block(part):
        return f_ref.at[part] if part < 2 else w_ref

    mine = y * NX + x
    loads = [
        pltpu.make_async_copy(q_ref, q_own, load_sem.at[0]),
        pltpu.make_async_copy(f_ref, f_own, load_sem.at[1]),
        pltpu.make_async_copy(w_ref, w_own, load_sem.at[2]),
        pltpu.make_async_copy(p_ref, pos_all.at[mine], load_sem.at[3]),
    ]
    for copy in loads:
        copy.start()
    greet([(det, right), (det, left), (partner, tm), (across, tm)] + far)

    started = []

    def start(copy):
        copy.start()
        started.append(copy)

    for k, peer in enumerate(far):
        start(remote(p_ref, pos_all.at[mine], pos_send.at[k], pos_recv.at[k], peer))
    start(remote(q_ref, strip(z, det), hi_send, hi_recv, (across, tm)))

    def send_block(link, slot, part, peer, own=False):
        start(
            remote(
                own_block(part) if own else block(slot, part), block(slot, part),
                block_send.at[link, part], block_recv.at[link, part], peer,
            )
        )

    def wait_block(link, slot, part):
        remote(own_block(part), block(slot, part), block_send.at[link, part], block_recv.at[link, part], side).wait_recv()

    for part in range(3):
        send_block(1, mine, part, up, True)
        send_block(2, mine, part, down, True)
        send_block(0, mine, part, side, True)

    def reach(half, direction):
        return NZ // 2 if half == direction else NZ // 2 - 1

    owner = (det, across)

    def send_strip(half, direction, step):
        slot = (z + NZ - step) % NZ if direction == 0 else (z + step) % NZ
        src = q_ref if half == 0 and step == 0 else strip(slot, owner[half])
        start(
            remote(
                src, strip(slot, owner[half]), ring_send.at[half, direction, step], ring_recv.at[half, direction, step],
                (det, right if direction == 0 else left),
            )
        )

    def take_strip(half, step):
        for direction in (0, 1):
            if step < reach(half, direction):
                slot = (z + NZ - step - 1) % NZ if direction == 0 else (z + step + 1) % NZ
                here = strip(slot, owner[half])
                remote(q_ref, here, ring_send.at[half, direction, step], ring_recv.at[half, direction, step], side).wait_recv()
                if step + 1 < reach(half, direction):
                    send_strip(half, direction, step + 1)
                index = 1 + direction * NZ // 2 + step
                start(remote(here, here, core_send.at[half, index], core_recv.at[half, index], (partner, tm)))

    for direction in (0, 1):
        send_strip(0, direction, 0)
    start(remote(q_ref, strip(z, det), core_send.at[0, 0], core_recv.at[0, 0], (partner, tm)))
    stores = []
    for i, (src, dst) in enumerate(((q_own, strip(z, det)), (f_own, fo_ref.at[mine]), (w_own, wo_ref.at[mine]))):
        loads[i].wait()
        copy = pltpu.make_async_copy(src, dst, store_sem.at[i])
        copy.start()
        stores.append(copy)

    remote(q_ref, strip(z, across), hi_send, hi_recv, (across, tm)).wait_recv()
    for direction in (0, 1):
        send_strip(1, direction, 0)
    start(remote(strip(z, across), strip(z, across), core_send.at[1, 0], core_recv.at[1, 0], (partner, tm)))

    slot_of = {1: behind * NX + x, 2: ahead * NX + x, 0: y * NX + other, 5: facing * NX + x, 6: facing * NX + other,
               3: behind * NX + other, 4: ahead * NX + other}

    def near(part):
        for link in (1, 2, 0):
            wait_block(link, slot_of[link], part)
            if link == 1 and part != 1:
                send_block(5, slot_of[1], part, up)
            if link == 2 and part == 1:
                send_block(5, slot_of[2], part, down)
            if link == 0:
                send_block(3, slot_of[0], part, up)
                send_block(4, slot_of[0], part, down)

    def opposite(part):
        wait_block(5, slot_of[5], part)
        send_block(6, slot_of[5], part, side)

    take_strip(0, 0)
    near(0)
    take_strip(1, 0)
    near(1)
    take_strip(0, 1)
    near(2)
    take_strip(1, 1)
    opposite(0)
    opposite(1)
    take_strip(0, 2)
    opposite(2)
    take_strip(1, 2)
    take_strip(0, 3)
    take_strip(1, 3)

    loads[3].wait()
    for k, peer in enumerate(far):
        remote(p_ref, pos_all.at[mine], pos_send.at[k], pos_recv.at[k], peer).wait_recv()
    run_order(pos_all, order_ref, y, x)

    for part in range(3):
        for link in (3, 4, 6):
            wait_block(link, slot_of[link], part)
    theirs = (partner, hi_of(partner))
    for half in (0, 1):
        for direction in (0, 1):
            for step in range(-1 if direction == 0 else 0, reach(half, direction)):
                slot = (z + NZ - step - 1) % NZ if direction == 0 else (z + step + 1) % NZ
                index = 0 if step < 0 else 1 + direction * NZ // 2 + step
                remote(
                    q_ref, strip(slot, theirs[half]), core_send.at[half, index], core_recv.at[half, index], (partner, tm)
                ).wait_recv()
    for copy in stores:
        copy.wait()
    for copy in started:
        copy.wait_send()


def gather_all(quarter, floats, fracs, positions):
    bf, f32, i32 = jnp.bfloat16, jnp.float32, jnp.int32
    return pl.pallas_call(
        gather_kernel,
        out_shape=(
            jax.ShapeDtypeStruct((NZ, TILE_DEV, 3, PIX, PIX), bf),
            jax.ShapeDtypeStruct((NB, *floats.shape), f32),
            jax.ShapeDtypeStruct((NB, *fracs.shape), bf),
            jax.ShapeDtypeStruct((2 * DET, LANE), i32),
        ),
        in_specs=[ANY] * 4,
        out_specs=(ANY, ANY, ANY, VM),
        scratch_shapes=[
            pltpu.VMEM(quarter.shape, bf),
            pltpu.VMEM(floats.shape, f32),
            pltpu.VMEM(fracs.shape, bf),
            pltpu.VMEM((NB, *positions.shape), i32),
            DMA((4,)),
            DMA((3,)),
            DMA((NB,)),
            DMA((NB,)),
            DMA((7, 3)),
            DMA((7, 3)),
            DMA((2, 2, NZ // 2)),
            DMA((2, 2, NZ // 2)),
            DMA((2, NZ + 1)),
            DMA((2, NZ + 1)),
            DMA,
            DMA,
        ],
        compiler_params=pltpu.CompilerParams(collective_id=0, has_side_effects=True),
        name="gather_all",
    )(quarter, floats, fracs, positions)


def sin_cos(v):
    quarter = jnp.round(v * 0.6366197723675814)
    u = v - quarter * 1.5703125
    u = u - quarter * 4.837512969970703e-4
    u = u - quarter * 7.549789948768648e-8
    u2 = u * u
    s = u + u * u2 * (-1.6666654611e-1 + u2 * (8.3321608736e-3 + u2 * -1.9515295891e-4))
    c = 1.0 - 0.5 * u2 + u2 * u2 * (4.166664568298827e-2 + u2 * (-1.388731625493765e-3 + u2 * 2.443315711809948e-5))
    q = quarter.astype(jnp.int32) & 3
    odd = (q & 1) == 1
    sin = jnp.where(odd, c, s)
    cos = jnp.where(odd, s, c)
    sin = jnp.where(q >= 2, -sin, sin)
    cos = jnp.where((q == 1) | (q == 2), -cos, cos)
    return sin, cos


def low_of(high):
    return (1.0 - high).astype(jnp.bfloat16).astype(jnp.float32)


def run_of(entry):
    run = entry & (ALL_RUNS - 1)
    return entry >> 10, (run >> 4) & (NB - 1), run >> 7, run & (RUNS - 1)


def spread(index, low, high, rows):
    bf = jnp.bfloat16
    wide = [jnp.broadcast_to(v, (HALF, LANE)).astype(bf) for v in (index, index + 1.0, low, high)]
    zero = jnp.zeros((HALF, LANE), bf)
    parts = []
    for b in range(PIX // HALF):
        row = rows[b * HALF : (b + 1) * HALF]
        parts.append(jnp.where(row == wide[0], wide[2], jnp.where(row == wide[1], wide[3], zero)))
    return jnp.concatenate(parts, axis=0)


def forward_kernel(list_ref, tiles_ref, f_ref, w_ref, sig_ref, cs_ref, hit_ref, frac_ref):
    def prepare(z, _):
        code = f_ref[z, 0]
        row = jnp.floor(code * (1.0 / PIX))
        hit_ref[z, 0] = row
        hit_ref[z, 1] = code - row * PIX
        sin, cos = sin_cos(2.0 * f_ref[z, 1])
        cs_ref[z, 0] = cos
        cs_ref[z, 1] = sin
        frac_ref[z, 0] = w_ref[z, 0].astype(jnp.float32)
        frac_ref[z, 1] = w_ref[z, 1].astype(jnp.float32)
        sig_ref[z] = jnp.zeros_like(sig_ref[z])
        return 0

    lax.fori_loop(0, NB, prepare, 0)
    count = list_ref[DET, 0]
    rows = lax.broadcasted_iota(jnp.int32, (PIX, LANE), 0).astype(jnp.float32).astype(jnp.bfloat16)

    def body(step, _):
        for u in range(UNROLL):
            k = step * UNROLL + u
            tile, z, d, r = run_of(list_ref[k >> 7, k & (LANE - 1)])
            at = (r, pl.ds(d, 1), slice(None))
            col_high = frac_ref[z, 1, *at]
            row_high = frac_ref[z, 0, *at]
            col_weight = spread(hit_ref[z, 1, *at], low_of(col_high), col_high, rows)
            row_weight = spread(hit_ref[z, 0, *at], low_of(row_high), row_high, rows).astype(jnp.float32)
            partial = jnp.dot(tiles_ref[tile], col_weight, preferred_element_type=jnp.float32)
            value = [
                jnp.sum(partial[p * PIX : (p + 1) * PIX] * row_weight, axis=0, keepdims=True) for p in range(3)
            ]
            total = value[0] + cs_ref[z, 0, *at] * value[1] + cs_ref[z, 1, *at] * value[2]
            sig_ref[z, d, pl.ds(r, 1), :] = jnp.where(k < count, total, 0.0)
        return 0

    lax.fori_loop(0, (count + UNROLL - 1) // UNROLL, body, 0)


def forward(order, tiles, floats, fracs):
    f32 = jnp.float32
    block = (NB, DET, RUNS, LANE)
    pair = (NB, 2, RUNS, DET, LANE)
    return pl.pallas_call(
        forward_kernel,
        out_shape=(jax.ShapeDtypeStruct(block, f32), jax.ShapeDtypeStruct(pair, f32)),
        in_specs=[SM, VM, VM, VM],
        out_specs=(VM, VM),
        scratch_shapes=[pltpu.VMEM(pair, f32), pltpu.VMEM(pair, f32)],
        name="forward",
    )(order, tiles, floats, fracs)


def backward_kernel(list_ref, f_ref, w_ref, cs_ref, filt_ref, acc_ref, hit_ref, frac_ref):
    def prepare(z, _):
        code = f_ref[z, 0]
        row = jnp.floor(code * (1.0 / PIX))
        hit_ref[z, 0] = row
        hit_ref[z, 1] = code - row * PIX
        frac_ref[z, 0] = w_ref[z, 0].astype(jnp.float32)
        frac_ref[z, 1] = w_ref[z, 1].astype(jnp.float32)
        return 0

    lax.fori_loop(0, NB, prepare, 0)

    def clear(t, _):
        acc_ref[t] = jnp.zeros_like(acc_ref[t])
        return 0

    lax.fori_loop(0, TILE_DEV * NZ, clear, 0)
    count = list_ref[DET, 0]
    rows = lax.broadcasted_iota(jnp.int32, (PIX, LANE), 0).astype(jnp.float32).astype(jnp.bfloat16)

    def body(step, _):
        for u in range(UNROLL):
            k = step * UNROLL + u
            tile, z, d, r = run_of(list_ref[k >> 7, k & (LANE - 1)])
            at = (r, pl.ds(d, 1), slice(None))
            col_high = frac_ref[z, 1, *at]
            row_high = frac_ref[z, 0, *at]
            row_low = low_of(row_high)
            col_weight = spread(hit_ref[z, 1, *at], low_of(col_high), col_high, rows)
            filt = jnp.where(k < count, filt_ref[z, d, pl.ds(r, 1), :], 0.0)
            hit = hit_ref[z, 0, *at]
            parts = []
            for p in range(3):
                scaled = filt if p == 0 else cs_ref[z, p - 1, *at] * filt
                parts.append(spread(hit, scaled * row_low, scaled * row_high, rows))
            weighted = jnp.concatenate(parts, axis=0)
            acc_ref[tile] += lax.dot_general(
                weighted, col_weight, (((1,), (1,)), ((), ())), preferred_element_type=jnp.float32
            )
        return 0

    lax.fori_loop(0, (count + UNROLL - 1) // UNROLL, body, 0)


def backward(order, floats, fracs, turns, filtered):
    f32 = jnp.float32
    pair = (NB, 2, RUNS, DET, LANE)
    return pl.pallas_call(
        backward_kernel,
        out_shape=jax.ShapeDtypeStruct((TILE_DEV * NZ, 3 * PIX, PIX), f32),
        in_specs=[SM, VM, VM, VM, VM],
        out_specs=VM,
        scratch_shapes=[pltpu.VMEM(pair, f32), pltpu.VMEM(pair, f32)],
        name="backward",
    )(order, floats, fracs, turns, filtered)


def toeplitz(noise_ref, line_ref, hi_ref, lo_ref):
    square = (LANE, LANE)
    lanes = lax.broadcasted_iota(jnp.int32, square, 1)
    rows = lax.broadcasted_iota(jnp.int32, square, 0)
    first = lax.broadcasted_iota(jnp.int32, (DET, LANE), 1) == 0
    for q in range(REACH):
        lags = noise_ref[:, q * LANE : (q + 1) * LANE]
        line_ref[q] = jnp.where(first, lags + 1.0, lags) if q == 0 else lags
    line_ref[REACH] = jnp.where(first, jnp.broadcast_to(noise_ref[:, REACH * LANE :], (DET, LANE)), 0.0)

    def one(d, _):
        def put(q, matrix):
            high = matrix.astype(jnp.bfloat16)
            hi_ref[d, q] = high
            lo_ref[d, q] = (matrix - high.astype(jnp.float32)).astype(jnp.bfloat16)

        before = None
        for q in range(REACH + 1):
            lags = line_ref[q, pl.ds(d, 1), :]
            after = pltpu.roll(jnp.broadcast_to(lags, square), 0, 1, stride=1, stride_axis=0)
            if q == 0:
                put(0, jnp.where(lanes >= rows, after, 0.0))
                put(REACH + 1, jnp.where(lanes > rows, after, 0.0))
            else:
                put(q, jnp.where(lanes >= rows, after, before))
            before = after
        return 0

    lax.fori_loop(0, DET, one, 0)


STRAIGHT = (((1,), (0,)), ((), ()))
CROSSED = (((1,), (1,)), ((), ()))


def filter_kernel(
    part_ref, noise_ref, out_ref, land, ext, filt, lags, t_hi, t_lo,
    own_sem, send, recv, halo_send, halo_recv, back_send, back_recv,
):
    det, tm, y, z, x = place()
    total_tm = NY * NZ * NX
    mine = y * NX + x
    prior, later = (tm + total_tm - 1) % total_tm, (tm + 1) % total_tm

    def slot(k, sign):
        dy, dx = PEERS[k]
        return ((y + sign * dy + NY) % NY) * NX + (x + dx) % NX

    peers = [(det, tm_of((y + dy) % NY, z, (x + dx) % NX)) for dy, dx in PEERS]
    greet(peers + [(det, later), (det, prior)])
    own = pltpu.make_async_copy(part_ref.at[mine], land.at[NB - 1], own_sem)
    own.start()
    sends = []
    for k, peer in enumerate(peers):
        copy = remote(part_ref.at[slot(k, 1)], land.at[k], send.at[k], recv.at[k], peer)
        copy.start()
        sends.append(copy)
    toeplitz(noise_ref, lags, t_hi, t_lo)
    own.wait()
    total = land[NB - 1]
    for k in range(NB - 1):
        sends[k].wait_recv()
        total = total + land[k]
    ext[:, REACH : REACH + RUNS, :] = total
    to_prior = remote(
        ext.at[:, pl.ds(REACH, REACH), :], ext.at[:, pl.ds(REACH + RUNS, REACH), :],
        halo_send.at[0], halo_recv.at[0], (det, prior),
    )
    to_later = remote(
        ext.at[:, pl.ds(RUNS, REACH), :], ext.at[:, pl.ds(0, REACH), :], halo_send.at[1], halo_recv.at[1], (det, later)
    )
    to_prior.start()
    to_later.start()
    to_prior.wait_recv()
    to_later.wait_recv()
    first, last = tm == 0, tm == total_tm - 1

    def product(left, right, crossed):
        return lax.dot_general(left, right, CROSSED if crossed else STRAIGHT, preferred_element_type=jnp.float32)

    for d in range(DET):
        line_all = jnp.concatenate(
            [
                jnp.where(first, 0.0, ext[d, :REACH]),
                ext[d, REACH : REACH + RUNS],
                jnp.where(last, 0.0, ext[d, REACH + RUNS :]),
            ],
            axis=0,
        )
        result = jnp.zeros((RUNS, LANE), jnp.float32)
        for m in range(2 * REACH + 1):
            window = line_all[m : m + RUNS]
            high = window.astype(jnp.bfloat16)
            low = (window - high.astype(jnp.float32)).astype(jnp.bfloat16)
            stack = jnp.concatenate([high, low], axis=0)
            q = REACH - m
            for index, crossed in [(q, False)] if q > 0 else [(-q, True)] if q < 0 else [(0, False), (REACH + 1, True)]:
                both = product(stack, t_hi[d, index], crossed)
                result += both[:RUNS] + both[RUNS:] + product(high, t_lo[d, index], crossed)
        filt[d] = result
    back = []
    for k, peer in enumerate(peers):
        copy = remote(filt, out_ref.at[mine], back_send.at[k], back_recv.at[k], peer)
        copy.start()
        back.append(copy)
    own = pltpu.make_async_copy(filt, out_ref.at[mine], own_sem)
    own.start()
    own.wait()
    for k, peer in enumerate(peers):
        remote(filt, out_ref.at[slot(k, -1)], back_send.at[k], back_recv.at[k], peer).wait_recv()
    for copy in sends + back + [to_prior, to_later]:
        copy.wait_send()


def filtered_of(partial, noise_coef):
    f32, bf = jnp.float32, jnp.bfloat16
    block = (DET, RUNS, LANE)
    matrices = (DET, REACH + 2, LANE, LANE)
    return pl.pallas_call(
        filter_kernel,
        out_shape=jax.ShapeDtypeStruct((NB, *block), f32),
        in_specs=[ANY, VM],
        out_specs=ANY,
        scratch_shapes=[
            pltpu.VMEM((NB, *block), f32),
            pltpu.VMEM((DET, RUNS + 2 * REACH, LANE), f32),
            pltpu.VMEM(block, f32),
            pltpu.VMEM((REACH + 1, DET, LANE), f32),
            pltpu.VMEM(matrices, bf),
            pltpu.VMEM(matrices, bf),
            DMA,
            DMA((NB,)),
            DMA((NB,)),
            DMA((2,)),
            DMA((2,)),
            DMA((NB,)),
            DMA((NB,)),
        ],
        compiler_params=pltpu.CompilerParams(collective_id=1, has_side_effects=True),
        name="filter",
    )(partial, noise_coef)


CHUNKS = [(t, p) for t in range(TILE_DEV) for p in range(3)]
HALF_Z = NZ // 2
OFFSETS = [4, 3, -3, 2, -2, 1, -1, 0]


def collect_kernel(
    acc_ref, out_ref, own, land_core, land, land_hi, total,
    own_sem, core_send, core_recv, ring_send, ring_recv, hi_send, hi_recv,
):
    det, tm, y, z, x = place()
    core, hi = det % 2, det // 2
    partner, across = core_of(det), hi_of(det)
    neighbours = ((det, tm_of(y, (z + 1) % NZ, x)), (det, tm_of(y, (z + NZ - 1) % NZ, x)))
    loads = []
    for k, offset in enumerate(OFFSETS):
        copy = pltpu.make_async_copy(acc_ref.at[(z + offset + NZ) % NZ, :, :, :, core], own.at[k], own_sem.at[k])
        copy.start()
        loads.append(copy)
    greet([(partner, tm), (across, tm), *neighbours])
    started = []

    def start(copy):
        copy.start()
        started.append(copy)

    for k, offset in enumerate(OFFSETS):
        start(
            remote(
                acc_ref.at[(z + offset + NZ) % NZ, :, :, :, 1 - core], land_core.at[k], core_send.at[k], core_recv.at[k],
                (partner, tm),
            )
        )

    def ring(direction, step, c):
        t, p = CHUNKS[c]
        sign = 1 if direction == 0 else -1
        k = OFFSETS.index(sign * (HALF_Z - step)) if step else 0
        return remote(
            own.at[k, t, p], land.at[direction, step, t, p],
            ring_send.at[direction, step, c], ring_recv.at[direction, step, c], neighbours[direction],
        )

    def swapped(k):
        loads[k].wait()
        remote(acc_ref.at[0, :, :, :, 0], land_core.at[k], core_send.at[k], core_recv.at[k], (partner, tm)).wait_recv()

    swapped(0)
    for direction in (0, 1):
        for c, (t, p) in enumerate(CHUNKS):
            if t == direction:
                own[0, t, p] = own[0, t, p] + land_core[0, t, p]
    for p in range(3):
        for direction in (0, 1):
            start(ring(direction, 0, direction * 3 + p))
    for step in range(1, HALF_Z):
        keys = [OFFSETS.index(HALF_Z - step), OFFSETS.index(step - HALF_Z)]
        for k in keys:
            swapped(k)
        for i in range(len(CHUNKS)):
            for direction in (0, 1):
                c = (i + 3 * (1 - direction)) % len(CHUNKS) if step == 1 else i
                t, p = CHUNKS[c]
                k = keys[direction]
                value = own[k, t, p] + land_core[k, t, p]
                if step > 1 or t == direction:
                    ring(direction, step - 1, c).wait_recv()
                    value = value + land[direction, step - 1, t, p]
                own[k, t, p] = value
                start(ring(direction, step, c))
    last = len(OFFSETS) - 1
    swapped(last)

    def across_copy(c):
        t, p = CHUNKS[c]
        return remote(total.at[t, p, 1 - hi], land_hi.at[t, p], hi_send.at[c], hi_recv.at[c], (across, tm))

    for c, (t, p) in enumerate(CHUNKS):
        value = own[last, t, p] + land_core[last, t, p]
        for direction in (0, 1):
            ring(direction, HALF_Z - 1, c).wait_recv()
            value = value + land[direction, HALF_Z - 1, t, p]
        total[t, p] = value
        start(across_copy(c))
    for c, (t, p) in enumerate(CHUNKS):
        across_copy(c).wait_recv()
        out_ref[t, p] = total[t, p, hi] + land_hi[t, p]
    for copy in started:
        copy.wait_send()


def collect(acc):
    f32 = jnp.float32
    half = (TILE_DEV, 3, 2, STRIP, PIX)
    quarter = (TILE_DEV, 3, STRIP, PIX)
    return pl.pallas_call(
        collect_kernel,
        out_shape=jax.ShapeDtypeStruct(quarter, f32),
        in_specs=[ANY],
        out_specs=VM,
        scratch_shapes=[
            pltpu.VMEM((NZ, *half), f32),
            pltpu.VMEM((NZ, *half), f32),
            pltpu.VMEM((2, HALF_Z, *half), f32),
            pltpu.VMEM(quarter, f32),
            pltpu.VMEM(half, f32),
            DMA((NZ,)),
            DMA((NZ,)),
            DMA((NZ,)),
            DMA((2, HALF_Z, 6)),
            DMA((2, HALF_Z, 6)),
            DMA((6,)),
            DMA((6,)),
        ],
        compiler_params=pltpu.CompilerParams(collective_id=2, has_side_effects=True),
        name="collect",
    )(acc.reshape(NZ, TILE_DEV, 3, 2, 2, STRIP, PIX))


def body(
    sky_map, tile_home, piece_tiles, run_slot, hit_row, hit_col, frac_row, frac_col, angle, noise_coef
):
    floats, fracs, positions = packed(
        tile_home, piece_tiles.reshape(1, LISTED), run_slot, hit_row, hit_col, frac_row, frac_col, angle
    )
    tiles, all_floats, all_fracs, order = gather_all(sky_map, floats, fracs, positions)
    partial, turns = forward(order, tiles.reshape(TILE_DEV * NZ, 3 * PIX, PIX), all_floats, all_fracs)
    filtered = filtered_of(partial, noise_coef)
    acc = backward(order, all_floats, all_fracs, turns, filtered)
    return collect(acc)


def solution(mesh):
    placed = (
        P("tm", None, "det", None),
        P(),
        P("det", "tm", None),
        P("det", "tm"),
        P("det", "tm"),
        P("det", "tm"),
        P("det", "tm"),
        P("det", "tm"),
        P("det", "tm"),
        P("det", None),
    )
    return jax.shard_map(
        body, mesh=mesh, in_specs=placed, out_specs=P("tm", None, "det", None), check_vma=False
    )
```

```python
import functools

import jax
import jax.numpy as jnp
from jax import lax
from jax.experimental import pallas as pl
from jax.experimental.pallas import tpu as pltpu
from jax.sharding import PartitionSpec as P

MESH = pl.DeviceIdType.MESH
NY, NZ, NX = 4, 8, 2
NB = NY * NX
DET, RUNS, LANE = 8, 16, 128
PIX = 128
STRIP = 32
LISTED = 32
TILE_DEV = 2
REACH = 8
UNROLL = 16
HALF = 16
SENT = 2
PIECE_RUNS = DET * RUNS
ALL_RUNS = NB * PIECE_RUNS
ANY = pl.BlockSpec(memory_space=pl.ANY)
VM = pl.BlockSpec(memory_space=pltpu.VMEM)
SM = pl.BlockSpec(memory_space=pltpu.SMEM)
DMA = pltpu.SemaphoreType.DMA
PEERS = [(dy, dx) for dy in range(NY) for dx in range(NX) if (dy, dx) != (0, 0)]


def place():
    det, tm = lax.axis_index("det"), lax.axis_index("tm")
    y, z, x = tm // (NZ * NX), (tm // NX) % NZ, tm % NX
    return det, tm, y, z, x


def tm_of(y, z, x):
    return (y * NZ + z) * NX + x


def core_of(det):
    return det + 1 - 2 * (det % 2)


def hi_of(det):
    return (det + 2) % 4


def greet(peers):
    barrier = pltpu.get_barrier_semaphore()
    for peer in peers:
        pl.semaphore_signal(barrier, inc=1, device_id=peer, device_id_type=MESH)
    pl.semaphore_wait(barrier, len(peers))


def remote(src, dst, send, recv, peer):
    return pltpu.make_async_remote_copy(
        src_ref=src, dst_ref=dst, send_sem=send, recv_sem=recv, device_id=peer, device_id_type=MESH
    )


def run_order(pos_ref, order_ref, y, x):
    f32, i32 = jnp.float32, jnp.int32
    lanes = lax.broadcasted_iota(i32, (RUNS, LANE), 1)
    offset = lax.broadcasted_iota(i32, (RUNS, LANE), 0)
    spot = jnp.zeros((DET, LANE), f32)
    for slot in range(NB):
        placed = (lanes == offset + slot * RUNS).astype(f32).astype(jnp.bfloat16)
        spot += jnp.dot(pos_ref[slot].astype(f32).astype(jnp.bfloat16), placed, preferred_element_type=f32)
    pos = spot.astype(i32)
    here = (pos // (TILE_DEV * NX * NZ) == y) & ((pos // TILE_DEV) % NX == x)
    tile = ((pos // (TILE_DEV * NX)) % NZ) * TILE_DEV + pos % TILE_DEV
    run = lax.broadcasted_iota(i32, (DET, LANE), 0) * LANE + lax.broadcasted_iota(i32, (DET, LANE), 1)
    key = (jnp.where(here, tile, TILE_DEV * NZ) * ALL_RUNS + run).astype(f32)
    entry_t = (tile * ALL_RUNS + run).astype(f32).T
    key_t = key.T
    square = (LANE, LANE)
    ranks = []
    for d in range(DET):
        mine = jnp.broadcast_to(key[d : d + 1], square)
        less = jnp.zeros(square, f32)
        for e in range(DET):
            less += jnp.where(jnp.broadcast_to(key_t[:, e : e + 1], square) < mine, 1.0, 0.0)
        ranks.append(jnp.sum(less, axis=0, keepdims=True))
    rank_t = jnp.concatenate(ranks, axis=0).T
    place = lax.broadcasted_iota(i32, square, 1).astype(f32)
    for d in range(DET):
        found = jnp.zeros(square, f32)
        for e in range(DET):
            at = jnp.broadcast_to(rank_t[:, e : e + 1], square) - (d * LANE)
            found += jnp.where(at == place, jnp.broadcast_to(entry_t[:, e : e + 1], square), 0.0)
        order_ref[d : d + 1, :] = jnp.sum(found, axis=0, keepdims=True).astype(i32)
    count = jnp.sum(jnp.sum(here.astype(f32), axis=1, keepdims=True), axis=0, keepdims=True)
    order_ref[DET:, :] = jnp.broadcast_to(count, (DET, LANE)).astype(i32)


def pack(home_ref, piece_ref, slot_ref, row_ref, col_ref, low_ref, high_ref, angle_ref, f_own, w_own, p_own):
    for r in range(RUNS):
        at = slice(r * LANE, (r + 1) * LANE)
        f_own[0, r] = (row_ref[:, at] * PIX + col_ref[:, at]).astype(jnp.float32)
        f_own[1, r] = angle_ref[:, at]
        w_own[0, r] = low_ref[:, at]
        w_own[1, r] = high_ref[:, at]
    slots = slot_ref[...]
    position = jnp.zeros_like(slots)
    for s in range(LISTED):
        position = jnp.where(slots == s, home_ref[piece_ref[0, s]], position)
    p_own[...] = position


def gather_kernel(
    home_ref, piece_ref, slot_ref, row_ref, col_ref, low_ref, high_ref, angle_ref, q_ref,
    tiles_ref, fo_ref, wo_ref, order_ref,
    q_own, f_own, w_own, p_own, pos_all, load_sem, store_sem,
    pos_send, pos_recv, block_send, block_recv, strip_send, strip_recv, core_send, core_recv, hi_send, hi_recv,
):
    det, tm, y, z, x = place()
    partner, across = core_of(det), hi_of(det)
    ahead, behind = (y + 1) % NY, (y + NY - 1) % NY
    facing = (y + NY // 2) % NY
    other = 1 - x
    up, down, side = (det, tm_of(ahead, z, x)), (det, tm_of(behind, z, x)), (det, tm_of(y, z, other))
    far = [(det, tm_of((y + dy) % NY, z, (x + dx) % NX)) for dy, dx in PEERS]

    def along(direction, jump):
        return (det, tm_of(y, (z + jump) % NZ if direction == 0 else (z + NZ - jump) % NZ, x))

    def strip(slot, d):
        return tiles_ref.at[slot, :, :, pl.ds(d * STRIP, STRIP), :]

    def block(slot, part):
        return fo_ref.at[slot, part] if part < 2 else wo_ref.at[slot]

    def own_block(part):
        return f_own.at[part] if part < 2 else w_own

    mine = y * NX + x
    load = pltpu.make_async_copy(q_ref, q_own, load_sem)
    load.start()
    greeted = [along(d, j) for d in (0, 1) for j in (1, 2)] + [(partner, tm), (across, tm)] + far
    barrier = pltpu.get_barrier_semaphore()
    for peer in greeted:
        pl.semaphore_signal(barrier, inc=1, device_id=peer, device_id_type=MESH)
    pack(home_ref, piece_ref, slot_ref, row_ref, col_ref, low_ref, high_ref, angle_ref, f_own, w_own, p_own)
    pl.semaphore_wait(barrier, len(greeted))

    started = []

    def start(copy):
        copy.start()
        started.append(copy)

    start(remote(q_ref, strip(z, det), hi_send, hi_recv, (across, tm)))
    for k, peer in enumerate(far):
        start(remote(p_own, pos_all.at[mine], pos_send.at[k], pos_recv.at[k], peer))

    def send_block(link, slot, part, peer, own=False):
        start(
            remote(
                own_block(part) if own else block(slot, part), block(slot, part),
                block_send.at[link, part], block_recv.at[link, part], peer,
            )
        )

    def wait_block(link, slot, part):
        remote(own_block(part), block(slot, part), block_send.at[link, part], block_recv.at[link, part], side).wait_recv()

    owner = (det, across)

    def source_slot(direction, distance):
        return (z + NZ - distance) % NZ if direction == 0 else (z + distance) % NZ

    def send_strip(half, direction, distance):
        slot = z if distance < 3 else source_slot(direction, 2)
        here = strip(slot, owner[half])
        start(
            remote(
                q_ref if half == 0 and distance < 3 else here, here,
                strip_send.at[half, direction, distance - 1], strip_recv.at[half, direction, distance - 1],
                along(direction, 2 - distance % 2),
            )
        )

    def reach(half, direction):
        return NZ // 2 if half == direction else NZ // 2 - 1

    def to_partner(half, index, slot):
        here = strip(slot, owner[half])
        start(
            remote(
                q_ref if half == 0 and index == 0 else here, here, core_send.at[half, index], core_recv.at[half, index],
                (partner, tm),
            )
        )

    def take_strip(half, distance):
        for direction in (0, 1):
            if distance <= reach(half, direction):
                slot = source_slot(direction, distance)
                remote(
                    q_ref, strip(slot, owner[half]),
                    strip_send.at[half, direction, distance - 1], strip_recv.at[half, direction, distance - 1], side,
                ).wait_recv()
                if distance == 2:
                    if reach(half, direction) == 4:
                        send_strip(half, direction, 4)
                    send_strip(half, direction, 3)
                to_partner(half, direction * NZ // 2 + distance, slot)

    def first_strips(half):
        for distance in (2, 1):
            for direction in (0, 1):
                send_strip(half, direction, distance)
        to_partner(half, 0, z)

    first_strips(0)
    for part in range(3):
        send_block(1, mine, part, up, True)
        send_block(2, mine, part, down, True)
        send_block(0, mine, part, side, True)
    load.wait()
    stores = []
    for i, (src, dst) in enumerate(
        ((q_own, strip(z, det)), (f_own, fo_ref.at[mine]), (w_own, wo_ref.at[mine]), (p_own, pos_all.at[mine]))
    ):
        copy = pltpu.make_async_copy(src, dst, store_sem.at[i])
        copy.start()
        stores.append(copy)

    slot_of = {1: behind * NX + x, 2: ahead * NX + x, 0: y * NX + other, 5: facing * NX + x, 6: facing * NX + other,
               3: behind * NX + other, 4: ahead * NX + other}

    def near(part):
        for link in (1, 2, 0):
            wait_block(link, slot_of[link], part)
            if link == 1 and part != 1:
                send_block(5, slot_of[1], part, up)
            if link == 2 and part == 1:
                send_block(5, slot_of[2], part, down)
            if link == 0:
                send_block(3, slot_of[0], part, up)
                send_block(4, slot_of[0], part, down)

    def opposite(part):
        wait_block(5, slot_of[5], part)
        send_block(6, slot_of[5], part, side)

    near(0)
    remote(q_ref, strip(z, across), hi_send, hi_recv, (across, tm)).wait_recv()
    first_strips(1)
    take_strip(0, 2)
    near(1)
    near(2)
    take_strip(0, 1)
    opposite(0)
    take_strip(1, 2)
    opposite(1)
    opposite(2)
    take_strip(1, 1)
    take_strip(0, 3)
    take_strip(0, 4)

    stores[3].wait()
    for k, peer in enumerate(far):
        remote(p_own, pos_all.at[mine], pos_send.at[k], pos_recv.at[k], peer).wait_recv()
    run_order(pos_all, order_ref, y, x)

    take_strip(1, 3)
    take_strip(1, 4)
    for part in range(3):
        for link in (3, 4, 6):
            wait_block(link, slot_of[link], part)
    theirs = (partner, hi_of(partner))
    for half in (0, 1):
        places = [(0, z)]
        for direction in (0, 1):
            for distance in range(1, reach(half, direction) + 1):
                places.append((direction * NZ // 2 + distance, source_slot(direction, distance)))
        for index, slot in places:
            remote(
                q_ref, strip(slot, theirs[half]), core_send.at[half, index], core_recv.at[half, index], (partner, tm)
            ).wait_recv()
    for copy in stores[:3]:
        copy.wait()
    for copy in started:
        copy.wait_send()


def gather_all(tile_home, piece_list, run_slot, hit_row, hit_col, frac_row, frac_col, angle, quarter):
    bf, f32, i32 = jnp.bfloat16, jnp.float32, jnp.int32
    samples = (2, RUNS, DET, LANE)
    return pl.pallas_call(
        gather_kernel,
        out_shape=(
            jax.ShapeDtypeStruct((NZ, TILE_DEV, 3, PIX, PIX), bf),
            jax.ShapeDtypeStruct((NB, *samples), f32),
            jax.ShapeDtypeStruct((NB, *samples), bf),
            jax.ShapeDtypeStruct((2 * DET, LANE), i32),
        ),
        in_specs=[SM, SM] + [VM] * 6 + [ANY],
        out_specs=(ANY, ANY, ANY, VM),
        scratch_shapes=[
            pltpu.VMEM(quarter.shape, bf),
            pltpu.VMEM(samples, f32),
            pltpu.VMEM(samples, bf),
            pltpu.VMEM((DET, RUNS), i32),
            pltpu.VMEM((NB, DET, RUNS), i32),
            DMA,
            DMA((4,)),
            DMA((NB,)),
            DMA((NB,)),
            DMA((7, 3)),
            DMA((7, 3)),
            DMA((2, 2, NZ // 2)),
            DMA((2, 2, NZ // 2)),
            DMA((2, NZ + 1)),
            DMA((2, NZ + 1)),
            DMA,
            DMA,
        ],
        compiler_params=pltpu.CompilerParams(collective_id=0, has_side_effects=True),
        name="gather_all",
    )(tile_home, piece_list, run_slot, hit_row, hit_col, frac_row, frac_col, angle, quarter)


def sin_cos(v):
    quarter = jnp.round(v * 0.6366197723675814)
    u = v - quarter * 1.5703125
    u = u - quarter * 4.837512969970703e-4
    u = u - quarter * 7.549789948768648e-8
    u2 = u * u
    s = u + u * u2 * (-1.6666654611e-1 + u2 * (8.3321608736e-3 + u2 * -1.9515295891e-4))
    c = 1.0 - 0.5 * u2 + u2 * u2 * (4.166664568298827e-2 + u2 * (-1.388731625493765e-3 + u2 * 2.443315711809948e-5))
    q = quarter.astype(jnp.int32) & 3
    odd = (q & 1) == 1
    sin = jnp.where(odd, c, s)
    cos = jnp.where(odd, s, c)
    sin = jnp.where(q >= 2, -sin, sin)
    cos = jnp.where((q == 1) | (q == 2), -cos, cos)
    return sin, cos


def low_of(high):
    return (1.0 - high).astype(jnp.bfloat16).astype(jnp.float32)


def run_of(entry):
    run = entry & (ALL_RUNS - 1)
    return entry >> 10, (run >> 4) & (NB - 1), run >> 7, run & (RUNS - 1)


def spread(index, low, high, rows):
    bf = jnp.bfloat16
    wide = [jnp.broadcast_to(v, (HALF, LANE)).astype(bf) for v in (index, index + 1.0, low, high)]
    zero = jnp.zeros((HALF, LANE), bf)
    parts = []
    for b in range(PIX // HALF):
        row = rows[b * HALF : (b + 1) * HALF]
        parts.append(jnp.where(row == wide[0], wide[2], jnp.where(row == wide[1], wide[3], zero)))
    return jnp.concatenate(parts, axis=0)


def forward_kernel(list_ref, tiles_ref, f_ref, w_ref, sig_ref, cs_ref, hit_ref, frac_ref):
    def prepare(z, _):
        code = f_ref[z, 0]
        row = jnp.floor(code * (1.0 / PIX))
        hit_ref[z, 0] = row
        hit_ref[z, 1] = code - row * PIX
        sin, cos = sin_cos(2.0 * f_ref[z, 1])
        cs_ref[z, 0] = cos
        cs_ref[z, 1] = sin
        frac_ref[z, 0] = w_ref[z, 0].astype(jnp.float32)
        frac_ref[z, 1] = w_ref[z, 1].astype(jnp.float32)
        sig_ref[z] = jnp.zeros_like(sig_ref[z])
        return 0

    lax.fori_loop(0, NB, prepare, 0)
    count = list_ref[DET, 0]
    rows = lax.broadcasted_iota(jnp.int32, (PIX, LANE), 0).astype(jnp.float32).astype(jnp.bfloat16)

    def body(step, _):
        for u in range(UNROLL):
            k = step * UNROLL + u
            tile, z, d, r = run_of(list_ref[k >> 7, k & (LANE - 1)])
            at = (r, pl.ds(d, 1), slice(None))
            col_high = frac_ref[z, 1, *at]
            row_high = frac_ref[z, 0, *at]
            col_weight = spread(hit_ref[z, 1, *at], low_of(col_high), col_high, rows)
            row_weight = spread(hit_ref[z, 0, *at], low_of(row_high), row_high, rows).astype(jnp.float32)
            partial = jnp.dot(tiles_ref[tile], col_weight, preferred_element_type=jnp.float32)
            value = [
                jnp.sum(partial[p * PIX : (p + 1) * PIX] * row_weight, axis=0, keepdims=True) for p in range(3)
            ]
            total = value[0] + cs_ref[z, 0, *at] * value[1] + cs_ref[z, 1, *at] * value[2]
            sig_ref[z, d, pl.ds(r, 1), :] = jnp.where(k < count, total, 0.0)
        return 0

    lax.fori_loop(0, (count + UNROLL - 1) // UNROLL, body, 0)


def forward(order, tiles, floats, fracs):
    f32 = jnp.float32
    block = (NB, DET, RUNS, LANE)
    pair = (NB, 2, RUNS, DET, LANE)
    return pl.pallas_call(
        forward_kernel,
        out_shape=(jax.ShapeDtypeStruct(block, f32), jax.ShapeDtypeStruct(pair, f32)),
        in_specs=[SM, VM, VM, VM],
        out_specs=(VM, VM),
        scratch_shapes=[pltpu.VMEM(pair, f32), pltpu.VMEM(pair, f32)],
        name="forward",
    )(order, tiles, floats, fracs)


def backward_kernel(list_ref, f_ref, w_ref, cs_ref, filt_ref, acc_ref, hit_ref, frac_ref):
    def prepare(z, _):
        code = f_ref[z, 0]
        row = jnp.floor(code * (1.0 / PIX))
        hit_ref[z, 0] = row
        hit_ref[z, 1] = code - row * PIX
        frac_ref[z, 0] = w_ref[z, 0].astype(jnp.float32)
        frac_ref[z, 1] = w_ref[z, 1].astype(jnp.float32)
        return 0

    lax.fori_loop(0, NB, prepare, 0)

    def clear(t, _):
        acc_ref[t] = jnp.zeros_like(acc_ref[t])
        return 0

    lax.fori_loop(0, TILE_DEV * NZ, clear, 0)
    count = list_ref[DET, 0]
    rows = lax.broadcasted_iota(jnp.int32, (PIX, LANE), 0).astype(jnp.float32).astype(jnp.bfloat16)

    def body(step, _):
        for u in range(UNROLL):
            k = step * UNROLL + u
            tile, z, d, r = run_of(list_ref[k >> 7, k & (LANE - 1)])
            at = (r, pl.ds(d, 1), slice(None))
            col_high = frac_ref[z, 1, *at]
            row_high = frac_ref[z, 0, *at]
            row_low = low_of(row_high)
            col_weight = spread(hit_ref[z, 1, *at], low_of(col_high), col_high, rows)
            filt = jnp.where(k < count, filt_ref[z, d, pl.ds(r, 1), :], 0.0)
            hit = hit_ref[z, 0, *at]
            parts = []
            for p in range(3):
                scaled = filt if p == 0 else cs_ref[z, p - 1, *at] * filt
                parts.append(spread(hit, scaled * row_low, scaled * row_high, rows))
            weighted = jnp.concatenate(parts, axis=0)
            acc_ref[tile] += lax.dot_general(
                weighted, col_weight, (((1,), (1,)), ((), ())), preferred_element_type=jnp.float32
            )
        return 0

    lax.fori_loop(0, (count + UNROLL - 1) // UNROLL, body, 0)


def backward(order, floats, fracs, turns, filtered):
    f32 = jnp.float32
    pair = (NB, 2, RUNS, DET, LANE)
    return pl.pallas_call(
        backward_kernel,
        out_shape=jax.ShapeDtypeStruct((TILE_DEV * NZ, 3 * PIX, PIX), f32),
        in_specs=[SM, VM, VM, VM, VM],
        out_specs=VM,
        scratch_shapes=[pltpu.VMEM(pair, f32), pltpu.VMEM(pair, f32)],
        name="backward",
    )(order, floats, fracs, turns, filtered)


def toeplitz(noise_ref, line_ref, hi_ref, lo_ref):
    square = (LANE, LANE)
    lanes = lax.broadcasted_iota(jnp.int32, square, 1)
    rows = lax.broadcasted_iota(jnp.int32, square, 0)
    first = lax.broadcasted_iota(jnp.int32, (DET, LANE), 1) == 0
    for q in range(REACH):
        lags = noise_ref[:, q * LANE : (q + 1) * LANE]
        line_ref[q] = jnp.where(first, lags + 1.0, lags) if q == 0 else lags
    line_ref[REACH] = jnp.where(first, jnp.broadcast_to(noise_ref[:, REACH * LANE :], (DET, LANE)), 0.0)

    def one(d, _):
        def put(q, matrix):
            high = matrix.astype(jnp.bfloat16)
            hi_ref[d, q] = high
            lo_ref[d, q] = (matrix - high.astype(jnp.float32)).astype(jnp.bfloat16)

        before = None
        for q in range(REACH + 1):
            lags = line_ref[q, pl.ds(d, 1), :]
            after = pltpu.roll(jnp.broadcast_to(lags, square), 0, 1, stride=1, stride_axis=0)
            if q == 0:
                put(0, jnp.where(lanes >= rows, after, 0.0))
                put(REACH + 1, jnp.where(lanes > rows, after, 0.0))
            else:
                put(q, jnp.where(lanes >= rows, after, before))
            before = after
        return 0

    lax.fori_loop(0, DET, one, 0)


STRAIGHT = (((1,), (0,)), ((), ()))
CROSSED = (((1,), (1,)), ((), ()))


def filter_kernel(
    part_ref, noise_ref, out_ref, land, ext, filt, lags, t_hi, t_lo,
    own_sem, store_sem, send, recv, halo_send, halo_recv, back_send, back_recv,
):
    det, tm, y, z, x = place()
    total_tm = NY * NZ * NX
    mine = y * NX + x
    prior, later = (tm + total_tm - 1) % total_tm, (tm + 1) % total_tm

    def slot(k, sign):
        dy, dx = PEERS[k]
        return ((y + sign * dy + NY) % NY) * NX + (x + dx) % NX

    peers = [(det, tm_of((y + dy) % NY, z, (x + dx) % NX)) for dy, dx in PEERS]
    greet(peers + [(det, later), (det, prior)])
    own = pltpu.make_async_copy(part_ref.at[mine], land.at[NB - 1], own_sem)
    own.start()
    sends = []
    for k, peer in enumerate(peers):
        copy = remote(part_ref.at[slot(k, 1)], land.at[k], send.at[k], recv.at[k], peer)
        copy.start()
        sends.append(copy)
    toeplitz(noise_ref, lags, t_hi, t_lo)
    own.wait()
    total = land[NB - 1]
    for k in range(NB - 1):
        sends[k].wait_recv()
        total = total + land[k]
    ext[:, REACH : REACH + RUNS, :] = total
    to_prior = remote(
        ext.at[:, pl.ds(REACH, REACH), :], ext.at[:, pl.ds(REACH + RUNS, REACH), :],
        halo_send.at[0], halo_recv.at[0], (det, prior),
    )
    to_later = remote(
        ext.at[:, pl.ds(RUNS, REACH), :], ext.at[:, pl.ds(0, REACH), :], halo_send.at[1], halo_recv.at[1], (det, later)
    )
    to_prior.start()
    to_later.start()
    to_prior.wait_recv()
    to_later.wait_recv()
    first, last = tm == 0, tm == total_tm - 1

    def product(left, right, crossed):
        return lax.dot_general(left, right, CROSSED if crossed else STRAIGHT, preferred_element_type=jnp.float32)

    back, own_copies = [], []

    def back_copy(c, k, source):
        rows = pl.ds(c * SENT, SENT)
        return remote(filt.at[rows], out_ref.at[source, rows], back_send.at[k, c], back_recv.at[k, c], peers[k])

    def send_back(c):
        for k in range(NB - 1):
            copy = back_copy(c, k, mine)
            copy.start()
            back.append(copy)
        rows = pl.ds(c * SENT, SENT)
        copy = pltpu.make_async_copy(filt.at[rows], out_ref.at[mine, rows], store_sem.at[c])
        copy.start()
        own_copies.append(copy)

    for d in range(DET):
        line_all = jnp.concatenate(
            [
                jnp.where(first, 0.0, ext[d, :REACH]),
                ext[d, REACH : REACH + RUNS],
                jnp.where(last, 0.0, ext[d, REACH + RUNS :]),
            ],
            axis=0,
        )
        result = jnp.zeros((RUNS, LANE), jnp.float32)
        for m in range(2 * REACH + 1):
            window = line_all[m : m + RUNS]
            high = window.astype(jnp.bfloat16)
            low = (window - high.astype(jnp.float32)).astype(jnp.bfloat16)
            stack = jnp.concatenate([high, low], axis=0)
            q = REACH - m
            for index, crossed in [(q, False)] if q > 0 else [(-q, True)] if q < 0 else [(0, False), (REACH + 1, True)]:
                both = product(stack, t_hi[d, index], crossed)
                result += both[:RUNS] + both[RUNS:] + product(high, t_lo[d, index], crossed)
        filt[d] = result
        if d % SENT == SENT - 1:
            send_back(d // SENT)
    for copy in own_copies:
        copy.wait()
    for c in range(DET // SENT):
        for k, peer in enumerate(peers):
            back_copy(c, k, slot(k, -1)).wait_recv()
    for copy in sends + back + [to_prior, to_later]:
        copy.wait_send()


def filtered_of(partial, noise_coef):
    f32, bf = jnp.float32, jnp.bfloat16
    block = (DET, RUNS, LANE)
    matrices = (DET, REACH + 2, LANE, LANE)
    return pl.pallas_call(
        filter_kernel,
        out_shape=jax.ShapeDtypeStruct((NB, *block), f32),
        in_specs=[ANY, VM],
        out_specs=ANY,
        scratch_shapes=[
            pltpu.VMEM((NB, *block), f32),
            pltpu.VMEM((DET, RUNS + 2 * REACH, LANE), f32),
            pltpu.VMEM(block, f32),
            pltpu.VMEM((REACH + 1, DET, LANE), f32),
            pltpu.VMEM(matrices, bf),
            pltpu.VMEM(matrices, bf),
            DMA,
            DMA((DET // SENT,)),
            DMA((NB,)),
            DMA((NB,)),
            DMA((2,)),
            DMA((2,)),
            DMA((NB, DET // SENT)),
            DMA((NB, DET // SENT)),
        ],
        compiler_params=pltpu.CompilerParams(collective_id=1, has_side_effects=True),
        name="filter",
    )(partial, noise_coef)


CHUNKS = [(t, p) for t in range(TILE_DEV) for p in range(3)]
HALF_Z = NZ // 2
OFFSETS = [4, 3, -3, 2, -2, 1, -1, 0]


def collect_kernel(
    acc_ref, out_ref, rest_ref, own, land_core, land, land_hi, total,
    own_sem, core_send, core_recv, ring_send, ring_recv, hi_send, hi_recv,
):
    det, tm, y, z, x = place()
    core, hi = det % 2, det // 2
    partner, across = core_of(det), hi_of(det)
    neighbours = ((det, tm_of(y, (z + 1) % NZ, x)), (det, tm_of(y, (z + NZ - 1) % NZ, x)))
    loads = []
    for k, offset in enumerate(OFFSETS):
        copy = pltpu.make_async_copy(acc_ref.at[(z + offset + NZ) % NZ, :, :, :, core], own.at[k], own_sem.at[k])
        copy.start()
        loads.append(copy)
    greet([(partner, tm), (across, tm), *neighbours])
    started = []

    def start(copy):
        copy.start()
        started.append(copy)

    for k, offset in enumerate(OFFSETS):
        start(
            remote(
                acc_ref.at[(z + offset + NZ) % NZ, :, :, :, 1 - core], land_core.at[k], core_send.at[k], core_recv.at[k],
                (partner, tm),
            )
        )

    def ring(direction, step, c):
        t, p = CHUNKS[c]
        sign = 1 if direction == 0 else -1
        k = OFFSETS.index(sign * (HALF_Z - step)) if step else 0
        return remote(
            own.at[k, t, p], land.at[direction, step, t, p],
            ring_send.at[direction, step, c], ring_recv.at[direction, step, c], neighbours[direction],
        )

    def swapped(k):
        loads[k].wait()
        remote(acc_ref.at[0, :, :, :, 0], land_core.at[k], core_send.at[k], core_recv.at[k], (partner, tm)).wait_recv()

    swapped(0)
    for direction in (0, 1):
        for c, (t, p) in enumerate(CHUNKS):
            if t == direction:
                own[0, t, p] = own[0, t, p] + land_core[0, t, p]
    for p in range(3):
        for direction in (0, 1):
            start(ring(direction, 0, direction * 3 + p))
    for step in range(1, HALF_Z):
        keys = [OFFSETS.index(HALF_Z - step), OFFSETS.index(step - HALF_Z)]
        for k in keys:
            swapped(k)
        for i in range(len(CHUNKS)):
            for direction in (0, 1):
                c = (i + 3 * (1 - direction)) % len(CHUNKS) if step == 1 else i
                t, p = CHUNKS[c]
                k = keys[direction]
                value = own[k, t, p] + land_core[k, t, p]
                if step > 1 or t == direction:
                    ring(direction, step - 1, c).wait_recv()
                    value = value + land[direction, step - 1, t, p]
                own[k, t, p] = value
                start(ring(direction, step, c))
    last = len(OFFSETS) - 1
    swapped(last)

    def across_copy(c):
        t, p = CHUNKS[c]
        return remote(total.at[t, p, 1 - hi], land_hi.at[t, p], hi_send.at[c], hi_recv.at[c], (across, tm))

    for c, (t, p) in enumerate(CHUNKS):
        value = own[last, t, p] + land_core[last, t, p]
        for direction in (0, 1):
            ring(direction, HALF_Z - 1, c).wait_recv()
            value = value + land[direction, HALF_Z - 1, t, p]
        total[t, p] = value
        start(across_copy(c))
        out_ref[t, p] = total[t, p, hi]
    for c, (t, p) in enumerate(CHUNKS):
        across_copy(c).wait_recv()
        rest_ref[t, p] = land_hi[t, p]
    for copy in started:
        copy.wait_send()


def collect(acc):
    f32 = jnp.float32
    half = (TILE_DEV, 3, 2, STRIP, PIX)
    quarter = (TILE_DEV, 3, STRIP, PIX)
    return pl.pallas_call(
        collect_kernel,
        out_shape=(jax.ShapeDtypeStruct(quarter, f32),) * 2,
        in_specs=[ANY],
        out_specs=(VM, VM),
        scratch_shapes=[
            pltpu.VMEM((NZ, *half), f32),
            pltpu.VMEM((NZ, *half), f32),
            pltpu.VMEM((2, HALF_Z, *half), f32),
            pltpu.VMEM(quarter, f32),
            pltpu.VMEM(half, f32),
            DMA((NZ,)),
            DMA((NZ,)),
            DMA((NZ,)),
            DMA((2, HALF_Z, 6)),
            DMA((2, HALF_Z, 6)),
            DMA((6,)),
            DMA((6,)),
        ],
        compiler_params=pltpu.CompilerParams(collective_id=2, has_side_effects=True),
        name="collect",
    )(acc.reshape(NZ, TILE_DEV, 3, 2, 2, STRIP, PIX))


def body(
    sky_map, tile_home, piece_tiles, run_slot, hit_row, hit_col, frac_row, frac_col, angle, noise_coef
):
    tiles, all_floats, all_fracs, order = gather_all(
        tile_home, piece_tiles.reshape(1, LISTED), run_slot, hit_row, hit_col, frac_row, frac_col, angle, sky_map
    )
    partial, turns = forward(order, tiles.reshape(TILE_DEV * NZ, 3 * PIX, PIX), all_floats, all_fracs)
    filtered = filtered_of(partial, noise_coef)
    acc = backward(order, all_floats, all_fracs, turns, filtered)
    near, rest = collect(acc)
    return near + rest


def solution(mesh):
    placed = (
        P("tm", None, "det", None),
        P(),
        P("det", "tm", None),
        P("det", "tm"),
        P("det", "tm"),
        P("det", "tm"),
        P("det", "tm"),
        P("det", "tm"),
        P("det", "tm"),
        P("det", None),
    )
    return jax.shard_map(
        body, mesh=mesh, in_specs=placed, out_specs=P("tm", None, "det", None), check_vma=False
    )
```

```python
import functools

import jax
import jax.numpy as jnp
from jax import lax
from jax.experimental import pallas as pl
from jax.experimental.pallas import tpu as pltpu
from jax.sharding import PartitionSpec as P

MESH = pl.DeviceIdType.MESH
NY, NZ, NX = 4, 8, 2
NB = NY * NX
DET, RUNS, LANE = 8, 16, 128
PIX = 128
STRIP = 32
LISTED = 32
TILE_DEV = 2
REACH = 8
UNROLL = 16
HALF = 16
SENT = 2
PIECE_RUNS = DET * RUNS
ALL_RUNS = NB * PIECE_RUNS
ANY = pl.BlockSpec(memory_space=pl.ANY)
VM = pl.BlockSpec(memory_space=pltpu.VMEM)
SM = pl.BlockSpec(memory_space=pltpu.SMEM)
DMA = pltpu.SemaphoreType.DMA
PEERS = [(dy, dx) for dy in range(NY) for dx in range(NX) if (dy, dx) != (0, 0)]


def place():
    det, tm = lax.axis_index("det"), lax.axis_index("tm")
    y, z, x = tm // (NZ * NX), (tm // NX) % NZ, tm % NX
    return det, tm, y, z, x


def tm_of(y, z, x):
    return (y * NZ + z) * NX + x


def core_of(det):
    return det + 1 - 2 * (det % 2)


def hi_of(det):
    return (det + 2) % 4


def greet(peers):
    barrier = pltpu.get_barrier_semaphore()
    for peer in peers:
        pl.semaphore_signal(barrier, inc=1, device_id=peer, device_id_type=MESH)
    pl.semaphore_wait(barrier, len(peers))


def remote(src, dst, send, recv, peer):
    return pltpu.make_async_remote_copy(
        src_ref=src, dst_ref=dst, send_sem=send, recv_sem=recv, device_id=peer, device_id_type=MESH
    )


def run_order(pos_ref, order_ref, y, x):
    f32, bf, i32 = jnp.float32, jnp.bfloat16, jnp.int32

    def iota(shape, dim):
        return lax.broadcasted_iota(i32, shape, dim)

    def whole(mask):
        return jnp.where(mask, 1.0, 0.0).astype(bf)

    def dot(left, right):
        return jnp.dot(left, right, preferred_element_type=f32)

    lanes, offset = iota((RUNS, LANE), 1), iota((RUNS, LANE), 0)
    spot = jnp.zeros((DET, LANE), f32)
    for slot in range(NB):
        spot += dot(pos_ref[slot].astype(f32).astype(bf), whole(lanes == offset + slot * RUNS))
    pos = spot.astype(i32)
    here = (pos // (TILE_DEV * NX * NZ) == y) & ((pos // TILE_DEV) % NX == x)
    tile = ((pos // (TILE_DEV * NX)) % NZ) * TILE_DEV + pos % TILE_DEV
    kinds, square = (2 * TILE_DEV * NZ, LANE), (LANE, LANE)
    kind = jnp.where(here, tile, TILE_DEV * NZ)
    tile = tile.astype(f32)
    before, every = whole(iota(square, 0) < iota(square, 1)), jnp.ones(square, bf)
    marks, prior, total = [], [], jnp.zeros(kinds, f32)
    for d in range(DET):
        mark = whole(jnp.broadcast_to(kind[d : d + 1], kinds) == iota(kinds, 0))
        marks.append(mark.astype(f32))
        prior.append(dot(mark, before) + total)
        total += dot(mark, every)
    lower = whole(iota((kinds[0], kinds[0]), 1) < iota((kinds[0], kinds[0]), 0))
    coarse = jnp.floor(total * (1.0 / 32.0))
    base = 32.0 * dot(lower, coarse.astype(bf)) + dot(lower, (total - 32.0 * coarse).astype(bf))
    high_rows, low_rows = iota((DET, LANE), 0).astype(f32), iota(square, 0).astype(f32)
    lane = iota((DET, LANE), 1).astype(f32)
    found = jnp.zeros((3 * DET, LANE), f32)
    for d in range(DET):
        rank = jnp.sum(marks[d] * (prior[d] + base), axis=0, keepdims=True)
        high = jnp.floor(rank * (1.0 / LANE))
        low = rank - LANE * high
        at = jnp.broadcast_to(high, (DET, LANE)) == high_rows
        values = (jnp.broadcast_to(tile[d : d + 1], (DET, LANE)), jnp.full((DET, LANE), float(d), f32), lane)
        left = jnp.concatenate([jnp.where(at, v, 0.0) for v in values], axis=0).astype(bf)
        right = whole(jnp.broadcast_to(low, square) == low_rows)
        found += lax.dot_general(left, right, (((1,), (1,)), ((), ())), preferred_element_type=f32)
    entry = found[:DET] * ALL_RUNS + found[DET : 2 * DET] * LANE + found[2 * DET :]
    order_ref[:DET, :] = entry.astype(i32)
    others = total[TILE_DEV * NZ : TILE_DEV * NZ + 1]
    order_ref[DET:, :] = jnp.broadcast_to(ALL_RUNS - others, (DET, LANE)).astype(i32)


def pack(home_ref, piece_ref, slot_ref, row_ref, col_ref, low_ref, high_ref, angle_ref, f_own, w_own, p_own):
    for r in range(RUNS):
        at = slice(r * LANE, (r + 1) * LANE)
        f_own[0, r] = (row_ref[:, at] * PIX + col_ref[:, at]).astype(jnp.float32)
        f_own[1, r] = angle_ref[:, at]
        w_own[0, r] = low_ref[:, at]
        w_own[1, r] = high_ref[:, at]
    slots = slot_ref[...]
    position = jnp.zeros_like(slots)
    for s in range(LISTED):
        position = jnp.where(slots == s, home_ref[piece_ref[0, s]], position)
    p_own[...] = position


def gather_kernel(
    home_ref, piece_ref, slot_ref, row_ref, col_ref, low_ref, high_ref, angle_ref, q_ref,
    tiles_ref, fo_ref, wo_ref, order_ref,
    q_own, f_own, w_own, p_own, pos_all, load_sem, store_sem,
    pos_send, pos_recv, block_send, block_recv, strip_send, strip_recv, core_send, core_recv, hi_send, hi_recv,
):
    det, tm, y, z, x = place()
    partner, across = core_of(det), hi_of(det)
    ahead, behind = (y + 1) % NY, (y + NY - 1) % NY
    facing = (y + NY // 2) % NY
    other = 1 - x
    up, down, side = (det, tm_of(ahead, z, x)), (det, tm_of(behind, z, x)), (det, tm_of(y, z, other))
    far = [(det, tm_of((y + dy) % NY, z, (x + dx) % NX)) for dy, dx in PEERS]

    def along(direction, jump):
        return (det, tm_of(y, (z + jump) % NZ if direction == 0 else (z + NZ - jump) % NZ, x))

    def strip(slot, d):
        return tiles_ref.at[slot, :, :, pl.ds(d * STRIP, STRIP), :]

    def block(slot, part):
        return fo_ref.at[slot, part] if part < 2 else wo_ref.at[slot]

    def own_block(part):
        return f_own.at[part] if part < 2 else w_own

    mine = y * NX + x
    load = pltpu.make_async_copy(q_ref, q_own, load_sem)
    load.start()
    greeted = [along(d, j) for d in (0, 1) for j in (1, 2)] + [(partner, tm), (across, tm)] + far
    barrier = pltpu.get_barrier_semaphore()
    for peer in greeted:
        pl.semaphore_signal(barrier, inc=1, device_id=peer, device_id_type=MESH)
    pack(home_ref, piece_ref, slot_ref, row_ref, col_ref, low_ref, high_ref, angle_ref, f_own, w_own, p_own)
    pl.semaphore_wait(barrier, len(greeted))

    started = []

    def start(copy):
        copy.start()
        started.append(copy)

    start(remote(q_ref, strip(z, det), hi_send, hi_recv, (across, tm)))
    for k, peer in enumerate(far):
        start(remote(p_own, pos_all.at[mine], pos_send.at[k], pos_recv.at[k], peer))

    def send_block(link, slot, part, peer, own=False):
        start(
            remote(
                own_block(part) if own else block(slot, part), block(slot, part),
                block_send.at[link, part], block_recv.at[link, part], peer,
            )
        )

    def wait_block(link, slot, part):
        remote(own_block(part), block(slot, part), block_send.at[link, part], block_recv.at[link, part], side).wait_recv()

    owner = (det, across)

    def source_slot(direction, distance):
        return (z + NZ - distance) % NZ if direction == 0 else (z + distance) % NZ

    def send_strip(half, direction, distance):
        slot = z if distance < 3 else source_slot(direction, 2)
        here = strip(slot, owner[half])
        start(
            remote(
                q_ref if half == 0 and distance < 3 else here, here,
                strip_send.at[half, direction, distance - 1], strip_recv.at[half, direction, distance - 1],
                along(direction, 2 - distance % 2),
            )
        )

    def reach(half, direction):
        return NZ // 2 if half == direction else NZ // 2 - 1

    def to_partner(half, index, slot):
        here = strip(slot, owner[half])
        start(
            remote(
                q_ref if half == 0 and index == 0 else here, here, core_send.at[half, index], core_recv.at[half, index],
                (partner, tm),
            )
        )

    def take_strip(half, distance):
        for direction in (0, 1):
            if distance <= reach(half, direction):
                slot = source_slot(direction, distance)
                remote(
                    q_ref, strip(slot, owner[half]),
                    strip_send.at[half, direction, distance - 1], strip_recv.at[half, direction, distance - 1], side,
                ).wait_recv()
                if distance == 2:
                    if reach(half, direction) == 4:
                        send_strip(half, direction, 4)
                    send_strip(half, direction, 3)
                to_partner(half, direction * NZ // 2 + distance, slot)

    def first_strips(half):
        for distance in (2, 1):
            for direction in (0, 1):
                send_strip(half, direction, distance)
        to_partner(half, 0, z)

    first_strips(0)
    for part in range(3):
        send_block(1, mine, part, up, True)
        send_block(2, mine, part, down, True)
        send_block(0, mine, part, side, True)
    load.wait()
    stores = []
    for i, (src, dst) in enumerate(
        ((q_own, strip(z, det)), (f_own, fo_ref.at[mine]), (w_own, wo_ref.at[mine]), (p_own, pos_all.at[mine]))
    ):
        copy = pltpu.make_async_copy(src, dst, store_sem.at[i])
        copy.start()
        stores.append(copy)

    slot_of = {1: behind * NX + x, 2: ahead * NX + x, 0: y * NX + other, 5: facing * NX + x, 6: facing * NX + other,
               3: behind * NX + other, 4: ahead * NX + other}

    def near(part):
        for link in (1, 2, 0):
            wait_block(link, slot_of[link], part)
            if link == 1 and part != 1:
                send_block(5, slot_of[1], part, up)
            if link == 2 and part == 1:
                send_block(5, slot_of[2], part, down)
            if link == 0:
                send_block(3, slot_of[0], part, up)
                send_block(4, slot_of[0], part, down)

    def opposite(part):
        wait_block(5, slot_of[5], part)
        send_block(6, slot_of[5], part, side)

    near(0)
    remote(q_ref, strip(z, across), hi_send, hi_recv, (across, tm)).wait_recv()
    first_strips(1)
    take_strip(0, 2)
    near(1)
    near(2)
    take_strip(0, 1)
    opposite(0)
    take_strip(1, 2)
    opposite(1)
    opposite(2)
    take_strip(1, 1)
    take_strip(0, 3)
    take_strip(0, 4)

    stores[3].wait()
    for k, peer in enumerate(far):
        remote(p_own, pos_all.at[mine], pos_send.at[k], pos_recv.at[k], peer).wait_recv()
    run_order(pos_all, order_ref, y, x)

    take_strip(1, 3)
    take_strip(1, 4)
    for part in range(3):
        for link in (3, 4, 6):
            wait_block(link, slot_of[link], part)
    theirs = (partner, hi_of(partner))
    for half in (0, 1):
        places = [(0, z)]
        for direction in (0, 1):
            for distance in range(1, reach(half, direction) + 1):
                places.append((direction * NZ // 2 + distance, source_slot(direction, distance)))
        for index, slot in places:
            remote(
                q_ref, strip(slot, theirs[half]), core_send.at[half, index], core_recv.at[half, index], (partner, tm)
            ).wait_recv()
    for copy in stores[:3]:
        copy.wait()
    for copy in started:
        copy.wait_send()


def gather_all(tile_home, piece_list, run_slot, hit_row, hit_col, frac_row, frac_col, angle, quarter):
    bf, f32, i32 = jnp.bfloat16, jnp.float32, jnp.int32
    samples = (2, RUNS, DET, LANE)
    return pl.pallas_call(
        gather_kernel,
        out_shape=(
            jax.ShapeDtypeStruct((NZ, TILE_DEV, 3, PIX, PIX), bf),
            jax.ShapeDtypeStruct((NB, *samples), f32),
            jax.ShapeDtypeStruct((NB, *samples), bf),
            jax.ShapeDtypeStruct((2 * DET, LANE), i32),
        ),
        in_specs=[SM, SM] + [VM] * 6 + [ANY],
        out_specs=(ANY, ANY, ANY, VM),
        scratch_shapes=[
            pltpu.VMEM(quarter.shape, bf),
            pltpu.VMEM(samples, f32),
            pltpu.VMEM(samples, bf),
            pltpu.VMEM((DET, RUNS), i32),
            pltpu.VMEM((NB, DET, RUNS), i32),
            DMA,
            DMA((4,)),
            DMA((NB,)),
            DMA((NB,)),
            DMA((7, 3)),
            DMA((7, 3)),
            DMA((2, 2, NZ // 2)),
            DMA((2, 2, NZ // 2)),
            DMA((2, NZ + 1)),
            DMA((2, NZ + 1)),
            DMA,
            DMA,
        ],
        compiler_params=pltpu.CompilerParams(collective_id=0, has_side_effects=True),
        name="gather_all",
    )(tile_home, piece_list, run_slot, hit_row, hit_col, frac_row, frac_col, angle, quarter)


def sin_cos(v):
    quarter = jnp.round(v * 0.6366197723675814)
    u = v - quarter * 1.5703125
    u = u - quarter * 4.837512969970703e-4
    u = u - quarter * 7.549789948768648e-8
    u2 = u * u
    s = u + u * u2 * (-1.6666654611e-1 + u2 * (8.3321608736e-3 + u2 * -1.9515295891e-4))
    c = 1.0 - 0.5 * u2 + u2 * u2 * (4.166664568298827e-2 + u2 * (-1.388731625493765e-3 + u2 * 2.443315711809948e-5))
    q = quarter.astype(jnp.int32) & 3
    odd = (q & 1) == 1
    sin = jnp.where(odd, c, s)
    cos = jnp.where(odd, s, c)
    sin = jnp.where(q >= 2, -sin, sin)
    cos = jnp.where((q == 1) | (q == 2), -cos, cos)
    return sin, cos


def low_of(high):
    return (1.0 - high).astype(jnp.bfloat16).astype(jnp.float32)


def run_of(entry):
    run = entry & (ALL_RUNS - 1)
    return entry >> 10, (run >> 4) & (NB - 1), run >> 7, run & (RUNS - 1)


def spread(index, low, high, rows):
    bf = jnp.bfloat16
    wide = [jnp.broadcast_to(v, (HALF, LANE)).astype(bf) for v in (index, index + 1.0, low, high)]
    zero = jnp.zeros((HALF, LANE), bf)
    parts = []
    for b in range(PIX // HALF):
        row = rows[b * HALF : (b + 1) * HALF]
        parts.append(jnp.where(row == wide[0], wide[2], jnp.where(row == wide[1], wide[3], zero)))
    return jnp.concatenate(parts, axis=0)


def forward_kernel(list_ref, tiles_ref, f_ref, w_ref, sig_ref, cs_ref, hit_ref, frac_ref):
    def prepare(z, _):
        code = f_ref[z, 0]
        row = jnp.floor(code * (1.0 / PIX))
        hit_ref[z, 0] = row
        hit_ref[z, 1] = code - row * PIX
        sin, cos = sin_cos(2.0 * f_ref[z, 1])
        cs_ref[z, 0] = cos
        cs_ref[z, 1] = sin
        frac_ref[z, 0] = w_ref[z, 0].astype(jnp.float32)
        frac_ref[z, 1] = w_ref[z, 1].astype(jnp.float32)
        sig_ref[z] = jnp.zeros_like(sig_ref[z])
        return 0

    lax.fori_loop(0, NB, prepare, 0)
    count = list_ref[DET, 0]
    rows = lax.broadcasted_iota(jnp.int32, (PIX, LANE), 0).astype(jnp.float32).astype(jnp.bfloat16)

    def body(step, _):
        for u in range(UNROLL):
            k = step * UNROLL + u
            tile, z, d, r = run_of(list_ref[k >> 7, k & (LANE - 1)])
            at = (r, pl.ds(d, 1), slice(None))
            col_high = frac_ref[z, 1, *at]
            row_high = frac_ref[z, 0, *at]
            col_weight = spread(hit_ref[z, 1, *at], low_of(col_high), col_high, rows)
            row_weight = spread(hit_ref[z, 0, *at], low_of(row_high), row_high, rows).astype(jnp.float32)
            partial = jnp.dot(tiles_ref[tile], col_weight, preferred_element_type=jnp.float32)
            value = [
                jnp.sum(partial[p * PIX : (p + 1) * PIX] * row_weight, axis=0, keepdims=True) for p in range(3)
            ]
            total = value[0] + cs_ref[z, 0, *at] * value[1] + cs_ref[z, 1, *at] * value[2]
            sig_ref[z, d, pl.ds(r, 1), :] = jnp.where(k < count, total, 0.0)
        return 0

    lax.fori_loop(0, (count + UNROLL - 1) // UNROLL, body, 0)


def forward(order, tiles, floats, fracs):
    f32 = jnp.float32
    block = (NB, DET, RUNS, LANE)
    pair = (NB, 2, RUNS, DET, LANE)
    return pl.pallas_call(
        forward_kernel,
        out_shape=(jax.ShapeDtypeStruct(block, f32), jax.ShapeDtypeStruct(pair, f32)),
        in_specs=[SM, VM, VM, VM],
        out_specs=(VM, VM),
        scratch_shapes=[pltpu.VMEM(pair, f32), pltpu.VMEM(pair, f32)],
        name="forward",
    )(order, tiles, floats, fracs)


def backward_kernel(list_ref, f_ref, w_ref, cs_ref, filt_ref, acc_ref, hit_ref, frac_ref):
    def prepare(z, _):
        code = f_ref[z, 0]
        row = jnp.floor(code * (1.0 / PIX))
        hit_ref[z, 0] = row
        hit_ref[z, 1] = code - row * PIX
        frac_ref[z, 0] = w_ref[z, 0].astype(jnp.float32)
        frac_ref[z, 1] = w_ref[z, 1].astype(jnp.float32)
        return 0

    lax.fori_loop(0, NB, prepare, 0)

    def clear(t, _):
        acc_ref[t] = jnp.zeros_like(acc_ref[t])
        return 0

    lax.fori_loop(0, TILE_DEV * NZ, clear, 0)
    count = list_ref[DET, 0]
    rows = lax.broadcasted_iota(jnp.int32, (PIX, LANE), 0).astype(jnp.float32).astype(jnp.bfloat16)

    def body(step, _):
        for u in range(UNROLL):
            k = step * UNROLL + u
            tile, z, d, r = run_of(list_ref[k >> 7, k & (LANE - 1)])
            at = (r, pl.ds(d, 1), slice(None))
            col_high = frac_ref[z, 1, *at]
            row_high = frac_ref[z, 0, *at]
            row_low = low_of(row_high)
            col_weight = spread(hit_ref[z, 1, *at], low_of(col_high), col_high, rows)
            filt = jnp.where(k < count, filt_ref[z, d, pl.ds(r, 1), :], 0.0)
            hit = hit_ref[z, 0, *at]
            parts = []
            for p in range(3):
                scaled = filt if p == 0 else cs_ref[z, p - 1, *at] * filt
                parts.append(spread(hit, scaled * row_low, scaled * row_high, rows))
            weighted = jnp.concatenate(parts, axis=0)
            acc_ref[tile] += lax.dot_general(
                weighted, col_weight, (((1,), (1,)), ((), ())), preferred_element_type=jnp.float32
            )
        return 0

    lax.fori_loop(0, (count + UNROLL - 1) // UNROLL, body, 0)


def backward(order, floats, fracs, turns, filtered):
    f32 = jnp.float32
    pair = (NB, 2, RUNS, DET, LANE)
    return pl.pallas_call(
        backward_kernel,
        out_shape=jax.ShapeDtypeStruct((TILE_DEV * NZ, 3 * PIX, PIX), f32),
        in_specs=[SM, VM, VM, VM, VM],
        out_specs=VM,
        scratch_shapes=[pltpu.VMEM(pair, f32), pltpu.VMEM(pair, f32)],
        name="backward",
    )(order, floats, fracs, turns, filtered)


def toeplitz(noise_ref, line_ref, hi_ref, lo_ref):
    square = (LANE, LANE)
    lanes = lax.broadcasted_iota(jnp.int32, square, 1)
    rows = lax.broadcasted_iota(jnp.int32, square, 0)
    first = lax.broadcasted_iota(jnp.int32, (DET, LANE), 1) == 0
    for q in range(REACH):
        lags = noise_ref[:, q * LANE : (q + 1) * LANE]
        line_ref[q] = jnp.where(first, lags + 1.0, lags) if q == 0 else lags
    line_ref[REACH] = jnp.where(first, jnp.broadcast_to(noise_ref[:, REACH * LANE :], (DET, LANE)), 0.0)

    def one(d, _):
        def put(q, matrix):
            high = matrix.astype(jnp.bfloat16)
            hi_ref[d, q] = high
            lo_ref[d, q] = (matrix - high.astype(jnp.float32)).astype(jnp.bfloat16)

        before = None
        for q in range(REACH + 1):
            lags = line_ref[q, pl.ds(d, 1), :]
            after = pltpu.roll(jnp.broadcast_to(lags, square), 0, 1, stride=1, stride_axis=0)
            if q == 0:
                put(0, jnp.where(lanes >= rows, after, 0.0))
                put(REACH + 1, jnp.where(lanes > rows, after, 0.0))
            else:
                put(q, jnp.where(lanes >= rows, after, before))
            before = after
        return 0

    lax.fori_loop(0, DET, one, 0)


STRAIGHT = (((1,), (0,)), ((), ()))
CROSSED = (((1,), (1,)), ((), ()))


def filter_kernel(
    part_ref, noise_ref, out_ref, land, ext, filt, lags, t_hi, t_lo,
    own_sem, store_sem, send, recv, halo_send, halo_recv, back_send, back_recv,
):
    det, tm, y, z, x = place()
    total_tm = NY * NZ * NX
    mine = y * NX + x
    prior, later = (tm + total_tm - 1) % total_tm, (tm + 1) % total_tm

    def slot(k, sign):
        dy, dx = PEERS[k]
        return ((y + sign * dy + NY) % NY) * NX + (x + dx) % NX

    peers = [(det, tm_of((y + dy) % NY, z, (x + dx) % NX)) for dy, dx in PEERS]
    greet(peers + [(det, later), (det, prior)])
    own = pltpu.make_async_copy(part_ref.at[mine], land.at[NB - 1], own_sem)
    own.start()
    sends = []
    for k, peer in enumerate(peers):
        copy = remote(part_ref.at[slot(k, 1)], land.at[k], send.at[k], recv.at[k], peer)
        copy.start()
        sends.append(copy)
    toeplitz(noise_ref, lags, t_hi, t_lo)
    own.wait()
    total = land[NB - 1]
    for k in range(NB - 1):
        sends[k].wait_recv()
        total = total + land[k]
    ext[:, REACH : REACH + RUNS, :] = total
    to_prior = remote(
        ext.at[:, pl.ds(REACH, REACH), :], ext.at[:, pl.ds(REACH + RUNS, REACH), :],
        halo_send.at[0], halo_recv.at[0], (det, prior),
    )
    to_later = remote(
        ext.at[:, pl.ds(RUNS, REACH), :], ext.at[:, pl.ds(0, REACH), :], halo_send.at[1], halo_recv.at[1], (det, later)
    )
    to_prior.start()
    to_later.start()
    to_prior.wait_recv()
    to_later.wait_recv()
    first, last = tm == 0, tm == total_tm - 1

    def product(left, right, crossed):
        return lax.dot_general(left, right, CROSSED if crossed else STRAIGHT, preferred_element_type=jnp.float32)

    back, own_copies = [], []

    def back_copy(c, k, source):
        rows = pl.ds(c * SENT, SENT)
        return remote(filt.at[rows], out_ref.at[source, rows], back_send.at[k, c], back_recv.at[k, c], peers[k])

    def send_back(c):
        for k in range(NB - 1):
            copy = back_copy(c, k, mine)
            copy.start()
            back.append(copy)
        rows = pl.ds(c * SENT, SENT)
        copy = pltpu.make_async_copy(filt.at[rows], out_ref.at[mine, rows], store_sem.at[c])
        copy.start()
        own_copies.append(copy)

    for d in range(DET):
        line_all = jnp.concatenate(
            [
                jnp.where(first, 0.0, ext[d, :REACH]),
                ext[d, REACH : REACH + RUNS],
                jnp.where(last, 0.0, ext[d, REACH + RUNS :]),
            ],
            axis=0,
        )
        result = jnp.zeros((RUNS, LANE), jnp.float32)
        for m in range(2 * REACH + 1):
            window = line_all[m : m + RUNS]
            high = window.astype(jnp.bfloat16)
            low = (window - high.astype(jnp.float32)).astype(jnp.bfloat16)
            stack = jnp.concatenate([high, low], axis=0)
            q = REACH - m
            for index, crossed in [(q, False)] if q > 0 else [(-q, True)] if q < 0 else [(0, False), (REACH + 1, True)]:
                both = product(stack, t_hi[d, index], crossed)
                result += both[:RUNS] + both[RUNS:] + product(high, t_lo[d, index], crossed)
        filt[d] = result
        if d % SENT == SENT - 1:
            send_back(d // SENT)
    for copy in own_copies:
        copy.wait()
    for c in range(DET // SENT):
        for k, peer in enumerate(peers):
            back_copy(c, k, slot(k, -1)).wait_recv()
    for copy in sends + back + [to_prior, to_later]:
        copy.wait_send()


def filtered_of(partial, noise_coef):
    f32, bf = jnp.float32, jnp.bfloat16
    block = (DET, RUNS, LANE)
    matrices = (DET, REACH + 2, LANE, LANE)
    return pl.pallas_call(
        filter_kernel,
        out_shape=jax.ShapeDtypeStruct((NB, *block), f32),
        in_specs=[ANY, VM],
        out_specs=ANY,
        scratch_shapes=[
            pltpu.VMEM((NB, *block), f32),
            pltpu.VMEM((DET, RUNS + 2 * REACH, LANE), f32),
            pltpu.VMEM(block, f32),
            pltpu.VMEM((REACH + 1, DET, LANE), f32),
            pltpu.VMEM(matrices, bf),
            pltpu.VMEM(matrices, bf),
            DMA,
            DMA((DET // SENT,)),
            DMA((NB,)),
            DMA((NB,)),
            DMA((2,)),
            DMA((2,)),
            DMA((NB, DET // SENT)),
            DMA((NB, DET // SENT)),
        ],
        compiler_params=pltpu.CompilerParams(collective_id=1, has_side_effects=True),
        name="filter",
    )(partial, noise_coef)


CHUNKS = [(t, p) for t in range(TILE_DEV) for p in range(3)]
HALF_Z = NZ // 2
WIRE = jnp.bfloat16
OFFSETS = [4, 3, -3, 2, -2, 1, -1, 0]


def collect_kernel(
    acc_ref, out_ref, own, land_core, packet, land, land_last, land_own,
    own_sem, core_send, core_recv, ring_send, ring_recv, last_send, last_recv, hi_send, hi_recv,
):
    f32 = jnp.float32
    det, tm, y, z, x = place()
    core, hi = det % 2, det // 2
    partner, across = core_of(det), hi_of(det)
    right, left = tm_of(y, (z + 1) % NZ, x), tm_of(y, (z + NZ - 1) % NZ, x)
    neighbours = ((det, right), (det, left))
    loads = []
    for k, offset in enumerate(OFFSETS):
        copy = pltpu.make_async_copy(acc_ref.at[(z + offset + NZ) % NZ, :, :, :, core], own.at[k], own_sem.at[k])
        copy.start()
        loads.append(copy)
    greet([(partner, tm), (across, tm), *neighbours, (across, right), (across, left)])
    started = []

    def start(copy):
        copy.start()
        started.append(copy)

    for k, offset in enumerate(OFFSETS):
        start(
            remote(
                acc_ref.at[(z + offset + NZ) % NZ, :, :, :, 1 - core], land_core.at[k], core_send.at[k], core_recv.at[k],
                (partner, tm),
            )
        )

    def ring(direction, step, c):
        t, p = CHUNKS[c]
        sign = 1 if direction == 0 else -1
        k = OFFSETS.index(sign * (HALF_Z - step)) if step else 0
        return remote(
            packet.at[k, t, p], land.at[direction, step, t, p],
            ring_send.at[direction, step, c], ring_recv.at[direction, step, c], neighbours[direction],
        )

    def last_hop(direction, c, crossing):
        t, p = CHUNKS[c]
        k = OFFSETS.index(1 if direction == 0 else -1)
        goal = (right, left)[direction]
        return remote(
            packet.at[k, t, p, 1 - hi if crossing else hi], land_last.at[crossing, direction, t, p],
            last_send.at[crossing, direction, c], last_recv.at[crossing, direction, c],
            (across if crossing else det, goal),
        )

    def own_copy(t):
        return remote(packet.at[len(OFFSETS) - 1, t, :, 1 - hi], land_own.at[t], hi_send.at[t], hi_recv.at[t], (across, tm))

    def swapped(k):
        loads[k].wait()
        remote(acc_ref.at[0, :, :, :, 0], land_core.at[k], core_send.at[k], core_recv.at[k], (partner, tm)).wait_recv()

    swapped(0)
    for direction in (0, 1):
        for c, (t, p) in enumerate(CHUNKS):
            if t == direction:
                packet[0, t, p] = (own[0, t, p] + land_core[0, t, p]).astype(WIRE)
    for p in range(3):
        for direction in (0, 1):
            start(ring(direction, 0, direction * 3 + p))
    last = len(OFFSETS) - 1
    for step in range(1, HALF_Z):
        keys = [OFFSETS.index(HALF_Z - step), OFFSETS.index(step - HALF_Z)]
        for k in keys:
            swapped(k)
        for i in range(len(CHUNKS)):
            for direction in (0, 1):
                c = (i + 3 * (1 - direction)) % len(CHUNKS) if step == 1 else i
                t, p = CHUNKS[c]
                k = keys[direction]
                value = own[k, t, p] + land_core[k, t, p]
                if step > 1 or t == direction:
                    ring(direction, step - 1, c).wait_recv()
                    value = value + land[direction, step - 1, t, p].astype(f32)
                packet[k, t, p] = value.astype(WIRE)
                if step < HALF_Z - 1:
                    start(ring(direction, step, c))
                else:
                    start(last_hop(direction, c, 1))
                    start(last_hop(direction, c, 0))
        if step == 1:
            swapped(last)
            for t in range(TILE_DEV):
                value = own[last, t] + land_core[last, t]
                packet[last, t] = value.astype(WIRE)
                start(own_copy(t))
                own[last, t] = value
    for t in range(TILE_DEV):
        own_copy(t).wait_recv()
    for c, (t, p) in enumerate(CHUNKS):
        value = own[last, t, p, hi] + land_own[t, p].astype(f32)
        for crossing in (0, 1):
            for direction in (0, 1):
                last_hop(direction, c, crossing).wait_recv()
                value = value + land_last[crossing, direction, t, p].astype(f32)
        out_ref[t, p] = value
    for copy in started:
        copy.wait_send()


def collect(acc):
    f32 = jnp.float32
    half = (TILE_DEV, 3, 2, STRIP, PIX)
    quarter = (TILE_DEV, 3, STRIP, PIX)
    return pl.pallas_call(
        collect_kernel,
        out_shape=jax.ShapeDtypeStruct(quarter, f32),
        in_specs=[ANY],
        out_specs=VM,
        scratch_shapes=[
            pltpu.VMEM((NZ, *half), f32),
            pltpu.VMEM((NZ, *half), f32),
            pltpu.VMEM((NZ, *half), WIRE),
            pltpu.VMEM((2, HALF_Z - 1, *half), WIRE),
            pltpu.VMEM((2, 2, *quarter), WIRE),
            pltpu.VMEM(quarter, WIRE),
            DMA((NZ,)),
            DMA((NZ,)),
            DMA((NZ,)),
            DMA((2, HALF_Z - 1, 6)),
            DMA((2, HALF_Z - 1, 6)),
            DMA((2, 2, 6)),
            DMA((2, 2, 6)),
            DMA((2,)),
            DMA((2,)),
        ],
        compiler_params=pltpu.CompilerParams(collective_id=2, has_side_effects=True),
        name="collect",
    )(acc.reshape(NZ, TILE_DEV, 3, 2, 2, STRIP, PIX))


def body(
    sky_map, tile_home, piece_tiles, run_slot, hit_row, hit_col, frac_row, frac_col, angle, noise_coef
):
    tiles, all_floats, all_fracs, order = gather_all(
        tile_home, piece_tiles.reshape(1, LISTED), run_slot, hit_row, hit_col, frac_row, frac_col, angle, sky_map
    )
    partial, turns = forward(order, tiles.reshape(TILE_DEV * NZ, 3 * PIX, PIX), all_floats, all_fracs)
    filtered = filtered_of(partial, noise_coef)
    acc = backward(order, all_floats, all_fracs, turns, filtered)
    return collect(acc)


def solution(mesh):
    placed = (
        P("tm", None, "det", None),
        P(),
        P("det", "tm", None),
        P("det", "tm"),
        P("det", "tm"),
        P("det", "tm"),
        P("det", "tm"),
        P("det", "tm"),
        P("det", "tm"),
        P("det", None),
    )
    return jax.shard_map(
        body, mesh=mesh, in_specs=placed, out_specs=P("tm", None, "det", None), check_vma=False
    )
```

```python
import functools

import jax
import jax.numpy as jnp
from jax import lax
from jax.experimental import pallas as pl
from jax.experimental.pallas import tpu as pltpu
from jax.sharding import PartitionSpec as P

MESH = pl.DeviceIdType.MESH
NY, NZ, NX = 4, 8, 2
NB = NY * NX
DET, RUNS, LANE = 8, 16, 128
PIX = 128
STRIP = 32
LISTED = 32
TILE_DEV = 2
REACH = 8
UNROLL = 16
HALF = 16
SENT = 2
PIECE_RUNS = DET * RUNS
ALL_RUNS = NB * PIECE_RUNS
ANY = pl.BlockSpec(memory_space=pl.ANY)
VM = pl.BlockSpec(memory_space=pltpu.VMEM)
SM = pl.BlockSpec(memory_space=pltpu.SMEM)
DMA = pltpu.SemaphoreType.DMA
PEERS = [(dy, dx) for dy in range(NY) for dx in range(NX) if (dy, dx) != (0, 0)]


def place():
    det, tm = lax.axis_index("det"), lax.axis_index("tm")
    y, z, x = tm // (NZ * NX), (tm // NX) % NZ, tm % NX
    return det, tm, y, z, x


def tm_of(y, z, x):
    return (y * NZ + z) * NX + x


def core_of(det):
    return det + 1 - 2 * (det % 2)


def hi_of(det):
    return (det + 2) % 4


def greet(peers):
    barrier = pltpu.get_barrier_semaphore()
    for peer in peers:
        pl.semaphore_signal(barrier, inc=1, device_id=peer, device_id_type=MESH)
    pl.semaphore_wait(barrier, len(peers))


def remote(src, dst, send, recv, peer):
    return pltpu.make_async_remote_copy(
        src_ref=src, dst_ref=dst, send_sem=send, recv_sem=recv, device_id=peer, device_id_type=MESH
    )


def run_order(pos_ref, order_ref, y, x):
    f32, bf, i32 = jnp.float32, jnp.bfloat16, jnp.int32

    def iota(shape, dim):
        return lax.broadcasted_iota(i32, shape, dim)

    def whole(mask):
        return jnp.where(mask, 1.0, 0.0).astype(bf)

    def dot(left, right):
        return jnp.dot(left, right, preferred_element_type=f32)

    lanes, offset = iota((RUNS, LANE), 1), iota((RUNS, LANE), 0)
    spot = jnp.zeros((DET, LANE), f32)
    for slot in range(NB):
        spot += dot(pos_ref[slot].astype(f32).astype(bf), whole(lanes == offset + slot * RUNS))
    pos = spot.astype(i32)
    here = (pos // (TILE_DEV * NX * NZ) == y) & ((pos // TILE_DEV) % NX == x)
    tile = ((pos // (TILE_DEV * NX)) % NZ) * TILE_DEV + pos % TILE_DEV
    kinds, square = (2 * TILE_DEV * NZ, LANE), (LANE, LANE)
    kind = jnp.where(here, tile, TILE_DEV * NZ)
    tile = tile.astype(f32)
    before, every = whole(iota(square, 0) < iota(square, 1)), jnp.ones(square, bf)
    marks, prior, total = [], [], jnp.zeros(kinds, f32)
    for d in range(DET):
        mark = whole(jnp.broadcast_to(kind[d : d + 1], kinds) == iota(kinds, 0))
        marks.append(mark.astype(f32))
        prior.append(dot(mark, before) + total)
        total += dot(mark, every)
    lower = whole(iota((kinds[0], kinds[0]), 1) < iota((kinds[0], kinds[0]), 0))
    coarse = jnp.floor(total * (1.0 / 32.0))
    base = 32.0 * dot(lower, coarse.astype(bf)) + dot(lower, (total - 32.0 * coarse).astype(bf))
    high_rows, low_rows = iota((DET, LANE), 0).astype(f32), iota(square, 0).astype(f32)
    lane = iota((DET, LANE), 1).astype(f32)
    found = jnp.zeros((3 * DET, LANE), f32)
    for d in range(DET):
        rank = jnp.sum(marks[d] * (prior[d] + base), axis=0, keepdims=True)
        high = jnp.floor(rank * (1.0 / LANE))
        low = rank - LANE * high
        at = jnp.broadcast_to(high, (DET, LANE)) == high_rows
        values = (jnp.broadcast_to(tile[d : d + 1], (DET, LANE)), jnp.full((DET, LANE), float(d), f32), lane)
        left = jnp.concatenate([jnp.where(at, v, 0.0) for v in values], axis=0).astype(bf)
        right = whole(jnp.broadcast_to(low, square) == low_rows)
        found += lax.dot_general(left, right, (((1,), (1,)), ((), ())), preferred_element_type=f32)
    entry = found[:DET] * ALL_RUNS + found[DET : 2 * DET] * LANE + found[2 * DET :]
    order_ref[:DET, :] = entry.astype(i32)
    others = total[TILE_DEV * NZ : TILE_DEV * NZ + 1]
    order_ref[DET:, :] = jnp.broadcast_to(ALL_RUNS - others, (DET, LANE)).astype(i32)


def pack(home_ref, piece_ref, slot_ref, row_ref, col_ref, low_ref, high_ref, angle_ref, f_own, w_own, p_own):
    for r in range(RUNS):
        at = slice(r * LANE, (r + 1) * LANE)
        f_own[0, r] = (row_ref[:, at] * PIX + col_ref[:, at]).astype(jnp.float32)
        f_own[1, r] = angle_ref[:, at]
        w_own[0, r] = low_ref[:, at]
        w_own[1, r] = high_ref[:, at]
    slots = slot_ref[...]
    position = jnp.zeros_like(slots)
    for s in range(LISTED):
        position = jnp.where(slots == s, home_ref[piece_ref[0, s]], position)
    p_own[...] = position


def gather_kernel(
    home_ref, piece_ref, slot_ref, row_ref, col_ref, low_ref, high_ref, angle_ref, q_ref,
    tiles_ref, fo_ref, wo_ref, order_ref,
    slot_own, row_own, col_own, low_own, high_own, angle_own,
    q_own, f_own, w_own, p_own, pos_all, load_sem, store_sem,
    pos_send, pos_recv, block_send, block_recv, strip_send, strip_recv, core_send, core_recv, hi_send, hi_recv,
):
    det, tm, y, z, x = place()
    partner, across = core_of(det), hi_of(det)
    ahead, behind = (y + 1) % NY, (y + NY - 1) % NY
    facing = (y + NY // 2) % NY
    other = 1 - x
    up, down, side = (det, tm_of(ahead, z, x)), (det, tm_of(behind, z, x)), (det, tm_of(y, z, other))
    far = [(det, tm_of((y + dy) % NY, z, (x + dx) % NX)) for dy, dx in PEERS]

    def along(direction, jump):
        return (det, tm_of(y, (z + jump) % NZ if direction == 0 else (z + NZ - jump) % NZ, x))

    def strip(slot, d):
        return tiles_ref.at[slot, :, :, pl.ds(d * STRIP, STRIP), :]

    def block(slot, part):
        return fo_ref.at[slot, part] if part < 2 else wo_ref.at[slot]

    def own_block(part):
        return f_own.at[part] if part < 2 else w_own

    mine = y * NX + x
    given = (slot_ref, row_ref, col_ref, low_ref, high_ref, angle_ref, q_ref)
    held = (slot_own, row_own, col_own, low_own, high_own, angle_own, q_own)
    loads = [pltpu.make_async_copy(src, dst, load_sem.at[i]) for i, (src, dst) in enumerate(zip(given, held))]
    for copy in loads:
        copy.start()
    greet([along(d, j) for d in (0, 1) for j in (1, 2)] + [(partner, tm), (across, tm)] + far)

    started = []

    def start(copy):
        copy.start()
        started.append(copy)

    start(remote(q_ref, strip(z, det), hi_send, hi_recv, (across, tm)))

    def send_block(link, slot, part, peer, own=False):
        start(
            remote(
                own_block(part) if own else block(slot, part), block(slot, part),
                block_send.at[link, part], block_recv.at[link, part], peer,
            )
        )

    def wait_block(link, slot, part):
        remote(own_block(part), block(slot, part), block_send.at[link, part], block_recv.at[link, part], side).wait_recv()

    owner = (det, across)

    def source_slot(direction, distance):
        return (z + NZ - distance) % NZ if direction == 0 else (z + distance) % NZ

    def send_strip(half, direction, distance):
        slot = z if distance < 3 else source_slot(direction, 2)
        here = strip(slot, owner[half])
        start(
            remote(
                q_ref if half == 0 and distance < 3 else here, here,
                strip_send.at[half, direction, distance - 1], strip_recv.at[half, direction, distance - 1],
                along(direction, 2 - distance % 2),
            )
        )

    def reach(half, direction):
        return NZ // 2 if half == direction else NZ // 2 - 1

    def to_partner(half, index, slot):
        here = strip(slot, owner[half])
        start(
            remote(
                q_ref if half == 0 and index == 0 else here, here, core_send.at[half, index], core_recv.at[half, index],
                (partner, tm),
            )
        )

    def take_strip(half, distance):
        for direction in (0, 1):
            if distance <= reach(half, direction):
                slot = source_slot(direction, distance)
                remote(
                    q_ref, strip(slot, owner[half]),
                    strip_send.at[half, direction, distance - 1], strip_recv.at[half, direction, distance - 1], side,
                ).wait_recv()
                if distance == 2:
                    if reach(half, direction) == 4:
                        send_strip(half, direction, 4)
                    send_strip(half, direction, 3)
                to_partner(half, direction * NZ // 2 + distance, slot)

    def first_strips(half):
        for distance in (2, 1):
            for direction in (0, 1):
                send_strip(half, direction, distance)
        to_partner(half, 0, z)

    first_strips(0)
    for copy in loads:
        copy.wait()
    pack(home_ref, piece_ref, slot_own, row_own, col_own, low_own, high_own, angle_own, f_own, w_own, p_own)
    for k, peer in enumerate(far):
        start(remote(p_own, pos_all.at[mine], pos_send.at[k], pos_recv.at[k], peer))
    for part in range(3):
        send_block(1, mine, part, up, True)
        send_block(2, mine, part, down, True)
        send_block(0, mine, part, side, True)
    stores = []
    for i, (src, dst) in enumerate(
        ((q_own, strip(z, det)), (f_own, fo_ref.at[mine]), (w_own, wo_ref.at[mine]), (p_own, pos_all.at[mine]))
    ):
        copy = pltpu.make_async_copy(src, dst, store_sem.at[i])
        copy.start()
        stores.append(copy)

    slot_of = {1: behind * NX + x, 2: ahead * NX + x, 0: y * NX + other, 5: facing * NX + x, 6: facing * NX + other,
               3: behind * NX + other, 4: ahead * NX + other}

    def near(part):
        for link in (1, 2, 0):
            wait_block(link, slot_of[link], part)
            if link == 1 and part != 1:
                send_block(5, slot_of[1], part, up)
            if link == 2 and part == 1:
                send_block(5, slot_of[2], part, down)
            if link == 0:
                send_block(3, slot_of[0], part, up)
                send_block(4, slot_of[0], part, down)

    def opposite(part):
        wait_block(5, slot_of[5], part)
        send_block(6, slot_of[5], part, side)

    near(0)
    remote(q_ref, strip(z, across), hi_send, hi_recv, (across, tm)).wait_recv()
    first_strips(1)
    take_strip(0, 2)
    near(1)
    near(2)
    take_strip(0, 1)
    opposite(0)
    take_strip(1, 2)
    opposite(1)
    opposite(2)
    take_strip(1, 1)
    take_strip(0, 3)
    take_strip(0, 4)

    stores[3].wait()
    for k, peer in enumerate(far):
        remote(p_own, pos_all.at[mine], pos_send.at[k], pos_recv.at[k], peer).wait_recv()
    run_order(pos_all, order_ref, y, x)

    take_strip(1, 3)
    take_strip(1, 4)
    for part in range(3):
        for link in (3, 4, 6):
            wait_block(link, slot_of[link], part)
    theirs = (partner, hi_of(partner))
    for half in (0, 1):
        places = [(0, z)]
        for direction in (0, 1):
            for distance in range(1, reach(half, direction) + 1):
                places.append((direction * NZ // 2 + distance, source_slot(direction, distance)))
        for index, slot in places:
            remote(
                q_ref, strip(slot, theirs[half]), core_send.at[half, index], core_recv.at[half, index], (partner, tm)
            ).wait_recv()
    for copy in stores[:3]:
        copy.wait()
    for copy in started:
        copy.wait_send()


def gather_all(tile_home, piece_list, run_slot, hit_row, hit_col, frac_row, frac_col, angle, quarter):
    bf, f32, i32 = jnp.bfloat16, jnp.float32, jnp.int32
    samples = (2, RUNS, DET, LANE)
    return pl.pallas_call(
        gather_kernel,
        out_shape=(
            jax.ShapeDtypeStruct((NZ, TILE_DEV, 3, PIX, PIX), bf),
            jax.ShapeDtypeStruct((NB, *samples), f32),
            jax.ShapeDtypeStruct((NB, *samples), bf),
            jax.ShapeDtypeStruct((2 * DET, LANE), i32),
        ),
        in_specs=[SM, SM] + [ANY] * 7,
        out_specs=(ANY, ANY, ANY, VM),
        scratch_shapes=[
            *(pltpu.VMEM(v.shape, v.dtype) for v in (run_slot, hit_row, hit_col, frac_row, frac_col, angle)),
            pltpu.VMEM(quarter.shape, bf),
            pltpu.VMEM(samples, f32),
            pltpu.VMEM(samples, bf),
            pltpu.VMEM((DET, RUNS), i32),
            pltpu.VMEM((NB, DET, RUNS), i32),
            DMA((7,)),
            DMA((4,)),
            DMA((NB,)),
            DMA((NB,)),
            DMA((7, 3)),
            DMA((7, 3)),
            DMA((2, 2, NZ // 2)),
            DMA((2, 2, NZ // 2)),
            DMA((2, NZ + 1)),
            DMA((2, NZ + 1)),
            DMA,
            DMA,
        ],
        compiler_params=pltpu.CompilerParams(collective_id=0, has_side_effects=True),
        name="gather_all",
    )(tile_home, piece_list, run_slot, hit_row, hit_col, frac_row, frac_col, angle, quarter)


def sin_cos(v):
    quarter = jnp.round(v * 0.6366197723675814)
    u = v - quarter * 1.5703125
    u = u - quarter * 4.837512969970703e-4
    u = u - quarter * 7.549789948768648e-8
    u2 = u * u
    s = u + u * u2 * (-1.6666654611e-1 + u2 * (8.3321608736e-3 + u2 * -1.9515295891e-4))
    c = 1.0 - 0.5 * u2 + u2 * u2 * (4.166664568298827e-2 + u2 * (-1.388731625493765e-3 + u2 * 2.443315711809948e-5))
    q = quarter.astype(jnp.int32) & 3
    odd = (q & 1) == 1
    sin = jnp.where(odd, c, s)
    cos = jnp.where(odd, s, c)
    sin = jnp.where(q >= 2, -sin, sin)
    cos = jnp.where((q == 1) | (q == 2), -cos, cos)
    return sin, cos


def low_of(high):
    return (1.0 - high).astype(jnp.bfloat16).astype(jnp.float32)


def run_of(entry):
    run = entry & (ALL_RUNS - 1)
    return entry >> 10, (run >> 4) & (NB - 1), run >> 7, run & (RUNS - 1)


def spread(index, low, high, rows):
    bf = jnp.bfloat16
    wide = [jnp.broadcast_to(v, (HALF, LANE)).astype(bf) for v in (index, index + 1.0, low, high)]
    zero = jnp.zeros((HALF, LANE), bf)
    parts = []
    for b in range(PIX // HALF):
        row = rows[b * HALF : (b + 1) * HALF]
        parts.append(jnp.where(row == wide[0], wide[2], jnp.where(row == wide[1], wide[3], zero)))
    return jnp.concatenate(parts, axis=0)


def forward_kernel(
    list_ref, tile_hbm, f_hbm, w_hbm, sig_ref, cs_hbm, hit_ref, frac_ref, cs_ref, tiles_ref, f_ref, w_ref,
    tile_sem, f_sem, w_sem, cs_sem,
):
    def f_copy(z):
        return pltpu.make_async_copy(f_hbm.at[z], f_ref.at[z], f_sem.at[z])

    def w_copy(z):
        return pltpu.make_async_copy(w_hbm.at[z], w_ref.at[z], w_sem.at[z])

    def cs_copy(z):
        return pltpu.make_async_copy(cs_ref.at[z], cs_hbm.at[z], cs_sem.at[z])

    for z in range(NB):
        f_copy(z).start()
        w_copy(z).start()
    tile_copy = pltpu.make_async_copy(tile_hbm, tiles_ref, tile_sem)
    tile_copy.start()

    def prepare(z, _):
        f_copy(z).wait()
        w_copy(z).wait()
        code = f_ref[z, 0]
        row = jnp.floor(code * (1.0 / PIX))
        hit_ref[z, 0] = row
        hit_ref[z, 1] = code - row * PIX
        sin, cos = sin_cos(2.0 * f_ref[z, 1])
        cs_ref[z, 0] = cos
        cs_ref[z, 1] = sin
        cs_copy(z).start()
        frac_ref[z, 0] = w_ref[z, 0].astype(jnp.float32)
        frac_ref[z, 1] = w_ref[z, 1].astype(jnp.float32)
        sig_ref[z] = jnp.zeros_like(sig_ref[z])
        return 0

    lax.fori_loop(0, NB, prepare, 0)
    tile_copy.wait()
    count = list_ref[DET, 0]
    rows = lax.broadcasted_iota(jnp.int32, (PIX, LANE), 0).astype(jnp.float32).astype(jnp.bfloat16)

    def body(step, _):
        for u in range(UNROLL):
            k = step * UNROLL + u
            tile, z, d, r = run_of(list_ref[k >> 7, k & (LANE - 1)])
            at = (r, pl.ds(d, 1), slice(None))
            col_high = frac_ref[z, 1, *at]
            row_high = frac_ref[z, 0, *at]
            col_weight = spread(hit_ref[z, 1, *at], low_of(col_high), col_high, rows)
            row_weight = spread(hit_ref[z, 0, *at], low_of(row_high), row_high, rows).astype(jnp.float32)
            partial = jnp.dot(tiles_ref[tile], col_weight, preferred_element_type=jnp.float32)
            value = [
                jnp.sum(partial[p * PIX : (p + 1) * PIX] * row_weight, axis=0, keepdims=True) for p in range(3)
            ]
            total = value[0] + cs_ref[z, 0, *at] * value[1] + cs_ref[z, 1, *at] * value[2]
            sig_ref[z, d, pl.ds(r, 1), :] = jnp.where(k < count, total, 0.0)
        return 0

    lax.fori_loop(0, (count + UNROLL - 1) // UNROLL, body, 0)
    for z in range(NB):
        cs_copy(z).wait()


def forward(order, tiles, floats, fracs):
    f32 = jnp.float32
    block = (NB, DET, RUNS, LANE)
    pair = (NB, 2, RUNS, DET, LANE)
    return pl.pallas_call(
        forward_kernel,
        out_shape=(jax.ShapeDtypeStruct(block, f32), jax.ShapeDtypeStruct(pair, f32)),
        in_specs=[SM, ANY, ANY, ANY],
        out_specs=(VM, ANY),
        scratch_shapes=[
            pltpu.VMEM(pair, f32),
            pltpu.VMEM(pair, f32),
            pltpu.VMEM(pair, f32),
            pltpu.VMEM(tiles.shape, tiles.dtype),
            pltpu.VMEM(pair, f32),
            pltpu.VMEM(pair, fracs.dtype),
            DMA,
            DMA((NB,)),
            DMA((NB,)),
            DMA((NB,)),
        ],
        name="forward",
    )(order, tiles, floats, fracs)


def backward_kernel(
    list_ref, f_hbm, w_hbm, cs_hbm, filt_hbm, acc_ref, hit_ref, frac_ref, f_ref, w_ref, cs_ref, filt_ref,
    f_sem, w_sem, late_sem,
):
    def f_copy(z):
        return pltpu.make_async_copy(f_hbm.at[z, 0], f_ref.at[z], f_sem.at[z])

    def w_copy(z):
        return pltpu.make_async_copy(w_hbm.at[z], w_ref.at[z], w_sem.at[z])

    late = [
        pltpu.make_async_copy(cs_hbm, cs_ref, late_sem.at[0]),
        pltpu.make_async_copy(filt_hbm, filt_ref, late_sem.at[1]),
    ]
    for z in range(NB):
        f_copy(z).start()
        w_copy(z).start()
    for copy in late:
        copy.start()

    def clear(t, _):
        acc_ref[t] = jnp.zeros_like(acc_ref[t])
        return 0

    lax.fori_loop(0, TILE_DEV * NZ, clear, 0)

    def prepare(z, _):
        f_copy(z).wait()
        w_copy(z).wait()
        code = f_ref[z]
        row = jnp.floor(code * (1.0 / PIX))
        hit_ref[z, 0] = row
        hit_ref[z, 1] = code - row * PIX
        frac_ref[z, 0] = w_ref[z, 0].astype(jnp.float32)
        frac_ref[z, 1] = w_ref[z, 1].astype(jnp.float32)
        return 0

    lax.fori_loop(0, NB, prepare, 0)
    for copy in late:
        copy.wait()
    count = list_ref[DET, 0]
    rows = lax.broadcasted_iota(jnp.int32, (PIX, LANE), 0).astype(jnp.float32).astype(jnp.bfloat16)

    def body(step, _):
        for u in range(UNROLL):
            k = step * UNROLL + u
            tile, z, d, r = run_of(list_ref[k >> 7, k & (LANE - 1)])
            at = (r, pl.ds(d, 1), slice(None))
            col_high = frac_ref[z, 1, *at]
            row_high = frac_ref[z, 0, *at]
            row_low = low_of(row_high)
            col_weight = spread(hit_ref[z, 1, *at], low_of(col_high), col_high, rows)
            filt = jnp.where(k < count, filt_ref[z, d, pl.ds(r, 1), :], 0.0)
            hit = hit_ref[z, 0, *at]
            parts = []
            for p in range(3):
                scaled = filt if p == 0 else cs_ref[z, p - 1, *at] * filt
                parts.append(spread(hit, scaled * row_low, scaled * row_high, rows))
            weighted = jnp.concatenate(parts, axis=0)
            acc_ref[tile] += lax.dot_general(
                weighted, col_weight, (((1,), (1,)), ((), ())), preferred_element_type=jnp.float32
            )
        return 0

    lax.fori_loop(0, (count + UNROLL - 1) // UNROLL, body, 0)


def backward(order, floats, fracs, turns, filtered):
    f32 = jnp.float32
    pair = (NB, 2, RUNS, DET, LANE)
    return pl.pallas_call(
        backward_kernel,
        out_shape=jax.ShapeDtypeStruct((TILE_DEV * NZ, 3 * PIX, PIX), f32),
        in_specs=[SM, ANY, ANY, ANY, ANY],
        out_specs=VM,
        scratch_shapes=[
            pltpu.VMEM(pair, f32),
            pltpu.VMEM(pair, f32),
            pltpu.VMEM((NB, RUNS, DET, LANE), f32),
            pltpu.VMEM(pair, fracs.dtype),
            pltpu.VMEM(pair, f32),
            pltpu.VMEM(filtered.shape, f32),
            DMA((NB,)),
            DMA((NB,)),
            DMA((2,)),
        ],
        name="backward",
    )(order, floats, fracs, turns, filtered)


def toeplitz(noise_ref, line_ref, hi_ref, lo_ref):
    square = (LANE, LANE)
    lanes = lax.broadcasted_iota(jnp.int32, square, 1)
    rows = lax.broadcasted_iota(jnp.int32, square, 0)
    first = lax.broadcasted_iota(jnp.int32, (DET, LANE), 1) == 0
    for q in range(REACH):
        lags = noise_ref[:, q * LANE : (q + 1) * LANE]
        line_ref[q] = jnp.where(first, lags + 1.0, lags) if q == 0 else lags
    line_ref[REACH] = jnp.where(first, jnp.broadcast_to(noise_ref[:, REACH * LANE :], (DET, LANE)), 0.0)

    def one(d, _):
        def put(q, matrix):
            high = matrix.astype(jnp.bfloat16)
            hi_ref[d, q] = high
            lo_ref[d, q] = (matrix - high.astype(jnp.float32)).astype(jnp.bfloat16)

        before = None
        for q in range(REACH + 1):
            lags = line_ref[q, pl.ds(d, 1), :]
            after = pltpu.roll(jnp.broadcast_to(lags, square), 0, 1, stride=1, stride_axis=0)
            if q == 0:
                put(0, jnp.where(lanes >= rows, after, 0.0))
                put(REACH + 1, jnp.where(lanes > rows, after, 0.0))
            else:
                put(q, jnp.where(lanes >= rows, after, before))
            before = after
        return 0

    lax.fori_loop(0, DET, one, 0)


STRAIGHT = (((1,), (0,)), ((), ()))
CROSSED = (((1,), (1,)), ((), ()))


def filter_kernel(
    part_ref, noise_ref, out_ref, land, ext, filt, lags, t_hi, t_lo,
    own_sem, store_sem, send, recv, halo_send, halo_recv, back_send, back_recv,
):
    det, tm, y, z, x = place()
    total_tm = NY * NZ * NX
    mine = y * NX + x
    prior, later = (tm + total_tm - 1) % total_tm, (tm + 1) % total_tm

    def slot(k, sign):
        dy, dx = PEERS[k]
        return ((y + sign * dy + NY) % NY) * NX + (x + dx) % NX

    peers = [(det, tm_of((y + dy) % NY, z, (x + dx) % NX)) for dy, dx in PEERS]
    greet(peers + [(det, later), (det, prior)])
    own = pltpu.make_async_copy(part_ref.at[mine], land.at[NB - 1], own_sem)
    own.start()
    sends = []
    for k, peer in enumerate(peers):
        copy = remote(part_ref.at[slot(k, 1)], land.at[k], send.at[k], recv.at[k], peer)
        copy.start()
        sends.append(copy)
    toeplitz(noise_ref, lags, t_hi, t_lo)
    own.wait()
    total = land[NB - 1]
    for k in range(NB - 1):
        sends[k].wait_recv()
        total = total + land[k]
    ext[:, REACH : REACH + RUNS, :] = total
    to_prior = remote(
        ext.at[:, pl.ds(REACH, REACH), :], ext.at[:, pl.ds(REACH + RUNS, REACH), :],
        halo_send.at[0], halo_recv.at[0], (det, prior),
    )
    to_later = remote(
        ext.at[:, pl.ds(RUNS, REACH), :], ext.at[:, pl.ds(0, REACH), :], halo_send.at[1], halo_recv.at[1], (det, later)
    )
    to_prior.start()
    to_later.start()
    to_prior.wait_recv()
    to_later.wait_recv()
    first, last = tm == 0, tm == total_tm - 1

    def product(left, right, crossed):
        return lax.dot_general(left, right, CROSSED if crossed else STRAIGHT, preferred_element_type=jnp.float32)

    back, own_copies = [], []

    def back_copy(c, k, source):
        rows = pl.ds(c * SENT, SENT)
        return remote(filt.at[rows], out_ref.at[source, rows], back_send.at[k, c], back_recv.at[k, c], peers[k])

    def send_back(c):
        for k in range(NB - 1):
            copy = back_copy(c, k, mine)
            copy.start()
            back.append(copy)
        rows = pl.ds(c * SENT, SENT)
        copy = pltpu.make_async_copy(filt.at[rows], out_ref.at[mine, rows], store_sem.at[c])
        copy.start()
        own_copies.append(copy)

    for c in range(DET // SENT):
        dets = range(c * SENT, (c + 1) * SENT)
        lines = [
            jnp.concatenate(
                [
                    jnp.where(first, 0.0, ext[d, :REACH]),
                    ext[d, REACH : REACH + RUNS],
                    jnp.where(last, 0.0, ext[d, REACH + RUNS :]),
                ],
                axis=0,
            )
            for d in dets
        ]
        full = [jnp.zeros((2 * RUNS, LANE), jnp.float32) for d in dets]
        fine = [jnp.zeros((RUNS, LANE), jnp.float32) for d in dets]
        for m in range(2 * REACH + 1):
            q = REACH - m
            for i, d in enumerate(dets):
                window = lines[i][m : m + RUNS]
                high = window.astype(jnp.bfloat16)
                low = (window - high.astype(jnp.float32)).astype(jnp.bfloat16)
                stack = jnp.concatenate([high, low], axis=0)
                for index, crossed in [(q, False)] if q > 0 else [(-q, True)] if q < 0 else [(0, False), (REACH + 1, True)]:
                    full[i] += product(stack, t_hi[d, index], crossed)
                    fine[i] += product(high, t_lo[d, index], crossed)
        for i, d in enumerate(dets):
            filt[d] = full[i][:RUNS] + full[i][RUNS:] + fine[i]
        send_back(c)
    for copy in own_copies:
        copy.wait()
    for c in range(DET // SENT):
        for k, peer in enumerate(peers):
            back_copy(c, k, slot(k, -1)).wait_recv()
    for copy in sends + back + [to_prior, to_later]:
        copy.wait_send()


def filtered_of(partial, noise_coef):
    f32, bf = jnp.float32, jnp.bfloat16
    block = (DET, RUNS, LANE)
    matrices = (DET, REACH + 2, LANE, LANE)
    return pl.pallas_call(
        filter_kernel,
        out_shape=jax.ShapeDtypeStruct((NB, *block), f32),
        in_specs=[ANY, VM],
        out_specs=ANY,
        scratch_shapes=[
            pltpu.VMEM((NB, *block), f32),
            pltpu.VMEM((DET, RUNS + 2 * REACH, LANE), f32),
            pltpu.VMEM(block, f32),
            pltpu.VMEM((REACH + 1, DET, LANE), f32),
            pltpu.VMEM(matrices, bf),
            pltpu.VMEM(matrices, bf),
            DMA,
            DMA((DET // SENT,)),
            DMA((NB,)),
            DMA((NB,)),
            DMA((2,)),
            DMA((2,)),
            DMA((NB, DET // SENT)),
            DMA((NB, DET // SENT)),
        ],
        compiler_params=pltpu.CompilerParams(collective_id=1, has_side_effects=True),
        name="filter",
    )(partial, noise_coef)


CHUNKS = [(t, p) for t in range(TILE_DEV) for p in range(3)]
HALF_Z = NZ // 2
WIRE = jnp.bfloat16
OFFSETS = [4, 3, -3, 2, -2, 1, -1, 0]


def collect_kernel(
    acc_ref, sum_ref, land_last, land_own, own, land_core, packet, land,
    own_sem, sum_sem, core_send, core_recv, ring_send, ring_recv, last_send, last_recv, hi_send, hi_recv,
):
    f32 = jnp.float32
    det, tm, y, z, x = place()
    core, hi = det % 2, det // 2
    partner, across = core_of(det), hi_of(det)
    right, left = tm_of(y, (z + 1) % NZ, x), tm_of(y, (z + NZ - 1) % NZ, x)
    neighbours = ((det, right), (det, left))
    loads = []
    for k, offset in enumerate(OFFSETS):
        copy = pltpu.make_async_copy(acc_ref.at[(z + offset + NZ) % NZ, :, :, :, core], own.at[k], own_sem.at[k])
        copy.start()
        loads.append(copy)
    greet([(partner, tm), (across, tm), *neighbours, (across, right), (across, left)])
    started = []

    def start(copy):
        copy.start()
        started.append(copy)

    for k, offset in enumerate(OFFSETS):
        start(
            remote(
                acc_ref.at[(z + offset + NZ) % NZ, :, :, :, 1 - core], land_core.at[k], core_send.at[k], core_recv.at[k],
                (partner, tm),
            )
        )

    def ring(direction, step, c):
        t, p = CHUNKS[c]
        sign = 1 if direction == 0 else -1
        k = OFFSETS.index(sign * (HALF_Z - step)) if step else 0
        return remote(
            packet.at[k, t, p], land.at[direction, step, t, p],
            ring_send.at[direction, step, c], ring_recv.at[direction, step, c], neighbours[direction],
        )

    def last_hop(direction, c, crossing):
        t, p = CHUNKS[c]
        k = OFFSETS.index(1 if direction == 0 else -1)
        goal = (right, left)[direction]
        return remote(
            packet.at[k, t, p, 1 - hi if crossing else hi], land_last.at[crossing, direction, t, p],
            last_send.at[crossing, direction, c], last_recv.at[crossing, direction, c],
            (across if crossing else det, goal),
        )

    def own_copy(t):
        return remote(packet.at[len(OFFSETS) - 1, t, :, 1 - hi], land_own.at[t], hi_send.at[t], hi_recv.at[t], (across, tm))

    def swapped(k):
        loads[k].wait()
        remote(acc_ref.at[0, :, :, :, 0], land_core.at[k], core_send.at[k], core_recv.at[k], (partner, tm)).wait_recv()

    swapped(0)
    for direction in (0, 1):
        for c, (t, p) in enumerate(CHUNKS):
            if t == direction:
                packet[0, t, p] = (own[0, t, p] + land_core[0, t, p]).astype(WIRE)
    for p in range(3):
        for direction in (0, 1):
            start(ring(direction, 0, direction * 3 + p))
    last = len(OFFSETS) - 1
    for step in range(1, HALF_Z):
        keys = [OFFSETS.index(HALF_Z - step), OFFSETS.index(step - HALF_Z)]
        for k in keys:
            swapped(k)
        for i in range(len(CHUNKS)):
            for direction in (0, 1):
                c = (i + 3 * (1 - direction)) % len(CHUNKS) if step == 1 else i
                t, p = CHUNKS[c]
                k = keys[direction]
                value = own[k, t, p] + land_core[k, t, p]
                if step > 1 or t == direction:
                    ring(direction, step - 1, c).wait_recv()
                    value = value + land[direction, step - 1, t, p].astype(f32)
                packet[k, t, p] = value.astype(WIRE)
                if step < HALF_Z - 1:
                    start(ring(direction, step, c))
                else:
                    start(last_hop(direction, c, 1))
                    start(last_hop(direction, c, 0))
        if step == 1:
            swapped(last)
            for t in range(TILE_DEV):
                value = own[last, t] + land_core[last, t]
                packet[last, t] = value.astype(WIRE)
                start(own_copy(t))
                own[last, t] = value
            keep = pltpu.make_async_copy(own.at[last, :, :, hi], sum_ref, sum_sem)
            keep.start()
    for t in range(TILE_DEV):
        own_copy(t).wait_recv()
    for c in range(len(CHUNKS)):
        for crossing in (0, 1):
            for direction in (0, 1):
                last_hop(direction, c, crossing).wait_recv()
    keep.wait()
    for copy in started:
        copy.wait_send()


def collect(acc):
    f32 = jnp.float32
    half = (TILE_DEV, 3, 2, STRIP, PIX)
    quarter = (TILE_DEV, 3, STRIP, PIX)
    return pl.pallas_call(
        collect_kernel,
        out_shape=(
            jax.ShapeDtypeStruct(quarter, f32),
            jax.ShapeDtypeStruct((2, 2, *quarter), WIRE),
            jax.ShapeDtypeStruct(quarter, WIRE),
        ),
        in_specs=[ANY],
        out_specs=(ANY, ANY, ANY),
        scratch_shapes=[
            pltpu.VMEM((NZ, *half), f32),
            pltpu.VMEM((NZ, *half), f32),
            pltpu.VMEM((NZ, *half), WIRE),
            pltpu.VMEM((2, HALF_Z - 1, *half), WIRE),
            DMA((NZ,)),
            DMA,
            DMA((NZ,)),
            DMA((NZ,)),
            DMA((2, HALF_Z - 1, 6)),
            DMA((2, HALF_Z - 1, 6)),
            DMA((2, 2, 6)),
            DMA((2, 2, 6)),
            DMA((2,)),
            DMA((2,)),
        ],
        compiler_params=pltpu.CompilerParams(collective_id=2, has_side_effects=True),
        name="collect",
    )(acc.reshape(NZ, TILE_DEV, 3, 2, 2, STRIP, PIX))


def body(
    sky_map, tile_home, piece_tiles, run_slot, hit_row, hit_col, frac_row, frac_col, angle, noise_coef
):
    tiles, all_floats, all_fracs, order = gather_all(
        tile_home, piece_tiles.reshape(1, LISTED), run_slot, hit_row, hit_col, frac_row, frac_col, angle, sky_map
    )
    partial, turns = forward(order, tiles.reshape(TILE_DEV * NZ, 3 * PIX, PIX), all_floats, all_fracs)
    filtered = filtered_of(partial, noise_coef)
    acc = backward(order, all_floats, all_fracs, turns, filtered)
    kept, landed, crossed = collect(acc)
    f32 = jnp.float32
    straight = landed[0, 0].astype(f32) + landed[0, 1].astype(f32)
    return kept + crossed.astype(f32) + straight + landed[1, 0].astype(f32) + landed[1, 1].astype(f32)


def solution(mesh):
    placed = (
        P("tm", None, "det", None),
        P(),
        P("det", "tm", None),
        P("det", "tm"),
        P("det", "tm"),
        P("det", "tm"),
        P("det", "tm"),
        P("det", "tm"),
        P("det", "tm"),
        P("det", None),
    )
    return jax.shard_map(
        body, mesh=mesh, in_specs=placed, out_specs=P("tm", None, "det", None), check_vma=False
    )
```

```python
import functools

import jax
import jax.numpy as jnp
from jax import lax
from jax.experimental import pallas as pl
from jax.experimental.pallas import tpu as pltpu
from jax.sharding import PartitionSpec as P

GRANT = 24 << 20
MESH = pl.DeviceIdType.MESH
NY, NZ, NX = 4, 8, 2
NB = NY * NX
DET, RUNS, LANE = 8, 16, 128
PIX = 128
STRIP = 32
LISTED = 32
TILE_DEV = 2
REACH = 8
UNROLL = 16
HALF = 16
SENT = 2
PIECE_RUNS = DET * RUNS
ALL_RUNS = NB * PIECE_RUNS
ANY = pl.BlockSpec(memory_space=pl.ANY)
VM = pl.BlockSpec(memory_space=pltpu.VMEM)
SM = pl.BlockSpec(memory_space=pltpu.SMEM)
DMA = pltpu.SemaphoreType.DMA
PEERS = [(dy, dx) for dy in range(NY) for dx in range(NX) if (dy, dx) != (0, 0)]


def place():
    det, tm = lax.axis_index("det"), lax.axis_index("tm")
    y, z, x = tm // (NZ * NX), (tm // NX) % NZ, tm % NX
    return det, tm, y, z, x


def tm_of(y, z, x):
    return (y * NZ + z) * NX + x


def core_of(det):
    return det + 1 - 2 * (det % 2)


def hi_of(det):
    return (det + 2) % 4


def greet(peers):
    barrier = pltpu.get_barrier_semaphore()
    for peer in peers:
        pl.semaphore_signal(barrier, inc=1, device_id=peer, device_id_type=MESH)
    pl.semaphore_wait(barrier, len(peers))


def remote(src, dst, send, recv, peer):
    return pltpu.make_async_remote_copy(
        src_ref=src, dst_ref=dst, send_sem=send, recv_sem=recv, device_id=peer, device_id_type=MESH
    )


def run_order(pos_ref, order_ref, y, x):
    f32, bf, i32 = jnp.float32, jnp.bfloat16, jnp.int32

    def iota(shape, dim):
        return lax.broadcasted_iota(i32, shape, dim)

    def whole(mask):
        return jnp.where(mask, 1.0, 0.0).astype(bf)

    def dot(left, right):
        return jnp.dot(left, right, preferred_element_type=f32)

    lanes, offset = iota((RUNS, LANE), 1), iota((RUNS, LANE), 0)
    spot = jnp.zeros((DET, LANE), f32)
    for slot in range(NB):
        spot += dot(pos_ref[slot].astype(f32).astype(bf), whole(lanes == offset + slot * RUNS))
    pos = spot.astype(i32)
    here = (pos // (TILE_DEV * NX * NZ) == y) & ((pos // TILE_DEV) % NX == x)
    tile = ((pos // (TILE_DEV * NX)) % NZ) * TILE_DEV + pos % TILE_DEV
    kinds, square = (2 * TILE_DEV * NZ, LANE), (LANE, LANE)
    kind = jnp.where(here, tile, TILE_DEV * NZ)
    tile = tile.astype(f32)
    before, every = whole(iota(square, 0) < iota(square, 1)), jnp.ones(square, bf)
    marks, prior, total = [], [], jnp.zeros(kinds, f32)
    for d in range(DET):
        mark = whole(jnp.broadcast_to(kind[d : d + 1], kinds) == iota(kinds, 0))
        marks.append(mark.astype(f32))
        prior.append(dot(mark, before) + total)
        total += dot(mark, every)
    lower = whole(iota((kinds[0], kinds[0]), 1) < iota((kinds[0], kinds[0]), 0))
    coarse = jnp.floor(total * (1.0 / 32.0))
    base = 32.0 * dot(lower, coarse.astype(bf)) + dot(lower, (total - 32.0 * coarse).astype(bf))
    high_rows, low_rows = iota((DET, LANE), 0).astype(f32), iota(square, 0).astype(f32)
    lane = iota((DET, LANE), 1).astype(f32)
    found = jnp.zeros((3 * DET, LANE), f32)
    for d in range(DET):
        rank = jnp.sum(marks[d] * (prior[d] + base), axis=0, keepdims=True)
        high = jnp.floor(rank * (1.0 / LANE))
        low = rank - LANE * high
        at = jnp.broadcast_to(high, (DET, LANE)) == high_rows
        values = (jnp.broadcast_to(tile[d : d + 1], (DET, LANE)), jnp.full((DET, LANE), float(d), f32), lane)
        left = jnp.concatenate([jnp.where(at, v, 0.0) for v in values], axis=0).astype(bf)
        right = whole(jnp.broadcast_to(low, square) == low_rows)
        found += lax.dot_general(left, right, (((1,), (1,)), ((), ())), preferred_element_type=f32)
    entry = found[:DET] * ALL_RUNS + found[DET : 2 * DET] * LANE + found[2 * DET :]
    order_ref[:DET, :] = entry.astype(i32)
    others = total[TILE_DEV * NZ : TILE_DEV * NZ + 1]
    order_ref[DET:, :] = jnp.broadcast_to(ALL_RUNS - others, (DET, LANE)).astype(i32)


def pack(home_ref, piece_ref, slot_ref, row_ref, col_ref, low_ref, high_ref, angle_ref, f_own, w_own, p_own):
    for r in range(RUNS):
        at = slice(r * LANE, (r + 1) * LANE)
        f_own[0, r] = (row_ref[:, at] * PIX + col_ref[:, at]).astype(jnp.float32)
        f_own[1, r] = angle_ref[:, at]
        w_own[0, r] = low_ref[:, at]
        w_own[1, r] = high_ref[:, at]
    slots = slot_ref[...]
    position = jnp.zeros_like(slots)
    for s in range(LISTED):
        position = jnp.where(slots == s, home_ref[piece_ref[0, s]], position)
    p_own[...] = position


def gather_kernel(
    home_ref, piece_ref, slot_ref, row_ref, col_ref, low_ref, high_ref, angle_ref, q_ref,
    tiles_ref, fo_ref, wo_ref, order_ref,
    q_own, f_own, w_own, p_own, pos_all, load_sem, store_sem,
    pos_send, pos_recv, block_send, block_recv, strip_send, strip_recv, core_send, core_recv, hi_send, hi_recv,
):
    det, tm, y, z, x = place()
    partner, across = core_of(det), hi_of(det)
    ahead, behind = (y + 1) % NY, (y + NY - 1) % NY
    facing = (y + NY // 2) % NY
    other = 1 - x
    up, down, side = (det, tm_of(ahead, z, x)), (det, tm_of(behind, z, x)), (det, tm_of(y, z, other))
    far = [(det, tm_of((y + dy) % NY, z, (x + dx) % NX)) for dy, dx in PEERS]

    def along(direction, jump):
        return (det, tm_of(y, (z + jump) % NZ if direction == 0 else (z + NZ - jump) % NZ, x))

    def strip(slot, d):
        return tiles_ref.at[slot, :, :, pl.ds(d * STRIP, STRIP), :]

    def block(slot, part):
        return fo_ref.at[slot, part] if part < 2 else wo_ref.at[slot]

    def own_block(part):
        return f_own.at[part] if part < 2 else w_own

    mine = y * NX + x
    load = pltpu.make_async_copy(q_ref, q_own, load_sem)
    load.start()
    greeted = [along(d, j) for d in (0, 1) for j in (1, 2)] + [(partner, tm), (across, tm)] + far
    barrier = pltpu.get_barrier_semaphore()
    for peer in greeted:
        pl.semaphore_signal(barrier, inc=1, device_id=peer, device_id_type=MESH)
    pack(home_ref, piece_ref, slot_ref, row_ref, col_ref, low_ref, high_ref, angle_ref, f_own, w_own, p_own)
    pl.semaphore_wait(barrier, len(greeted))

    started = []

    def start(copy):
        copy.start()
        started.append(copy)

    start(remote(q_ref, strip(z, det), hi_send, hi_recv, (across, tm)))
    for k, peer in enumerate(far):
        start(remote(p_own, pos_all.at[mine], pos_send.at[k], pos_recv.at[k], peer))

    def send_block(link, slot, part, peer, own=False):
        start(
            remote(
                own_block(part) if own else block(slot, part), block(slot, part),
                block_send.at[link, part], block_recv.at[link, part], peer,
            )
        )

    def wait_block(link, slot, part):
        remote(own_block(part), block(slot, part), block_send.at[link, part], block_recv.at[link, part], side).wait_recv()

    owner = (det, across)

    def source_slot(direction, distance):
        return (z + NZ - distance) % NZ if direction == 0 else (z + distance) % NZ

    def send_strip(half, direction, distance):
        slot = z if distance < 3 else source_slot(direction, 2)
        here = strip(slot, owner[half])
        start(
            remote(
                q_ref if half == 0 and distance < 3 else here, here,
                strip_send.at[half, direction, distance - 1], strip_recv.at[half, direction, distance - 1],
                along(direction, 2 - distance % 2),
            )
        )

    def reach(half, direction):
        return NZ // 2 if half == direction else NZ // 2 - 1

    def to_partner(half, index, slot):
        here = strip(slot, owner[half])
        start(
            remote(
                q_ref if half == 0 and index == 0 else here, here, core_send.at[half, index], core_recv.at[half, index],
                (partner, tm),
            )
        )

    def take_strip(half, distance):
        for direction in (0, 1):
            if distance <= reach(half, direction):
                slot = source_slot(direction, distance)
                remote(
                    q_ref, strip(slot, owner[half]),
                    strip_send.at[half, direction, distance - 1], strip_recv.at[half, direction, distance - 1], side,
                ).wait_recv()
                if distance == 2:
                    if reach(half, direction) == 4:
                        send_strip(half, direction, 4)
                    send_strip(half, direction, 3)
                to_partner(half, direction * NZ // 2 + distance, slot)

    def first_strips(half):
        for distance in (2, 1):
            for direction in (0, 1):
                send_strip(half, direction, distance)
        to_partner(half, 0, z)

    first_strips(0)
    for part in range(3):
        send_block(1, mine, part, up, True)
        send_block(2, mine, part, down, True)
        send_block(0, mine, part, side, True)
    load.wait()
    stores = []
    for i, (src, dst) in enumerate(
        ((q_own, strip(z, det)), (f_own, fo_ref.at[mine]), (w_own, wo_ref.at[mine]), (p_own, pos_all.at[mine]))
    ):
        copy = pltpu.make_async_copy(src, dst, store_sem.at[i])
        copy.start()
        stores.append(copy)

    slot_of = {1: behind * NX + x, 2: ahead * NX + x, 0: y * NX + other, 5: facing * NX + x, 6: facing * NX + other,
               3: behind * NX + other, 4: ahead * NX + other}

    def near(part):
        for link in (1, 2, 0):
            wait_block(link, slot_of[link], part)
            if link == 1 and part != 1:
                send_block(5, slot_of[1], part, up)
            if link == 2 and part == 1:
                send_block(5, slot_of[2], part, down)
            if link == 0:
                send_block(3, slot_of[0], part, up)
                send_block(4, slot_of[0], part, down)

    def opposite(part):
        wait_block(5, slot_of[5], part)
        send_block(6, slot_of[5], part, side)

    near(0)
    remote(q_ref, strip(z, across), hi_send, hi_recv, (across, tm)).wait_recv()
    first_strips(1)
    take_strip(0, 2)
    near(1)
    near(2)
    take_strip(0, 1)
    opposite(0)
    take_strip(1, 2)
    opposite(1)
    opposite(2)
    take_strip(1, 1)
    take_strip(0, 3)
    take_strip(0, 4)

    stores[3].wait()
    for k, peer in enumerate(far):
        remote(p_own, pos_all.at[mine], pos_send.at[k], pos_recv.at[k], peer).wait_recv()
    run_order(pos_all, order_ref, y, x)

    take_strip(1, 3)
    take_strip(1, 4)
    for part in range(3):
        for link in (3, 4, 6):
            wait_block(link, slot_of[link], part)
    theirs = (partner, hi_of(partner))
    for half in (0, 1):
        places = [(0, z)]
        for direction in (0, 1):
            for distance in range(1, reach(half, direction) + 1):
                places.append((direction * NZ // 2 + distance, source_slot(direction, distance)))
        for index, slot in places:
            remote(
                q_ref, strip(slot, theirs[half]), core_send.at[half, index], core_recv.at[half, index], (partner, tm)
            ).wait_recv()
    for copy in stores[:3]:
        copy.wait()
    for copy in started:
        copy.wait_send()


def gather_all(tile_home, piece_list, run_slot, hit_row, hit_col, frac_row, frac_col, angle, quarter):
    bf, f32, i32 = jnp.bfloat16, jnp.float32, jnp.int32
    samples = (2, RUNS, DET, LANE)
    return pl.pallas_call(
        gather_kernel,
        out_shape=(
            jax.ShapeDtypeStruct((NZ, TILE_DEV, 3, PIX, PIX), bf),
            jax.ShapeDtypeStruct((NB, *samples), f32),
            jax.ShapeDtypeStruct((NB, *samples), bf),
            jax.ShapeDtypeStruct((2 * DET, LANE), i32),
        ),
        in_specs=[SM, SM] + [VM] * 6 + [ANY],
        out_specs=(ANY, ANY, ANY, VM),
        scratch_shapes=[
            pltpu.VMEM(quarter.shape, bf),
            pltpu.VMEM(samples, f32),
            pltpu.VMEM(samples, bf),
            pltpu.VMEM((DET, RUNS), i32),
            pltpu.VMEM((NB, DET, RUNS), i32),
            DMA,
            DMA((4,)),
            DMA((NB,)),
            DMA((NB,)),
            DMA((7, 3)),
            DMA((7, 3)),
            DMA((2, 2, NZ // 2)),
            DMA((2, 2, NZ // 2)),
            DMA((2, NZ + 1)),
            DMA((2, NZ + 1)),
            DMA,
            DMA,
        ],
        compiler_params=pltpu.CompilerParams(collective_id=0, has_side_effects=True, vmem_limit_bytes=GRANT),
        name="gather_all",
    )(tile_home, piece_list, run_slot, hit_row, hit_col, frac_row, frac_col, angle, quarter)


def sin_cos(v):
    quarter = jnp.round(v * 0.6366197723675814)
    u = v - quarter * 1.5703125
    u = u - quarter * 4.837512969970703e-4
    u = u - quarter * 7.549789948768648e-8
    u2 = u * u
    s = u + u * u2 * (-1.6666654611e-1 + u2 * (8.3321608736e-3 + u2 * -1.9515295891e-4))
    c = 1.0 - 0.5 * u2 + u2 * u2 * (4.166664568298827e-2 + u2 * (-1.388731625493765e-3 + u2 * 2.443315711809948e-5))
    q = quarter.astype(jnp.int32) & 3
    odd = (q & 1) == 1
    sin = jnp.where(odd, c, s)
    cos = jnp.where(odd, s, c)
    sin = jnp.where(q >= 2, -sin, sin)
    cos = jnp.where((q == 1) | (q == 2), -cos, cos)
    return sin, cos


def low_of(high):
    return (1.0 - high).astype(jnp.bfloat16).astype(jnp.float32)


def run_of(entry):
    run = entry & (ALL_RUNS - 1)
    return entry >> 10, (run >> 4) & (NB - 1), run >> 7, run & (RUNS - 1)


def spread(index, low, high, rows):
    bf = jnp.bfloat16
    wide = [jnp.broadcast_to(v, (HALF, LANE)).astype(bf) for v in (index, index + 1.0, low, high)]
    zero = jnp.zeros((HALF, LANE), bf)
    parts = []
    for b in range(PIX // HALF):
        row = rows[b * HALF : (b + 1) * HALF]
        parts.append(jnp.where(row == wide[0], wide[2], jnp.where(row == wide[1], wide[3], zero)))
    return jnp.concatenate(parts, axis=0)


def forward_kernel(list_ref, tiles_ref, f_ref, w_ref, sig_ref, cs_ref, hit_ref, frac_ref):
    def prepare(z, _):
        code = f_ref[z, 0]
        row = jnp.floor(code * (1.0 / PIX))
        hit_ref[z, 0] = row
        hit_ref[z, 1] = code - row * PIX
        sin, cos = sin_cos(2.0 * f_ref[z, 1])
        cs_ref[z, 0] = cos
        cs_ref[z, 1] = sin
        frac_ref[z, 0] = w_ref[z, 0].astype(jnp.float32)
        frac_ref[z, 1] = w_ref[z, 1].astype(jnp.float32)
        sig_ref[z] = jnp.zeros_like(sig_ref[z])
        return 0

    lax.fori_loop(0, NB, prepare, 0)
    count = list_ref[DET, 0]
    rows = lax.broadcasted_iota(jnp.int32, (PIX, LANE), 0).astype(jnp.float32).astype(jnp.bfloat16)

    def body(step, _):
        for u in range(UNROLL):
            k = step * UNROLL + u
            tile, z, d, r = run_of(list_ref[k >> 7, k & (LANE - 1)])
            at = (r, pl.ds(d, 1), slice(None))
            col_high = frac_ref[z, 1, *at]
            row_high = frac_ref[z, 0, *at]
            col_weight = spread(hit_ref[z, 1, *at], low_of(col_high), col_high, rows)
            row_weight = spread(hit_ref[z, 0, *at], low_of(row_high), row_high, rows).astype(jnp.float32)
            partial = jnp.dot(tiles_ref[tile], col_weight, preferred_element_type=jnp.float32)
            value = [
                jnp.sum(partial[p * PIX : (p + 1) * PIX] * row_weight, axis=0, keepdims=True) for p in range(3)
            ]
            total = value[0] + cs_ref[z, 0, *at] * value[1] + cs_ref[z, 1, *at] * value[2]
            sig_ref[z, d, pl.ds(r, 1), :] = jnp.where(k < count, total, 0.0)
        return 0

    lax.fori_loop(0, (count + UNROLL - 1) // UNROLL, body, 0)


def forward(order, tiles, floats, fracs):
    f32 = jnp.float32
    block = (NB, DET, RUNS, LANE)
    pair = (NB, 2, RUNS, DET, LANE)
    return pl.pallas_call(
        forward_kernel,
        out_shape=(jax.ShapeDtypeStruct(block, f32), jax.ShapeDtypeStruct(pair, f32)),
        in_specs=[SM, VM, VM, VM],
        out_specs=(VM, VM),
        scratch_shapes=[pltpu.VMEM(pair, f32), pltpu.VMEM(pair, f32)],
        compiler_params=pltpu.CompilerParams(vmem_limit_bytes=GRANT),
        name="forward",
    )(order, tiles, floats, fracs)


def backward_kernel(list_ref, f_ref, w_ref, cs_ref, filt_ref, acc_ref, hit_ref, frac_ref):
    def prepare(z, _):
        code = f_ref[z, 0]
        row = jnp.floor(code * (1.0 / PIX))
        hit_ref[z, 0] = row
        hit_ref[z, 1] = code - row * PIX
        frac_ref[z, 0] = w_ref[z, 0].astype(jnp.float32)
        frac_ref[z, 1] = w_ref[z, 1].astype(jnp.float32)
        return 0

    lax.fori_loop(0, NB, prepare, 0)

    def clear(t, _):
        acc_ref[t] = jnp.zeros_like(acc_ref[t])
        return 0

    lax.fori_loop(0, TILE_DEV * NZ, clear, 0)
    count = list_ref[DET, 0]
    rows = lax.broadcasted_iota(jnp.int32, (PIX, LANE), 0).astype(jnp.float32).astype(jnp.bfloat16)

    def body(step, _):
        for u in range(UNROLL):
            k = step * UNROLL + u
            tile, z, d, r = run_of(list_ref[k >> 7, k & (LANE - 1)])
            at = (r, pl.ds(d, 1), slice(None))
            col_high = frac_ref[z, 1, *at]
            row_high = frac_ref[z, 0, *at]
            row_low = low_of(row_high)
            col_weight = spread(hit_ref[z, 1, *at], low_of(col_high), col_high, rows)
            filt = jnp.where(k < count, filt_ref[z, d, pl.ds(r, 1), :], 0.0)
            hit = hit_ref[z, 0, *at]
            parts = []
            for p in range(3):
                scaled = filt if p == 0 else cs_ref[z, p - 1, *at] * filt
                parts.append(spread(hit, scaled * row_low, scaled * row_high, rows))
            weighted = jnp.concatenate(parts, axis=0)
            acc_ref[tile] += lax.dot_general(
                weighted, col_weight, (((1,), (1,)), ((), ())), preferred_element_type=jnp.float32
            )
        return 0

    lax.fori_loop(0, (count + UNROLL - 1) // UNROLL, body, 0)


def backward(order, floats, fracs, turns, filtered):
    f32 = jnp.float32
    pair = (NB, 2, RUNS, DET, LANE)
    return pl.pallas_call(
        backward_kernel,
        out_shape=jax.ShapeDtypeStruct((TILE_DEV * NZ, 3 * PIX, PIX), f32),
        in_specs=[SM, VM, VM, VM, VM],
        out_specs=VM,
        scratch_shapes=[pltpu.VMEM(pair, f32), pltpu.VMEM(pair, f32)],
        compiler_params=pltpu.CompilerParams(vmem_limit_bytes=GRANT),
        name="backward",
    )(order, floats, fracs, turns, filtered)


def toeplitz(noise_ref, line_ref, hi_ref, lo_ref):
    square = (LANE, LANE)
    lanes = lax.broadcasted_iota(jnp.int32, square, 1)
    rows = lax.broadcasted_iota(jnp.int32, square, 0)
    first = lax.broadcasted_iota(jnp.int32, (DET, LANE), 1) == 0
    for q in range(REACH):
        lags = noise_ref[:, q * LANE : (q + 1) * LANE]
        line_ref[q] = jnp.where(first, lags + 1.0, lags) if q == 0 else lags
    line_ref[REACH] = jnp.where(first, jnp.broadcast_to(noise_ref[:, REACH * LANE :], (DET, LANE)), 0.0)

    def one(d, _):
        def put(q, matrix):
            high = matrix.astype(jnp.bfloat16)
            hi_ref[d, q] = high
            lo_ref[d, q] = (matrix - high.astype(jnp.float32)).astype(jnp.bfloat16)

        before = None
        for q in range(REACH + 1):
            lags = line_ref[q, pl.ds(d, 1), :]
            after = pltpu.roll(jnp.broadcast_to(lags, square), 0, 1, stride=1, stride_axis=0)
            if q == 0:
                put(0, jnp.where(lanes >= rows, after, 0.0))
                put(REACH + 1, jnp.where(lanes > rows, after, 0.0))
            else:
                put(q, jnp.where(lanes >= rows, after, before))
            before = after
        return 0

    lax.fori_loop(0, DET, one, 0)


STRAIGHT = (((1,), (0,)), ((), ()))
CROSSED = (((1,), (1,)), ((), ()))


def filter_kernel(
    part_ref, noise_ref, out_ref, land, ext, filt, lags, t_hi, t_lo,
    own_sem, store_sem, send, recv, halo_send, halo_recv, back_send, back_recv,
):
    det, tm, y, z, x = place()
    total_tm = NY * NZ * NX
    mine = y * NX + x
    prior, later = (tm + total_tm - 1) % total_tm, (tm + 1) % total_tm

    def slot(k, sign):
        dy, dx = PEERS[k]
        return ((y + sign * dy + NY) % NY) * NX + (x + dx) % NX

    peers = [(det, tm_of((y + dy) % NY, z, (x + dx) % NX)) for dy, dx in PEERS]
    greet(peers + [(det, later), (det, prior)])
    own = pltpu.make_async_copy(part_ref.at[mine], land.at[NB - 1], own_sem)
    own.start()
    sends = []
    for k, peer in enumerate(peers):
        copy = remote(part_ref.at[slot(k, 1)], land.at[k], send.at[k], recv.at[k], peer)
        copy.start()
        sends.append(copy)
    toeplitz(noise_ref, lags, t_hi, t_lo)
    own.wait()
    total = land[NB - 1]
    for k in range(NB - 1):
        sends[k].wait_recv()
        total = total + land[k]
    ext[:, REACH : REACH + RUNS, :] = total
    to_prior = remote(
        ext.at[:, pl.ds(REACH, REACH), :], ext.at[:, pl.ds(REACH + RUNS, REACH), :],
        halo_send.at[0], halo_recv.at[0], (det, prior),
    )
    to_later = remote(
        ext.at[:, pl.ds(RUNS, REACH), :], ext.at[:, pl.ds(0, REACH), :], halo_send.at[1], halo_recv.at[1], (det, later)
    )
    to_prior.start()
    to_later.start()
    to_prior.wait_recv()
    to_later.wait_recv()
    first, last = tm == 0, tm == total_tm - 1

    def product(left, right, crossed):
        return lax.dot_general(left, right, CROSSED if crossed else STRAIGHT, preferred_element_type=jnp.float32)

    back, own_copies = [], []

    def back_copy(c, k, source):
        rows = pl.ds(c * SENT, SENT)
        return remote(filt.at[rows], out_ref.at[source, rows], back_send.at[k, c], back_recv.at[k, c], peers[k])

    def send_back(c):
        for k in range(NB - 1):
            copy = back_copy(c, k, mine)
            copy.start()
            back.append(copy)
        rows = pl.ds(c * SENT, SENT)
        copy = pltpu.make_async_copy(filt.at[rows], out_ref.at[mine, rows], store_sem.at[c])
        copy.start()
        own_copies.append(copy)

    for d in range(DET):
        line_all = jnp.concatenate(
            [
                jnp.where(first, 0.0, ext[d, :REACH]),
                ext[d, REACH : REACH + RUNS],
                jnp.where(last, 0.0, ext[d, REACH + RUNS :]),
            ],
            axis=0,
        )
        result = jnp.zeros((RUNS, LANE), jnp.float32)
        for m in range(2 * REACH + 1):
            window = line_all[m : m + RUNS]
            high = window.astype(jnp.bfloat16)
            low = (window - high.astype(jnp.float32)).astype(jnp.bfloat16)
            stack = jnp.concatenate([high, low], axis=0)
            q = REACH - m
            for index, crossed in [(q, False)] if q > 0 else [(-q, True)] if q < 0 else [(0, False), (REACH + 1, True)]:
                both = product(stack, t_hi[d, index], crossed)
                result += both[:RUNS] + both[RUNS:] + product(high, t_lo[d, index], crossed)
        filt[d] = result
        if d % SENT == SENT - 1:
            send_back(d // SENT)
    for copy in own_copies:
        copy.wait()
    for c in range(DET // SENT):
        for k, peer in enumerate(peers):
            back_copy(c, k, slot(k, -1)).wait_recv()
    for copy in sends + back + [to_prior, to_later]:
        copy.wait_send()


def filtered_of(partial, noise_coef):
    f32, bf = jnp.float32, jnp.bfloat16
    block = (DET, RUNS, LANE)
    matrices = (DET, REACH + 2, LANE, LANE)
    return pl.pallas_call(
        filter_kernel,
        out_shape=jax.ShapeDtypeStruct((NB, *block), f32),
        in_specs=[ANY, VM],
        out_specs=ANY,
        scratch_shapes=[
            pltpu.VMEM((NB, *block), f32),
            pltpu.VMEM((DET, RUNS + 2 * REACH, LANE), f32),
            pltpu.VMEM(block, f32),
            pltpu.VMEM((REACH + 1, DET, LANE), f32),
            pltpu.VMEM(matrices, bf),
            pltpu.VMEM(matrices, bf),
            DMA,
            DMA((DET // SENT,)),
            DMA((NB,)),
            DMA((NB,)),
            DMA((2,)),
            DMA((2,)),
            DMA((NB, DET // SENT)),
            DMA((NB, DET // SENT)),
        ],
        compiler_params=pltpu.CompilerParams(collective_id=1, has_side_effects=True, vmem_limit_bytes=GRANT),
        name="filter",
    )(partial, noise_coef)


CHUNKS = [(t, p) for t in range(TILE_DEV) for p in range(3)]
HALF_Z = NZ // 2
WIRE = jnp.bfloat16
OFFSETS = [4, 3, -3, 2, -2, 1, -1, 0]


def collect_kernel(
    acc_ref, out_ref, own, land_core, packet, land, land_last, land_own,
    own_sem, core_send, core_recv, ring_send, ring_recv, last_send, last_recv, hi_send, hi_recv,
):
    f32 = jnp.float32
    det, tm, y, z, x = place()
    core, hi = det % 2, det // 2
    partner, across = core_of(det), hi_of(det)
    right, left = tm_of(y, (z + 1) % NZ, x), tm_of(y, (z + NZ - 1) % NZ, x)
    neighbours = ((det, right), (det, left))
    loads = []
    for k, offset in enumerate(OFFSETS):
        copy = pltpu.make_async_copy(acc_ref.at[(z + offset + NZ) % NZ, :, :, :, core], own.at[k], own_sem.at[k])
        copy.start()
        loads.append(copy)
    greet([(partner, tm), (across, tm), *neighbours, (across, right), (across, left)])
    started = []

    def start(copy):
        copy.start()
        started.append(copy)

    for k, offset in enumerate(OFFSETS):
        start(
            remote(
                acc_ref.at[(z + offset + NZ) % NZ, :, :, :, 1 - core], land_core.at[k], core_send.at[k], core_recv.at[k],
                (partner, tm),
            )
        )

    def ring(direction, step, c):
        t, p = CHUNKS[c]
        sign = 1 if direction == 0 else -1
        k = OFFSETS.index(sign * (HALF_Z - step)) if step else 0
        return remote(
            packet.at[k, t, p], land.at[direction, step, t, p],
            ring_send.at[direction, step, c], ring_recv.at[direction, step, c], neighbours[direction],
        )

    def last_hop(direction, c, crossing):
        t, p = CHUNKS[c]
        k = OFFSETS.index(1 if direction == 0 else -1)
        goal = (right, left)[direction]
        return remote(
            packet.at[k, t, p, 1 - hi if crossing else hi], land_last.at[crossing, direction, t, p],
            last_send.at[crossing, direction, c], last_recv.at[crossing, direction, c],
            (across if crossing else det, goal),
        )

    def own_copy(t):
        return remote(packet.at[len(OFFSETS) - 1, t, :, 1 - hi], land_own.at[t], hi_send.at[t], hi_recv.at[t], (across, tm))

    def swapped(k):
        loads[k].wait()
        remote(acc_ref.at[0, :, :, :, 0], land_core.at[k], core_send.at[k], core_recv.at[k], (partner, tm)).wait_recv()

    swapped(0)
    for direction in (0, 1):
        for c, (t, p) in enumerate(CHUNKS):
            if t == direction:
                packet[0, t, p] = (own[0, t, p] + land_core[0, t, p]).astype(WIRE)
    for p in range(3):
        for direction in (0, 1):
            start(ring(direction, 0, direction * 3 + p))
    last = len(OFFSETS) - 1
    for step in range(1, HALF_Z):
        keys = [OFFSETS.index(HALF_Z - step), OFFSETS.index(step - HALF_Z)]
        for k in keys:
            swapped(k)
        for i in range(len(CHUNKS)):
            for direction in (0, 1):
                c = (i + 3 * (1 - direction)) % len(CHUNKS) if step == 1 else i
                t, p = CHUNKS[c]
                k = keys[direction]
                value = own[k, t, p] + land_core[k, t, p]
                if step > 1 or t == direction:
                    ring(direction, step - 1, c).wait_recv()
                    value = value + land[direction, step - 1, t, p].astype(f32)
                packet[k, t, p] = value.astype(WIRE)
                if step < HALF_Z - 1:
                    start(ring(direction, step, c))
                else:
                    start(last_hop(direction, c, 1))
                    start(last_hop(direction, c, 0))
        if step == 1:
            swapped(last)
            for t in range(TILE_DEV):
                value = own[last, t] + land_core[last, t]
                packet[last, t] = value.astype(WIRE)
                start(own_copy(t))
                own[last, t] = value
    for t in range(TILE_DEV):
        own_copy(t).wait_recv()
    for c, (t, p) in enumerate(CHUNKS):
        value = own[last, t, p, hi] + land_own[t, p].astype(f32)
        for crossing in (0, 1):
            for direction in (0, 1):
                last_hop(direction, c, crossing).wait_recv()
                value = value + land_last[crossing, direction, t, p].astype(f32)
        out_ref[t, p] = value
    for copy in started:
        copy.wait_send()


def collect(acc):
    f32 = jnp.float32
    half = (TILE_DEV, 3, 2, STRIP, PIX)
    quarter = (TILE_DEV, 3, STRIP, PIX)
    return pl.pallas_call(
        collect_kernel,
        out_shape=jax.ShapeDtypeStruct(quarter, f32),
        in_specs=[ANY],
        out_specs=VM,
        scratch_shapes=[
            pltpu.VMEM((NZ, *half), f32),
            pltpu.VMEM((NZ, *half), f32),
            pltpu.VMEM((NZ, *half), WIRE),
            pltpu.VMEM((2, HALF_Z - 1, *half), WIRE),
            pltpu.VMEM((2, 2, *quarter), WIRE),
            pltpu.VMEM(quarter, WIRE),
            DMA((NZ,)),
            DMA((NZ,)),
            DMA((NZ,)),
            DMA((2, HALF_Z - 1, 6)),
            DMA((2, HALF_Z - 1, 6)),
            DMA((2, 2, 6)),
            DMA((2, 2, 6)),
            DMA((2,)),
            DMA((2,)),
        ],
        compiler_params=pltpu.CompilerParams(collective_id=2, has_side_effects=True, vmem_limit_bytes=GRANT),
        name="collect",
    )(acc.reshape(NZ, TILE_DEV, 3, 2, 2, STRIP, PIX))


def body(
    sky_map, tile_home, piece_tiles, run_slot, hit_row, hit_col, frac_row, frac_col, angle, noise_coef
):
    tiles, all_floats, all_fracs, order = gather_all(
        tile_home, piece_tiles.reshape(1, LISTED), run_slot, hit_row, hit_col, frac_row, frac_col, angle, sky_map
    )
    partial, turns = forward(order, tiles.reshape(TILE_DEV * NZ, 3 * PIX, PIX), all_floats, all_fracs)
    filtered = filtered_of(partial, noise_coef)
    acc = backward(order, all_floats, all_fracs, turns, filtered)
    return collect(acc)


def solution(mesh):
    placed = (
        P("tm", None, "det", None),
        P(),
        P("det", "tm", None),
        P("det", "tm"),
        P("det", "tm"),
        P("det", "tm"),
        P("det", "tm"),
        P("det", "tm"),
        P("det", "tm"),
        P("det", None),
    )
    return jax.shard_map(
        body, mesh=mesh, in_specs=placed, out_specs=P("tm", None, "det", None), check_vma=False
    )
```

```python
import functools

import jax
import jax.numpy as jnp
from jax import lax
from jax.experimental import pallas as pl
from jax.experimental.pallas import tpu as pltpu
from jax.sharding import PartitionSpec as P

GRANT = 24 << 20
MESH = pl.DeviceIdType.MESH
NY, NZ, NX = 4, 8, 2
NB = NY * NX
DET, RUNS, LANE = 8, 16, 128
PIX = 128
STRIP = 32
N_STRIP = 4
LISTED = 32
TILE_DEV = 2
REACH = 8
UNROLL = 16
HALF = 16
SENT = 2
PIECE_RUNS = DET * RUNS
ALL_RUNS = NB * PIECE_RUNS
ANY = pl.BlockSpec(memory_space=pl.ANY)
VM = pl.BlockSpec(memory_space=pltpu.VMEM)
SM = pl.BlockSpec(memory_space=pltpu.SMEM)
DMA = pltpu.SemaphoreType.DMA
PEERS = [(dy, dx) for dy in range(NY) for dx in range(NX) if (dy, dx) != (0, 0)]


def place():
    det, tm = lax.axis_index("det"), lax.axis_index("tm")
    y, z, x = tm // (NZ * NX), (tm // NX) % NZ, tm % NX
    return det, tm, y, z, x


def tm_of(y, z, x):
    return (y * NZ + z) * NX + x


def core_of(det):
    return det + 1 - 2 * (det % 2)


def hi_of(det):
    return (det + 2) % 4


def greet(peers):
    barrier = pltpu.get_barrier_semaphore()
    for peer in peers:
        pl.semaphore_signal(barrier, inc=1, device_id=peer, device_id_type=MESH)
    pl.semaphore_wait(barrier, len(peers))


def remote(src, dst, send, recv, peer):
    return pltpu.make_async_remote_copy(
        src_ref=src, dst_ref=dst, send_sem=send, recv_sem=recv, device_id=peer, device_id_type=MESH
    )


def run_order(pos_ref, order_ref, y, x):
    f32, bf, i32 = jnp.float32, jnp.bfloat16, jnp.int32

    def iota(shape, dim):
        return lax.broadcasted_iota(i32, shape, dim)

    def whole(mask):
        return jnp.where(mask, 1.0, 0.0).astype(bf)

    def dot(left, right):
        return jnp.dot(left, right, preferred_element_type=f32)

    lanes, offset = iota((LANE, LANE), 1), iota((LANE, LANE), 0)
    spot = jnp.zeros((DET, LANE), f32)
    for slot in range(NB):
        spot += dot(pos_ref[slot].astype(bf), whole((offset < RUNS) & (lanes == offset + slot * RUNS)))
    pos = spot.astype(i32)
    here = (pos // (TILE_DEV * NX * NZ) == y) & ((pos // TILE_DEV) % NX == x)
    tile = ((pos // (TILE_DEV * NX)) % NZ) * TILE_DEV + pos % TILE_DEV
    kinds, square = (2 * TILE_DEV * NZ, LANE), (LANE, LANE)
    kind = jnp.where(here, tile, TILE_DEV * NZ)
    tile = tile.astype(f32)
    before, every = whole(iota(square, 0) < iota(square, 1)), jnp.ones(square, bf)
    marks, prior, total = [], [], jnp.zeros(kinds, f32)
    for d in range(DET):
        mark = whole(jnp.broadcast_to(kind[d : d + 1], kinds) == iota(kinds, 0))
        marks.append(mark.astype(f32))
        prior.append(dot(mark, before) + total)
        total += dot(mark, every)
    lower = whole(iota((kinds[0], kinds[0]), 1) < iota((kinds[0], kinds[0]), 0))
    coarse = jnp.floor(total * (1.0 / 32.0))
    base = 32.0 * dot(lower, coarse.astype(bf)) + dot(lower, (total - 32.0 * coarse).astype(bf))
    high_rows, low_rows = iota((DET, LANE), 0).astype(f32), iota(square, 0).astype(f32)
    lane = iota((DET, LANE), 1).astype(f32)
    found = jnp.zeros((3 * DET, LANE), f32)
    for d in range(DET):
        rank = jnp.sum(marks[d] * (prior[d] + base), axis=0, keepdims=True)
        high = jnp.floor(rank * (1.0 / LANE))
        low = rank - LANE * high
        at = jnp.broadcast_to(high, (DET, LANE)) == high_rows
        values = (jnp.broadcast_to(tile[d : d + 1], (DET, LANE)), jnp.full((DET, LANE), float(d), f32), lane)
        left = jnp.concatenate([jnp.where(at, v, 0.0) for v in values], axis=0).astype(bf)
        right = whole(jnp.broadcast_to(low, square) == low_rows)
        found += lax.dot_general(left, right, (((1,), (1,)), ((), ())), preferred_element_type=f32)
    entry = found[:DET] * ALL_RUNS + found[DET : 2 * DET] * LANE + found[2 * DET :]
    order_ref[:DET, :] = entry.astype(i32)
    others = total[TILE_DEV * NZ : TILE_DEV * NZ + 1]
    order_ref[DET:, :] = jnp.broadcast_to(ALL_RUNS - others, (DET, LANE)).astype(i32)


def pack_kernel(
    home_ref, piece_ref, slot_ref, row_ref, col_ref, low_ref, high_ref, angle_ref, q_ref, float_ref, half_ref
):
    for r in range(RUNS):
        at = slice(r * LANE, (r + 1) * LANE)
        for part, value in enumerate(((row_ref[:, at] * PIX + col_ref[:, at]).astype(jnp.float32), angle_ref[:, at])):
            float_ref[part * PIECE_RUNS + r * DET : part * PIECE_RUNS + (r + 1) * DET] = value
        for part, source in enumerate((low_ref, high_ref)):
            half_ref[part * PIECE_RUNS + r * DET : part * PIECE_RUNS + (r + 1) * DET] = source[:, at]
    slots = slot_ref[...]
    position = jnp.zeros(slots.shape, jnp.float32)
    for s in range(LISTED):
        position = jnp.where(slots == s, home_ref[piece_ref[0, s]].astype(jnp.float32), position)
    float_ref[2 * PIECE_RUNS :] = jnp.concatenate(
        [position, jnp.zeros((DET, LANE - RUNS), jnp.float32)], axis=1
    )
    half_ref[2 * PIECE_RUNS :] = q_ref[...]


def packed(tile_home, piece_list, run_slot, hit_row, hit_col, frac_row, frac_col, angle, quarter):
    return pl.pallas_call(
        pack_kernel,
        out_shape=(
            jax.ShapeDtypeStruct((2 * PIECE_RUNS + DET, LANE), jnp.float32),
            jax.ShapeDtypeStruct((2 * PIECE_RUNS + quarter.shape[0], LANE), jnp.bfloat16),
        ),
        in_specs=[SM, SM] + [VM] * 7,
        out_specs=(VM,) * 2,
        name="pack",
    )(tile_home, piece_list, run_slot, hit_row, hit_col, frac_row, frac_col, angle, quarter)


def gather_kernel(
    float_ref, half_ref,
    tiles_ref, fo_ref, wo_ref, order_ref,
    pos_all, store_sem,
    pos_send, pos_recv, block_send, block_recv, strip_send, strip_recv, core_send, core_recv, hi_send, hi_recv,
):
    det, tm, y, z, x = place()
    partner, across = core_of(det), hi_of(det)
    ahead, behind = (y + 1) % NY, (y + NY - 1) % NY
    facing = (y + NY // 2) % NY
    other = 1 - x
    up, down, side = (det, tm_of(ahead, z, x)), (det, tm_of(behind, z, x)), (det, tm_of(y, z, other))
    far = [(det, tm_of((y + dy) % NY, z, (x + dx) % NX)) for dy, dx in PEERS]

    def along(direction, jump):
        return (det, tm_of(y, (z + jump) % NZ if direction == 0 else (z + NZ - jump) % NZ, x))

    f_ref, p_ref = float_ref.at[pl.ds(0, 2 * PIECE_RUNS)], float_ref.at[pl.ds(2 * PIECE_RUNS, DET)]
    w_ref = half_ref.at[pl.ds(0, 2 * PIECE_RUNS)]
    q_ref = half_ref.at[pl.ds(2 * PIECE_RUNS, TILE_DEV * 3 * STRIP)]

    def strip(slot, d):
        return tiles_ref.at[slot, d]

    def block(slot, part):
        return fo_ref.at[slot, pl.ds(part * PIECE_RUNS, PIECE_RUNS)] if part < 2 else wo_ref.at[slot]

    def own_block(part):
        return float_ref.at[pl.ds(part * PIECE_RUNS, PIECE_RUNS)] if part < 2 else w_ref

    mine = y * NX + x
    greet([along(d, j) for d in (0, 1) for j in (1, 2)] + [(partner, tm), (across, tm)] + far)

    started = []

    def start(copy):
        copy.start()
        started.append(copy)

    start(remote(q_ref, strip(z, det), hi_send, hi_recv, (across, tm)))

    def send_block(link, slot, part, peer, own=False):
        start(
            remote(
                own_block(part) if own else block(slot, part), block(slot, part),
                block_send.at[link, part], block_recv.at[link, part], peer,
            )
        )

    def wait_block(link, slot, part):
        remote(own_block(part), block(slot, part), block_send.at[link, part], block_recv.at[link, part], side).wait_recv()

    owner = (det, across)

    def source_slot(direction, distance):
        return (z + NZ - distance) % NZ if direction == 0 else (z + distance) % NZ

    def send_strip(half, direction, distance):
        slot = z if distance < 3 else source_slot(direction, 2)
        here = strip(slot, owner[half])
        start(
            remote(
                q_ref if half == 0 and distance < 3 else here, here,
                strip_send.at[half, direction, distance - 1], strip_recv.at[half, direction, distance - 1],
                along(direction, 2 - distance % 2),
            )
        )

    def reach(half, direction):
        return NZ // 2 if half == direction else NZ // 2 - 1

    def to_partner(half, index, slot):
        here = strip(slot, owner[half])
        start(
            remote(
                q_ref if half == 0 and index == 0 else here, here, core_send.at[half, index], core_recv.at[half, index],
                (partner, tm),
            )
        )

    def take_strip(half, distance):
        for direction in (0, 1):
            if distance <= reach(half, direction):
                slot = source_slot(direction, distance)
                remote(
                    q_ref, strip(slot, owner[half]),
                    strip_send.at[half, direction, distance - 1], strip_recv.at[half, direction, distance - 1], side,
                ).wait_recv()
                if distance == 2:
                    if reach(half, direction) == 4:
                        send_strip(half, direction, 4)
                    send_strip(half, direction, 3)
                to_partner(half, direction * NZ // 2 + distance, slot)

    def first_strips(half):
        for distance in (2, 1):
            for direction in (0, 1):
                send_strip(half, direction, distance)
        to_partner(half, 0, z)

    first_strips(0)
    for k, peer in enumerate(far):
        start(remote(p_ref, pos_all.at[mine], pos_send.at[k], pos_recv.at[k], peer))
    for part in range(3):
        send_block(1, mine, part, up, True)
        send_block(2, mine, part, down, True)
        send_block(0, mine, part, side, True)
    stores = []
    for i, (src, dst) in enumerate(
        ((q_ref, strip(z, det)), (f_ref, fo_ref.at[mine]), (w_ref, wo_ref.at[mine]), (p_ref, pos_all.at[mine]))
    ):
        copy = pltpu.make_async_copy(src, dst, store_sem.at[i])
        copy.start()
        stores.append(copy)

    slot_of = {1: behind * NX + x, 2: ahead * NX + x, 0: y * NX + other, 5: facing * NX + x, 6: facing * NX + other,
               3: behind * NX + other, 4: ahead * NX + other}

    def near(part):
        for link in (1, 2, 0):
            wait_block(link, slot_of[link], part)
            if link == 1 and part != 1:
                send_block(5, slot_of[1], part, up)
            if link == 2 and part == 1:
                send_block(5, slot_of[2], part, down)
            if link == 0:
                send_block(3, slot_of[0], part, up)
                send_block(4, slot_of[0], part, down)

    def opposite(part):
        wait_block(5, slot_of[5], part)
        send_block(6, slot_of[5], part, side)

    near(0)
    remote(q_ref, strip(z, across), hi_send, hi_recv, (across, tm)).wait_recv()
    first_strips(1)
    take_strip(0, 2)
    near(1)
    near(2)
    take_strip(0, 1)
    opposite(0)
    take_strip(1, 2)
    opposite(1)
    opposite(2)
    take_strip(1, 1)
    take_strip(0, 3)
    take_strip(0, 4)

    stores[3].wait()
    for k, peer in enumerate(far):
        remote(p_ref, pos_all.at[mine], pos_send.at[k], pos_recv.at[k], peer).wait_recv()
    run_order(pos_all, order_ref, y, x)

    take_strip(1, 3)
    take_strip(1, 4)
    for part in range(3):
        for link in (3, 4, 6):
            wait_block(link, slot_of[link], part)
    theirs = (partner, hi_of(partner))
    for half in (0, 1):
        places = [(0, z)]
        for direction in (0, 1):
            for distance in range(1, reach(half, direction) + 1):
                places.append((direction * NZ // 2 + distance, source_slot(direction, distance)))
        for index, slot in places:
            remote(
                q_ref, strip(slot, theirs[half]), core_send.at[half, index], core_recv.at[half, index], (partner, tm)
            ).wait_recv()
    for copy in stores[:3]:
        copy.wait()
    for copy in started:
        copy.wait_send()


def gather_all(floats, halves):
    bf, f32, i32 = jnp.bfloat16, jnp.float32, jnp.int32
    samples = (2 * PIECE_RUNS, LANE)
    return pl.pallas_call(
        gather_kernel,
        out_shape=(
            jax.ShapeDtypeStruct((NZ, N_STRIP, TILE_DEV * 3 * STRIP, PIX), bf),
            jax.ShapeDtypeStruct((NB, *samples), f32),
            jax.ShapeDtypeStruct((NB, *samples), bf),
            jax.ShapeDtypeStruct((2 * DET, LANE), i32),
        ),
        in_specs=[ANY] * 2,
        out_specs=(ANY, ANY, ANY, VM),
        scratch_shapes=[
            pltpu.VMEM((NB, DET, LANE), f32),
            DMA((4,)),
            DMA((NB,)),
            DMA((NB,)),
            DMA((7, 3)),
            DMA((7, 3)),
            DMA((2, 2, NZ // 2)),
            DMA((2, 2, NZ // 2)),
            DMA((2, NZ + 1)),
            DMA((2, NZ + 1)),
            DMA,
            DMA,
        ],
        compiler_params=pltpu.CompilerParams(collective_id=0, has_side_effects=True, vmem_limit_bytes=GRANT),
        name="gather_all",
    )(floats, halves)


def sin_cos(v):
    quarter = jnp.round(v * 0.6366197723675814)
    u = v - quarter * 1.5703125
    u = u - quarter * 4.837512969970703e-4
    u = u - quarter * 7.549789948768648e-8
    u2 = u * u
    s = u + u * u2 * (-1.6666654611e-1 + u2 * (8.3321608736e-3 + u2 * -1.9515295891e-4))
    c = 1.0 - 0.5 * u2 + u2 * u2 * (4.166664568298827e-2 + u2 * (-1.388731625493765e-3 + u2 * 2.443315711809948e-5))
    q = quarter.astype(jnp.int32) & 3
    odd = (q & 1) == 1
    sin = jnp.where(odd, c, s)
    cos = jnp.where(odd, s, c)
    sin = jnp.where(q >= 2, -sin, sin)
    cos = jnp.where((q == 1) | (q == 2), -cos, cos)
    return sin, cos


def low_of(high):
    return (1.0 - high).astype(jnp.bfloat16).astype(jnp.float32)


def run_of(entry):
    run = entry & (ALL_RUNS - 1)
    return entry >> 10, (run >> 4) & (NB - 1), run >> 7, run & (RUNS - 1)


def spread(index, low, high, rows):
    bf = jnp.bfloat16
    wide = [jnp.broadcast_to(v, (HALF, LANE)).astype(bf) for v in (index, index + 1.0, low, high)]
    zero = jnp.zeros((HALF, LANE), bf)
    parts = []
    for b in range(PIX // HALF):
        row = rows[b * HALF : (b + 1) * HALF]
        parts.append(jnp.where(row == wide[0], wide[2], jnp.where(row == wide[1], wide[3], zero)))
    return jnp.concatenate(parts, axis=0)


def forward_kernel(list_ref, tiles_ref, f_ref, w_ref, sig_ref, cs_ref, hit_ref, frac_ref):
    def prepare(z, _):
        code = f_ref[z, :PIECE_RUNS].reshape(RUNS, DET, LANE)
        row = jnp.floor(code * (1.0 / PIX))
        hit_ref[z, 0] = row
        hit_ref[z, 1] = code - row * PIX
        sin, cos = sin_cos(2.0 * f_ref[z, PIECE_RUNS:].reshape(RUNS, DET, LANE))
        cs_ref[z, 0] = cos
        cs_ref[z, 1] = sin
        fracs = w_ref[z].astype(jnp.float32)
        frac_ref[z] = fracs.reshape(2, RUNS, DET, LANE)
        sig_ref[z] = jnp.zeros_like(sig_ref[z])
        return 0

    lax.fori_loop(0, NB, prepare, 0)
    count = list_ref[DET, 0]
    rows = lax.broadcasted_iota(jnp.int32, (PIX, LANE), 0).astype(jnp.float32).astype(jnp.bfloat16)

    def body(step, _):
        for u in range(UNROLL):
            n = step * UNROLL + u
            tile, z, d, r = run_of(list_ref[n >> 7, n & (LANE - 1)])
            at = (r, pl.ds(d, 1), slice(None))
            col_high = frac_ref[z, 1, *at]
            row_high = frac_ref[z, 0, *at]
            col_weight = spread(hit_ref[z, 1, *at], low_of(col_high), col_high, rows)
            row_weight = spread(hit_ref[z, 0, *at], low_of(row_high), row_high, rows).astype(jnp.float32)
            rows_of_tile = jnp.concatenate([tiles_ref[tile // TILE_DEV, k, tile % TILE_DEV] for k in range(N_STRIP)], axis=0)
            partial = jnp.dot(rows_of_tile, col_weight, preferred_element_type=jnp.float32)
            value = []
            for p in range(3):
                terms = [
                    partial[(k * 3 + p) * STRIP : (k * 3 + p + 1) * STRIP] * row_weight[k * STRIP : (k + 1) * STRIP]
                    for k in range(N_STRIP)
                ]
                value.append(jnp.sum(sum(terms[1:], terms[0]), axis=0, keepdims=True))
            total = value[0] + cs_ref[z, 0, *at] * value[1] + cs_ref[z, 1, *at] * value[2]
            sig_ref[z, d, pl.ds(r, 1), :] = jnp.where(n < count, total, 0.0)
        return 0

    lax.fori_loop(0, (count + UNROLL - 1) // UNROLL, body, 0)


def forward(order, tiles, floats, fracs):
    f32 = jnp.float32
    block = (NB, DET, RUNS, LANE)
    pair = (NB, 2, RUNS, DET, LANE)
    return pl.pallas_call(
        forward_kernel,
        out_shape=(jax.ShapeDtypeStruct(block, f32), jax.ShapeDtypeStruct(pair, f32)),
        in_specs=[SM, VM, VM, VM],
        out_specs=(VM, VM),
        scratch_shapes=[pltpu.VMEM(pair, f32), pltpu.VMEM(pair, f32)],
        compiler_params=pltpu.CompilerParams(vmem_limit_bytes=GRANT),
        name="forward",
    )(order, tiles, floats, fracs)


def backward_kernel(list_ref, f_ref, w_ref, cs_ref, filt_ref, acc_ref, hit_ref, frac_ref):
    def prepare(z, _):
        code = f_ref[z, :PIECE_RUNS].reshape(RUNS, DET, LANE)
        row = jnp.floor(code * (1.0 / PIX))
        hit_ref[z, 0] = row
        hit_ref[z, 1] = code - row * PIX
        fracs = w_ref[z].astype(jnp.float32)
        frac_ref[z] = fracs.reshape(2, RUNS, DET, LANE)
        return 0

    lax.fori_loop(0, NB, prepare, 0)

    def clear(t, _):
        acc_ref[t] = jnp.zeros_like(acc_ref[t])
        return 0

    lax.fori_loop(0, TILE_DEV * NZ, clear, 0)
    count = list_ref[DET, 0]
    rows = lax.broadcasted_iota(jnp.int32, (PIX, LANE), 0).astype(jnp.float32).astype(jnp.bfloat16)

    def body(step, _):
        for u in range(UNROLL):
            k = step * UNROLL + u
            tile, z, d, r = run_of(list_ref[k >> 7, k & (LANE - 1)])
            at = (r, pl.ds(d, 1), slice(None))
            col_high = frac_ref[z, 1, *at]
            row_high = frac_ref[z, 0, *at]
            row_low = low_of(row_high)
            col_weight = spread(hit_ref[z, 1, *at], low_of(col_high), col_high, rows)
            filt = jnp.where(k < count, filt_ref[z, d, pl.ds(r, 1), :], 0.0)
            hit = hit_ref[z, 0, *at]
            parts = []
            for p in range(3):
                scaled = filt if p == 0 else cs_ref[z, p - 1, *at] * filt
                parts.append(spread(hit, scaled * row_low, scaled * row_high, rows))
            weighted = jnp.concatenate(parts, axis=0)
            acc_ref[tile] += lax.dot_general(
                weighted, col_weight, (((1,), (1,)), ((), ())), preferred_element_type=jnp.float32
            )
        return 0

    lax.fori_loop(0, (count + UNROLL - 1) // UNROLL, body, 0)


def backward(order, floats, fracs, turns, filtered):
    f32 = jnp.float32
    pair = (NB, 2, RUNS, DET, LANE)
    return pl.pallas_call(
        backward_kernel,
        out_shape=jax.ShapeDtypeStruct((TILE_DEV * NZ, 3 * PIX, PIX), f32),
        in_specs=[SM, VM, VM, VM, VM],
        out_specs=VM,
        scratch_shapes=[pltpu.VMEM(pair, f32), pltpu.VMEM(pair, f32)],
        compiler_params=pltpu.CompilerParams(vmem_limit_bytes=GRANT),
        name="backward",
    )(order, floats, fracs, turns, filtered)


def toeplitz(noise_ref, line_ref, hi_ref, lo_ref):
    square = (LANE, LANE)
    lanes = lax.broadcasted_iota(jnp.int32, square, 1)
    rows = lax.broadcasted_iota(jnp.int32, square, 0)
    first = lax.broadcasted_iota(jnp.int32, (DET, LANE), 1) == 0
    for q in range(REACH):
        lags = noise_ref[:, q * LANE : (q + 1) * LANE]
        line_ref[q] = jnp.where(first, lags + 1.0, lags) if q == 0 else lags
    line_ref[REACH] = jnp.where(first, jnp.broadcast_to(noise_ref[:, REACH * LANE :], (DET, LANE)), 0.0)

    def one(d, _):
        def put(q, matrix):
            high = matrix.astype(jnp.bfloat16)
            hi_ref[d, q] = high
            lo_ref[d, q] = (matrix - high.astype(jnp.float32)).astype(jnp.bfloat16)

        before = None
        for q in range(REACH + 1):
            lags = line_ref[q, pl.ds(d, 1), :]
            after = pltpu.roll(jnp.broadcast_to(lags, square), 0, 1, stride=1, stride_axis=0)
            if q == 0:
                put(0, jnp.where(lanes >= rows, after, 0.0))
                put(REACH + 1, jnp.where(lanes > rows, after, 0.0))
            else:
                put(q, jnp.where(lanes >= rows, after, before))
            before = after
        return 0

    lax.fori_loop(0, DET, one, 0)


STRAIGHT = (((1,), (0,)), ((), ()))
CROSSED = (((1,), (1,)), ((), ()))


def filter_kernel(
    part_ref, noise_ref, out_ref, land, ext, filt, lags, t_hi, t_lo,
    store_sem, send, recv, halo_send, halo_recv, back_send, back_recv,
):
    det, tm, y, z, x = place()
    total_tm = NY * NZ * NX
    mine = y * NX + x
    prior, later = (tm + total_tm - 1) % total_tm, (tm + 1) % total_tm

    def slot(k, sign):
        dy, dx = PEERS[k]
        return ((y + sign * dy + NY) % NY) * NX + (x + dx) % NX

    peers = [(det, tm_of((y + dy) % NY, z, (x + dx) % NX)) for dy, dx in PEERS]
    greet(peers + [(det, later), (det, prior)])
    sends = []
    for k, peer in enumerate(peers):
        copy = remote(part_ref.at[slot(k, 1)], land.at[k], send.at[k], recv.at[k], peer)
        copy.start()
        sends.append(copy)
    toeplitz(noise_ref, lags, t_hi, t_lo)
    total = part_ref[mine]
    for k in range(NB - 1):
        sends[k].wait_recv()
        total = total + land[k]
    ext[:, REACH : REACH + RUNS, :] = total
    to_prior = remote(
        ext.at[:, pl.ds(REACH, REACH), :], ext.at[:, pl.ds(REACH + RUNS, REACH), :],
        halo_send.at[0], halo_recv.at[0], (det, prior),
    )
    to_later = remote(
        ext.at[:, pl.ds(RUNS, REACH), :], ext.at[:, pl.ds(0, REACH), :], halo_send.at[1], halo_recv.at[1], (det, later)
    )
    to_prior.start()
    to_later.start()
    to_prior.wait_recv()
    to_later.wait_recv()
    first, last = tm == 0, tm == total_tm - 1

    def product(left, right, crossed):
        return lax.dot_general(left, right, CROSSED if crossed else STRAIGHT, preferred_element_type=jnp.float32)

    back, own_copies = [], []

    def back_copy(c, k, source):
        rows = pl.ds(c * SENT, SENT)
        return remote(filt.at[rows], out_ref.at[source, rows], back_send.at[k, c], back_recv.at[k, c], peers[k])

    def send_back(c):
        for k in range(NB - 1):
            copy = back_copy(c, k, mine)
            copy.start()
            back.append(copy)
        rows = pl.ds(c * SENT, SENT)
        copy = pltpu.make_async_copy(filt.at[rows], out_ref.at[mine, rows], store_sem.at[c])
        copy.start()
        own_copies.append(copy)

    for c in range(DET // SENT):
        dets = range(c * SENT, (c + 1) * SENT)
        lines = [
            jnp.concatenate(
                [
                    jnp.where(first, 0.0, ext[d, :REACH]),
                    ext[d, REACH : REACH + RUNS],
                    jnp.where(last, 0.0, ext[d, REACH + RUNS :]),
                ],
                axis=0,
            )
            for d in dets
        ]
        full = [jnp.zeros((2 * RUNS, LANE), jnp.float32) for d in dets]
        fine = [jnp.zeros((RUNS, LANE), jnp.float32) for d in dets]
        for m in range(2 * REACH + 1):
            q = REACH - m
            for i, d in enumerate(dets):
                window = lines[i][m : m + RUNS]
                high = window.astype(jnp.bfloat16)
                low = (window - high.astype(jnp.float32)).astype(jnp.bfloat16)
                stack = jnp.concatenate([high, low], axis=0)
                for index, crossed in [(q, False)] if q > 0 else [(-q, True)] if q < 0 else [(0, False), (REACH + 1, True)]:
                    full[i] += product(stack, t_hi[d, index], crossed)
                    fine[i] += product(high, t_lo[d, index], crossed)
        for i, d in enumerate(dets):
            filt[d] = full[i][:RUNS] + full[i][RUNS:] + fine[i]
        send_back(c)
    for copy in own_copies:
        copy.wait()
    for c in range(DET // SENT):
        for k, peer in enumerate(peers):
            back_copy(c, k, slot(k, -1)).wait_recv()
    for copy in sends + back + [to_prior, to_later]:
        copy.wait_send()


def filtered_of(partial, noise_coef):
    f32, bf = jnp.float32, jnp.bfloat16
    block = (DET, RUNS, LANE)
    matrices = (DET, REACH + 2, LANE, LANE)
    return pl.pallas_call(
        filter_kernel,
        out_shape=jax.ShapeDtypeStruct((NB, *block), f32),
        in_specs=[VM, VM],
        out_specs=ANY,
        scratch_shapes=[
            pltpu.VMEM((NB - 1, *block), f32),
            pltpu.VMEM((DET, RUNS + 2 * REACH, LANE), f32),
            pltpu.VMEM(block, f32),
            pltpu.VMEM((REACH + 1, DET, LANE), f32),
            pltpu.VMEM(matrices, bf),
            pltpu.VMEM(matrices, bf),
            DMA((DET // SENT,)),
            DMA((NB,)),
            DMA((NB,)),
            DMA((2,)),
            DMA((2,)),
            DMA((NB, DET // SENT)),
            DMA((NB, DET // SENT)),
        ],
        compiler_params=pltpu.CompilerParams(collective_id=1, has_side_effects=True, vmem_limit_bytes=GRANT),
        name="filter",
    )(partial, noise_coef)


CHUNKS = [(t, p) for t in range(TILE_DEV) for p in range(3)]
HALF_Z = NZ // 2
WIRE = jnp.bfloat16
OFFSETS = [4, 3, -3, 2, -2, 1, -1, 0]


def collect_kernel(
    acc_ref, out_ref, land_core, packet, land, land_last, land_own,
    core_send, core_recv, ring_send, ring_recv, last_send, last_recv, hi_send, hi_recv,
):
    f32 = jnp.float32
    det, tm, y, z, x = place()
    core, hi = det % 2, det // 2
    partner, across = core_of(det), hi_of(det)
    right, left = tm_of(y, (z + 1) % NZ, x), tm_of(y, (z + NZ - 1) % NZ, x)
    neighbours = ((det, right), (det, left))
    greet([(partner, tm), (across, tm), *neighbours, (across, right), (across, left)])
    started = []

    def start(copy):
        copy.start()
        started.append(copy)

    for k, offset in enumerate(OFFSETS):
        start(
            remote(
                acc_ref.at[(z + offset + NZ) % NZ, :, :, :, 1 - core], land_core.at[k], core_send.at[k], core_recv.at[k],
                (partner, tm),
            )
        )

    def ring(direction, step, c):
        t, p = CHUNKS[c]
        sign = 1 if direction == 0 else -1
        k = OFFSETS.index(sign * (HALF_Z - step)) if step else 0
        return remote(
            packet.at[k, t, p], land.at[direction, step, t, p],
            ring_send.at[direction, step, c], ring_recv.at[direction, step, c], neighbours[direction],
        )

    def last_hop(direction, c, crossing):
        t, p = CHUNKS[c]
        k = OFFSETS.index(1 if direction == 0 else -1)
        goal = (right, left)[direction]
        return remote(
            packet.at[k, t, p, 1 - hi if crossing else hi], land_last.at[crossing, direction, t, p],
            last_send.at[crossing, direction, c], last_recv.at[crossing, direction, c],
            (across if crossing else det, goal),
        )

    def own_copy(t):
        return remote(packet.at[len(OFFSETS) - 1, t, :, 1 - hi], land_own.at[t], hi_send.at[t], hi_recv.at[t], (across, tm))

    def own(k, t, p):
        return acc_ref[(z + OFFSETS[k] + NZ) % NZ, t, p, :, core]

    def swapped(k):
        remote(acc_ref.at[0, :, :, :, 0], land_core.at[k], core_send.at[k], core_recv.at[k], (partner, tm)).wait_recv()

    swapped(0)
    for direction in (0, 1):
        for c, (t, p) in enumerate(CHUNKS):
            if t == direction:
                packet[0, t, p] = (own(0, t, p) + land_core[0, t, p]).astype(WIRE)
    for p in range(3):
        for direction in (0, 1):
            start(ring(direction, 0, direction * 3 + p))
    last = len(OFFSETS) - 1
    for step in range(1, HALF_Z):
        keys = [OFFSETS.index(HALF_Z - step), OFFSETS.index(step - HALF_Z)]
        for k in keys:
            swapped(k)
        for i in range(len(CHUNKS)):
            for direction in (0, 1):
                c = (i + 3 * (1 - direction)) % len(CHUNKS) if step == 1 else i
                t, p = CHUNKS[c]
                k = keys[direction]
                value = own(k, t, p) + land_core[k, t, p]
                if step > 1 or t == direction:
                    ring(direction, step - 1, c).wait_recv()
                    value = value + land[direction, step - 1, t, p].astype(f32)
                packet[k, t, p] = value.astype(WIRE)
                if step < HALF_Z - 1:
                    start(ring(direction, step, c))
                else:
                    start(last_hop(direction, c, 1))
                    start(last_hop(direction, c, 0))
        if step == 1:
            swapped(last)
            for t in range(TILE_DEV):
                for p in range(3):
                    value = own(last, t, p) + land_core[last, t, p]
                    packet[last, t, p] = value.astype(WIRE)
                    land_core[last, t, p] = value
                start(own_copy(t))
    for t in range(TILE_DEV):
        own_copy(t).wait_recv()
    for c, (t, p) in enumerate(CHUNKS):
        value = land_core[last, t, p, hi] + land_own[t, p].astype(f32)
        for crossing in (0, 1):
            for direction in (0, 1):
                last_hop(direction, c, crossing).wait_recv()
                value = value + land_last[crossing, direction, t, p].astype(f32)
        out_ref[t, p] = value
    for copy in started:
        copy.wait_send()


def collect(acc):
    f32 = jnp.float32
    half = (TILE_DEV, 3, 2, STRIP, PIX)
    quarter = (TILE_DEV, 3, STRIP, PIX)
    return pl.pallas_call(
        collect_kernel,
        out_shape=jax.ShapeDtypeStruct(quarter, f32),
        in_specs=[VM],
        out_specs=VM,
        scratch_shapes=[
            pltpu.VMEM((NZ, *half), f32),
            pltpu.VMEM((NZ, *half), WIRE),
            pltpu.VMEM((2, HALF_Z - 1, *half), WIRE),
            pltpu.VMEM((2, 2, *quarter), WIRE),
            pltpu.VMEM(quarter, WIRE),
            DMA((NZ,)),
            DMA((NZ,)),
            DMA((2, HALF_Z - 1, 6)),
            DMA((2, HALF_Z - 1, 6)),
            DMA((2, 2, 6)),
            DMA((2, 2, 6)),
            DMA((2,)),
            DMA((2,)),
        ],
        compiler_params=pltpu.CompilerParams(collective_id=2, has_side_effects=True, vmem_limit_bytes=GRANT),
        name="collect",
    )(acc.reshape(NZ, TILE_DEV, 3, 2, 2, STRIP, PIX))


def body(
    sky_map, tile_home, piece_tiles, run_slot, hit_row, hit_col, frac_row, frac_col, angle, noise_coef
):
    floats, halves = packed(
        tile_home, piece_tiles.reshape(1, LISTED), run_slot, hit_row, hit_col, frac_row, frac_col, angle,
        sky_map.reshape(TILE_DEV * 3 * STRIP, PIX),
    )
    tiles, all_floats, all_fracs, order = gather_all(floats, halves)
    partial, turns = forward(
        order, tiles.reshape(NZ, N_STRIP, TILE_DEV, 3 * STRIP, PIX), all_floats, all_fracs
    )
    filtered = filtered_of(partial, noise_coef)
    acc = backward(order, all_floats, all_fracs, turns, filtered)
    return collect(acc)


def solution(mesh):
    placed = (
        P("tm", None, "det", None),
        P(),
        P("det", "tm", None),
        P("det", "tm"),
        P("det", "tm"),
        P("det", "tm"),
        P("det", "tm"),
        P("det", "tm"),
        P("det", "tm"),
        P("det", None),
    )
    return jax.shard_map(
        body, mesh=mesh, in_specs=placed, out_specs=P("tm", None, "det", None), check_vma=False
    )
```

```python
import functools

import jax
import jax.numpy as jnp
from jax import lax
from jax.experimental import pallas as pl
from jax.experimental.pallas import tpu as pltpu
from jax.sharding import PartitionSpec as P

GRANT = 24 << 20
MESH = pl.DeviceIdType.MESH
NY, NZ, NX = 4, 8, 2
NB = NY * NX
DET, RUNS, LANE = 8, 16, 128
PIX = 128
STRIP = 32
N_STRIP = 4
LISTED = 32
TILE_DEV = 2
REACH = 8
UNROLL = 16
HALF = 16
SENT = 2
PIECE_RUNS = DET * RUNS
ALL_RUNS = NB * PIECE_RUNS
ANY = pl.BlockSpec(memory_space=pl.ANY)
VM = pl.BlockSpec(memory_space=pltpu.VMEM)
SM = pl.BlockSpec(memory_space=pltpu.SMEM)
DMA = pltpu.SemaphoreType.DMA
PEERS = [(dy, dx) for dy in range(NY) for dx in range(NX) if (dy, dx) != (0, 0)]


def place():
    det, tm = lax.axis_index("det"), lax.axis_index("tm")
    y, z, x = tm // (NZ * NX), (tm // NX) % NZ, tm % NX
    return det, tm, y, z, x


def tm_of(y, z, x):
    return (y * NZ + z) * NX + x


def core_of(det):
    return det + 1 - 2 * (det % 2)


def hi_of(det):
    return (det + 2) % 4


def greet(peers):
    barrier = pltpu.get_barrier_semaphore()
    for peer in peers:
        pl.semaphore_signal(barrier, inc=1, device_id=peer, device_id_type=MESH)
    pl.semaphore_wait(barrier, len(peers))


def remote(src, dst, send, recv, peer):
    return pltpu.make_async_remote_copy(
        src_ref=src, dst_ref=dst, send_sem=send, recv_sem=recv, device_id=peer, device_id_type=MESH
    )


def run_order(pos_ref, order_ref, y, x):
    f32, bf, i32 = jnp.float32, jnp.bfloat16, jnp.int32

    def iota(shape, dim):
        return lax.broadcasted_iota(i32, shape, dim)

    def whole(mask):
        return jnp.where(mask, 1.0, 0.0).astype(bf)

    def dot(left, right):
        return jnp.dot(left, right, preferred_element_type=f32)

    lanes, offset = iota((LANE, LANE), 1), iota((LANE, LANE), 0)
    spot = jnp.zeros((DET, LANE), f32)
    for slot in range(NB):
        spot += dot(pos_ref[slot].astype(bf), whole((offset < RUNS) & (lanes == offset + slot * RUNS)))
    pos = spot.astype(i32)
    here = (pos // (TILE_DEV * NX * NZ) == y) & ((pos // TILE_DEV) % NX == x)
    tile = ((pos // (TILE_DEV * NX)) % NZ) * TILE_DEV + pos % TILE_DEV
    kinds, square = (2 * TILE_DEV * NZ, LANE), (LANE, LANE)
    kind = jnp.where(here, tile, TILE_DEV * NZ)
    tile = tile.astype(f32)
    before, every = whole(iota(square, 0) < iota(square, 1)), jnp.ones(square, bf)
    marks, prior, total = [], [], jnp.zeros(kinds, f32)
    for d in range(DET):
        mark = whole(jnp.broadcast_to(kind[d : d + 1], kinds) == iota(kinds, 0))
        marks.append(mark.astype(f32))
        prior.append(dot(mark, before) + total)
        total += dot(mark, every)
    lower = whole(iota((kinds[0], kinds[0]), 1) < iota((kinds[0], kinds[0]), 0))
    coarse = jnp.floor(total * (1.0 / 32.0))
    base = 32.0 * dot(lower, coarse.astype(bf)) + dot(lower, (total - 32.0 * coarse).astype(bf))
    high_rows, low_rows = iota((DET, LANE), 0).astype(f32), iota(square, 0).astype(f32)
    lane = iota((DET, LANE), 1).astype(f32)
    found = jnp.zeros((3 * DET, LANE), f32)
    for d in range(DET):
        rank = jnp.sum(marks[d] * (prior[d] + base), axis=0, keepdims=True)
        high = jnp.floor(rank * (1.0 / LANE))
        low = rank - LANE * high
        at = jnp.broadcast_to(high, (DET, LANE)) == high_rows
        values = (jnp.broadcast_to(tile[d : d + 1], (DET, LANE)), jnp.full((DET, LANE), float(d), f32), lane)
        left = jnp.concatenate([jnp.where(at, v, 0.0) for v in values], axis=0).astype(bf)
        right = whole(jnp.broadcast_to(low, square) == low_rows)
        found += lax.dot_general(left, right, (((1,), (1,)), ((), ())), preferred_element_type=f32)
    entry = found[:DET] * ALL_RUNS + found[DET : 2 * DET] * LANE + found[2 * DET :]
    order_ref[:DET, :] = entry.astype(i32)
    others = total[TILE_DEV * NZ : TILE_DEV * NZ + 1]
    order_ref[DET:, :] = jnp.broadcast_to(ALL_RUNS - others, (DET, LANE)).astype(i32)


def pack_kernel(
    home_ref, piece_ref, slot_ref, row_ref, col_ref, low_ref, high_ref, angle_ref, q_ref, float_ref, half_ref
):
    for r in range(RUNS):
        at = slice(r * LANE, (r + 1) * LANE)
        for part, value in enumerate(((row_ref[:, at] * PIX + col_ref[:, at]).astype(jnp.float32), angle_ref[:, at])):
            float_ref[part * PIECE_RUNS + r * DET : part * PIECE_RUNS + (r + 1) * DET] = value
        for part, source in enumerate((low_ref, high_ref)):
            half_ref[part * PIECE_RUNS + r * DET : part * PIECE_RUNS + (r + 1) * DET] = source[:, at]
    slots = slot_ref[...]
    position = jnp.zeros(slots.shape, jnp.float32)
    for s in range(LISTED):
        position = jnp.where(slots == s, home_ref[piece_ref[0, s]].astype(jnp.float32), position)
    float_ref[2 * PIECE_RUNS :] = jnp.concatenate(
        [position, jnp.zeros((DET, LANE - RUNS), jnp.float32)], axis=1
    )
    half_ref[2 * PIECE_RUNS :] = q_ref[...]


def packed(tile_home, piece_list, run_slot, hit_row, hit_col, frac_row, frac_col, angle, quarter):
    return pl.pallas_call(
        pack_kernel,
        out_shape=(
            jax.ShapeDtypeStruct((2 * PIECE_RUNS + DET, LANE), jnp.float32),
            jax.ShapeDtypeStruct((2 * PIECE_RUNS + quarter.shape[0], LANE), jnp.bfloat16),
        ),
        in_specs=[SM, SM] + [VM] * 7,
        out_specs=(VM,) * 2,
        name="pack",
    )(tile_home, piece_list, run_slot, hit_row, hit_col, frac_row, frac_col, angle, quarter)


def gather_kernel(
    float_ref, half_ref,
    tiles_ref, fo_ref, wo_ref, order_ref,
    pos_all, store_sem,
    pos_send, pos_recv, block_send, block_recv, strip_send, strip_recv, core_send, core_recv, hi_send, hi_recv,
):
    det, tm, y, z, x = place()
    partner, across = core_of(det), hi_of(det)
    ahead, behind = (y + 1) % NY, (y + NY - 1) % NY
    facing = (y + NY // 2) % NY
    other = 1 - x
    up, down, side = (det, tm_of(ahead, z, x)), (det, tm_of(behind, z, x)), (det, tm_of(y, z, other))
    far = [(det, tm_of((y + dy) % NY, z, (x + dx) % NX)) for dy, dx in PEERS]

    def along(direction, jump):
        return (det, tm_of(y, (z + jump) % NZ if direction == 0 else (z + NZ - jump) % NZ, x))

    f_ref, p_ref = float_ref.at[pl.ds(0, 2 * PIECE_RUNS)], float_ref.at[pl.ds(2 * PIECE_RUNS, DET)]
    w_ref = half_ref.at[pl.ds(0, 2 * PIECE_RUNS)]
    q_ref = half_ref.at[pl.ds(2 * PIECE_RUNS, TILE_DEV * 3 * STRIP)]

    def strip(slot, d):
        return tiles_ref.at[slot, d]

    def block(slot, part):
        return fo_ref.at[slot, pl.ds(part * PIECE_RUNS, PIECE_RUNS)] if part < 2 else wo_ref.at[slot]

    def own_block(part):
        return float_ref.at[pl.ds(part * PIECE_RUNS, PIECE_RUNS)] if part < 2 else w_ref

    mine = y * NX + x
    greet([along(d, j) for d in (0, 1) for j in (1, 2)] + [(partner, tm), (across, tm)] + far)

    started = []

    def start(copy):
        copy.start()
        started.append(copy)

    start(remote(q_ref, strip(z, det), hi_send, hi_recv, (across, tm)))

    def send_block(link, slot, part, peer, own=False):
        start(
            remote(
                own_block(part) if own else block(slot, part), block(slot, part),
                block_send.at[link, part], block_recv.at[link, part], peer,
            )
        )

    def wait_block(link, slot, part):
        remote(own_block(part), block(slot, part), block_send.at[link, part], block_recv.at[link, part], side).wait_recv()

    owner = (det, across)

    def source_slot(direction, distance):
        return (z + NZ - distance) % NZ if direction == 0 else (z + distance) % NZ

    def send_strip(half, direction, distance):
        slot = z if distance < 3 else source_slot(direction, 2)
        here = strip(slot, owner[half])
        start(
            remote(
                q_ref if half == 0 and distance < 3 else here, here,
                strip_send.at[half, direction, distance - 1], strip_recv.at[half, direction, distance - 1],
                along(direction, 2 - distance % 2),
            )
        )

    def reach(half, direction):
        return NZ // 2 if half == direction else NZ // 2 - 1

    def to_partner(half, index, slot):
        here = strip(slot, owner[half])
        start(
            remote(
                q_ref if half == 0 and index == 0 else here, here, core_send.at[half, index], core_recv.at[half, index],
                (partner, tm),
            )
        )

    def take_strip(half, distance):
        for direction in (0, 1):
            if distance <= reach(half, direction):
                slot = source_slot(direction, distance)
                remote(
                    q_ref, strip(slot, owner[half]),
                    strip_send.at[half, direction, distance - 1], strip_recv.at[half, direction, distance - 1], side,
                ).wait_recv()
                if distance == 2:
                    if reach(half, direction) == 4:
                        send_strip(half, direction, 4)
                    send_strip(half, direction, 3)
                to_partner(half, direction * NZ // 2 + distance, slot)

    def first_strips(half):
        for distance in (2, 1):
            for direction in (0, 1):
                send_strip(half, direction, distance)
        to_partner(half, 0, z)

    first_strips(0)
    for k, peer in enumerate(far):
        start(remote(p_ref, pos_all.at[mine], pos_send.at[k], pos_recv.at[k], peer))
    for part in range(3):
        send_block(1, mine, part, up, True)
        send_block(2, mine, part, down, True)
        send_block(0, mine, part, side, True)
    stores = []
    for i, (src, dst) in enumerate(
        ((q_ref, strip(z, det)), (f_ref, fo_ref.at[mine]), (w_ref, wo_ref.at[mine]), (p_ref, pos_all.at[mine]))
    ):
        copy = pltpu.make_async_copy(src, dst, store_sem.at[i])
        copy.start()
        stores.append(copy)

    slot_of = {1: behind * NX + x, 2: ahead * NX + x, 0: y * NX + other, 5: facing * NX + x, 6: facing * NX + other,
               3: behind * NX + other, 4: ahead * NX + other}

    def near(part):
        for link in (1, 2, 0):
            wait_block(link, slot_of[link], part)
            if link == 1 and part != 1:
                send_block(5, slot_of[1], part, up)
            if link == 2 and part == 1:
                send_block(5, slot_of[2], part, down)
            if link == 1 and part == 2:
                send_block(3, slot_of[1], part, side)
            if link == 0:
                if part != 2:
                    send_block(3, slot_of[0], part, up)
                send_block(4, slot_of[0], part, down)

    def opposite(part):
        wait_block(5, slot_of[5], part)
        send_block(6, slot_of[5], part, side)

    near(0)
    remote(q_ref, strip(z, across), hi_send, hi_recv, (across, tm)).wait_recv()
    first_strips(1)
    take_strip(0, 2)
    near(1)
    near(2)
    take_strip(0, 1)
    opposite(0)
    take_strip(1, 2)
    opposite(1)
    opposite(2)
    take_strip(1, 1)
    take_strip(0, 3)
    take_strip(0, 4)

    stores[3].wait()
    for k, peer in enumerate(far):
        remote(p_ref, pos_all.at[mine], pos_send.at[k], pos_recv.at[k], peer).wait_recv()
    run_order(pos_all, order_ref, y, x)

    take_strip(1, 3)
    take_strip(1, 4)
    for part in range(3):
        for link in (3, 4, 6):
            wait_block(link, slot_of[link], part)
    theirs = (partner, hi_of(partner))
    for half in (0, 1):
        places = [(0, z)]
        for direction in (0, 1):
            for distance in range(1, reach(half, direction) + 1):
                places.append((direction * NZ // 2 + distance, source_slot(direction, distance)))
        for index, slot in places:
            remote(
                q_ref, strip(slot, theirs[half]), core_send.at[half, index], core_recv.at[half, index], (partner, tm)
            ).wait_recv()
    for copy in stores[:3]:
        copy.wait()
    for copy in started:
        copy.wait_send()


def gather_all(floats, halves):
    bf, f32, i32 = jnp.bfloat16, jnp.float32, jnp.int32
    samples = (2 * PIECE_RUNS, LANE)
    return pl.pallas_call(
        gather_kernel,
        out_shape=(
            jax.ShapeDtypeStruct((NZ, N_STRIP, TILE_DEV * 3 * STRIP, PIX), bf),
            jax.ShapeDtypeStruct((NB, *samples), f32),
            jax.ShapeDtypeStruct((NB, *samples), bf),
            jax.ShapeDtypeStruct((2 * DET, LANE), i32),
        ),
        in_specs=[ANY] * 2,
        out_specs=(ANY, ANY, ANY, VM),
        scratch_shapes=[
            pltpu.VMEM((NB, DET, LANE), f32),
            DMA((4,)),
            DMA((NB,)),
            DMA((NB,)),
            DMA((7, 3)),
            DMA((7, 3)),
            DMA((2, 2, NZ // 2)),
            DMA((2, 2, NZ // 2)),
            DMA((2, NZ + 1)),
            DMA((2, NZ + 1)),
            DMA,
            DMA,
        ],
        compiler_params=pltpu.CompilerParams(collective_id=0, has_side_effects=True, vmem_limit_bytes=GRANT),
        name="gather_all",
    )(floats, halves)


def sin_cos(v):
    quarter = jnp.round(v * 0.6366197723675814)
    u = v - quarter * 1.5703125
    u = u - quarter * 4.837512969970703e-4
    u = u - quarter * 7.549789948768648e-8
    u2 = u * u
    s = u + u * u2 * (-1.6666654611e-1 + u2 * (8.3321608736e-3 + u2 * -1.9515295891e-4))
    c = 1.0 - 0.5 * u2 + u2 * u2 * (4.166664568298827e-2 + u2 * (-1.388731625493765e-3 + u2 * 2.443315711809948e-5))
    q = quarter.astype(jnp.int32) & 3
    odd = (q & 1) == 1
    sin = jnp.where(odd, c, s)
    cos = jnp.where(odd, s, c)
    sin = jnp.where(q >= 2, -sin, sin)
    cos = jnp.where((q == 1) | (q == 2), -cos, cos)
    return sin, cos


def low_of(high):
    return (1.0 - high).astype(jnp.bfloat16).astype(jnp.float32)


def run_of(entry):
    run = entry & (ALL_RUNS - 1)
    return entry >> 10, (run >> 4) & (NB - 1), run >> 7, run & (RUNS - 1)


def spread(index, low, high, rows):
    bf = jnp.bfloat16
    wide = [jnp.broadcast_to(v, (HALF, LANE)).astype(bf) for v in (index, index + 1.0, low, high)]
    zero = jnp.zeros((HALF, LANE), bf)
    parts = []
    for b in range(PIX // HALF):
        row = rows[b * HALF : (b + 1) * HALF]
        parts.append(jnp.where(row == wide[0], wide[2], jnp.where(row == wide[1], wide[3], zero)))
    return jnp.concatenate(parts, axis=0)


def forward_kernel(list_ref, tiles_ref, f_ref, w_ref, sig_ref, cs_ref, hit_ref, frac_ref):
    def prepare(z, _):
        code = f_ref[z, :PIECE_RUNS].reshape(RUNS, DET, LANE)
        row = jnp.floor(code * (1.0 / PIX))
        hit_ref[z, 0] = row
        hit_ref[z, 1] = code - row * PIX
        sin, cos = sin_cos(2.0 * f_ref[z, PIECE_RUNS:].reshape(RUNS, DET, LANE))
        cs_ref[z, 0] = cos
        cs_ref[z, 1] = sin
        fracs = w_ref[z].astype(jnp.float32)
        frac_ref[z] = fracs.reshape(2, RUNS, DET, LANE)
        sig_ref[z] = jnp.zeros_like(sig_ref[z])
        return 0

    lax.fori_loop(0, NB, prepare, 0)
    count = list_ref[DET, 0]
    rows = lax.broadcasted_iota(jnp.int32, (PIX, LANE), 0).astype(jnp.float32).astype(jnp.bfloat16)

    def body(step, _):
        for u in range(UNROLL):
            n = step * UNROLL + u
            tile, z, d, r = run_of(list_ref[n >> 7, n & (LANE - 1)])
            at = (r, pl.ds(d, 1), slice(None))
            col_high = frac_ref[z, 1, *at]
            row_high = frac_ref[z, 0, *at]
            col_weight = spread(hit_ref[z, 1, *at], low_of(col_high), col_high, rows)
            row_weight = spread(hit_ref[z, 0, *at], low_of(row_high), row_high, rows).astype(jnp.float32)
            rows_of_tile = jnp.concatenate([tiles_ref[tile // TILE_DEV, k, tile % TILE_DEV] for k in range(N_STRIP)], axis=0)
            partial = jnp.dot(rows_of_tile, col_weight, preferred_element_type=jnp.float32)
            value = []
            for p in range(3):
                terms = [
                    partial[(k * 3 + p) * STRIP : (k * 3 + p + 1) * STRIP] * row_weight[k * STRIP : (k + 1) * STRIP]
                    for k in range(N_STRIP)
                ]
                value.append(jnp.sum(sum(terms[1:], terms[0]), axis=0, keepdims=True))
            total = value[0] + cs_ref[z, 0, *at] * value[1] + cs_ref[z, 1, *at] * value[2]
            sig_ref[z, d, pl.ds(r, 1), :] = jnp.where(n < count, total, 0.0)
        return 0

    lax.fori_loop(0, (count + UNROLL - 1) // UNROLL, body, 0)


def forward(order, tiles, floats, fracs):
    f32 = jnp.float32
    block = (NB, DET, RUNS, LANE)
    pair = (NB, 2, RUNS, DET, LANE)
    return pl.pallas_call(
        forward_kernel,
        out_shape=(jax.ShapeDtypeStruct(block, f32), jax.ShapeDtypeStruct(pair, f32)),
        in_specs=[SM, VM, VM, VM],
        out_specs=(VM, VM),
        scratch_shapes=[pltpu.VMEM(pair, f32), pltpu.VMEM(pair, f32)],
        compiler_params=pltpu.CompilerParams(vmem_limit_bytes=GRANT),
        name="forward",
    )(order, tiles, floats, fracs)


def backward_kernel(list_ref, f_ref, w_ref, cs_ref, filt_ref, acc_ref, hit_ref, frac_ref):
    def prepare(z, _):
        code = f_ref[z, :PIECE_RUNS].reshape(RUNS, DET, LANE)
        row = jnp.floor(code * (1.0 / PIX))
        hit_ref[z, 0] = row
        hit_ref[z, 1] = code - row * PIX
        fracs = w_ref[z].astype(jnp.float32)
        frac_ref[z] = fracs.reshape(2, RUNS, DET, LANE)
        return 0

    lax.fori_loop(0, NB, prepare, 0)

    def clear(t, _):
        acc_ref[t] = jnp.zeros_like(acc_ref[t])
        return 0

    lax.fori_loop(0, TILE_DEV * NZ, clear, 0)
    count = list_ref[DET, 0]
    rows = lax.broadcasted_iota(jnp.int32, (PIX, LANE), 0).astype(jnp.float32).astype(jnp.bfloat16)

    def body(step, _):
        for u in range(UNROLL):
            k = step * UNROLL + u
            tile, z, d, r = run_of(list_ref[k >> 7, k & (LANE - 1)])
            at = (r, pl.ds(d, 1), slice(None))
            col_high = frac_ref[z, 1, *at]
            row_high = frac_ref[z, 0, *at]
            row_low = low_of(row_high)
            col_weight = spread(hit_ref[z, 1, *at], low_of(col_high), col_high, rows)
            filt = jnp.where(k < count, filt_ref[z, d, pl.ds(r, 1), :], 0.0)
            hit = hit_ref[z, 0, *at]
            parts = []
            for p in range(3):
                scaled = filt if p == 0 else cs_ref[z, p - 1, *at] * filt
                parts.append(spread(hit, scaled * row_low, scaled * row_high, rows))
            weighted = jnp.concatenate(parts, axis=0)
            acc_ref[tile] += lax.dot_general(
                weighted, col_weight, (((1,), (1,)), ((), ())), preferred_element_type=jnp.float32
            )
        return 0

    lax.fori_loop(0, (count + UNROLL - 1) // UNROLL, body, 0)


def backward(order, floats, fracs, turns, filtered):
    f32 = jnp.float32
    pair = (NB, 2, RUNS, DET, LANE)
    return pl.pallas_call(
        backward_kernel,
        out_shape=jax.ShapeDtypeStruct((TILE_DEV * NZ, 3 * PIX, PIX), f32),
        in_specs=[SM, VM, VM, VM, VM],
        out_specs=VM,
        scratch_shapes=[pltpu.VMEM(pair, f32), pltpu.VMEM(pair, f32)],
        compiler_params=pltpu.CompilerParams(vmem_limit_bytes=GRANT),
        name="backward",
    )(order, floats, fracs, turns, filtered)


def toeplitz(noise_ref, line_ref, hi_ref, lo_ref):
    square = (LANE, LANE)
    lanes = lax.broadcasted_iota(jnp.int32, square, 1)
    rows = lax.broadcasted_iota(jnp.int32, square, 0)
    first = lax.broadcasted_iota(jnp.int32, (DET, LANE), 1) == 0
    for q in range(REACH):
        lags = noise_ref[:, q * LANE : (q + 1) * LANE]
        line_ref[q] = jnp.where(first, lags + 1.0, lags) if q == 0 else lags
    line_ref[REACH] = jnp.where(first, jnp.broadcast_to(noise_ref[:, REACH * LANE :], (DET, LANE)), 0.0)

    def one(d, _):
        def put(q, matrix):
            high = matrix.astype(jnp.bfloat16)
            hi_ref[d, q] = high
            lo_ref[d, q] = (matrix - high.astype(jnp.float32)).astype(jnp.bfloat16)

        before = None
        for q in range(REACH + 1):
            lags = line_ref[q, pl.ds(d, 1), :]
            after = pltpu.roll(jnp.broadcast_to(lags, square), 0, 1, stride=1, stride_axis=0)
            if q == 0:
                put(0, jnp.where(lanes >= rows, after, 0.0))
                put(REACH + 1, jnp.where(lanes > rows, after, 0.0))
            else:
                put(q, jnp.where(lanes >= rows, after, before))
            before = after
        return 0

    lax.fori_loop(0, DET, one, 0)


STRAIGHT = (((1,), (0,)), ((), ()))
CROSSED = (((1,), (1,)), ((), ()))


def filter_kernel(
    part_ref, noise_ref, out_ref, land, ext, filt, lags, t_hi, t_lo,
    store_sem, send, recv, halo_send, halo_recv, back_send, back_recv,
):
    det, tm, y, z, x = place()
    total_tm = NY * NZ * NX
    mine = y * NX + x
    prior, later = (tm + total_tm - 1) % total_tm, (tm + 1) % total_tm

    def slot(k, sign):
        dy, dx = PEERS[k]
        return ((y + sign * dy + NY) % NY) * NX + (x + dx) % NX

    peers = [(det, tm_of((y + dy) % NY, z, (x + dx) % NX)) for dy, dx in PEERS]
    greet(peers + [(det, later), (det, prior)])
    sends = []

    def part_copy(c, k):
        rows = pl.ds(c * SENT, SENT)
        return remote(part_ref.at[slot(k, 1), rows], land.at[k, rows], send.at[k, c], recv.at[k, c], peers[k])

    def halo_copies(c):
        rows = pl.ds(c * SENT, SENT)
        return (
            remote(
                ext.at[rows, pl.ds(REACH, REACH), :], ext.at[rows, pl.ds(REACH + RUNS, REACH), :],
                halo_send.at[0, c], halo_recv.at[0, c], (det, prior),
            ),
            remote(
                ext.at[rows, pl.ds(RUNS, REACH), :], ext.at[rows, pl.ds(0, REACH), :],
                halo_send.at[1, c], halo_recv.at[1, c], (det, later),
            ),
        )

    for c in range(DET // SENT):
        for k in range(NB - 1):
            copy = part_copy(c, k)
            copy.start()
            sends.append(copy)
    toeplitz(noise_ref, lags, t_hi, t_lo)

    def gathered(c):
        rows = slice(c * SENT, (c + 1) * SENT)
        total = part_ref[mine, rows]
        for k in range(NB - 1):
            part_copy(c, k).wait_recv()
            total = total + land[k, rows]
        ext[rows, REACH : REACH + RUNS, :] = total
        for copy in halo_copies(c):
            copy.start()
            sends.append(copy)

    first, last = tm == 0, tm == total_tm - 1

    def product(left, right, crossed):
        return lax.dot_general(left, right, CROSSED if crossed else STRAIGHT, preferred_element_type=jnp.float32)

    back, own_copies = [], []

    def back_copy(c, k, source):
        rows = pl.ds(c * SENT, SENT)
        return remote(filt.at[rows], out_ref.at[source, rows], back_send.at[k, c], back_recv.at[k, c], peers[k])

    def send_back(c):
        for k in range(NB - 1):
            copy = back_copy(c, k, mine)
            copy.start()
            back.append(copy)
        rows = pl.ds(c * SENT, SENT)
        copy = pltpu.make_async_copy(filt.at[rows], out_ref.at[mine, rows], store_sem.at[c])
        copy.start()
        own_copies.append(copy)

    def filtered(c):
        for copy in halo_copies(c):
            copy.wait_recv()
        dets = range(c * SENT, (c + 1) * SENT)
        lines = [
            jnp.concatenate(
                [
                    jnp.where(first, 0.0, ext[d, :REACH]),
                    ext[d, REACH : REACH + RUNS],
                    jnp.where(last, 0.0, ext[d, REACH + RUNS :]),
                ],
                axis=0,
            )
            for d in dets
        ]
        full = [jnp.zeros((2 * RUNS, LANE), jnp.float32) for d in dets]
        fine = [jnp.zeros((RUNS, LANE), jnp.float32) for d in dets]
        for m in range(2 * REACH + 1):
            q = REACH - m
            for i, d in enumerate(dets):
                window = lines[i][m : m + RUNS]
                high = window.astype(jnp.bfloat16)
                low = (window - high.astype(jnp.float32)).astype(jnp.bfloat16)
                stack = jnp.concatenate([high, low], axis=0)
                for index, crossed in [(q, False)] if q > 0 else [(-q, True)] if q < 0 else [(0, False), (REACH + 1, True)]:
                    full[i] += product(stack, t_hi[d, index], crossed)
                    fine[i] += product(high, t_lo[d, index], crossed)
        for i, d in enumerate(dets):
            filt[d] = full[i][:RUNS] + full[i][RUNS:] + fine[i]
        send_back(c)

    chunks = DET // SENT
    gathered(0)
    gathered(1)
    for c in range(chunks):
        filtered(c)
        if c + 2 < chunks:
            gathered(c + 2)
    for copy in own_copies:
        copy.wait()
    for c in range(DET // SENT):
        for k, peer in enumerate(peers):
            back_copy(c, k, slot(k, -1)).wait_recv()
    for copy in sends + back:
        copy.wait_send()


def filtered_of(partial, noise_coef):
    f32, bf = jnp.float32, jnp.bfloat16
    block = (DET, RUNS, LANE)
    matrices = (DET, REACH + 2, LANE, LANE)
    return pl.pallas_call(
        filter_kernel,
        out_shape=jax.ShapeDtypeStruct((NB, *block), f32),
        in_specs=[VM, VM],
        out_specs=ANY,
        scratch_shapes=[
            pltpu.VMEM((NB - 1, *block), f32),
            pltpu.VMEM((DET, RUNS + 2 * REACH, LANE), f32),
            pltpu.VMEM(block, f32),
            pltpu.VMEM((REACH + 1, DET, LANE), f32),
            pltpu.VMEM(matrices, bf),
            pltpu.VMEM(matrices, bf),
            DMA((DET // SENT,)),
            DMA((NB, DET // SENT)),
            DMA((NB, DET // SENT)),
            DMA((2, DET // SENT)),
            DMA((2, DET // SENT)),
            DMA((NB, DET // SENT)),
            DMA((NB, DET // SENT)),
        ],
        compiler_params=pltpu.CompilerParams(collective_id=1, has_side_effects=True, vmem_limit_bytes=GRANT),
        name="filter",
    )(partial, noise_coef)


CHUNKS = [(t, p) for t in range(TILE_DEV) for p in range(3)]
HALF_Z = NZ // 2
WIRE = jnp.bfloat16
OFFSETS = [4, 3, -3, 2, -2, 1, -1, 0]


def collect_kernel(
    acc_ref, out_ref, land_core, packet, land, land_last, land_own,
    core_send, core_recv, ring_send, ring_recv, last_send, last_recv, hi_send, hi_recv,
):
    f32 = jnp.float32
    det, tm, y, z, x = place()
    core, hi = det % 2, det // 2
    partner, across = core_of(det), hi_of(det)
    right, left = tm_of(y, (z + 1) % NZ, x), tm_of(y, (z + NZ - 1) % NZ, x)
    neighbours = ((det, right), (det, left))
    greet([(partner, tm), (across, tm), *neighbours, (across, right), (across, left)])
    started = []

    def start(copy):
        copy.start()
        started.append(copy)

    for k, offset in enumerate(OFFSETS):
        start(
            remote(
                acc_ref.at[(z + offset + NZ) % NZ, :, :, :, 1 - core], land_core.at[k], core_send.at[k], core_recv.at[k],
                (partner, tm),
            )
        )

    def ring(direction, step, c):
        t, p = CHUNKS[c]
        sign = 1 if direction == 0 else -1
        k = OFFSETS.index(sign * (HALF_Z - step)) if step else 0
        return remote(
            packet.at[k, t, p], land.at[direction, step, t, p],
            ring_send.at[direction, step, c], ring_recv.at[direction, step, c], neighbours[direction],
        )

    def last_hop(direction, c, crossing):
        t, p = CHUNKS[c]
        k = OFFSETS.index(1 if direction == 0 else -1)
        goal = (right, left)[direction]
        return remote(
            packet.at[k, t, p, 1 - hi if crossing else hi], land_last.at[crossing, direction, t, p],
            last_send.at[crossing, direction, c], last_recv.at[crossing, direction, c],
            (across if crossing else det, goal),
        )

    def own_copy(t):
        return remote(packet.at[len(OFFSETS) - 1, t, :, 1 - hi], land_own.at[t], hi_send.at[t], hi_recv.at[t], (across, tm))

    def own(k, t, p):
        return acc_ref[(z + OFFSETS[k] + NZ) % NZ, t, p, :, core]

    def swapped(k):
        remote(acc_ref.at[0, :, :, :, 0], land_core.at[k], core_send.at[k], core_recv.at[k], (partner, tm)).wait_recv()

    swapped(0)
    for direction in (0, 1):
        for c, (t, p) in enumerate(CHUNKS):
            if t == direction:
                packet[0, t, p] = (own(0, t, p) + land_core[0, t, p]).astype(WIRE)
    for p in range(3):
        for direction in (0, 1):
            start(ring(direction, 0, direction * 3 + p))
    last = len(OFFSETS) - 1
    for step in range(1, HALF_Z):
        keys = [OFFSETS.index(HALF_Z - step), OFFSETS.index(step - HALF_Z)]
        for k in keys:
            swapped(k)
        for i in range(len(CHUNKS)):
            for direction in (0, 1):
                c = (i + 3 * (1 - direction)) % len(CHUNKS) if step == 1 else i
                t, p = CHUNKS[c]
                k = keys[direction]
                value = own(k, t, p) + land_core[k, t, p]
                if step > 1 or t == direction:
                    ring(direction, step - 1, c).wait_recv()
                    value = value + land[direction, step - 1, t, p].astype(f32)
                packet[k, t, p] = value.astype(WIRE)
                if step < HALF_Z - 1:
                    start(ring(direction, step, c))
                else:
                    start(last_hop(direction, c, 1))
                    start(last_hop(direction, c, 0))
        if step == 1:
            swapped(last)
            for t in range(TILE_DEV):
                for p in range(3):
                    value = own(last, t, p) + land_core[last, t, p]
                    packet[last, t, p] = value.astype(WIRE)
                    land_core[last, t, p] = value
                start(own_copy(t))
    for t in range(TILE_DEV):
        own_copy(t).wait_recv()
    for c, (t, p) in enumerate(CHUNKS):
        value = land_core[last, t, p, hi] + land_own[t, p].astype(f32)
        for crossing in (0, 1):
            for direction in (0, 1):
                last_hop(direction, c, crossing).wait_recv()
                value = value + land_last[crossing, direction, t, p].astype(f32)
        out_ref[t, p] = value
    for copy in started:
        copy.wait_send()


def collect(acc):
    f32 = jnp.float32
    half = (TILE_DEV, 3, 2, STRIP, PIX)
    quarter = (TILE_DEV, 3, STRIP, PIX)
    return pl.pallas_call(
        collect_kernel,
        out_shape=jax.ShapeDtypeStruct(quarter, f32),
        in_specs=[VM],
        out_specs=VM,
        scratch_shapes=[
            pltpu.VMEM((NZ, *half), f32),
            pltpu.VMEM((NZ, *half), WIRE),
            pltpu.VMEM((2, HALF_Z - 1, *half), WIRE),
            pltpu.VMEM((2, 2, *quarter), WIRE),
            pltpu.VMEM(quarter, WIRE),
            DMA((NZ,)),
            DMA((NZ,)),
            DMA((2, HALF_Z - 1, 6)),
            DMA((2, HALF_Z - 1, 6)),
            DMA((2, 2, 6)),
            DMA((2, 2, 6)),
            DMA((2,)),
            DMA((2,)),
        ],
        compiler_params=pltpu.CompilerParams(collective_id=2, has_side_effects=True, vmem_limit_bytes=GRANT),
        name="collect",
    )(acc.reshape(NZ, TILE_DEV, 3, 2, 2, STRIP, PIX))


def body(
    sky_map, tile_home, piece_tiles, run_slot, hit_row, hit_col, frac_row, frac_col, angle, noise_coef
):
    floats, halves = packed(
        tile_home, piece_tiles.reshape(1, LISTED), run_slot, hit_row, hit_col, frac_row, frac_col, angle,
        sky_map.reshape(TILE_DEV * 3 * STRIP, PIX),
    )
    tiles, all_floats, all_fracs, order = gather_all(floats, halves)
    partial, turns = forward(
        order, tiles.reshape(NZ, N_STRIP, TILE_DEV, 3 * STRIP, PIX), all_floats, all_fracs
    )
    filtered = filtered_of(partial, noise_coef)
    acc = backward(order, all_floats, all_fracs, turns, filtered)
    return collect(acc)


def solution(mesh):
    placed = (
        P("tm", None, "det", None),
        P(),
        P("det", "tm", None),
        P("det", "tm"),
        P("det", "tm"),
        P("det", "tm"),
        P("det", "tm"),
        P("det", "tm"),
        P("det", "tm"),
        P("det", None),
    )
    return jax.shard_map(
        body, mesh=mesh, in_specs=placed, out_specs=P("tm", None, "det", None), check_vma=False
    )
```

```python
import functools

import jax
import jax.numpy as jnp
from jax import lax
from jax.experimental import pallas as pl
from jax.experimental.pallas import tpu as pltpu
from jax.sharding import PartitionSpec as P

GRANT = 24 << 20
MESH = pl.DeviceIdType.MESH
NY, NZ, NX = 4, 8, 2
NB = NY * NX
DET, RUNS, LANE = 8, 16, 128
PIX = 128
STRIP = 32
N_STRIP = 4
LISTED = 32
TILE_DEV = 2
REACH = 8
UNROLL = 16
HALF = 16
SENT = 2
PIECE_RUNS = DET * RUNS
ALL_RUNS = NB * PIECE_RUNS
SAMPLE_ROWS = 6 * PIECE_RUNS
ANY = pl.BlockSpec(memory_space=pl.ANY)
VM = pl.BlockSpec(memory_space=pltpu.VMEM)
SM = pl.BlockSpec(memory_space=pltpu.SMEM)
DMA = pltpu.SemaphoreType.DMA
PEERS = [(dy, dx) for dy in range(NY) for dx in range(NX) if (dy, dx) != (0, 0)]


def place():
    det, tm = lax.axis_index("det"), lax.axis_index("tm")
    y, z, x = tm // (NZ * NX), (tm // NX) % NZ, tm % NX
    return det, tm, y, z, x


def tm_of(y, z, x):
    return (y * NZ + z) * NX + x


def core_of(det):
    return det + 1 - 2 * (det % 2)


def hi_of(det):
    return (det + 2) % 4


def greet(peers):
    barrier = pltpu.get_barrier_semaphore()
    for peer in peers:
        pl.semaphore_signal(barrier, inc=1, device_id=peer, device_id_type=MESH)
    pl.semaphore_wait(barrier, len(peers))


def remote(src, dst, send, recv, peer):
    return pltpu.make_async_remote_copy(
        src_ref=src, dst_ref=dst, send_sem=send, recv_sem=recv, device_id=peer, device_id_type=MESH
    )


def run_order(pos_ref, order_ref, y, x):
    f32, bf, i32 = jnp.float32, jnp.bfloat16, jnp.int32

    def iota(shape, dim):
        return lax.broadcasted_iota(i32, shape, dim)

    def whole(mask):
        return jnp.where(mask, 1.0, 0.0).astype(bf)

    def dot(left, right):
        return jnp.dot(left, right, preferred_element_type=f32)

    lanes, offset = iota((LANE, LANE), 1), iota((LANE, LANE), 0)
    spot = jnp.zeros((2 * DET, LANE), f32)
    for slot in range(NB):
        spot += dot(pos_ref[slot], whole((offset < RUNS) & (lanes == offset + slot * RUNS)))
    pos = spot[:DET].astype(i32)
    here = (pos // (TILE_DEV * NX * NZ) == y) & ((pos // TILE_DEV) % NX == x)
    tile = ((pos // (TILE_DEV * NX)) % NZ) * TILE_DEV + pos % TILE_DEV
    kinds, square = (2 * TILE_DEV * NZ, LANE), (LANE, LANE)
    kind = jnp.where(here, tile, TILE_DEV * NZ)
    tile = tile.astype(f32)
    before, every = whole(iota(square, 0) < iota(square, 1)), jnp.ones(square, bf)
    marks, prior, total = [], [], jnp.zeros(kinds, f32)
    for d in range(DET):
        mark = whole(jnp.broadcast_to(kind[d : d + 1], kinds) == iota(kinds, 0))
        marks.append(mark.astype(f32))
        prior.append(dot(mark, before) + total)
        total += dot(mark, every)
    lower = whole(iota((kinds[0], kinds[0]), 1) < iota((kinds[0], kinds[0]), 0))
    coarse = jnp.floor(total * (1.0 / 32.0))
    base = 32.0 * dot(lower, coarse.astype(bf)) + dot(lower, (total - 32.0 * coarse).astype(bf))
    high_rows, low_rows = iota((DET, LANE), 0).astype(f32), iota(square, 0).astype(f32)
    lane = iota((DET, LANE), 1).astype(f32)
    found = jnp.zeros((3 * DET, LANE), f32)
    for d in range(DET):
        rank = jnp.sum(marks[d] * (prior[d] + base), axis=0, keepdims=True)
        high = jnp.floor(rank * (1.0 / LANE))
        low = rank - LANE * high
        at = jnp.broadcast_to(high, (DET, LANE)) == high_rows
        values = (jnp.broadcast_to(tile[d : d + 1], (DET, LANE)), jnp.full((DET, LANE), float(d), f32), lane)
        left = jnp.concatenate([jnp.where(at, v, 0.0) for v in values], axis=0).astype(bf)
        right = whole(jnp.broadcast_to(low, square) == low_rows)
        found += lax.dot_general(left, right, (((1,), (1,)), ((), ())), preferred_element_type=f32)
    entry = found[:DET] * ALL_RUNS + found[DET : 2 * DET] * LANE + found[2 * DET :]
    order_ref[:DET, :] = entry.astype(i32)
    others = total[TILE_DEV * NZ : TILE_DEV * NZ + 1]
    order_ref[DET:, :] = jnp.broadcast_to(ALL_RUNS - others, (DET, LANE)).astype(i32)


def pack_kernel(home_ref, piece_ref, slot_ref, row_ref, col_ref, low_ref, high_ref, angle_ref, q_ref, out_ref):
    f32, bf = jnp.float32, jnp.bfloat16
    for r in range(RUNS):
        at = slice(r * LANE, (r + 1) * LANE)
        angle = angle_ref[:, at]
        coarse = angle.astype(bf)
        fine = (angle - coarse.astype(f32)).astype(bf)
        row, col = row_ref[:, at].astype(f32).astype(bf), col_ref[:, at].astype(f32).astype(bf)
        for part, value in enumerate((row, col, coarse, fine, low_ref[:, at], high_ref[:, at])):
            out_ref[part * PIECE_RUNS + r * DET : part * PIECE_RUNS + (r + 1) * DET] = value
    slots = slot_ref[...]
    position = jnp.zeros(slots.shape, f32)
    for s in range(LISTED):
        position = jnp.where(slots == s, home_ref[piece_ref[0, s]].astype(f32), position)
    wide = jnp.concatenate([position, jnp.zeros((DET, LANE - RUNS), f32)], axis=1)
    out_ref[SAMPLE_ROWS : SAMPLE_ROWS + 2 * DET] = jnp.concatenate([wide, jnp.zeros_like(wide)], axis=0).astype(bf)
    out_ref[SAMPLE_ROWS + 2 * DET :] = q_ref[...]


def packed(tile_home, piece_list, run_slot, hit_row, hit_col, frac_row, frac_col, angle, quarter):
    return pl.pallas_call(
        pack_kernel,
        out_shape=jax.ShapeDtypeStruct((SAMPLE_ROWS + 2 * DET + quarter.shape[0], LANE), jnp.bfloat16),
        in_specs=[SM, SM] + [VM] * 7,
        out_specs=VM,
        name="pack",
    )(tile_home, piece_list, run_slot, hit_row, hit_col, frac_row, frac_col, angle, quarter)


def gather_kernel(
    pack_ref,
    tiles_ref, all_ref, order_ref,
    pos_all, store_sem,
    pos_send, pos_recv, block_send, block_recv, strip_send, strip_recv, core_send, core_recv, hi_send, hi_recv,
):
    det, tm, y, z, x = place()
    partner, across = core_of(det), hi_of(det)
    ahead, behind = (y + 1) % NY, (y + NY - 1) % NY
    facing = (y + NY // 2) % NY
    other = 1 - x
    up, down, side = (det, tm_of(ahead, z, x)), (det, tm_of(behind, z, x)), (det, tm_of(y, z, other))
    far = [(det, tm_of((y + dy) % NY, z, (x + dx) % NX)) for dy, dx in PEERS]

    def along(direction, jump):
        return (det, tm_of(y, (z + jump) % NZ if direction == 0 else (z + NZ - jump) % NZ, x))

    samples_ref, p_ref = pack_ref.at[pl.ds(0, SAMPLE_ROWS)], pack_ref.at[pl.ds(SAMPLE_ROWS, 2 * DET)]
    q_ref = pack_ref.at[pl.ds(SAMPLE_ROWS + 2 * DET, TILE_DEV * 3 * STRIP)]

    def strip(slot, d):
        return tiles_ref.at[slot, d]

    def block(slot, part):
        return all_ref.at[slot, pl.ds(part * 2 * PIECE_RUNS, 2 * PIECE_RUNS)]

    def own_block(part):
        return pack_ref.at[pl.ds(part * 2 * PIECE_RUNS, 2 * PIECE_RUNS)]

    mine = y * NX + x
    greet([along(d, j) for d in (0, 1) for j in (1, 2)] + [(partner, tm), (across, tm)] + far)

    started = []

    def start(copy):
        copy.start()
        started.append(copy)

    start(remote(q_ref, strip(z, det), hi_send, hi_recv, (across, tm)))

    def send_block(link, slot, part, peer, own=False):
        start(
            remote(
                own_block(part) if own else block(slot, part), block(slot, part),
                block_send.at[link, part], block_recv.at[link, part], peer,
            )
        )

    def wait_block(link, slot, part):
        remote(own_block(part), block(slot, part), block_send.at[link, part], block_recv.at[link, part], side).wait_recv()

    owner = (det, across)

    def source_slot(direction, distance):
        return (z + NZ - distance) % NZ if direction == 0 else (z + distance) % NZ

    def send_strip(half, direction, distance):
        slot = z if distance < 3 else source_slot(direction, 2)
        here = strip(slot, owner[half])
        start(
            remote(
                q_ref if half == 0 and distance < 3 else here, here,
                strip_send.at[half, direction, distance - 1], strip_recv.at[half, direction, distance - 1],
                along(direction, 2 - distance % 2),
            )
        )

    def reach(half, direction):
        return NZ // 2 if half == direction else NZ // 2 - 1

    def to_partner(half, index, slot):
        here = strip(slot, owner[half])
        start(
            remote(
                q_ref if half == 0 and index == 0 else here, here, core_send.at[half, index], core_recv.at[half, index],
                (partner, tm),
            )
        )

    def take_strip(half, distance):
        for direction in (0, 1):
            if distance <= reach(half, direction):
                slot = source_slot(direction, distance)
                remote(
                    q_ref, strip(slot, owner[half]),
                    strip_send.at[half, direction, distance - 1], strip_recv.at[half, direction, distance - 1], side,
                ).wait_recv()
                if distance == 2:
                    if reach(half, direction) == 4:
                        send_strip(half, direction, 4)
                    send_strip(half, direction, 3)
                to_partner(half, direction * NZ // 2 + distance, slot)

    def first_strips(half):
        for distance in (2, 1):
            for direction in (0, 1):
                send_strip(half, direction, distance)
        to_partner(half, 0, z)

    for k, peer in enumerate(far):
        start(remote(p_ref, pos_all.at[mine], pos_send.at[k], pos_recv.at[k], peer))
    first_strips(0)
    for part in range(3):
        send_block(1, mine, part, up, True)
        send_block(2, mine, part, down, True)
        send_block(0, mine, part, side, True)
    stores = []
    for i, (src, dst) in enumerate(
        ((q_ref, strip(z, det)), (samples_ref, all_ref.at[mine]), (p_ref, pos_all.at[mine]))
    ):
        copy = pltpu.make_async_copy(src, dst, store_sem.at[i])
        copy.start()
        stores.append(copy)

    slot_of = {1: behind * NX + x, 2: ahead * NX + x, 0: y * NX + other, 5: facing * NX + x, 6: facing * NX + other,
               3: behind * NX + other, 4: ahead * NX + other}

    def near(part):
        for link in (1, 2, 0):
            wait_block(link, slot_of[link], part)
            if link == 1 and part != 1:
                send_block(5, slot_of[1], part, up)
            if link == 2 and part == 1:
                send_block(5, slot_of[2], part, down)
            if link == 1 and part == 2:
                send_block(3, slot_of[1], part, side)
            if link == 0:
                if part != 2:
                    send_block(3, slot_of[0], part, up)
                send_block(4, slot_of[0], part, down)

    def opposite(part):
        wait_block(5, slot_of[5], part)
        send_block(6, slot_of[5], part, side)

    stores[2].wait()
    for k, peer in enumerate(far):
        remote(p_ref, pos_all.at[mine], pos_send.at[k], pos_recv.at[k], peer).wait_recv()
    run_order(pos_all, order_ref, y, x)

    near(0)
    remote(q_ref, strip(z, across), hi_send, hi_recv, (across, tm)).wait_recv()
    first_strips(1)
    take_strip(0, 2)
    near(1)
    near(2)
    take_strip(0, 1)
    opposite(0)
    take_strip(1, 2)
    opposite(1)
    opposite(2)
    take_strip(1, 1)
    take_strip(0, 3)
    take_strip(0, 4)

    take_strip(1, 3)
    take_strip(1, 4)
    for part in range(3):
        for link in (3, 4, 6):
            wait_block(link, slot_of[link], part)
    theirs = (partner, hi_of(partner))
    for half in (0, 1):
        places = [(0, z)]
        for direction in (0, 1):
            for distance in range(1, reach(half, direction) + 1):
                places.append((direction * NZ // 2 + distance, source_slot(direction, distance)))
        for index, slot in places:
            remote(
                q_ref, strip(slot, theirs[half]), core_send.at[half, index], core_recv.at[half, index], (partner, tm)
            ).wait_recv()
    for copy in stores[:2]:
        copy.wait()
    for copy in started:
        copy.wait_send()


def gather_all(pack):
    bf, i32 = jnp.bfloat16, jnp.int32
    return pl.pallas_call(
        gather_kernel,
        out_shape=(
            jax.ShapeDtypeStruct((NZ, N_STRIP, TILE_DEV * 3 * STRIP, PIX), bf),
            jax.ShapeDtypeStruct((NB, SAMPLE_ROWS, LANE), bf),
            jax.ShapeDtypeStruct((2 * DET, LANE), i32),
        ),
        in_specs=[ANY],
        out_specs=(ANY, ANY, VM),
        scratch_shapes=[
            pltpu.VMEM((NB, 2 * DET, LANE), bf),
            DMA((3,)),
            DMA((NB,)),
            DMA((NB,)),
            DMA((7, 3)),
            DMA((7, 3)),
            DMA((2, 2, NZ // 2)),
            DMA((2, 2, NZ // 2)),
            DMA((2, NZ + 1)),
            DMA((2, NZ + 1)),
            DMA,
            DMA,
        ],
        compiler_params=pltpu.CompilerParams(collective_id=0, has_side_effects=True, vmem_limit_bytes=GRANT),
        name="gather_all",
    )(pack)


def sin_cos(v):
    quarter = jnp.round(v * 0.6366197723675814)
    u = v - quarter * 1.5703125
    u = u - quarter * 4.837512969970703e-4
    u = u - quarter * 7.549789948768648e-8
    u2 = u * u
    s = u + u * u2 * (-1.6666654611e-1 + u2 * (8.3321608736e-3 + u2 * -1.9515295891e-4))
    c = 1.0 - 0.5 * u2 + u2 * u2 * (4.166664568298827e-2 + u2 * (-1.388731625493765e-3 + u2 * 2.443315711809948e-5))
    q = quarter.astype(jnp.int32) & 3
    odd = (q & 1) == 1
    sin = jnp.where(odd, c, s)
    cos = jnp.where(odd, s, c)
    sin = jnp.where(q >= 2, -sin, sin)
    cos = jnp.where((q == 1) | (q == 2), -cos, cos)
    return sin, cos


def low_of(high):
    return (1.0 - high).astype(jnp.bfloat16).astype(jnp.float32)


def run_of(entry):
    run = entry & (ALL_RUNS - 1)
    return entry >> 10, (run >> 4) & (NB - 1), run >> 7, run & (RUNS - 1)


def spread(index, low, high, rows):
    bf = jnp.bfloat16
    wide = [jnp.broadcast_to(v, (HALF, LANE)).astype(bf) for v in (index, index + 1.0, low, high)]
    zero = jnp.zeros((HALF, LANE), bf)
    parts = []
    for b in range(PIX // HALF):
        row = rows[b * HALF : (b + 1) * HALF]
        parts.append(jnp.where(row == wide[0], wide[2], jnp.where(row == wide[1], wide[3], zero)))
    return jnp.concatenate(parts, axis=0)


def samples_of(all_ref, z, part):
    rows = slice(part * 2 * PIECE_RUNS, (part + 1) * 2 * PIECE_RUNS)
    return all_ref[z, rows].astype(jnp.float32).reshape(2, RUNS, DET, LANE)


def forward_kernel(list_ref, tiles_ref, all_ref, sig_ref, cs_ref, hit_ref, frac_ref):
    def prepare(z, _):
        hit_ref[z] = samples_of(all_ref, z, 0)
        halves = samples_of(all_ref, z, 1)
        sin, cos = sin_cos(2.0 * (halves[0] + halves[1]))
        cs_ref[z, 0] = cos
        cs_ref[z, 1] = sin
        frac_ref[z] = samples_of(all_ref, z, 2)
        sig_ref[z] = jnp.zeros_like(sig_ref[z])
        return 0

    lax.fori_loop(0, NB, prepare, 0)
    count = list_ref[DET, 0]
    rows = lax.broadcasted_iota(jnp.int32, (PIX, LANE), 0).astype(jnp.float32).astype(jnp.bfloat16)

    def body(step, _):
        for u in range(UNROLL):
            n = step * UNROLL + u
            tile, z, d, r = run_of(list_ref[n >> 7, n & (LANE - 1)])
            at = (r, pl.ds(d, 1), slice(None))
            col_high = frac_ref[z, 1, *at]
            row_high = frac_ref[z, 0, *at]
            col_weight = spread(hit_ref[z, 1, *at], low_of(col_high), col_high, rows)
            row_weight = spread(hit_ref[z, 0, *at], low_of(row_high), row_high, rows).astype(jnp.float32)
            rows_of_tile = jnp.concatenate([tiles_ref[tile // TILE_DEV, k, tile % TILE_DEV] for k in range(N_STRIP)], axis=0)
            partial = jnp.dot(rows_of_tile, col_weight, preferred_element_type=jnp.float32)
            value = []
            for p in range(3):
                terms = [
                    partial[(k * 3 + p) * STRIP : (k * 3 + p + 1) * STRIP] * row_weight[k * STRIP : (k + 1) * STRIP]
                    for k in range(N_STRIP)
                ]
                value.append(jnp.sum(sum(terms[1:], terms[0]), axis=0, keepdims=True))
            total = value[0] + cs_ref[z, 0, *at] * value[1] + cs_ref[z, 1, *at] * value[2]
            sig_ref[z, d, pl.ds(r, 1), :] = jnp.where(n < count, total, 0.0)
        return 0

    lax.fori_loop(0, (count + UNROLL - 1) // UNROLL, body, 0)


def forward(order, tiles, samples):
    f32 = jnp.float32
    block = (NB, DET, RUNS, LANE)
    pair = (NB, 2, RUNS, DET, LANE)
    return pl.pallas_call(
        forward_kernel,
        out_shape=(jax.ShapeDtypeStruct(block, f32), jax.ShapeDtypeStruct(pair, f32)),
        in_specs=[SM, VM, VM],
        out_specs=(VM, VM),
        scratch_shapes=[pltpu.VMEM(pair, f32), pltpu.VMEM(pair, f32)],
        compiler_params=pltpu.CompilerParams(vmem_limit_bytes=GRANT),
        name="forward",
    )(order, tiles, samples)


def backward_kernel(list_ref, all_ref, cs_ref, filt_ref, acc_ref, hit_ref, frac_ref):
    def prepare(z, _):
        hit_ref[z] = samples_of(all_ref, z, 0)
        frac_ref[z] = samples_of(all_ref, z, 2)
        return 0

    lax.fori_loop(0, NB, prepare, 0)

    def clear(t, _):
        acc_ref[t] = jnp.zeros_like(acc_ref[t])
        return 0

    lax.fori_loop(0, TILE_DEV * NZ, clear, 0)
    count = list_ref[DET, 0]
    rows = lax.broadcasted_iota(jnp.int32, (PIX, LANE), 0).astype(jnp.float32).astype(jnp.bfloat16)

    def body(step, _):
        for u in range(UNROLL):
            k = step * UNROLL + u
            tile, z, d, r = run_of(list_ref[k >> 7, k & (LANE - 1)])
            at = (r, pl.ds(d, 1), slice(None))
            col_high = frac_ref[z, 1, *at]
            row_high = frac_ref[z, 0, *at]
            row_low = low_of(row_high)
            col_weight = spread(hit_ref[z, 1, *at], low_of(col_high), col_high, rows)
            filt = jnp.where(k < count, filt_ref[z, d, pl.ds(r, 1), :], 0.0)
            hit = hit_ref[z, 0, *at]
            parts = []
            for p in range(3):
                scaled = filt if p == 0 else cs_ref[z, p - 1, *at] * filt
                parts.append(spread(hit, scaled * row_low, scaled * row_high, rows))
            weighted = jnp.concatenate(parts, axis=0)
            acc_ref[tile] += lax.dot_general(
                weighted, col_weight, (((1,), (1,)), ((), ())), preferred_element_type=jnp.float32
            )
        return 0

    lax.fori_loop(0, (count + UNROLL - 1) // UNROLL, body, 0)


def backward(order, samples, turns, filtered):
    f32 = jnp.float32
    pair = (NB, 2, RUNS, DET, LANE)
    return pl.pallas_call(
        backward_kernel,
        out_shape=jax.ShapeDtypeStruct((TILE_DEV * NZ, 3 * PIX, PIX), f32),
        in_specs=[SM, VM, VM, VM],
        out_specs=VM,
        scratch_shapes=[pltpu.VMEM(pair, f32), pltpu.VMEM(pair, f32)],
        compiler_params=pltpu.CompilerParams(vmem_limit_bytes=GRANT),
        name="backward",
    )(order, samples, turns, filtered)


def toeplitz(noise_ref, line_ref, hi_ref, lo_ref):
    square = (LANE, LANE)
    lanes = lax.broadcasted_iota(jnp.int32, square, 1)
    rows = lax.broadcasted_iota(jnp.int32, square, 0)
    first = lax.broadcasted_iota(jnp.int32, (DET, LANE), 1) == 0
    for q in range(REACH):
        lags = noise_ref[:, q * LANE : (q + 1) * LANE]
        line_ref[q] = jnp.where(first, lags + 1.0, lags) if q == 0 else lags
    line_ref[REACH] = jnp.where(first, jnp.broadcast_to(noise_ref[:, REACH * LANE :], (DET, LANE)), 0.0)

    def one(d, _):
        def put(q, matrix):
            high = matrix.astype(jnp.bfloat16)
            hi_ref[d, q] = high
            lo_ref[d, q] = (matrix - high.astype(jnp.float32)).astype(jnp.bfloat16)

        before = None
        for q in range(REACH + 1):
            lags = line_ref[q, pl.ds(d, 1), :]
            after = pltpu.roll(jnp.broadcast_to(lags, square), 0, 1, stride=1, stride_axis=0)
            if q == 0:
                put(0, jnp.where(lanes >= rows, after, 0.0))
                put(REACH + 1, jnp.where(lanes > rows, after, 0.0))
            else:
                put(q, jnp.where(lanes >= rows, after, before))
            before = after
        return 0

    lax.fori_loop(0, DET, one, 0)


STRAIGHT = (((1,), (0,)), ((), ()))
CROSSED = (((1,), (1,)), ((), ()))


def filter_kernel(
    part_ref, noise_ref, out_ref, land, ext, filt, lags, t_hi, t_lo,
    store_sem, send, recv, halo_send, halo_recv, back_send, back_recv,
):
    det, tm, y, z, x = place()
    total_tm = NY * NZ * NX
    mine = y * NX + x
    prior, later = (tm + total_tm - 1) % total_tm, (tm + 1) % total_tm

    def slot(k, sign):
        dy, dx = PEERS[k]
        return ((y + sign * dy + NY) % NY) * NX + (x + dx) % NX

    peers = [(det, tm_of((y + dy) % NY, z, (x + dx) % NX)) for dy, dx in PEERS]
    greet(peers + [(det, later), (det, prior)])
    sends = []

    def part_copy(c, k):
        rows = pl.ds(c * SENT, SENT)
        return remote(part_ref.at[slot(k, 1), rows], land.at[k, rows], send.at[k, c], recv.at[k, c], peers[k])

    def halo_copies(c):
        rows = pl.ds(c * SENT, SENT)
        return (
            remote(
                ext.at[rows, pl.ds(REACH, REACH), :], ext.at[rows, pl.ds(REACH + RUNS, REACH), :],
                halo_send.at[0, c], halo_recv.at[0, c], (det, prior),
            ),
            remote(
                ext.at[rows, pl.ds(RUNS, REACH), :], ext.at[rows, pl.ds(0, REACH), :],
                halo_send.at[1, c], halo_recv.at[1, c], (det, later),
            ),
        )

    for c in range(DET // SENT):
        for k in range(NB - 1):
            copy = part_copy(c, k)
            copy.start()
            sends.append(copy)
    toeplitz(noise_ref, lags, t_hi, t_lo)

    def gathered(c):
        rows = slice(c * SENT, (c + 1) * SENT)
        total = part_ref[mine, rows]
        for k in range(NB - 1):
            part_copy(c, k).wait_recv()
            total = total + land[k, rows]
        ext[rows, REACH : REACH + RUNS, :] = total
        for copy in halo_copies(c):
            copy.start()
            sends.append(copy)

    first, last = tm == 0, tm == total_tm - 1

    def product(left, right, crossed):
        return lax.dot_general(left, right, CROSSED if crossed else STRAIGHT, preferred_element_type=jnp.float32)

    back, own_copies = [], []

    def back_copy(c, k, source):
        rows = pl.ds(c * SENT, SENT)
        return remote(filt.at[rows], out_ref.at[source, rows], back_send.at[k, c], back_recv.at[k, c], peers[k])

    def send_back(c):
        for k in range(NB - 1):
            copy = back_copy(c, k, mine)
            copy.start()
            back.append(copy)
        rows = pl.ds(c * SENT, SENT)
        copy = pltpu.make_async_copy(filt.at[rows], out_ref.at[mine, rows], store_sem.at[c])
        copy.start()
        own_copies.append(copy)

    def filtered(c):
        for copy in halo_copies(c):
            copy.wait_recv()
        dets = range(c * SENT, (c + 1) * SENT)
        lines = [
            jnp.concatenate(
                [
                    jnp.where(first, 0.0, ext[d, :REACH]),
                    ext[d, REACH : REACH + RUNS],
                    jnp.where(last, 0.0, ext[d, REACH + RUNS :]),
                ],
                axis=0,
            )
            for d in dets
        ]
        full = [jnp.zeros((2 * RUNS, LANE), jnp.float32) for d in dets]
        fine = [jnp.zeros((RUNS, LANE), jnp.float32) for d in dets]
        for m in range(2 * REACH + 1):
            q = REACH - m
            for i, d in enumerate(dets):
                window = lines[i][m : m + RUNS]
                high = window.astype(jnp.bfloat16)
                low = (window - high.astype(jnp.float32)).astype(jnp.bfloat16)
                stack = jnp.concatenate([high, low], axis=0)
                for index, crossed in [(q, False)] if q > 0 else [(-q, True)] if q < 0 else [(0, False), (REACH + 1, True)]:
                    full[i] += product(stack, t_hi[d, index], crossed)
                    fine[i] += product(high, t_lo[d, index], crossed)
        for i, d in enumerate(dets):
            filt[d] = full[i][:RUNS] + full[i][RUNS:] + fine[i]
        send_back(c)

    chunks = DET // SENT
    gathered(0)
    gathered(1)
    for c in range(chunks):
        filtered(c)
        if c + 2 < chunks:
            gathered(c + 2)
    for copy in own_copies:
        copy.wait()
    for c in range(DET // SENT):
        for k, peer in enumerate(peers):
            back_copy(c, k, slot(k, -1)).wait_recv()
    for copy in sends + back:
        copy.wait_send()


def filtered_of(partial, noise_coef):
    f32, bf = jnp.float32, jnp.bfloat16
    block = (DET, RUNS, LANE)
    matrices = (DET, REACH + 2, LANE, LANE)
    return pl.pallas_call(
        filter_kernel,
        out_shape=jax.ShapeDtypeStruct((NB, *block), f32),
        in_specs=[VM, VM],
        out_specs=ANY,
        scratch_shapes=[
            pltpu.VMEM((NB - 1, *block), f32),
            pltpu.VMEM((DET, RUNS + 2 * REACH, LANE), f32),
            pltpu.VMEM(block, f32),
            pltpu.VMEM((REACH + 1, DET, LANE), f32),
            pltpu.VMEM(matrices, bf),
            pltpu.VMEM(matrices, bf),
            DMA((DET // SENT,)),
            DMA((NB, DET // SENT)),
            DMA((NB, DET // SENT)),
            DMA((2, DET // SENT)),
            DMA((2, DET // SENT)),
            DMA((NB, DET // SENT)),
            DMA((NB, DET // SENT)),
        ],
        compiler_params=pltpu.CompilerParams(collective_id=1, has_side_effects=True, vmem_limit_bytes=GRANT),
        name="filter",
    )(partial, noise_coef)


CHUNKS = [(t, p) for t in range(TILE_DEV) for p in range(3)]
HALF_Z = NZ // 2
WIRE = jnp.bfloat16
OFFSETS = [4, 3, -3, 2, -2, 1, -1, 0]


def collect_kernel(
    acc_ref, out_ref, land_core, packet, land, land_last, land_own,
    core_send, core_recv, ring_send, ring_recv, last_send, last_recv, hi_send, hi_recv,
):
    f32 = jnp.float32
    det, tm, y, z, x = place()
    core, hi = det % 2, det // 2
    partner, across = core_of(det), hi_of(det)
    right, left = tm_of(y, (z + 1) % NZ, x), tm_of(y, (z + NZ - 1) % NZ, x)
    neighbours = ((det, right), (det, left))
    greet([(partner, tm), (across, tm), *neighbours, (across, right), (across, left)])
    started = []

    def start(copy):
        copy.start()
        started.append(copy)

    for k, offset in enumerate(OFFSETS):
        start(
            remote(
                acc_ref.at[(z + offset + NZ) % NZ, :, :, :, 1 - core], land_core.at[k], core_send.at[k], core_recv.at[k],
                (partner, tm),
            )
        )

    def ring(direction, step, c):
        t, p = CHUNKS[c]
        sign = 1 if direction == 0 else -1
        k = OFFSETS.index(sign * (HALF_Z - step)) if step else 0
        return remote(
            packet.at[k, t, p], land.at[direction, step, t, p],
            ring_send.at[direction, step, c], ring_recv.at[direction, step, c], neighbours[direction],
        )

    def last_hop(direction, c, crossing):
        t, p = CHUNKS[c]
        k = OFFSETS.index(1 if direction == 0 else -1)
        goal = (right, left)[direction]
        return remote(
            packet.at[k, t, p, 1 - hi if crossing else hi], land_last.at[crossing, direction, t, p],
            last_send.at[crossing, direction, c], last_recv.at[crossing, direction, c],
            (across if crossing else det, goal),
        )

    def own_copy(t):
        return remote(packet.at[len(OFFSETS) - 1, t, :, 1 - hi], land_own.at[t], hi_send.at[t], hi_recv.at[t], (across, tm))

    def own(k, t, p):
        return acc_ref[(z + OFFSETS[k] + NZ) % NZ, t, p, :, core]

    def swapped(k):
        remote(acc_ref.at[0, :, :, :, 0], land_core.at[k], core_send.at[k], core_recv.at[k], (partner, tm)).wait_recv()

    swapped(0)
    for direction in (0, 1):
        for c, (t, p) in enumerate(CHUNKS):
            if t == direction:
                packet[0, t, p] = (own(0, t, p) + land_core[0, t, p]).astype(WIRE)
    for p in range(3):
        for direction in (0, 1):
            start(ring(direction, 0, direction * 3 + p))
    last = len(OFFSETS) - 1
    for step in range(1, HALF_Z):
        keys = [OFFSETS.index(HALF_Z - step), OFFSETS.index(step - HALF_Z)]
        for k in keys:
            swapped(k)
        for i in range(len(CHUNKS)):
            for direction in (0, 1):
                c = (i + 3 * (1 - direction)) % len(CHUNKS) if step == 1 else i
                t, p = CHUNKS[c]
                k = keys[direction]
                value = own(k, t, p) + land_core[k, t, p]
                if step > 1 or t == direction:
                    ring(direction, step - 1, c).wait_recv()
                    value = value + land[direction, step - 1, t, p].astype(f32)
                packet[k, t, p] = value.astype(WIRE)
                if step < HALF_Z - 1:
                    start(ring(direction, step, c))
                else:
                    start(last_hop(direction, c, 1))
                    start(last_hop(direction, c, 0))
        if step == 1:
            swapped(last)
            for t in range(TILE_DEV):
                for p in range(3):
                    value = own(last, t, p) + land_core[last, t, p]
                    packet[last, t, p] = value.astype(WIRE)
                    land_core[last, t, p] = value
                start(own_copy(t))
    for t in range(TILE_DEV):
        own_copy(t).wait_recv()
    for c, (t, p) in enumerate(CHUNKS):
        value = land_core[last, t, p, hi] + land_own[t, p].astype(f32)
        for crossing in (0, 1):
            for direction in (0, 1):
                last_hop(direction, c, crossing).wait_recv()
                value = value + land_last[crossing, direction, t, p].astype(f32)
        out_ref[t, p] = value
    for copy in started:
        copy.wait_send()


def collect(acc):
    f32 = jnp.float32
    half = (TILE_DEV, 3, 2, STRIP, PIX)
    quarter = (TILE_DEV, 3, STRIP, PIX)
    return pl.pallas_call(
        collect_kernel,
        out_shape=jax.ShapeDtypeStruct(quarter, f32),
        in_specs=[VM],
        out_specs=VM,
        scratch_shapes=[
            pltpu.VMEM((NZ, *half), f32),
            pltpu.VMEM((NZ, *half), WIRE),
            pltpu.VMEM((2, HALF_Z - 1, *half), WIRE),
            pltpu.VMEM((2, 2, *quarter), WIRE),
            pltpu.VMEM(quarter, WIRE),
            DMA((NZ,)),
            DMA((NZ,)),
            DMA((2, HALF_Z - 1, 6)),
            DMA((2, HALF_Z - 1, 6)),
            DMA((2, 2, 6)),
            DMA((2, 2, 6)),
            DMA((2,)),
            DMA((2,)),
        ],
        compiler_params=pltpu.CompilerParams(collective_id=2, has_side_effects=True, vmem_limit_bytes=GRANT),
        name="collect",
    )(acc.reshape(NZ, TILE_DEV, 3, 2, 2, STRIP, PIX))


def body(
    sky_map, tile_home, piece_tiles, run_slot, hit_row, hit_col, frac_row, frac_col, angle, noise_coef
):
    pack = packed(
        tile_home, piece_tiles.reshape(1, LISTED), run_slot, hit_row, hit_col, frac_row, frac_col, angle,
        sky_map.reshape(TILE_DEV * 3 * STRIP, PIX),
    )
    tiles, samples, order = gather_all(pack)
    partial, turns = forward(
        order, tiles.reshape(NZ, N_STRIP, TILE_DEV, 3 * STRIP, PIX), samples
    )
    filtered = filtered_of(partial, noise_coef)
    acc = backward(order, samples, turns, filtered)
    return collect(acc)


def solution(mesh):
    placed = (
        P("tm", None, "det", None),
        P(),
        P("det", "tm", None),
        P("det", "tm"),
        P("det", "tm"),
        P("det", "tm"),
        P("det", "tm"),
        P("det", "tm"),
        P("det", "tm"),
        P("det", None),
    )
    return jax.shard_map(
        body, mesh=mesh, in_specs=placed, out_specs=P("tm", None, "det", None), check_vma=False
    )
```

```python
import functools

import jax
import jax.numpy as jnp
from jax import lax
from jax.experimental import pallas as pl
from jax.experimental.pallas import tpu as pltpu
from jax.sharding import PartitionSpec as P

GRANT = 24 << 20
MESH = pl.DeviceIdType.MESH
NY, NZ, NX = 4, 8, 2
NB = NY * NX
DET, RUNS, LANE = 8, 16, 128
PIX = 128
STRIP = 32
N_STRIP = 4
LISTED = 32
TILE_DEV = 2
REACH = 8
UNROLL = 16
HALF = 16
SENT = 4
PIECE_RUNS = DET * RUNS
ALL_RUNS = NB * PIECE_RUNS
SAMPLE_ROWS = 6 * PIECE_RUNS
ANY = pl.BlockSpec(memory_space=pl.ANY)
VM = pl.BlockSpec(memory_space=pltpu.VMEM)
SM = pl.BlockSpec(memory_space=pltpu.SMEM)
DMA = pltpu.SemaphoreType.DMA
PEERS = [(dy, dx) for dy in range(NY) for dx in range(NX) if (dy, dx) != (0, 0)]


def place():
    det, tm = lax.axis_index("det"), lax.axis_index("tm")
    y, z, x = tm // (NZ * NX), (tm // NX) % NZ, tm % NX
    return det, tm, y, z, x


def tm_of(y, z, x):
    return (y * NZ + z) * NX + x


def core_of(det):
    return det + 1 - 2 * (det % 2)


def hi_of(det):
    return (det + 2) % 4


def greet(peers):
    barrier = pltpu.get_barrier_semaphore()
    for peer in peers:
        pl.semaphore_signal(barrier, inc=1, device_id=peer, device_id_type=MESH)
    pl.semaphore_wait(barrier, len(peers))


def remote(src, dst, send, recv, peer):
    return pltpu.make_async_remote_copy(
        src_ref=src, dst_ref=dst, send_sem=send, recv_sem=recv, device_id=peer, device_id_type=MESH
    )


def run_order(pos_ref, order_ref, y, x):
    f32, bf, i32 = jnp.float32, jnp.bfloat16, jnp.int32

    def iota(shape, dim):
        return lax.broadcasted_iota(i32, shape, dim)

    def whole(mask):
        return jnp.where(mask, 1.0, 0.0).astype(bf)

    def dot(left, right):
        return jnp.dot(left, right, preferred_element_type=f32)

    lanes, offset = iota((LANE, LANE), 1), iota((LANE, LANE), 0)
    spot = jnp.zeros((2 * DET, LANE), f32)
    for slot in range(NB):
        spot += dot(pos_ref[slot], whole((offset < RUNS) & (lanes == offset + slot * RUNS)))
    pos = spot[:DET].astype(i32)
    here = (pos // (TILE_DEV * NX * NZ) == y) & ((pos // TILE_DEV) % NX == x)
    tile = ((pos // (TILE_DEV * NX)) % NZ) * TILE_DEV + pos % TILE_DEV
    kinds, square = (2 * TILE_DEV * NZ, LANE), (LANE, LANE)
    kind = jnp.where(here, tile, TILE_DEV * NZ)
    tile = tile.astype(f32)
    before, every = whole(iota(square, 0) < iota(square, 1)), jnp.ones(square, bf)
    marks, prior, total = [], [], jnp.zeros(kinds, f32)
    for d in range(DET):
        mark = whole(jnp.broadcast_to(kind[d : d + 1], kinds) == iota(kinds, 0))
        marks.append(mark.astype(f32))
        prior.append(dot(mark, before) + total)
        total += dot(mark, every)
    lower = whole(iota((kinds[0], kinds[0]), 1) < iota((kinds[0], kinds[0]), 0))
    coarse = jnp.floor(total * (1.0 / 32.0))
    base = 32.0 * dot(lower, coarse.astype(bf)) + dot(lower, (total - 32.0 * coarse).astype(bf))
    high_rows, low_rows = iota((DET, LANE), 0).astype(f32), iota(square, 0).astype(f32)
    lane = iota((DET, LANE), 1).astype(f32)
    found = jnp.zeros((3 * DET, LANE), f32)
    for d in range(DET):
        rank = jnp.sum(marks[d] * (prior[d] + base), axis=0, keepdims=True)
        high = jnp.floor(rank * (1.0 / LANE))
        low = rank - LANE * high
        at = jnp.broadcast_to(high, (DET, LANE)) == high_rows
        values = (jnp.broadcast_to(tile[d : d + 1], (DET, LANE)), jnp.full((DET, LANE), float(d), f32), lane)
        left = jnp.concatenate([jnp.where(at, v, 0.0) for v in values], axis=0).astype(bf)
        right = whole(jnp.broadcast_to(low, square) == low_rows)
        found += lax.dot_general(left, right, (((1,), (1,)), ((), ())), preferred_element_type=f32)
    entry = found[:DET] * ALL_RUNS + found[DET : 2 * DET] * LANE + found[2 * DET :]
    order_ref[:DET, :] = entry.astype(i32)
    others = total[TILE_DEV * NZ : TILE_DEV * NZ + 1]
    order_ref[DET:, :] = jnp.broadcast_to(ALL_RUNS - others, (DET, LANE)).astype(i32)


def pack_kernel(home_ref, piece_ref, slot_ref, row_ref, col_ref, low_ref, high_ref, angle_ref, q_ref, out_ref):
    f32, bf = jnp.float32, jnp.bfloat16
    for r in range(RUNS):
        at = slice(r * LANE, (r + 1) * LANE)
        angle = angle_ref[:, at]
        coarse = angle.astype(bf)
        fine = (angle - coarse.astype(f32)).astype(bf)
        row, col = row_ref[:, at].astype(f32).astype(bf), col_ref[:, at].astype(f32).astype(bf)
        for part, value in enumerate((row, col, coarse, fine, low_ref[:, at], high_ref[:, at])):
            out_ref[part * PIECE_RUNS + r * DET : part * PIECE_RUNS + (r + 1) * DET] = value
    slots = slot_ref[...]
    position = jnp.zeros(slots.shape, f32)
    for s in range(LISTED):
        position = jnp.where(slots == s, home_ref[piece_ref[0, s]].astype(f32), position)
    wide = jnp.concatenate([position, jnp.zeros((DET, LANE - RUNS), f32)], axis=1)
    out_ref[SAMPLE_ROWS : SAMPLE_ROWS + 2 * DET] = jnp.concatenate([wide, jnp.zeros_like(wide)], axis=0).astype(bf)
    out_ref[SAMPLE_ROWS + 2 * DET :] = q_ref[...]


def packed(tile_home, piece_list, run_slot, hit_row, hit_col, frac_row, frac_col, angle, quarter):
    return pl.pallas_call(
        pack_kernel,
        out_shape=jax.ShapeDtypeStruct((SAMPLE_ROWS + 2 * DET + quarter.shape[0], LANE), jnp.bfloat16),
        in_specs=[SM, SM] + [VM] * 7,
        out_specs=VM,
        name="pack",
    )(tile_home, piece_list, run_slot, hit_row, hit_col, frac_row, frac_col, angle, quarter)


def gather_kernel(
    pack_ref,
    tiles_ref, all_ref, order_ref,
    pos_all, store_sem,
    pos_send, pos_recv, block_send, block_recv, strip_send, strip_recv, core_send, core_recv, hi_send, hi_recv,
):
    det, tm, y, z, x = place()
    partner, across = core_of(det), hi_of(det)
    ahead, behind = (y + 1) % NY, (y + NY - 1) % NY
    facing = (y + NY // 2) % NY
    other = 1 - x
    up, down, side = (det, tm_of(ahead, z, x)), (det, tm_of(behind, z, x)), (det, tm_of(y, z, other))
    far = [(det, tm_of((y + dy) % NY, z, (x + dx) % NX)) for dy, dx in PEERS]

    def along(direction, jump):
        return (det, tm_of(y, (z + jump) % NZ if direction == 0 else (z + NZ - jump) % NZ, x))

    samples_ref, p_ref = pack_ref.at[pl.ds(0, SAMPLE_ROWS)], pack_ref.at[pl.ds(SAMPLE_ROWS, 2 * DET)]
    q_ref = pack_ref.at[pl.ds(SAMPLE_ROWS + 2 * DET, TILE_DEV * 3 * STRIP)]

    def strip(slot, d):
        return tiles_ref.at[slot, d]

    def block(slot, part):
        return all_ref.at[slot, pl.ds(part * 2 * PIECE_RUNS, 2 * PIECE_RUNS)]

    def own_block(part):
        return pack_ref.at[pl.ds(part * 2 * PIECE_RUNS, 2 * PIECE_RUNS)]

    mine = y * NX + x
    greet([along(d, j) for d in (0, 1) for j in (1, 2)] + [(partner, tm), (across, tm)] + far)

    started = []

    def start(copy):
        copy.start()
        started.append(copy)

    start(remote(q_ref, strip(z, det), hi_send, hi_recv, (across, tm)))

    def send_block(link, slot, part, peer, own=False):
        start(
            remote(
                own_block(part) if own else block(slot, part), block(slot, part),
                block_send.at[link, part], block_recv.at[link, part], peer,
            )
        )

    def wait_block(link, slot, part):
        remote(own_block(part), block(slot, part), block_send.at[link, part], block_recv.at[link, part], side).wait_recv()

    owner = (det, across)

    def source_slot(direction, distance):
        return (z + NZ - distance) % NZ if direction == 0 else (z + distance) % NZ

    def send_strip(half, direction, distance):
        slot = z if distance < 3 else source_slot(direction, 2)
        here = strip(slot, owner[half])
        start(
            remote(
                q_ref if half == 0 and distance < 3 else here, here,
                strip_send.at[half, direction, distance - 1], strip_recv.at[half, direction, distance - 1],
                along(direction, 2 - distance % 2),
            )
        )

    def reach(half, direction):
        return NZ // 2 if half == direction else NZ // 2 - 1

    def to_partner(half, index, slot):
        here = strip(slot, owner[half])
        start(
            remote(
                q_ref if half == 0 and index == 0 else here, here, core_send.at[half, index], core_recv.at[half, index],
                (partner, tm),
            )
        )

    def take_strip(half, distance):
        for direction in (0, 1):
            if distance <= reach(half, direction):
                slot = source_slot(direction, distance)
                remote(
                    q_ref, strip(slot, owner[half]),
                    strip_send.at[half, direction, distance - 1], strip_recv.at[half, direction, distance - 1], side,
                ).wait_recv()
                if distance == 2:
                    if reach(half, direction) == 4:
                        send_strip(half, direction, 4)
                    send_strip(half, direction, 3)
                to_partner(half, direction * NZ // 2 + distance, slot)

    def first_strips(half):
        for distance in (2, 1):
            for direction in (0, 1):
                send_strip(half, direction, distance)
        to_partner(half, 0, z)

    for k, peer in enumerate(far):
        start(remote(p_ref, pos_all.at[mine], pos_send.at[k], pos_recv.at[k], peer))
    first_strips(0)
    for part in range(3):
        send_block(1, mine, part, up, True)
        send_block(2, mine, part, down, True)
        send_block(0, mine, part, side, True)
    stores = []
    for i, (src, dst) in enumerate(
        ((q_ref, strip(z, det)), (samples_ref, all_ref.at[mine]), (p_ref, pos_all.at[mine]))
    ):
        copy = pltpu.make_async_copy(src, dst, store_sem.at[i])
        copy.start()
        stores.append(copy)

    slot_of = {1: behind * NX + x, 2: ahead * NX + x, 0: y * NX + other, 5: facing * NX + x, 6: facing * NX + other,
               3: behind * NX + other, 4: ahead * NX + other}

    def near(part):
        for link in (1, 2, 0):
            wait_block(link, slot_of[link], part)
            if link == 1 and part != 1:
                send_block(5, slot_of[1], part, up)
            if link == 2 and part == 1:
                send_block(5, slot_of[2], part, down)
            if link == 1 and part == 2:
                send_block(3, slot_of[1], part, side)
            if link == 0:
                if part != 2:
                    send_block(3, slot_of[0], part, up)
                send_block(4, slot_of[0], part, down)

    def opposite(part):
        wait_block(5, slot_of[5], part)
        send_block(6, slot_of[5], part, side)

    stores[2].wait()
    for k, peer in enumerate(far):
        remote(p_ref, pos_all.at[mine], pos_send.at[k], pos_recv.at[k], peer).wait_recv()
    run_order(pos_all, order_ref, y, x)

    near(0)
    remote(q_ref, strip(z, across), hi_send, hi_recv, (across, tm)).wait_recv()
    first_strips(1)
    take_strip(0, 2)
    near(1)
    near(2)
    take_strip(0, 1)
    opposite(0)
    take_strip(1, 2)
    opposite(1)
    opposite(2)
    take_strip(1, 1)
    take_strip(0, 3)
    take_strip(0, 4)

    take_strip(1, 3)
    take_strip(1, 4)
    for part in range(3):
        for link in (3, 4, 6):
            wait_block(link, slot_of[link], part)
    theirs = (partner, hi_of(partner))
    for half in (0, 1):
        places = [(0, z)]
        for direction in (0, 1):
            for distance in range(1, reach(half, direction) + 1):
                places.append((direction * NZ // 2 + distance, source_slot(direction, distance)))
        for index, slot in places:
            remote(
                q_ref, strip(slot, theirs[half]), core_send.at[half, index], core_recv.at[half, index], (partner, tm)
            ).wait_recv()
    for copy in stores[:2]:
        copy.wait()
    for copy in started:
        copy.wait_send()


def gather_all(pack):
    bf, i32 = jnp.bfloat16, jnp.int32
    return pl.pallas_call(
        gather_kernel,
        out_shape=(
            jax.ShapeDtypeStruct((NZ, N_STRIP, TILE_DEV * 3 * STRIP, PIX), bf),
            jax.ShapeDtypeStruct((NB, SAMPLE_ROWS, LANE), bf),
            jax.ShapeDtypeStruct((2 * DET, LANE), i32),
        ),
        in_specs=[ANY],
        out_specs=(ANY, ANY, VM),
        scratch_shapes=[
            pltpu.VMEM((NB, 2 * DET, LANE), bf),
            DMA((3,)),
            DMA((NB,)),
            DMA((NB,)),
            DMA((7, 3)),
            DMA((7, 3)),
            DMA((2, 2, NZ // 2)),
            DMA((2, 2, NZ // 2)),
            DMA((2, NZ + 1)),
            DMA((2, NZ + 1)),
            DMA,
            DMA,
        ],
        compiler_params=pltpu.CompilerParams(collective_id=0, has_side_effects=True, vmem_limit_bytes=GRANT),
        name="gather_all",
    )(pack)


def sin_cos(v):
    quarter = jnp.round(v * 0.6366197723675814)
    u = v - quarter * 1.5703125
    u = u - quarter * 4.837512969970703e-4
    u = u - quarter * 7.549789948768648e-8
    u2 = u * u
    s = u + u * u2 * (-1.6666654611e-1 + u2 * (8.3321608736e-3 + u2 * -1.9515295891e-4))
    c = 1.0 - 0.5 * u2 + u2 * u2 * (4.166664568298827e-2 + u2 * (-1.388731625493765e-3 + u2 * 2.443315711809948e-5))
    q = quarter.astype(jnp.int32) & 3
    odd = (q & 1) == 1
    sin = jnp.where(odd, c, s)
    cos = jnp.where(odd, s, c)
    sin = jnp.where(q >= 2, -sin, sin)
    cos = jnp.where((q == 1) | (q == 2), -cos, cos)
    return sin, cos


def low_of(high):
    return (1.0 - high).astype(jnp.bfloat16).astype(jnp.float32)


def run_of(entry):
    run = entry & (ALL_RUNS - 1)
    return entry >> 10, (run >> 4) & (NB - 1), run >> 7, run & (RUNS - 1)


def spread(index, low, high, rows):
    bf = jnp.bfloat16
    wide = [jnp.broadcast_to(v, (HALF, LANE)).astype(bf) for v in (index, index + 1.0, low, high)]
    zero = jnp.zeros((HALF, LANE), bf)
    parts = []
    for b in range(PIX // HALF):
        row = rows[b * HALF : (b + 1) * HALF]
        parts.append(jnp.where(row == wide[0], wide[2], jnp.where(row == wide[1], wide[3], zero)))
    return jnp.concatenate(parts, axis=0)


def samples_of(all_ref, z, part):
    rows = slice(part * 2 * PIECE_RUNS, (part + 1) * 2 * PIECE_RUNS)
    return all_ref[z, rows].astype(jnp.float32).reshape(2, RUNS, DET, LANE)


def forward_kernel(list_ref, tiles_ref, all_ref, sig_ref, cs_ref, hit_ref, frac_ref):
    def prepare(z, _):
        hit_ref[z] = samples_of(all_ref, z, 0)
        halves = samples_of(all_ref, z, 1)
        sin, cos = sin_cos(2.0 * (halves[0] + halves[1]))
        cs_ref[z, 0] = cos
        cs_ref[z, 1] = sin
        frac_ref[z] = samples_of(all_ref, z, 2)
        sig_ref[z] = jnp.zeros_like(sig_ref[z])
        return 0

    lax.fori_loop(0, NB, prepare, 0)
    count = list_ref[DET, 0]
    rows = lax.broadcasted_iota(jnp.int32, (PIX, LANE), 0).astype(jnp.float32).astype(jnp.bfloat16)

    def body(step, _):
        for u in range(UNROLL):
            n = step * UNROLL + u
            tile, z, d, r = run_of(list_ref[n >> 7, n & (LANE - 1)])
            at = (r, pl.ds(d, 1), slice(None))
            col_high = frac_ref[z, 1, *at]
            row_high = frac_ref[z, 0, *at]
            col_weight = spread(hit_ref[z, 1, *at], low_of(col_high), col_high, rows)
            row_weight = spread(hit_ref[z, 0, *at], low_of(row_high), row_high, rows).astype(jnp.float32)
            rows_of_tile = jnp.concatenate([tiles_ref[tile // TILE_DEV, k, tile % TILE_DEV] for k in range(N_STRIP)], axis=0)
            partial = jnp.dot(rows_of_tile, col_weight, preferred_element_type=jnp.float32)
            value = []
            for p in range(3):
                terms = [
                    partial[(k * 3 + p) * STRIP : (k * 3 + p + 1) * STRIP] * row_weight[k * STRIP : (k + 1) * STRIP]
                    for k in range(N_STRIP)
                ]
                value.append(jnp.sum(sum(terms[1:], terms[0]), axis=0, keepdims=True))
            total = value[0] + cs_ref[z, 0, *at] * value[1] + cs_ref[z, 1, *at] * value[2]
            sig_ref[z, d, pl.ds(r, 1), :] = jnp.where(n < count, total, 0.0)
        return 0

    lax.fori_loop(0, (count + UNROLL - 1) // UNROLL, body, 0)


def forward(order, tiles, samples):
    f32 = jnp.float32
    block = (NB, DET, RUNS, LANE)
    pair = (NB, 2, RUNS, DET, LANE)
    return pl.pallas_call(
        forward_kernel,
        out_shape=(jax.ShapeDtypeStruct(block, f32), jax.ShapeDtypeStruct(pair, f32)),
        in_specs=[SM, VM, VM],
        out_specs=(VM, VM),
        scratch_shapes=[pltpu.VMEM(pair, f32), pltpu.VMEM(pair, f32)],
        compiler_params=pltpu.CompilerParams(vmem_limit_bytes=GRANT),
        name="forward",
    )(order, tiles, samples)


def backward_kernel(list_ref, all_ref, cs_ref, filt_ref, acc_ref, hit_ref, frac_ref):
    def prepare(z, _):
        hit_ref[z] = samples_of(all_ref, z, 0)
        frac_ref[z] = samples_of(all_ref, z, 2)
        return 0

    lax.fori_loop(0, NB, prepare, 0)

    def clear(t, _):
        acc_ref[t] = jnp.zeros_like(acc_ref[t])
        return 0

    lax.fori_loop(0, TILE_DEV * NZ, clear, 0)
    count = list_ref[DET, 0]
    rows = lax.broadcasted_iota(jnp.int32, (PIX, LANE), 0).astype(jnp.float32).astype(jnp.bfloat16)

    def body(step, _):
        for u in range(UNROLL):
            k = step * UNROLL + u
            tile, z, d, r = run_of(list_ref[k >> 7, k & (LANE - 1)])
            at = (r, pl.ds(d, 1), slice(None))
            col_high = frac_ref[z, 1, *at]
            row_high = frac_ref[z, 0, *at]
            row_low = low_of(row_high)
            col_weight = spread(hit_ref[z, 1, *at], low_of(col_high), col_high, rows)
            filt = jnp.where(k < count, filt_ref[z, d, pl.ds(r, 1), :], 0.0)
            hit = hit_ref[z, 0, *at]
            parts = []
            for p in range(3):
                scaled = filt if p == 0 else cs_ref[z, p - 1, *at] * filt
                parts.append(spread(hit, scaled * row_low, scaled * row_high, rows))
            weighted = jnp.concatenate(parts, axis=0)
            acc_ref[tile] += lax.dot_general(
                weighted, col_weight, (((1,), (1,)), ((), ())), preferred_element_type=jnp.float32
            )
        return 0

    lax.fori_loop(0, (count + UNROLL - 1) // UNROLL, body, 0)


def backward(order, samples, turns, filtered):
    f32 = jnp.float32
    pair = (NB, 2, RUNS, DET, LANE)
    return pl.pallas_call(
        backward_kernel,
        out_shape=jax.ShapeDtypeStruct((TILE_DEV * NZ, 3 * PIX, PIX), f32),
        in_specs=[SM, VM, VM, VM],
        out_specs=VM,
        scratch_shapes=[pltpu.VMEM(pair, f32), pltpu.VMEM(pair, f32)],
        compiler_params=pltpu.CompilerParams(vmem_limit_bytes=GRANT),
        name="backward",
    )(order, samples, turns, filtered)


def toeplitz(noise_ref, line_ref, hi_ref, lo_ref):
    square = (LANE, LANE)
    lanes = lax.broadcasted_iota(jnp.int32, square, 1)
    rows = lax.broadcasted_iota(jnp.int32, square, 0)
    first = lax.broadcasted_iota(jnp.int32, (DET, LANE), 1) == 0
    for q in range(REACH):
        lags = noise_ref[:, q * LANE : (q + 1) * LANE]
        line_ref[q] = jnp.where(first, lags + 1.0, lags) if q == 0 else lags
    line_ref[REACH] = jnp.where(first, jnp.broadcast_to(noise_ref[:, REACH * LANE :], (DET, LANE)), 0.0)

    def one(d, _):
        def put(q, matrix):
            high = matrix.astype(jnp.bfloat16)
            hi_ref[d, q] = high
            lo_ref[d, q] = (matrix - high.astype(jnp.float32)).astype(jnp.bfloat16)

        before = None
        for q in range(REACH + 1):
            lags = line_ref[q, pl.ds(d, 1), :]
            after = pltpu.roll(jnp.broadcast_to(lags, square), 0, 1, stride=1, stride_axis=0)
            if q == 0:
                put(0, jnp.where(lanes >= rows, after, 0.0))
                put(REACH + 1, jnp.where(lanes > rows, after, 0.0))
            else:
                put(q, jnp.where(lanes >= rows, after, before))
            before = after
        return 0

    lax.fori_loop(0, DET, one, 0)


STRAIGHT = (((1,), (0,)), ((), ()))
CROSSED = (((1,), (1,)), ((), ()))


def filter_kernel(
    part_ref, noise_ref, out_ref, land, ext, filt, lags, t_hi, t_lo,
    store_sem, send, recv, halo_send, halo_recv, back_send, back_recv,
):
    det, tm, y, z, x = place()
    total_tm = NY * NZ * NX
    mine = y * NX + x
    prior, later = (tm + total_tm - 1) % total_tm, (tm + 1) % total_tm

    def slot(k, sign):
        dy, dx = PEERS[k]
        return ((y + sign * dy + NY) % NY) * NX + (x + dx) % NX

    peers = [(det, tm_of((y + dy) % NY, z, (x + dx) % NX)) for dy, dx in PEERS]
    greet(peers + [(det, later), (det, prior)])
    sends = []

    def part_copy(c, k):
        rows = pl.ds(c * SENT, SENT)
        return remote(part_ref.at[slot(k, 1), rows], land.at[k, rows], send.at[k, c], recv.at[k, c], peers[k])

    def halo_copies(c):
        rows = pl.ds(c * SENT, SENT)
        return (
            remote(
                ext.at[rows, pl.ds(REACH, REACH), :], ext.at[rows, pl.ds(REACH + RUNS, REACH), :],
                halo_send.at[0, c], halo_recv.at[0, c], (det, prior),
            ),
            remote(
                ext.at[rows, pl.ds(RUNS, REACH), :], ext.at[rows, pl.ds(0, REACH), :],
                halo_send.at[1, c], halo_recv.at[1, c], (det, later),
            ),
        )

    for c in range(DET // SENT):
        for k in range(NB - 1):
            copy = part_copy(c, k)
            copy.start()
            sends.append(copy)
    toeplitz(noise_ref, lags, t_hi, t_lo)

    def gathered(c):
        rows = slice(c * SENT, (c + 1) * SENT)
        total = part_ref[mine, rows]
        for k in range(NB - 1):
            part_copy(c, k).wait_recv()
            total = total + land[k, rows]
        ext[rows, REACH : REACH + RUNS, :] = total
        for copy in halo_copies(c):
            copy.start()
            sends.append(copy)

    first, last = tm == 0, tm == total_tm - 1

    def product(left, right, crossed):
        return lax.dot_general(left, right, CROSSED if crossed else STRAIGHT, preferred_element_type=jnp.float32)

    back, own_copies = [], []

    def back_copy(c, k, source):
        rows = pl.ds(c * SENT, SENT)
        return remote(filt.at[rows], out_ref.at[source, rows], back_send.at[k, c], back_recv.at[k, c], peers[k])

    def send_back(c):
        for k in range(NB - 1):
            copy = back_copy(c, k, mine)
            copy.start()
            back.append(copy)
        rows = pl.ds(c * SENT, SENT)
        copy = pltpu.make_async_copy(filt.at[rows], out_ref.at[mine, rows], store_sem.at[c])
        copy.start()
        own_copies.append(copy)

    def filtered(c):
        for copy in halo_copies(c):
            copy.wait_recv()
        dets = range(c * SENT, (c + 1) * SENT)
        lines = [
            jnp.concatenate(
                [
                    jnp.where(first, 0.0, ext[d, :REACH]),
                    ext[d, REACH : REACH + RUNS],
                    jnp.where(last, 0.0, ext[d, REACH + RUNS :]),
                ],
                axis=0,
            )
            for d in dets
        ]
        full = [jnp.zeros((2 * RUNS, LANE), jnp.float32) for d in dets]
        fine = [jnp.zeros((RUNS, LANE), jnp.float32) for d in dets]
        for m in range(2 * REACH + 1):
            q = REACH - m
            for i, d in enumerate(dets):
                window = lines[i][m : m + RUNS]
                high = window.astype(jnp.bfloat16)
                low = (window - high.astype(jnp.float32)).astype(jnp.bfloat16)
                stack = jnp.concatenate([high, low], axis=0)
                for index, crossed in [(q, False)] if q > 0 else [(-q, True)] if q < 0 else [(0, False), (REACH + 1, True)]:
                    full[i] += product(stack, t_hi[d, index], crossed)
                    fine[i] += product(high, t_lo[d, index], crossed)
        for i, d in enumerate(dets):
            filt[d] = full[i][:RUNS] + full[i][RUNS:] + fine[i]
        send_back(c)

    chunks = DET // SENT
    gathered(0)
    gathered(1)
    for c in range(chunks):
        filtered(c)
        if c + 2 < chunks:
            gathered(c + 2)
    for copy in own_copies:
        copy.wait()
    for c in range(DET // SENT):
        for k, peer in enumerate(peers):
            back_copy(c, k, slot(k, -1)).wait_recv()
    for copy in sends + back:
        copy.wait_send()


def filtered_of(partial, noise_coef):
    f32, bf = jnp.float32, jnp.bfloat16
    block = (DET, RUNS, LANE)
    matrices = (DET, REACH + 2, LANE, LANE)
    return pl.pallas_call(
        filter_kernel,
        out_shape=jax.ShapeDtypeStruct((NB, *block), f32),
        in_specs=[VM, VM],
        out_specs=ANY,
        scratch_shapes=[
            pltpu.VMEM((NB - 1, *block), f32),
            pltpu.VMEM((DET, RUNS + 2 * REACH, LANE), f32),
            pltpu.VMEM(block, f32),
            pltpu.VMEM((REACH + 1, DET, LANE), f32),
            pltpu.VMEM(matrices, bf),
            pltpu.VMEM(matrices, bf),
            DMA((DET // SENT,)),
            DMA((NB, DET // SENT)),
            DMA((NB, DET // SENT)),
            DMA((2, DET // SENT)),
            DMA((2, DET // SENT)),
            DMA((NB, DET // SENT)),
            DMA((NB, DET // SENT)),
        ],
        compiler_params=pltpu.CompilerParams(collective_id=1, has_side_effects=True, vmem_limit_bytes=GRANT),
        name="filter",
    )(partial, noise_coef)


CHUNKS = [(t, p) for t in range(TILE_DEV) for p in range(3)]
HALF_Z = NZ // 2
WIRE = jnp.bfloat16
OFFSETS = [4, 3, -3, 2, -2, 1, -1, 0]


def collect_kernel(
    acc_ref, out_ref, land_core, packet, land, land_last, land_own,
    core_send, core_recv, ring_send, ring_recv, last_send, last_recv, hi_send, hi_recv,
):
    f32 = jnp.float32
    det, tm, y, z, x = place()
    core, hi = det % 2, det // 2
    partner, across = core_of(det), hi_of(det)
    right, left = tm_of(y, (z + 1) % NZ, x), tm_of(y, (z + NZ - 1) % NZ, x)
    neighbours = ((det, right), (det, left))
    greet([(partner, tm), (across, tm), *neighbours, (across, right), (across, left)])
    started = []

    def start(copy):
        copy.start()
        started.append(copy)

    for k, offset in enumerate(OFFSETS):
        start(
            remote(
                acc_ref.at[(z + offset + NZ) % NZ, :, :, :, 1 - core], land_core.at[k], core_send.at[k], core_recv.at[k],
                (partner, tm),
            )
        )

    def ring(direction, step, c):
        t, p = CHUNKS[c]
        sign = 1 if direction == 0 else -1
        k = OFFSETS.index(sign * (HALF_Z - step)) if step else 0
        return remote(
            packet.at[k, t, p], land.at[direction, step, t, p],
            ring_send.at[direction, step, c], ring_recv.at[direction, step, c], neighbours[direction],
        )

    def last_hop(direction, c, crossing):
        t, p = CHUNKS[c]
        k = OFFSETS.index(1 if direction == 0 else -1)
        goal = (right, left)[direction]
        return remote(
            packet.at[k, t, p, 1 - hi if crossing else hi], land_last.at[crossing, direction, t, p],
            last_send.at[crossing, direction, c], last_recv.at[crossing, direction, c],
            (across if crossing else det, goal),
        )

    def own_copy(t):
        return remote(packet.at[len(OFFSETS) - 1, t, :, 1 - hi], land_own.at[t], hi_send.at[t], hi_recv.at[t], (across, tm))

    def own(k, t, p):
        return acc_ref[(z + OFFSETS[k] + NZ) % NZ, t, p, :, core]

    def swapped(k):
        remote(acc_ref.at[0, :, :, :, 0], land_core.at[k], core_send.at[k], core_recv.at[k], (partner, tm)).wait_recv()

    swapped(0)
    for direction in (0, 1):
        for c, (t, p) in enumerate(CHUNKS):
            if t == direction:
                packet[0, t, p] = (own(0, t, p) + land_core[0, t, p]).astype(WIRE)
    for p in range(3):
        for direction in (0, 1):
            start(ring(direction, 0, direction * 3 + p))
    last = len(OFFSETS) - 1
    for step in range(1, HALF_Z):
        keys = [OFFSETS.index(HALF_Z - step), OFFSETS.index(step - HALF_Z)]
        for k in keys:
            swapped(k)
        for i in range(len(CHUNKS)):
            for direction in (0, 1):
                c = (i + 3 * (1 - direction)) % len(CHUNKS) if step == 1 else i
                t, p = CHUNKS[c]
                k = keys[direction]
                value = own(k, t, p) + land_core[k, t, p]
                if step > 1 or t == direction:
                    ring(direction, step - 1, c).wait_recv()
                    value = value + land[direction, step - 1, t, p].astype(f32)
                packet[k, t, p] = value.astype(WIRE)
                if step < HALF_Z - 1:
                    start(ring(direction, step, c))
                else:
                    start(last_hop(direction, c, 1))
                    start(last_hop(direction, c, 0))
        if step == 1:
            swapped(last)
            for t in range(TILE_DEV):
                for p in range(3):
                    value = own(last, t, p) + land_core[last, t, p]
                    packet[last, t, p] = value.astype(WIRE)
                    land_core[last, t, p] = value
                start(own_copy(t))
    for t in range(TILE_DEV):
        own_copy(t).wait_recv()
    for c, (t, p) in enumerate(CHUNKS):
        value = land_core[last, t, p, hi] + land_own[t, p].astype(f32)
        for crossing in (0, 1):
            for direction in (0, 1):
                last_hop(direction, c, crossing).wait_recv()
                value = value + land_last[crossing, direction, t, p].astype(f32)
        out_ref[t, p] = value
    for copy in started:
        copy.wait_send()


def collect(acc):
    f32 = jnp.float32
    half = (TILE_DEV, 3, 2, STRIP, PIX)
    quarter = (TILE_DEV, 3, STRIP, PIX)
    return pl.pallas_call(
        collect_kernel,
        out_shape=jax.ShapeDtypeStruct(quarter, f32),
        in_specs=[VM],
        out_specs=VM,
        scratch_shapes=[
            pltpu.VMEM((NZ, *half), f32),
            pltpu.VMEM((NZ, *half), WIRE),
            pltpu.VMEM((2, HALF_Z - 1, *half), WIRE),
            pltpu.VMEM((2, 2, *quarter), WIRE),
            pltpu.VMEM(quarter, WIRE),
            DMA((NZ,)),
            DMA((NZ,)),
            DMA((2, HALF_Z - 1, 6)),
            DMA((2, HALF_Z - 1, 6)),
            DMA((2, 2, 6)),
            DMA((2, 2, 6)),
            DMA((2,)),
            DMA((2,)),
        ],
        compiler_params=pltpu.CompilerParams(collective_id=2, has_side_effects=True, vmem_limit_bytes=GRANT),
        name="collect",
    )(acc.reshape(NZ, TILE_DEV, 3, 2, 2, STRIP, PIX))


def body(
    sky_map, tile_home, piece_tiles, run_slot, hit_row, hit_col, frac_row, frac_col, angle, noise_coef
):
    pack = packed(
        tile_home, piece_tiles.reshape(1, LISTED), run_slot, hit_row, hit_col, frac_row, frac_col, angle,
        sky_map.reshape(TILE_DEV * 3 * STRIP, PIX),
    )
    tiles, samples, order = gather_all(pack)
    partial, turns = forward(
        order, tiles.reshape(NZ, N_STRIP, TILE_DEV, 3 * STRIP, PIX), samples
    )
    filtered = filtered_of(partial, noise_coef)
    acc = backward(order, samples, turns, filtered)
    return collect(acc)


def solution(mesh):
    placed = (
        P("tm", None, "det", None),
        P(),
        P("det", "tm", None),
        P("det", "tm"),
        P("det", "tm"),
        P("det", "tm"),
        P("det", "tm"),
        P("det", "tm"),
        P("det", "tm"),
        P("det", None),
    )
    return jax.shard_map(
        body, mesh=mesh, in_specs=placed, out_specs=P("tm", None, "det", None), check_vma=False
    )
```

```python
import functools

import jax
import jax.numpy as jnp
from jax import lax
from jax.experimental import pallas as pl
from jax.experimental.pallas import tpu as pltpu
from jax.sharding import PartitionSpec as P

GRANT = 24 << 20
MESH = pl.DeviceIdType.MESH
NY, NZ, NX = 4, 8, 2
NB = NY * NX
DET, RUNS, LANE = 8, 16, 128
PIX = 128
STRIP = 32
N_STRIP = 4
LISTED = 32
TILE_DEV = 2
REACH = 8
UNROLL = 16
HALF = 16
SENT = 4
PIECE_RUNS = DET * RUNS
ALL_RUNS = NB * PIECE_RUNS
SAMPLE_ROWS = 6 * PIECE_RUNS
ANY = pl.BlockSpec(memory_space=pl.ANY)
VM = pl.BlockSpec(memory_space=pltpu.VMEM)
SM = pl.BlockSpec(memory_space=pltpu.SMEM)
DMA = pltpu.SemaphoreType.DMA
PEERS = [(dy, dx) for dy in range(NY) for dx in range(NX) if (dy, dx) != (0, 0)]


def place():
    det, tm = lax.axis_index("det"), lax.axis_index("tm")
    y, z, x = tm // (NZ * NX), (tm // NX) % NZ, tm % NX
    return det, tm, y, z, x


def tm_of(y, z, x):
    return (y * NZ + z) * NX + x


def core_of(det):
    return det + 1 - 2 * (det % 2)


def hi_of(det):
    return (det + 2) % 4


def greet(peers):
    barrier = pltpu.get_barrier_semaphore()
    for peer in peers:
        pl.semaphore_signal(barrier, inc=1, device_id=peer, device_id_type=MESH)
    pl.semaphore_wait(barrier, len(peers))


def remote(src, dst, send, recv, peer):
    return pltpu.make_async_remote_copy(
        src_ref=src, dst_ref=dst, send_sem=send, recv_sem=recv, device_id=peer, device_id_type=MESH
    )


def run_order(pos_ref, order_ref, y, x):
    f32, bf, i32 = jnp.float32, jnp.bfloat16, jnp.int32

    def iota(shape, dim):
        return lax.broadcasted_iota(i32, shape, dim)

    def whole(mask):
        return jnp.where(mask, 1.0, 0.0).astype(bf)

    def dot(left, right):
        return jnp.dot(left, right, preferred_element_type=f32)

    lanes, offset = iota((LANE, LANE), 1), iota((LANE, LANE), 0)
    spot = jnp.zeros((2 * DET, LANE), f32)
    for slot in range(NB):
        spot += dot(pos_ref[slot], whole((offset < RUNS) & (lanes == offset + slot * RUNS)))
    pos = spot[:DET].astype(i32)
    here = (pos // (TILE_DEV * NX * NZ) == y) & ((pos // TILE_DEV) % NX == x)
    tile = ((pos // (TILE_DEV * NX)) % NZ) * TILE_DEV + pos % TILE_DEV
    kinds, square = (2 * TILE_DEV * NZ, LANE), (LANE, LANE)
    kind = jnp.where(here, tile, TILE_DEV * NZ)
    tile = tile.astype(f32)
    before, every = whole(iota(square, 0) < iota(square, 1)), jnp.ones(square, bf)
    marks, prior, total = [], [], jnp.zeros(kinds, f32)
    for d in range(DET):
        mark = whole(jnp.broadcast_to(kind[d : d + 1], kinds) == iota(kinds, 0))
        marks.append(mark.astype(f32))
        prior.append(dot(mark, before) + total)
        total += dot(mark, every)
    lower = whole(iota((kinds[0], kinds[0]), 1) < iota((kinds[0], kinds[0]), 0))
    coarse = jnp.floor(total * (1.0 / 32.0))
    base = 32.0 * dot(lower, coarse.astype(bf)) + dot(lower, (total - 32.0 * coarse).astype(bf))
    high_rows, low_rows = iota((DET, LANE), 0).astype(f32), iota(square, 0).astype(f32)
    lane = iota((DET, LANE), 1).astype(f32)
    found = jnp.zeros((3 * DET, LANE), f32)
    for d in range(DET):
        rank = jnp.sum(marks[d] * (prior[d] + base), axis=0, keepdims=True)
        high = jnp.floor(rank * (1.0 / LANE))
        low = rank - LANE * high
        at = jnp.broadcast_to(high, (DET, LANE)) == high_rows
        values = (jnp.broadcast_to(tile[d : d + 1], (DET, LANE)), jnp.full((DET, LANE), float(d), f32), lane)
        left = jnp.concatenate([jnp.where(at, v, 0.0) for v in values], axis=0).astype(bf)
        right = whole(jnp.broadcast_to(low, square) == low_rows)
        found += lax.dot_general(left, right, (((1,), (1,)), ((), ())), preferred_element_type=f32)
    entry = found[:DET] * ALL_RUNS + found[DET : 2 * DET] * LANE + found[2 * DET :]
    order_ref[:DET, :] = entry.astype(i32)
    others = total[TILE_DEV * NZ : TILE_DEV * NZ + 1]
    order_ref[DET:, :] = jnp.broadcast_to(ALL_RUNS - others, (DET, LANE)).astype(i32)


def pack_kernel(home_ref, piece_ref, slot_ref, row_ref, col_ref, low_ref, high_ref, angle_ref, q_ref, out_ref):
    f32, bf = jnp.float32, jnp.bfloat16
    for r in range(RUNS):
        at = slice(r * LANE, (r + 1) * LANE)
        angle = angle_ref[:, at]
        coarse = angle.astype(bf)
        fine = (angle - coarse.astype(f32)).astype(bf)
        row, col = row_ref[:, at].astype(f32).astype(bf), col_ref[:, at].astype(f32).astype(bf)
        for part, value in enumerate((row, col, coarse, fine, low_ref[:, at], high_ref[:, at])):
            out_ref[part * PIECE_RUNS + r * DET : part * PIECE_RUNS + (r + 1) * DET] = value
    slots = slot_ref[...]
    position = jnp.zeros(slots.shape, f32)
    for s in range(LISTED):
        position = jnp.where(slots == s, home_ref[piece_ref[0, s]].astype(f32), position)
    wide = jnp.concatenate([position, jnp.zeros((DET, LANE - RUNS), f32)], axis=1)
    out_ref[SAMPLE_ROWS : SAMPLE_ROWS + 2 * DET] = jnp.concatenate([wide, jnp.zeros_like(wide)], axis=0).astype(bf)
    out_ref[SAMPLE_ROWS + 2 * DET :] = q_ref[...]


def packed(tile_home, piece_list, run_slot, hit_row, hit_col, frac_row, frac_col, angle, quarter):
    return pl.pallas_call(
        pack_kernel,
        out_shape=jax.ShapeDtypeStruct((SAMPLE_ROWS + 2 * DET + quarter.shape[0], LANE), jnp.bfloat16),
        in_specs=[SM, SM] + [VM] * 7,
        out_specs=VM,
        name="pack",
    )(tile_home, piece_list, run_slot, hit_row, hit_col, frac_row, frac_col, angle, quarter)


def gather_kernel(
    pack_ref,
    tiles_ref, all_ref, order_ref,
    pos_all, store_sem,
    pos_send, pos_recv, block_send, block_recv, strip_send, strip_recv, core_send, core_recv, hi_send, hi_recv,
):
    det, tm, y, z, x = place()
    partner, across = core_of(det), hi_of(det)
    ahead, behind = (y + 1) % NY, (y + NY - 1) % NY
    facing = (y + NY // 2) % NY
    other = 1 - x
    up, down, side = (det, tm_of(ahead, z, x)), (det, tm_of(behind, z, x)), (det, tm_of(y, z, other))
    far = [(det, tm_of((y + dy) % NY, z, (x + dx) % NX)) for dy, dx in PEERS]

    def along(direction, jump):
        return (det, tm_of(y, (z + jump) % NZ if direction == 0 else (z + NZ - jump) % NZ, x))

    samples_ref, p_ref = pack_ref.at[pl.ds(0, SAMPLE_ROWS)], pack_ref.at[pl.ds(SAMPLE_ROWS, 2 * DET)]
    q_ref = pack_ref.at[pl.ds(SAMPLE_ROWS + 2 * DET, TILE_DEV * 3 * STRIP)]

    def strip(slot, d):
        return tiles_ref.at[slot, d]

    def block(slot, part):
        return all_ref.at[slot, pl.ds(part * 2 * PIECE_RUNS, 2 * PIECE_RUNS)]

    def own_block(part):
        return pack_ref.at[pl.ds(part * 2 * PIECE_RUNS, 2 * PIECE_RUNS)]

    mine = y * NX + x
    greet([along(d, j) for d in (0, 1) for j in (1, 2)] + [(partner, tm), (across, tm)] + far)

    started = []

    def start(copy):
        copy.start()
        started.append(copy)

    start(remote(q_ref, strip(z, det), hi_send, hi_recv, (across, tm)))

    def send_block(link, slot, part, peer, own=False):
        start(
            remote(
                own_block(part) if own else block(slot, part), block(slot, part),
                block_send.at[link, part], block_recv.at[link, part], peer,
            )
        )

    def wait_block(link, slot, part):
        remote(own_block(part), block(slot, part), block_send.at[link, part], block_recv.at[link, part], side).wait_recv()

    owner = (det, across)

    def source_slot(direction, distance):
        return (z + NZ - distance) % NZ if direction == 0 else (z + distance) % NZ

    def send_strip(half, direction, distance):
        slot = z if distance < 3 else source_slot(direction, 2)
        here = strip(slot, owner[half])
        start(
            remote(
                q_ref if half == 0 and distance < 3 else here, here,
                strip_send.at[half, direction, distance - 1], strip_recv.at[half, direction, distance - 1],
                along(direction, 2 - distance % 2),
            )
        )

    def reach(half, direction):
        return NZ // 2 if half == direction else NZ // 2 - 1

    def to_partner(half, index, slot):
        here = strip(slot, owner[half])
        start(
            remote(
                q_ref if half == 0 and index == 0 else here, here, core_send.at[half, index], core_recv.at[half, index],
                (partner, tm),
            )
        )

    def take_strip(half, distance):
        for direction in (0, 1):
            if distance <= reach(half, direction):
                slot = source_slot(direction, distance)
                remote(
                    q_ref, strip(slot, owner[half]),
                    strip_send.at[half, direction, distance - 1], strip_recv.at[half, direction, distance - 1], side,
                ).wait_recv()
                if distance == 2:
                    if reach(half, direction) == 4:
                        send_strip(half, direction, 4)
                    send_strip(half, direction, 3)
                to_partner(half, direction * NZ // 2 + distance, slot)

    def first_strips(half):
        for distance in (2, 1):
            for direction in (0, 1):
                send_strip(half, direction, distance)
        to_partner(half, 0, z)

    for k, peer in enumerate(far):
        start(remote(p_ref, pos_all.at[mine], pos_send.at[k], pos_recv.at[k], peer))
    first_strips(0)
    for part in range(3):
        send_block(1, mine, part, up, True)
        send_block(2, mine, part, down, True)
        send_block(0, mine, part, side, True)
    stores = []
    for i, (src, dst) in enumerate(
        ((q_ref, strip(z, det)), (samples_ref, all_ref.at[mine]), (p_ref, pos_all.at[mine]))
    ):
        copy = pltpu.make_async_copy(src, dst, store_sem.at[i])
        copy.start()
        stores.append(copy)

    slot_of = {1: behind * NX + x, 2: ahead * NX + x, 0: y * NX + other, 5: facing * NX + x, 6: facing * NX + other,
               3: behind * NX + other, 4: ahead * NX + other}

    def near(part):
        for link in (1, 2, 0):
            wait_block(link, slot_of[link], part)
            if link == 1 and part != 1:
                send_block(5, slot_of[1], part, up)
            if link == 2 and part == 1:
                send_block(5, slot_of[2], part, down)
            if link == 1 and part == 2:
                send_block(3, slot_of[1], part, side)
            if link == 0:
                if part != 2:
                    send_block(3, slot_of[0], part, up)
                send_block(4, slot_of[0], part, down)

    def opposite(part):
        wait_block(5, slot_of[5], part)
        send_block(6, slot_of[5], part, side)

    near(0)
    remote(q_ref, strip(z, across), hi_send, hi_recv, (across, tm)).wait_recv()
    first_strips(1)
    take_strip(0, 2)
    near(1)
    near(2)
    take_strip(0, 1)
    opposite(0)
    take_strip(1, 2)
    opposite(1)
    opposite(2)
    take_strip(1, 1)
    take_strip(0, 3)
    take_strip(0, 4)

    stores[2].wait()
    for k, peer in enumerate(far):
        remote(p_ref, pos_all.at[mine], pos_send.at[k], pos_recv.at[k], peer).wait_recv()
    run_order(pos_all, order_ref, y, x)

    take_strip(1, 3)
    take_strip(1, 4)
    for part in range(3):
        for link in (3, 4, 6):
            wait_block(link, slot_of[link], part)
    theirs = (partner, hi_of(partner))
    for half in (0, 1):
        places = [(0, z)]
        for direction in (0, 1):
            for distance in range(1, reach(half, direction) + 1):
                places.append((direction * NZ // 2 + distance, source_slot(direction, distance)))
        for index, slot in places:
            remote(
                q_ref, strip(slot, theirs[half]), core_send.at[half, index], core_recv.at[half, index], (partner, tm)
            ).wait_recv()
    for copy in stores[:2]:
        copy.wait()
    for copy in started:
        copy.wait_send()


def gather_all(pack):
    bf, i32 = jnp.bfloat16, jnp.int32
    return pl.pallas_call(
        gather_kernel,
        out_shape=(
            jax.ShapeDtypeStruct((NZ, N_STRIP, TILE_DEV * 3 * STRIP, PIX), bf),
            jax.ShapeDtypeStruct((NB, SAMPLE_ROWS, LANE), bf),
            jax.ShapeDtypeStruct((2 * DET, LANE), i32),
        ),
        in_specs=[ANY],
        out_specs=(ANY, ANY, VM),
        scratch_shapes=[
            pltpu.VMEM((NB, 2 * DET, LANE), bf),
            DMA((3,)),
            DMA((NB,)),
            DMA((NB,)),
            DMA((7, 3)),
            DMA((7, 3)),
            DMA((2, 2, NZ // 2)),
            DMA((2, 2, NZ // 2)),
            DMA((2, NZ + 1)),
            DMA((2, NZ + 1)),
            DMA,
            DMA,
        ],
        compiler_params=pltpu.CompilerParams(collective_id=0, has_side_effects=True, vmem_limit_bytes=GRANT),
        name="gather_all",
    )(pack)


def sin_cos(v):
    quarter = jnp.round(v * 0.6366197723675814)
    u = v - quarter * 1.5703125
    u = u - quarter * 4.837512969970703e-4
    u = u - quarter * 7.549789948768648e-8
    u2 = u * u
    s = u + u * u2 * (-1.6666654611e-1 + u2 * (8.3321608736e-3 + u2 * -1.9515295891e-4))
    c = 1.0 - 0.5 * u2 + u2 * u2 * (4.166664568298827e-2 + u2 * (-1.388731625493765e-3 + u2 * 2.443315711809948e-5))
    q = quarter.astype(jnp.int32) & 3
    odd = (q & 1) == 1
    sin = jnp.where(odd, c, s)
    cos = jnp.where(odd, s, c)
    sin = jnp.where(q >= 2, -sin, sin)
    cos = jnp.where((q == 1) | (q == 2), -cos, cos)
    return sin, cos


def low_of(high):
    return (1.0 - high).astype(jnp.bfloat16).astype(jnp.float32)


def run_of(entry):
    run = entry & (ALL_RUNS - 1)
    return entry >> 10, (run >> 4) & (NB - 1), run >> 7, run & (RUNS - 1)


def spread(index, low, high, rows):
    bf = jnp.bfloat16
    wide = [jnp.broadcast_to(v, (HALF, LANE)).astype(bf) for v in (index, index + 1.0, low, high)]
    zero = jnp.zeros((HALF, LANE), bf)
    parts = []
    for b in range(PIX // HALF):
        row = rows[b * HALF : (b + 1) * HALF]
        parts.append(jnp.where(row == wide[0], wide[2], jnp.where(row == wide[1], wide[3], zero)))
    return jnp.concatenate(parts, axis=0)


def samples_of(all_ref, z, part):
    rows = slice(part * 2 * PIECE_RUNS, (part + 1) * 2 * PIECE_RUNS)
    return all_ref[z, rows].astype(jnp.float32).reshape(2, RUNS, DET, LANE)


def forward_kernel(list_ref, tiles_ref, all_ref, sig_ref, cs_ref, hit_ref, frac_ref):
    def prepare(z, _):
        hit_ref[z] = samples_of(all_ref, z, 0)
        halves = samples_of(all_ref, z, 1)
        sin, cos = sin_cos(2.0 * (halves[0] + halves[1]))
        cs_ref[z, 0] = cos
        cs_ref[z, 1] = sin
        frac_ref[z] = samples_of(all_ref, z, 2)
        sig_ref[z] = jnp.zeros_like(sig_ref[z])
        return 0

    lax.fori_loop(0, NB, prepare, 0)
    count = list_ref[DET, 0]
    rows = lax.broadcasted_iota(jnp.int32, (PIX, LANE), 0).astype(jnp.float32).astype(jnp.bfloat16)

    def body(step, _):
        for u in range(UNROLL):
            n = step * UNROLL + u
            tile, z, d, r = run_of(list_ref[n >> 7, n & (LANE - 1)])
            at = (r, pl.ds(d, 1), slice(None))
            col_high = frac_ref[z, 1, *at]
            row_high = frac_ref[z, 0, *at]
            col_weight = spread(hit_ref[z, 1, *at], low_of(col_high), col_high, rows)
            row_weight = spread(hit_ref[z, 0, *at], low_of(row_high), row_high, rows).astype(jnp.float32)
            rows_of_tile = jnp.concatenate([tiles_ref[tile // TILE_DEV, k, tile % TILE_DEV] for k in range(N_STRIP)], axis=0)
            partial = jnp.dot(rows_of_tile, col_weight, preferred_element_type=jnp.float32)
            value = []
            for p in range(3):
                terms = [
                    partial[(k * 3 + p) * STRIP : (k * 3 + p + 1) * STRIP] * row_weight[k * STRIP : (k + 1) * STRIP]
                    for k in range(N_STRIP)
                ]
                value.append(jnp.sum(sum(terms[1:], terms[0]), axis=0, keepdims=True))
            total = value[0] + cs_ref[z, 0, *at] * value[1] + cs_ref[z, 1, *at] * value[2]
            sig_ref[z, d, pl.ds(r, 1), :] = jnp.where(n < count, total, 0.0)
        return 0

    lax.fori_loop(0, (count + UNROLL - 1) // UNROLL, body, 0)


def forward(order, tiles, samples):
    f32 = jnp.float32
    block = (NB, DET, RUNS, LANE)
    pair = (NB, 2, RUNS, DET, LANE)
    return pl.pallas_call(
        forward_kernel,
        out_shape=(jax.ShapeDtypeStruct(block, f32), jax.ShapeDtypeStruct(pair, f32)),
        in_specs=[SM, VM, VM],
        out_specs=(VM, VM),
        scratch_shapes=[pltpu.VMEM(pair, f32), pltpu.VMEM(pair, f32)],
        compiler_params=pltpu.CompilerParams(vmem_limit_bytes=GRANT),
        name="forward",
    )(order, tiles, samples)


def backward_kernel(list_ref, all_ref, cs_ref, filt_ref, acc_ref, hit_ref, frac_ref):
    def prepare(z, _):
        hit_ref[z] = samples_of(all_ref, z, 0)
        frac_ref[z] = samples_of(all_ref, z, 2)
        return 0

    lax.fori_loop(0, NB, prepare, 0)

    def clear(t, _):
        acc_ref[t] = jnp.zeros_like(acc_ref[t])
        return 0

    lax.fori_loop(0, TILE_DEV * NZ, clear, 0)
    count = list_ref[DET, 0]
    rows = lax.broadcasted_iota(jnp.int32, (PIX, LANE), 0).astype(jnp.float32).astype(jnp.bfloat16)

    def body(step, _):
        for u in range(UNROLL):
            k = step * UNROLL + u
            tile, z, d, r = run_of(list_ref[k >> 7, k & (LANE - 1)])
            at = (r, pl.ds(d, 1), slice(None))
            col_high = frac_ref[z, 1, *at]
            row_high = frac_ref[z, 0, *at]
            row_low = low_of(row_high)
            col_weight = spread(hit_ref[z, 1, *at], low_of(col_high), col_high, rows)
            filt = jnp.where(k < count, filt_ref[z, d, pl.ds(r, 1), :], 0.0)
            hit = hit_ref[z, 0, *at]
            parts = []
            for p in range(3):
                scaled = filt if p == 0 else cs_ref[z, p - 1, *at] * filt
                parts.append(spread(hit, scaled * row_low, scaled * row_high, rows))
            weighted = jnp.concatenate(parts, axis=0)
            acc_ref[tile] += lax.dot_general(
                weighted, col_weight, (((1,), (1,)), ((), ())), preferred_element_type=jnp.float32
            )
        return 0

    lax.fori_loop(0, (count + UNROLL - 1) // UNROLL, body, 0)


def backward(order, samples, turns, filtered):
    f32 = jnp.float32
    pair = (NB, 2, RUNS, DET, LANE)
    return pl.pallas_call(
        backward_kernel,
        out_shape=jax.ShapeDtypeStruct((TILE_DEV * NZ, 3 * PIX, PIX), f32),
        in_specs=[SM, VM, VM, VM],
        out_specs=VM,
        scratch_shapes=[pltpu.VMEM(pair, f32), pltpu.VMEM(pair, f32)],
        compiler_params=pltpu.CompilerParams(vmem_limit_bytes=GRANT),
        name="backward",
    )(order, samples, turns, filtered)


def toeplitz(noise_ref, line_ref, hi_ref, lo_ref):
    square = (LANE, LANE)
    lanes = lax.broadcasted_iota(jnp.int32, square, 1)
    rows = lax.broadcasted_iota(jnp.int32, square, 0)
    first = lax.broadcasted_iota(jnp.int32, (DET, LANE), 1) == 0
    for q in range(REACH):
        lags = noise_ref[:, q * LANE : (q + 1) * LANE]
        line_ref[q] = jnp.where(first, lags + 1.0, lags) if q == 0 else lags
    line_ref[REACH] = jnp.where(first, jnp.broadcast_to(noise_ref[:, REACH * LANE :], (DET, LANE)), 0.0)

    def one(d, _):
        def put(q, matrix):
            high = matrix.astype(jnp.bfloat16)
            hi_ref[d, q] = high
            lo_ref[d, q] = (matrix - high.astype(jnp.float32)).astype(jnp.bfloat16)

        before = None
        for q in range(REACH + 1):
            lags = line_ref[q, pl.ds(d, 1), :]
            after = pltpu.roll(jnp.broadcast_to(lags, square), 0, 1, stride=1, stride_axis=0)
            if q == 0:
                put(0, jnp.where(lanes >= rows, after, 0.0))
                put(REACH + 1, jnp.where(lanes > rows, after, 0.0))
            else:
                put(q, jnp.where(lanes >= rows, after, before))
            before = after
        return 0

    lax.fori_loop(0, DET, one, 0)


STRAIGHT = (((1,), (0,)), ((), ()))
CROSSED = (((1,), (1,)), ((), ()))


def filter_kernel(
    part_ref, noise_ref, out_ref, land, ext, filt, lags, t_hi, t_lo,
    store_sem, send, recv, halo_send, halo_recv, back_send, back_recv,
):
    det, tm, y, z, x = place()
    total_tm = NY * NZ * NX
    mine = y * NX + x
    prior, later = (tm + total_tm - 1) % total_tm, (tm + 1) % total_tm

    def slot(k, sign):
        dy, dx = PEERS[k]
        return ((y + sign * dy + NY) % NY) * NX + (x + dx) % NX

    peers = [(det, tm_of((y + dy) % NY, z, (x + dx) % NX)) for dy, dx in PEERS]
    greet(peers + [(det, later), (det, prior)])
    sends = []

    def part_copy(c, k):
        rows = pl.ds(c * SENT, SENT)
        return remote(part_ref.at[slot(k, 1), rows], land.at[k, rows], send.at[k, c], recv.at[k, c], peers[k])

    def halo_copies(c):
        rows = pl.ds(c * SENT, SENT)
        return (
            remote(
                ext.at[rows, pl.ds(REACH, REACH), :], ext.at[rows, pl.ds(REACH + RUNS, REACH), :],
                halo_send.at[0, c], halo_recv.at[0, c], (det, prior),
            ),
            remote(
                ext.at[rows, pl.ds(RUNS, REACH), :], ext.at[rows, pl.ds(0, REACH), :],
                halo_send.at[1, c], halo_recv.at[1, c], (det, later),
            ),
        )

    for c in range(DET // SENT):
        for k in range(NB - 1):
            copy = part_copy(c, k)
            copy.start()
            sends.append(copy)
    toeplitz(noise_ref, lags, t_hi, t_lo)

    def gathered(c):
        rows = slice(c * SENT, (c + 1) * SENT)
        total = part_ref[mine, rows]
        for k in range(NB - 1):
            part_copy(c, k).wait_recv()
            total = total + land[k, rows]
        ext[rows, REACH : REACH + RUNS, :] = total
        for copy in halo_copies(c):
            copy.start()
            sends.append(copy)

    first, last = tm == 0, tm == total_tm - 1

    def product(left, right, crossed):
        return lax.dot_general(left, right, CROSSED if crossed else STRAIGHT, preferred_element_type=jnp.float32)

    back, own_copies = [], []

    def back_copy(c, k, source):
        rows = pl.ds(c * SENT, SENT)
        return remote(filt.at[rows], out_ref.at[source, rows], back_send.at[k, c], back_recv.at[k, c], peers[k])

    def send_back(c):
        for k in range(NB - 1):
            copy = back_copy(c, k, mine)
            copy.start()
            back.append(copy)
        rows = pl.ds(c * SENT, SENT)
        copy = pltpu.make_async_copy(filt.at[rows], out_ref.at[mine, rows], store_sem.at[c])
        copy.start()
        own_copies.append(copy)

    def filtered(c):
        for copy in halo_copies(c):
            copy.wait_recv()
        dets = range(c * SENT, (c + 1) * SENT)
        lines = [
            jnp.concatenate(
                [
                    jnp.where(first, 0.0, ext[d, :REACH]),
                    ext[d, REACH : REACH + RUNS],
                    jnp.where(last, 0.0, ext[d, REACH + RUNS :]),
                ],
                axis=0,
            )
            for d in dets
        ]
        full = [jnp.zeros((2 * RUNS, LANE), jnp.float32) for d in dets]
        fine = [jnp.zeros((RUNS, LANE), jnp.float32) for d in dets]
        for m in range(2 * REACH + 1):
            q = REACH - m
            for i, d in enumerate(dets):
                window = lines[i][m : m + RUNS]
                high = window.astype(jnp.bfloat16)
                low = (window - high.astype(jnp.float32)).astype(jnp.bfloat16)
                stack = jnp.concatenate([high, low], axis=0)
                for index, crossed in [(q, False)] if q > 0 else [(-q, True)] if q < 0 else [(0, False), (REACH + 1, True)]:
                    full[i] += product(stack, t_hi[d, index], crossed)
                    fine[i] += product(high, t_lo[d, index], crossed)
        for i, d in enumerate(dets):
            filt[d] = full[i][:RUNS] + full[i][RUNS:] + fine[i]
        send_back(c)

    chunks = DET // SENT
    gathered(0)
    gathered(1)
    for c in range(chunks):
        filtered(c)
        if c + 2 < chunks:
            gathered(c + 2)
    for copy in own_copies:
        copy.wait()
    for c in range(DET // SENT):
        for k, peer in enumerate(peers):
            back_copy(c, k, slot(k, -1)).wait_recv()
    for copy in sends + back:
        copy.wait_send()


def filtered_of(partial, noise_coef):
    f32, bf = jnp.float32, jnp.bfloat16
    block = (DET, RUNS, LANE)
    matrices = (DET, REACH + 2, LANE, LANE)
    return pl.pallas_call(
        filter_kernel,
        out_shape=jax.ShapeDtypeStruct((NB, *block), f32),
        in_specs=[VM, VM],
        out_specs=ANY,
        scratch_shapes=[
            pltpu.VMEM((NB - 1, *block), f32),
            pltpu.VMEM((DET, RUNS + 2 * REACH, LANE), f32),
            pltpu.VMEM(block, f32),
            pltpu.VMEM((REACH + 1, DET, LANE), f32),
            pltpu.VMEM(matrices, bf),
            pltpu.VMEM(matrices, bf),
            DMA((DET // SENT,)),
            DMA((NB, DET // SENT)),
            DMA((NB, DET // SENT)),
            DMA((2, DET // SENT)),
            DMA((2, DET // SENT)),
            DMA((NB, DET // SENT)),
            DMA((NB, DET // SENT)),
        ],
        compiler_params=pltpu.CompilerParams(collective_id=1, has_side_effects=True, vmem_limit_bytes=GRANT),
        name="filter",
    )(partial, noise_coef)


CHUNKS = [(t, p) for t in range(TILE_DEV) for p in range(3)]
HALF_Z = NZ // 2
WIRE = jnp.bfloat16
OFFSETS = [4, 3, -3, 2, -2, 1, -1, 0]


def collect_kernel(
    acc_ref, out_ref, land_core, packet, land, land_last, land_own,
    core_send, core_recv, ring_send, ring_recv, last_send, last_recv, hi_send, hi_recv,
):
    f32 = jnp.float32
    det, tm, y, z, x = place()
    core, hi = det % 2, det // 2
    partner, across = core_of(det), hi_of(det)
    right, left = tm_of(y, (z + 1) % NZ, x), tm_of(y, (z + NZ - 1) % NZ, x)
    neighbours = ((det, right), (det, left))
    greet([(partner, tm), (across, tm), *neighbours, (across, right), (across, left)])
    started = []

    def start(copy):
        copy.start()
        started.append(copy)

    for k, offset in enumerate(OFFSETS):
        start(
            remote(
                acc_ref.at[(z + offset + NZ) % NZ, :, :, :, 1 - core], land_core.at[k], core_send.at[k], core_recv.at[k],
                (partner, tm),
            )
        )

    def ring(direction, step, c):
        t, p = CHUNKS[c]
        sign = 1 if direction == 0 else -1
        k = OFFSETS.index(sign * (HALF_Z - step)) if step else 0
        return remote(
            packet.at[k, t, p], land.at[direction, step, t, p],
            ring_send.at[direction, step, c], ring_recv.at[direction, step, c], neighbours[direction],
        )

    def last_hop(direction, c, crossing):
        t, p = CHUNKS[c]
        k = OFFSETS.index(1 if direction == 0 else -1)
        goal = (right, left)[direction]
        return remote(
            packet.at[k, t, p, 1 - hi if crossing else hi], land_last.at[crossing, direction, t, p],
            last_send.at[crossing, direction, c], last_recv.at[crossing, direction, c],
            (across if crossing else det, goal),
        )

    def own_copy(t):
        return remote(packet.at[len(OFFSETS) - 1, t, :, 1 - hi], land_own.at[t], hi_send.at[t], hi_recv.at[t], (across, tm))

    def own(k, t, p):
        return acc_ref[(z + OFFSETS[k] + NZ) % NZ, t, p, :, core]

    def swapped(k):
        remote(acc_ref.at[0, :, :, :, 0], land_core.at[k], core_send.at[k], core_recv.at[k], (partner, tm)).wait_recv()

    swapped(0)
    for direction in (0, 1):
        for c, (t, p) in enumerate(CHUNKS):
            if t == direction:
                packet[0, t, p] = (own(0, t, p) + land_core[0, t, p]).astype(WIRE)
    for p in range(3):
        for direction in (0, 1):
            start(ring(direction, 0, direction * 3 + p))
    last = len(OFFSETS) - 1
    for step in range(1, HALF_Z):
        keys = [OFFSETS.index(HALF_Z - step), OFFSETS.index(step - HALF_Z)]
        for k in keys:
            swapped(k)
        for i in range(len(CHUNKS)):
            for direction in (0, 1):
                c = (i + 3 * (1 - direction)) % len(CHUNKS) if step == 1 else i
                t, p = CHUNKS[c]
                k = keys[direction]
                value = own(k, t, p) + land_core[k, t, p]
                if step > 1 or t == direction:
                    ring(direction, step - 1, c).wait_recv()
                    value = value + land[direction, step - 1, t, p].astype(f32)
                packet[k, t, p] = value.astype(WIRE)
                if step < HALF_Z - 1:
                    start(ring(direction, step, c))
                else:
                    start(last_hop(direction, c, 1))
                    start(last_hop(direction, c, 0))
        if step == 1:
            swapped(last)
            for t in range(TILE_DEV):
                for p in range(3):
                    value = own(last, t, p) + land_core[last, t, p]
                    packet[last, t, p] = value.astype(WIRE)
                    land_core[last, t, p] = value
                start(own_copy(t))
    for t in range(TILE_DEV):
        own_copy(t).wait_recv()
    for c, (t, p) in enumerate(CHUNKS):
        value = land_core[last, t, p, hi] + land_own[t, p].astype(f32)
        for crossing in (0, 1):
            for direction in (0, 1):
                last_hop(direction, c, crossing).wait_recv()
                value = value + land_last[crossing, direction, t, p].astype(f32)
        out_ref[t, p] = value
    for copy in started:
        copy.wait_send()


def collect(acc):
    f32 = jnp.float32
    half = (TILE_DEV, 3, 2, STRIP, PIX)
    quarter = (TILE_DEV, 3, STRIP, PIX)
    return pl.pallas_call(
        collect_kernel,
        out_shape=jax.ShapeDtypeStruct(quarter, f32),
        in_specs=[VM],
        out_specs=VM,
        scratch_shapes=[
            pltpu.VMEM((NZ, *half), f32),
            pltpu.VMEM((NZ, *half), WIRE),
            pltpu.VMEM((2, HALF_Z - 1, *half), WIRE),
            pltpu.VMEM((2, 2, *quarter), WIRE),
            pltpu.VMEM(quarter, WIRE),
            DMA((NZ,)),
            DMA((NZ,)),
            DMA((2, HALF_Z - 1, 6)),
            DMA((2, HALF_Z - 1, 6)),
            DMA((2, 2, 6)),
            DMA((2, 2, 6)),
            DMA((2,)),
            DMA((2,)),
        ],
        compiler_params=pltpu.CompilerParams(collective_id=2, has_side_effects=True, vmem_limit_bytes=GRANT),
        name="collect",
    )(acc.reshape(NZ, TILE_DEV, 3, 2, 2, STRIP, PIX))


def body(
    sky_map, tile_home, piece_tiles, run_slot, hit_row, hit_col, frac_row, frac_col, angle, noise_coef
):
    pack = packed(
        tile_home, piece_tiles.reshape(1, LISTED), run_slot, hit_row, hit_col, frac_row, frac_col, angle,
        sky_map.reshape(TILE_DEV * 3 * STRIP, PIX),
    )
    tiles, samples, order = gather_all(pack)
    partial, turns = forward(
        order, tiles.reshape(NZ, N_STRIP, TILE_DEV, 3 * STRIP, PIX), samples
    )
    filtered = filtered_of(partial, noise_coef)
    acc = backward(order, samples, turns, filtered)
    return collect(acc)


def solution(mesh):
    placed = (
        P("tm", None, "det", None),
        P(),
        P("det", "tm", None),
        P("det", "tm"),
        P("det", "tm"),
        P("det", "tm"),
        P("det", "tm"),
        P("det", "tm"),
        P("det", "tm"),
        P("det", None),
    )
    return jax.shard_map(
        body, mesh=mesh, in_specs=placed, out_specs=P("tm", None, "det", None), check_vma=False
    )
```

```python
import functools

import jax
import jax.numpy as jnp
from jax import lax
from jax.experimental import pallas as pl
from jax.experimental.pallas import tpu as pltpu
from jax.sharding import PartitionSpec as P

GRANT = 24 << 20
MESH = pl.DeviceIdType.MESH
NY, NZ, NX = 4, 8, 2
NB = NY * NX
DET, RUNS, LANE = 8, 16, 128
PIX = 128
STRIP = 32
N_STRIP = 4
LISTED = 32
TILE_DEV = 2
REACH = 8
UNROLL = 16
HALF = 16
SENT = 4
PIECE_RUNS = DET * RUNS
ALL_RUNS = NB * PIECE_RUNS
SAMPLE_ROWS = 6 * PIECE_RUNS
ANY = pl.BlockSpec(memory_space=pl.ANY)
VM = pl.BlockSpec(memory_space=pltpu.VMEM)
SM = pl.BlockSpec(memory_space=pltpu.SMEM)
DMA = pltpu.SemaphoreType.DMA
PEERS = [(dy, dx) for dy in range(NY) for dx in range(NX) if (dy, dx) != (0, 0)]


def place():
    det, tm = lax.axis_index("det"), lax.axis_index("tm")
    y, z, x = tm // (NZ * NX), (tm // NX) % NZ, tm % NX
    return det, tm, y, z, x


def tm_of(y, z, x):
    return (y * NZ + z) * NX + x


def core_of(det):
    return det + 1 - 2 * (det % 2)


def hi_of(det):
    return (det + 2) % 4


def greet(peers):
    barrier = pltpu.get_barrier_semaphore()
    for peer in peers:
        pl.semaphore_signal(barrier, inc=1, device_id=peer, device_id_type=MESH)
    pl.semaphore_wait(barrier, len(peers))


def remote(src, dst, send, recv, peer):
    return pltpu.make_async_remote_copy(
        src_ref=src, dst_ref=dst, send_sem=send, recv_sem=recv, device_id=peer, device_id_type=MESH
    )


def run_order(pos_ref, order_ref, y, x):
    f32, bf, i32 = jnp.float32, jnp.bfloat16, jnp.int32

    def iota(shape, dim):
        return lax.broadcasted_iota(i32, shape, dim)

    def whole(mask):
        return jnp.where(mask, 1.0, 0.0).astype(bf)

    def dot(left, right):
        return jnp.dot(left, right, preferred_element_type=f32)

    lanes, offset = iota((LANE, LANE), 1), iota((LANE, LANE), 0)
    spot = jnp.zeros((2 * DET, LANE), f32)
    for slot in range(NB):
        spot += dot(pos_ref[slot], whole((offset < RUNS) & (lanes == offset + slot * RUNS)))
    pos = spot[:DET].astype(i32)
    here = (pos // (TILE_DEV * NX * NZ) == y) & ((pos // TILE_DEV) % NX == x)
    tile = ((pos // (TILE_DEV * NX)) % NZ) * TILE_DEV + pos % TILE_DEV
    kinds, square = (2 * TILE_DEV * NZ, LANE), (LANE, LANE)
    kind = jnp.where(here, tile, TILE_DEV * NZ)
    tile = tile.astype(f32)
    before, every = whole(iota(square, 0) < iota(square, 1)), jnp.ones(square, bf)
    marks, prior, total = [], [], jnp.zeros(kinds, f32)
    for d in range(DET):
        mark = whole(jnp.broadcast_to(kind[d : d + 1], kinds) == iota(kinds, 0))
        marks.append(mark.astype(f32))
        prior.append(dot(mark, before) + total)
        total += dot(mark, every)
    lower = whole(iota((kinds[0], kinds[0]), 1) < iota((kinds[0], kinds[0]), 0))
    coarse = jnp.floor(total * (1.0 / 32.0))
    base = 32.0 * dot(lower, coarse.astype(bf)) + dot(lower, (total - 32.0 * coarse).astype(bf))
    high_rows, low_rows = iota((DET, LANE), 0).astype(f32), iota(square, 0).astype(f32)
    lane = iota((DET, LANE), 1).astype(f32)
    found = jnp.zeros((3 * DET, LANE), f32)
    for d in range(DET):
        rank = jnp.sum(marks[d] * (prior[d] + base), axis=0, keepdims=True)
        high = jnp.floor(rank * (1.0 / LANE))
        low = rank - LANE * high
        at = jnp.broadcast_to(high, (DET, LANE)) == high_rows
        values = (jnp.broadcast_to(tile[d : d + 1], (DET, LANE)), jnp.full((DET, LANE), float(d), f32), lane)
        left = jnp.concatenate([jnp.where(at, v, 0.0) for v in values], axis=0).astype(bf)
        right = whole(jnp.broadcast_to(low, square) == low_rows)
        found += lax.dot_general(left, right, (((1,), (1,)), ((), ())), preferred_element_type=f32)
    entry = found[:DET] * ALL_RUNS + found[DET : 2 * DET] * LANE + found[2 * DET :]
    order_ref[:DET, :] = entry.astype(i32)
    others = total[TILE_DEV * NZ : TILE_DEV * NZ + 1]
    order_ref[DET:, :] = jnp.broadcast_to(ALL_RUNS - others, (DET, LANE)).astype(i32)


def pack_kernel(home_ref, piece_ref, slot_ref, row_ref, col_ref, low_ref, high_ref, angle_ref, q_ref, out_ref):
    f32, bf = jnp.float32, jnp.bfloat16
    for r in range(RUNS):
        at = slice(r * LANE, (r + 1) * LANE)
        angle = angle_ref[:, at]
        coarse = angle.astype(bf)
        fine = (angle - coarse.astype(f32)).astype(bf)
        row, col = row_ref[:, at].astype(f32).astype(bf), col_ref[:, at].astype(f32).astype(bf)
        for part, value in enumerate((row, col, coarse, fine, low_ref[:, at], high_ref[:, at])):
            out_ref[part * PIECE_RUNS + r * DET : part * PIECE_RUNS + (r + 1) * DET] = value
    slots = slot_ref[...]
    position = jnp.zeros(slots.shape, f32)
    for s in range(LISTED):
        position = jnp.where(slots == s, home_ref[piece_ref[0, s]].astype(f32), position)
    wide = jnp.concatenate([position, jnp.zeros((DET, LANE - RUNS), f32)], axis=1)
    out_ref[SAMPLE_ROWS : SAMPLE_ROWS + 2 * DET] = jnp.concatenate([wide, jnp.zeros_like(wide)], axis=0).astype(bf)
    out_ref[SAMPLE_ROWS + 2 * DET :] = q_ref[...]


def packed(tile_home, piece_list, run_slot, hit_row, hit_col, frac_row, frac_col, angle, quarter):
    return pl.pallas_call(
        pack_kernel,
        out_shape=jax.ShapeDtypeStruct((SAMPLE_ROWS + 2 * DET + quarter.shape[0], LANE), jnp.bfloat16),
        in_specs=[SM, SM] + [VM] * 7,
        out_specs=VM,
        name="pack",
    )(tile_home, piece_list, run_slot, hit_row, hit_col, frac_row, frac_col, angle, quarter)


def gather_kernel(
    pack_ref,
    tiles_ref, all_ref, order_ref,
    pos_all, store_sem,
    pos_send, pos_recv, block_send, block_recv, strip_send, strip_recv, core_send, core_recv, hi_send, hi_recv,
):
    det, tm, y, z, x = place()
    partner, across = core_of(det), hi_of(det)
    ahead, behind = (y + 1) % NY, (y + NY - 1) % NY
    facing = (y + NY // 2) % NY
    other = 1 - x
    up, down, side = (det, tm_of(ahead, z, x)), (det, tm_of(behind, z, x)), (det, tm_of(y, z, other))
    far = [(det, tm_of((y + dy) % NY, z, (x + dx) % NX)) for dy, dx in PEERS]

    def along(direction, jump):
        return (det, tm_of(y, (z + jump) % NZ if direction == 0 else (z + NZ - jump) % NZ, x))

    samples_ref, p_ref = pack_ref.at[pl.ds(0, SAMPLE_ROWS)], pack_ref.at[pl.ds(SAMPLE_ROWS, 2 * DET)]
    q_ref = pack_ref.at[pl.ds(SAMPLE_ROWS + 2 * DET, TILE_DEV * 3 * STRIP)]

    def strip(slot, d):
        return tiles_ref.at[slot, d]

    def block(slot, part):
        return all_ref.at[slot, pl.ds(part * 2 * PIECE_RUNS, 2 * PIECE_RUNS)]

    def own_block(part):
        return pack_ref.at[pl.ds(part * 2 * PIECE_RUNS, 2 * PIECE_RUNS)]

    mine = y * NX + x
    greet([along(d, j) for d in (0, 1) for j in (1, 2)] + [(partner, tm), (across, tm)] + far)

    started = []

    def start(copy):
        copy.start()
        started.append(copy)

    start(remote(q_ref, strip(z, det), hi_send, hi_recv, (across, tm)))

    def send_block(link, slot, part, peer, own=False):
        start(
            remote(
                own_block(part) if own else block(slot, part), block(slot, part),
                block_send.at[link, part], block_recv.at[link, part], peer,
            )
        )

    def wait_block(link, slot, part):
        remote(own_block(part), block(slot, part), block_send.at[link, part], block_recv.at[link, part], side).wait_recv()

    owner = (det, across)

    def source_slot(direction, distance):
        return (z + NZ - distance) % NZ if direction == 0 else (z + distance) % NZ

    def send_strip(half, direction, distance):
        slot = z if distance < 3 else source_slot(direction, 2)
        here = strip(slot, owner[half])
        start(
            remote(
                q_ref if half == 0 and distance < 3 else here, here,
                strip_send.at[half, direction, distance - 1], strip_recv.at[half, direction, distance - 1],
                along(direction, 2 - distance % 2),
            )
        )

    def reach(half, direction):
        return NZ // 2 if half == direction else NZ // 2 - 1

    def to_partner(half, index, slot):
        here = strip(slot, owner[half])
        start(
            remote(
                q_ref if half == 0 and index == 0 else here, here, core_send.at[half, index], core_recv.at[half, index],
                (partner, tm),
            )
        )

    def take_strip(half, distance):
        for direction in (0, 1):
            if distance <= reach(half, direction):
                slot = source_slot(direction, distance)
                remote(
                    q_ref, strip(slot, owner[half]),
                    strip_send.at[half, direction, distance - 1], strip_recv.at[half, direction, distance - 1], side,
                ).wait_recv()
                if distance == 2:
                    if reach(half, direction) == 4:
                        send_strip(half, direction, 4)
                    send_strip(half, direction, 3)
                to_partner(half, direction * NZ // 2 + distance, slot)

    def first_strips(half):
        for distance in (2, 1):
            for direction in (0, 1):
                send_strip(half, direction, distance)
        to_partner(half, 0, z)

    for k, peer in enumerate(far):
        start(remote(p_ref, pos_all.at[mine], pos_send.at[k], pos_recv.at[k], peer))
    first_strips(0)
    for part in range(3):
        send_block(1, mine, part, up, True)
        send_block(2, mine, part, down, True)
        send_block(0, mine, part, side, True)
    stores = []
    for i, (src, dst) in enumerate(
        ((q_ref, strip(z, det)), (samples_ref, all_ref.at[mine]), (p_ref, pos_all.at[mine]))
    ):
        copy = pltpu.make_async_copy(src, dst, store_sem.at[i])
        copy.start()
        stores.append(copy)

    slot_of = {1: behind * NX + x, 2: ahead * NX + x, 0: y * NX + other, 5: facing * NX + x, 6: facing * NX + other,
               3: behind * NX + other, 4: ahead * NX + other}

    def near(part):
        for link in (1, 2, 0):
            wait_block(link, slot_of[link], part)
            if link == 1 and part != 1:
                send_block(5, slot_of[1], part, up)
            if link == 2 and part == 1:
                send_block(5, slot_of[2], part, down)
            if link == 1 and part == 2:
                send_block(3, slot_of[1], part, side)
            if link == 0:
                if part != 2:
                    send_block(3, slot_of[0], part, up)
                send_block(4, slot_of[0], part, down)

    def opposite(part):
        wait_block(5, slot_of[5], part)
        send_block(6, slot_of[5], part, side)

    near(0)
    remote(q_ref, strip(z, across), hi_send, hi_recv, (across, tm)).wait_recv()
    first_strips(1)
    take_strip(0, 2)
    near(1)
    near(2)
    take_strip(0, 1)
    opposite(0)
    take_strip(1, 2)
    opposite(1)
    opposite(2)
    take_strip(1, 1)
    take_strip(0, 3)
    take_strip(0, 4)

    stores[2].wait()
    for k, peer in enumerate(far):
        remote(p_ref, pos_all.at[mine], pos_send.at[k], pos_recv.at[k], peer).wait_recv()
    run_order(pos_all, order_ref, y, x)

    take_strip(1, 3)
    take_strip(1, 4)
    for part in range(3):
        for link in (3, 4, 6):
            wait_block(link, slot_of[link], part)
    theirs = (partner, hi_of(partner))
    for half in (0, 1):
        places = [(0, z)]
        for direction in (0, 1):
            for distance in range(1, reach(half, direction) + 1):
                places.append((direction * NZ // 2 + distance, source_slot(direction, distance)))
        for index, slot in places:
            remote(
                q_ref, strip(slot, theirs[half]), core_send.at[half, index], core_recv.at[half, index], (partner, tm)
            ).wait_recv()
    for copy in stores[:2]:
        copy.wait()
    for copy in started:
        copy.wait_send()


def gather_all(pack):
    bf, i32 = jnp.bfloat16, jnp.int32
    return pl.pallas_call(
        gather_kernel,
        out_shape=(
            jax.ShapeDtypeStruct((NZ, N_STRIP, TILE_DEV * 3 * STRIP, PIX), bf),
            jax.ShapeDtypeStruct((NB, SAMPLE_ROWS, LANE), bf),
            jax.ShapeDtypeStruct((2 * DET, LANE), i32),
        ),
        in_specs=[ANY],
        out_specs=(ANY, ANY, VM),
        scratch_shapes=[
            pltpu.VMEM((NB, 2 * DET, LANE), bf),
            DMA((3,)),
            DMA((NB,)),
            DMA((NB,)),
            DMA((7, 3)),
            DMA((7, 3)),
            DMA((2, 2, NZ // 2)),
            DMA((2, 2, NZ // 2)),
            DMA((2, NZ + 1)),
            DMA((2, NZ + 1)),
            DMA,
            DMA,
        ],
        compiler_params=pltpu.CompilerParams(collective_id=0, has_side_effects=True, vmem_limit_bytes=GRANT),
        name="gather_all",
    )(pack)


def sin_cos(v):
    quarter = jnp.round(v * 0.6366197723675814)
    u = v - quarter * 1.5703125
    u = u - quarter * 4.837512969970703e-4
    u = u - quarter * 7.549789948768648e-8
    u2 = u * u
    s = u + u * u2 * (-1.6666654611e-1 + u2 * (8.3321608736e-3 + u2 * -1.9515295891e-4))
    c = 1.0 - 0.5 * u2 + u2 * u2 * (4.166664568298827e-2 + u2 * (-1.388731625493765e-3 + u2 * 2.443315711809948e-5))
    q = quarter.astype(jnp.int32) & 3
    odd = (q & 1) == 1
    sin = jnp.where(odd, c, s)
    cos = jnp.where(odd, s, c)
    sin = jnp.where(q >= 2, -sin, sin)
    cos = jnp.where((q == 1) | (q == 2), -cos, cos)
    return sin, cos


def low_of(high):
    return (1.0 - high).astype(jnp.bfloat16).astype(jnp.float32)


def run_of(entry):
    run = entry & (ALL_RUNS - 1)
    return entry >> 10, (run >> 4) & (NB - 1), run >> 7, run & (RUNS - 1)


def spread(index, low, high, rows):
    bf = jnp.bfloat16
    wide = [jnp.broadcast_to(v, (HALF, LANE)).astype(bf) for v in (index, index + 1.0, low, high)]
    zero = jnp.zeros((HALF, LANE), bf)
    parts = []
    for b in range(PIX // HALF):
        row = rows[b * HALF : (b + 1) * HALF]
        parts.append(jnp.where(row == wide[0], wide[2], jnp.where(row == wide[1], wide[3], zero)))
    return jnp.concatenate(parts, axis=0)


def samples_of(all_ref, z, part):
    rows = slice(part * 2 * PIECE_RUNS, (part + 1) * 2 * PIECE_RUNS)
    return all_ref[z, rows].astype(jnp.float32).reshape(2, RUNS, DET, LANE)


def forward_kernel(list_ref, tiles_ref, all_ref, sig_ref, cs_ref, hit_ref, frac_ref):
    def prepare(z, _):
        hit_ref[z] = samples_of(all_ref, z, 0)
        halves = samples_of(all_ref, z, 1)
        sin, cos = sin_cos(2.0 * (halves[0] + halves[1]))
        cs_ref[z, 0] = cos
        cs_ref[z, 1] = sin
        frac_ref[z] = samples_of(all_ref, z, 2)
        sig_ref[z] = jnp.zeros_like(sig_ref[z])
        return 0

    lax.fori_loop(0, NB, prepare, 0)
    count = list_ref[DET, 0]
    rows = lax.broadcasted_iota(jnp.int32, (PIX, LANE), 0).astype(jnp.float32).astype(jnp.bfloat16)

    def body(step, _):
        for u in range(UNROLL):
            n = step * UNROLL + u
            tile, z, d, r = run_of(list_ref[n >> 7, n & (LANE - 1)])
            at = (r, pl.ds(d, 1), slice(None))
            col_high = frac_ref[z, 1, *at]
            row_high = frac_ref[z, 0, *at]
            col_weight = spread(hit_ref[z, 1, *at], low_of(col_high), col_high, rows)
            row_weight = spread(hit_ref[z, 0, *at], low_of(row_high), row_high, rows).astype(jnp.float32)
            rows_of_tile = jnp.concatenate([tiles_ref[tile // TILE_DEV, k, tile % TILE_DEV] for k in range(N_STRIP)], axis=0)
            partial = jnp.dot(rows_of_tile, col_weight, preferred_element_type=jnp.float32)
            value = []
            for p in range(3):
                terms = [
                    partial[(k * 3 + p) * STRIP : (k * 3 + p + 1) * STRIP] * row_weight[k * STRIP : (k + 1) * STRIP]
                    for k in range(N_STRIP)
                ]
                value.append(jnp.sum(sum(terms[1:], terms[0]), axis=0, keepdims=True))
            total = value[0] + cs_ref[z, 0, *at] * value[1] + cs_ref[z, 1, *at] * value[2]
            sig_ref[z, d, pl.ds(r, 1), :] = jnp.where(n < count, total, 0.0)
        return 0

    lax.fori_loop(0, (count + UNROLL - 1) // UNROLL, body, 0)


def forward(order, tiles, samples):
    f32 = jnp.float32
    block = (NB, DET, RUNS, LANE)
    pair = (NB, 2, RUNS, DET, LANE)
    return pl.pallas_call(
        forward_kernel,
        out_shape=(jax.ShapeDtypeStruct(block, f32), jax.ShapeDtypeStruct(pair, f32)),
        in_specs=[SM, VM, VM],
        out_specs=(VM, VM),
        scratch_shapes=[pltpu.VMEM(pair, f32), pltpu.VMEM(pair, f32)],
        compiler_params=pltpu.CompilerParams(vmem_limit_bytes=GRANT),
        name="forward",
    )(order, tiles, samples)


def backward_kernel(list_ref, all_ref, cs_ref, filt_ref, acc_ref, hit_ref, frac_ref):
    def prepare(z, _):
        hit_ref[z] = samples_of(all_ref, z, 0)
        frac_ref[z] = samples_of(all_ref, z, 2)
        return 0

    lax.fori_loop(0, NB, prepare, 0)

    def clear(t, _):
        acc_ref[t] = jnp.zeros_like(acc_ref[t])
        return 0

    lax.fori_loop(0, TILE_DEV * NZ, clear, 0)
    count = list_ref[DET, 0]
    rows = lax.broadcasted_iota(jnp.int32, (PIX, LANE), 0).astype(jnp.float32).astype(jnp.bfloat16)

    def body(step, _):
        for u in range(UNROLL):
            k = step * UNROLL + u
            tile, z, d, r = run_of(list_ref[k >> 7, k & (LANE - 1)])
            at = (r, pl.ds(d, 1), slice(None))
            col_high = frac_ref[z, 1, *at]
            row_high = frac_ref[z, 0, *at]
            row_low = low_of(row_high)
            col_weight = spread(hit_ref[z, 1, *at], low_of(col_high), col_high, rows)
            filt = jnp.where(k < count, filt_ref[z, d, pl.ds(r, 1), :], 0.0)
            hit = hit_ref[z, 0, *at]
            parts = []
            for p in range(3):
                scaled = filt if p == 0 else cs_ref[z, p - 1, *at] * filt
                parts.append(spread(hit, scaled * row_low, scaled * row_high, rows))
            weighted = jnp.concatenate(parts, axis=0)
            acc_ref[tile] += lax.dot_general(
                weighted, col_weight, (((1,), (1,)), ((), ())), preferred_element_type=jnp.float32
            )
        return 0

    lax.fori_loop(0, (count + UNROLL - 1) // UNROLL, body, 0)


def backward(order, samples, turns, filtered):
    f32 = jnp.float32
    pair = (NB, 2, RUNS, DET, LANE)
    return pl.pallas_call(
        backward_kernel,
        out_shape=jax.ShapeDtypeStruct((TILE_DEV * NZ, 3 * PIX, PIX), f32),
        in_specs=[SM, VM, VM, VM],
        out_specs=VM,
        scratch_shapes=[pltpu.VMEM(pair, f32), pltpu.VMEM(pair, f32)],
        compiler_params=pltpu.CompilerParams(vmem_limit_bytes=GRANT),
        name="backward",
    )(order, samples, turns, filtered)


def toeplitz(noise_ref, line_ref, hi_ref, lo_ref):
    square = (LANE, LANE)
    lanes = lax.broadcasted_iota(jnp.int32, square, 1)
    rows = lax.broadcasted_iota(jnp.int32, square, 0)
    first = lax.broadcasted_iota(jnp.int32, (DET, LANE), 1) == 0
    for q in range(REACH):
        lags = noise_ref[:, q * LANE : (q + 1) * LANE]
        line_ref[q] = jnp.where(first, lags + 1.0, lags) if q == 0 else lags
    line_ref[REACH] = jnp.where(first, jnp.broadcast_to(noise_ref[:, REACH * LANE :], (DET, LANE)), 0.0)

    def one(d, _):
        def put(q, matrix):
            high = matrix.astype(jnp.bfloat16)
            hi_ref[d, q] = high
            lo_ref[d, q] = (matrix - high.astype(jnp.float32)).astype(jnp.bfloat16)

        before = None
        for q in range(REACH + 1):
            lags = line_ref[q, pl.ds(d, 1), :]
            after = pltpu.roll(jnp.broadcast_to(lags, square), 0, 1, stride=1, stride_axis=0)
            if q == 0:
                put(0, jnp.where(lanes >= rows, after, 0.0))
                put(REACH + 1, jnp.where(lanes > rows, after, 0.0))
            else:
                put(q, jnp.where(lanes >= rows, after, before))
            before = after
        return 0

    lax.fori_loop(0, DET, one, 0)


STRAIGHT = (((1,), (0,)), ((), ()))
CROSSED = (((1,), (1,)), ((), ()))


def filter_kernel(
    part_ref, noise_ref, out_ref, land, ext, filt, lags, t_hi, t_lo,
    store_sem, send, recv, halo_send, halo_recv, back_send, back_recv,
):
    det, tm, y, z, x = place()
    total_tm = NY * NZ * NX
    mine = y * NX + x
    prior, later = (tm + total_tm - 1) % total_tm, (tm + 1) % total_tm

    def slot(k, sign):
        dy, dx = PEERS[k]
        return ((y + sign * dy + NY) % NY) * NX + (x + dx) % NX

    peers = [(det, tm_of((y + dy) % NY, z, (x + dx) % NX)) for dy, dx in PEERS]
    greet(peers + [(det, later), (det, prior)])
    sends = []

    def part_copy(c, k):
        rows = pl.ds(c * SENT, SENT)
        return remote(part_ref.at[slot(k, 1), rows], land.at[k, rows], send.at[k, c], recv.at[k, c], peers[k])

    def halo_copies(c):
        rows = pl.ds(c * SENT, SENT)
        return (
            remote(
                ext.at[rows, pl.ds(REACH, REACH), :], ext.at[rows, pl.ds(REACH + RUNS, REACH), :],
                halo_send.at[0, c], halo_recv.at[0, c], (det, prior),
            ),
            remote(
                ext.at[rows, pl.ds(RUNS, REACH), :], ext.at[rows, pl.ds(0, REACH), :],
                halo_send.at[1, c], halo_recv.at[1, c], (det, later),
            ),
        )

    for c in range(DET // SENT):
        for k in range(NB - 1):
            copy = part_copy(c, k)
            copy.start()
            sends.append(copy)
    toeplitz(noise_ref, lags, t_hi, t_lo)

    def gathered(c):
        rows = slice(c * SENT, (c + 1) * SENT)
        total = part_ref[mine, rows]
        for k in range(NB - 1):
            part_copy(c, k).wait_recv()
            total = total + land[k, rows]
        ext[rows, REACH : REACH + RUNS, :] = total
        for copy in halo_copies(c):
            copy.start()
            sends.append(copy)

    first, last = tm == 0, tm == total_tm - 1

    def product(left, right, crossed):
        return lax.dot_general(left, right, CROSSED if crossed else STRAIGHT, preferred_element_type=jnp.float32)

    back, own_copies = [], []

    def back_copy(c, k, source):
        rows = pl.ds(c * SENT, SENT)
        return remote(filt.at[rows], out_ref.at[source, rows], back_send.at[k, c], back_recv.at[k, c], peers[k])

    def send_back(c):
        for k in range(NB - 1):
            copy = back_copy(c, k, mine)
            copy.start()
            back.append(copy)
        rows = pl.ds(c * SENT, SENT)
        copy = pltpu.make_async_copy(filt.at[rows], out_ref.at[mine, rows], store_sem.at[c])
        copy.start()
        own_copies.append(copy)

    def filtered(c):
        for copy in halo_copies(c):
            copy.wait_recv()
        dets = range(c * SENT, (c + 1) * SENT)
        lines = [
            jnp.concatenate(
                [
                    jnp.where(first, 0.0, ext[d, :REACH]),
                    ext[d, REACH : REACH + RUNS],
                    jnp.where(last, 0.0, ext[d, REACH + RUNS :]),
                ],
                axis=0,
            )
            for d in dets
        ]
        full = [jnp.zeros((2 * RUNS, LANE), jnp.float32) for d in dets]
        fine = [jnp.zeros((RUNS, LANE), jnp.float32) for d in dets]
        for m in range(2 * REACH + 1):
            q = REACH - m
            for i, d in enumerate(dets):
                window = lines[i][m : m + RUNS]
                high = window.astype(jnp.bfloat16)
                low = (window - high.astype(jnp.float32)).astype(jnp.bfloat16)
                stack = jnp.concatenate([high, low], axis=0)
                for index, crossed in [(q, False)] if q > 0 else [(-q, True)] if q < 0 else [(0, False), (REACH + 1, True)]:
                    full[i] += product(stack, t_hi[d, index], crossed)
                    fine[i] += product(high, t_lo[d, index], crossed)
        for i, d in enumerate(dets):
            filt[d] = full[i][:RUNS] + full[i][RUNS:] + fine[i]
        send_back(c)

    chunks = DET // SENT
    gathered(0)
    gathered(1)
    for c in range(chunks):
        filtered(c)
        if c + 2 < chunks:
            gathered(c + 2)
    for copy in own_copies:
        copy.wait()
    for c in range(DET // SENT):
        for k, peer in enumerate(peers):
            back_copy(c, k, slot(k, -1)).wait_recv()
    for copy in sends + back:
        copy.wait_send()


def filtered_of(partial, noise_coef):
    f32, bf = jnp.float32, jnp.bfloat16
    block = (DET, RUNS, LANE)
    matrices = (DET, REACH + 2, LANE, LANE)
    return pl.pallas_call(
        filter_kernel,
        out_shape=jax.ShapeDtypeStruct((NB, *block), f32),
        in_specs=[VM, VM],
        out_specs=ANY,
        scratch_shapes=[
            pltpu.VMEM((NB - 1, *block), f32),
            pltpu.VMEM((DET, RUNS + 2 * REACH, LANE), f32),
            pltpu.VMEM(block, f32),
            pltpu.VMEM((REACH + 1, DET, LANE), f32),
            pltpu.VMEM(matrices, bf),
            pltpu.VMEM(matrices, bf),
            DMA((DET // SENT,)),
            DMA((NB, DET // SENT)),
            DMA((NB, DET // SENT)),
            DMA((2, DET // SENT)),
            DMA((2, DET // SENT)),
            DMA((NB, DET // SENT)),
            DMA((NB, DET // SENT)),
        ],
        compiler_params=pltpu.CompilerParams(collective_id=1, has_side_effects=True, vmem_limit_bytes=GRANT),
        name="filter",
    )(partial, noise_coef)


CHUNKS = [(t, p) for t in range(TILE_DEV) for p in range(3)]
HALF_Z = NZ // 2
WIRE = jnp.bfloat16
OFFSETS = [4, 3, -3, 2, -2, 1, -1, 0]


def collect_kernel(
    acc_ref, out_ref, land_core, packet, land, land_last, land_own,
    core_send, core_recv, ring_send, ring_recv, last_send, last_recv, hi_send, hi_recv,
):
    f32 = jnp.float32
    det, tm, y, z, x = place()
    core, hi = det % 2, det // 2
    partner, across = core_of(det), hi_of(det)
    right, left = tm_of(y, (z + 1) % NZ, x), tm_of(y, (z + NZ - 1) % NZ, x)
    neighbours = ((det, right), (det, left))
    greet([(partner, tm), (across, tm), *neighbours, (across, right), (across, left)])
    started = []

    def start(copy):
        copy.start()
        started.append(copy)

    for k, offset in enumerate(OFFSETS):
        start(
            remote(
                acc_ref.at[(z + offset + NZ) % NZ, :, :, :, 1 - core], land_core.at[k], core_send.at[k], core_recv.at[k],
                (partner, tm),
            )
        )

    def ring(direction, step, c):
        t, p = CHUNKS[c]
        sign = 1 if direction == 0 else -1
        k = OFFSETS.index(sign * (HALF_Z - step)) if step else 0
        return remote(
            packet.at[k, t, p], land.at[direction, step, t, p],
            ring_send.at[direction, step, c], ring_recv.at[direction, step, c], neighbours[direction],
        )

    def last_hop(direction, c, crossing):
        t, p = CHUNKS[c]
        k = OFFSETS.index(1 if direction == 0 else -1)
        goal = (right, left)[direction]
        return remote(
            packet.at[k, t, p, 1 - hi if crossing else hi], land_last.at[crossing, direction, t, p],
            last_send.at[crossing, direction, c], last_recv.at[crossing, direction, c],
            (across if crossing else det, goal),
        )

    def own_copy(t):
        return remote(packet.at[len(OFFSETS) - 1, t, :, 1 - hi], land_own.at[t], hi_send.at[t], hi_recv.at[t], (across, tm))

    def own(k, t, p):
        return acc_ref[(z + OFFSETS[k] + NZ) % NZ, t, p, :, core]

    def swapped(k):
        remote(acc_ref.at[0, :, :, :, 0], land_core.at[k], core_send.at[k], core_recv.at[k], (partner, tm)).wait_recv()

    swapped(0)
    for direction in (0, 1):
        for c, (t, p) in enumerate(CHUNKS):
            if t == direction:
                packet[0, t, p] = (own(0, t, p) + land_core[0, t, p]).astype(WIRE)
    for p in range(3):
        for direction in (0, 1):
            start(ring(direction, 0, direction * 3 + p))
    last = len(OFFSETS) - 1
    for step in range(1, HALF_Z):
        keys = [OFFSETS.index(HALF_Z - step), OFFSETS.index(step - HALF_Z)]
        for k in keys:
            swapped(k)
        for i in range(len(CHUNKS)):
            for direction in (0, 1):
                c = (i + 3 * (1 - direction)) % len(CHUNKS) if step == 1 else i
                t, p = CHUNKS[c]
                k = keys[direction]
                value = own(k, t, p) + land_core[k, t, p]
                if step > 1 or t == direction:
                    ring(direction, step - 1, c).wait_recv()
                    value = value + land[direction, step - 1, t, p].astype(f32)
                packet[k, t, p] = value.astype(WIRE)
                if step < HALF_Z - 1:
                    start(ring(direction, step, c))
                else:
                    start(last_hop(direction, c, 1))
                    start(last_hop(direction, c, 0))
        if step == HALF_Z - 1:
            swapped(last)
            for t in range(TILE_DEV):
                for p in range(3):
                    value = own(last, t, p) + land_core[last, t, p]
                    packet[last, t, p] = value.astype(WIRE)
                    land_core[last, t, p] = value
                start(own_copy(t))
    for t in range(TILE_DEV):
        own_copy(t).wait_recv()
    for c, (t, p) in enumerate(CHUNKS):
        value = land_core[last, t, p, hi] + land_own[t, p].astype(f32)
        for crossing in (0, 1):
            for direction in (0, 1):
                last_hop(direction, c, crossing).wait_recv()
                value = value + land_last[crossing, direction, t, p].astype(f32)
        out_ref[t, p] = value
    for copy in started:
        copy.wait_send()


def collect(acc):
    f32 = jnp.float32
    half = (TILE_DEV, 3, 2, STRIP, PIX)
    quarter = (TILE_DEV, 3, STRIP, PIX)
    return pl.pallas_call(
        collect_kernel,
        out_shape=jax.ShapeDtypeStruct(quarter, f32),
        in_specs=[VM],
        out_specs=VM,
        scratch_shapes=[
            pltpu.VMEM((NZ, *half), f32),
            pltpu.VMEM((NZ, *half), WIRE),
            pltpu.VMEM((2, HALF_Z - 1, *half), WIRE),
            pltpu.VMEM((2, 2, *quarter), WIRE),
            pltpu.VMEM(quarter, WIRE),
            DMA((NZ,)),
            DMA((NZ,)),
            DMA((2, HALF_Z - 1, 6)),
            DMA((2, HALF_Z - 1, 6)),
            DMA((2, 2, 6)),
            DMA((2, 2, 6)),
            DMA((2,)),
            DMA((2,)),
        ],
        compiler_params=pltpu.CompilerParams(collective_id=2, has_side_effects=True, vmem_limit_bytes=GRANT),
        name="collect",
    )(acc.reshape(NZ, TILE_DEV, 3, 2, 2, STRIP, PIX))


def body(
    sky_map, tile_home, piece_tiles, run_slot, hit_row, hit_col, frac_row, frac_col, angle, noise_coef
):
    pack = packed(
        tile_home, piece_tiles.reshape(1, LISTED), run_slot, hit_row, hit_col, frac_row, frac_col, angle,
        sky_map.reshape(TILE_DEV * 3 * STRIP, PIX),
    )
    tiles, samples, order = gather_all(pack)
    partial, turns = forward(
        order, tiles.reshape(NZ, N_STRIP, TILE_DEV, 3 * STRIP, PIX), samples
    )
    filtered = filtered_of(partial, noise_coef)
    acc = backward(order, samples, turns, filtered)
    return collect(acc)


def solution(mesh):
    placed = (
        P("tm", None, "det", None),
        P(),
        P("det", "tm", None),
        P("det", "tm"),
        P("det", "tm"),
        P("det", "tm"),
        P("det", "tm"),
        P("det", "tm"),
        P("det", "tm"),
        P("det", None),
    )
    return jax.shard_map(
        body, mesh=mesh, in_specs=placed, out_specs=P("tm", None, "det", None), check_vma=False
    )
```
